32 devices in a mesh: dp: 16 (over z, y, x), tensor: 2 (over core).
Axes of the slice: x: 2, y: 2, z: 4, core: 2. Of those that a mesh axis runs over, the one named last changes fastest.
Arguments:
- tokens: bfloat16 [32, 1024, 768], P('dp'), may hold values from -6 to 6
- segments: int32 [32, 1024], P('dp'), may hold values from 0 to 8, as said below
- qkv_weight: bfloat16 [768, 3, 768], P(('dp', 'tensor')), may hold values from -0.21875 to 0.21875
- out_weight: bfloat16 [768, 768], P(('dp', 'tensor')), may hold values from -1.75 to 1.75
- norm_gain: bfloat16 [768, 2], P(('dp', 'tensor')), may hold values from 0.5 to 1.5
- norm_shift: bfloat16 [768, 2], P(('dp', 'tensor')), may hold values from -3 to 3
- gate_up: bfloat16 [768, 2, 3072], P('dp', None, 'tensor'), may hold values from -0.21875 to 0.21875
- down_weight: bfloat16 [768, 3072], P('dp', 'tensor'), may hold values from -0.109375 to 0.109375
- cotangent: bfloat16 [32, 1024, 768], P('dp', 'tensor'), may hold values from -6 to 6
Outputs:
- output: bfloat16 [32, 1024, 768], P('dp', 'tensor')
- input_grad: float32 [32, 1024, 768], P('dp', 'tensor')
- qkv_grad: float32 [768, 3, 768], P(('dp', 'tensor'))
- out_weight_grad: float32 [768, 768], P(('dp', 'tensor'))
- gain_grad: float32 [768, 2], P(('dp', 'tensor'))
- shift_grad: float32 [768, 2], P(('dp', 'tensor'))
- gate_up_grad: float32 [768, 2, 3072], P('dp', None, 'tensor')
- down_grad: float32 [768, 3072], P('dp', 'tensor')
The draws below stay inside these ranges and needn't reach their ends.
Inputs may be any that keep to these rules, and one draw needn't show every extreme that they name: `segments`: never falling along a sequence; each of the 8 documents has at least one token, and exactly one of them holds 512 tokens, more than any other; the value 8 marks padding, which every sequence has.
All inputs are finite; a program needn't handle non-finite values.
Results may differ from the reference program's by a relative error of at most 0.015.
Values may be sent and summed in bfloat16 or wider, within the bound.
No kernel may reach another device: no remote copies, remote signals or barrier semaphores. Data moves between devices by JAX's collectives and lax.ppermute only.
A program may use at most 320 MiB of HBM per device.

```python
import jax
import jax.numpy as jnp
from jax import lax

D = 768
HEADS = 12
HEAD = 64
FF = 3072
SEQ = 1024
NDOC = 8
NSEQ = 32


def documents(key):
    base = jax.random.fold_in(key, 17)
    pad_key, power_key, extra_key, place_key = jax.random.split(base, 4)
    padding = jax.random.randint(pad_key, (NSEQ,), 1, SEQ // 8 + 1, dtype=jnp.int32)
    longest = SEQ // 2
    rest_tokens = SEQ - padding - longest
    others = NDOC - 1
    powers = jax.random.randint(power_key, (NSEQ, others), 0, 8, dtype=jnp.int32)
    extras = jax.random.randint(extra_key, (NSEQ, others), 1, 16, dtype=jnp.int32)
    weights = jnp.left_shift(jnp.ones_like(powers), powers) + extras
    spare_tokens = rest_tokens - others
    shares = 1 + spare_tokens[:, None] * weights // jnp.sum(weights, axis=1, keepdims=True)
    leftover = rest_tokens - jnp.sum(shares, axis=1)
    short_lengths = jnp.concatenate([shares[:, :1] + leftover[:, None], shares[:, 1:]], axis=1)
    place = jax.random.randint(place_key, (NSEQ, 1), 0, NDOC, dtype=jnp.int32)
    slots = jnp.arange(NDOC, dtype=jnp.int32)[None, :]
    source = jnp.clip(slots - (slots > place).astype(jnp.int32), 0, others - 1)
    picked = jnp.take_along_axis(short_lengths, source, axis=1)
    doc_lengths = jnp.where(slots == place, longest, picked).astype(jnp.int32)
    doc_ends = jnp.cumsum(doc_lengths, axis=1)
    places = jnp.arange(SEQ, dtype=jnp.int32)
    labels = jnp.sum((places[None, :, None] >= doc_ends[:, None, :]).astype(jnp.int32), axis=2)
    return labels.astype(jnp.int32)


def draw_segments(key, part):
    return documents(key)


def steps_of(own_key, extent, pieces, smallest, largest):
    loudness, own = 1.0, jax.random.fold_in(own_key, 6)
    for axis_at, parts in pieces:
        draws = jnp.exp(jax.random.uniform(jax.random.fold_in(own, axis_at), (parts,), jnp.float32, smallest / len(pieces), largest / len(pieces)))
        loudness = loudness * jnp.repeat(draws, extent[axis_at] // parts).reshape([-1 if axis == axis_at else 1 for axis in range(len(extent))])
    return loudness


def bell_draw(stream_key, extent, spread, bound, cuts=(), kind=jnp.bfloat16):
    values = spread * jax.random.normal(stream_key, extent, jnp.float32)
    if cuts:
        values = values * steps_of(stream_key, extent, cuts, -0.22, 0.18)
    return jnp.clip(values, -bound, bound).astype(kind)


def setup_inputs(seed: int = 0) -> dict:
    key_list = jax.random.split(jax.random.key(seed), 10)
    return {
        "tokens": bell_draw(key_list[0], (NSEQ, SEQ, D), 1.0, 6.0, ((0, 16),)),
        "segments": draw_segments(jax.random.fold_in(key_list[9], 71), 0),
        "qkv_weight": bell_draw(key_list[2], (D, 3, D), D ** -0.5, 0.21875, ((0, 32),)),
        "out_weight": bell_draw(key_list[3], (D, D), (D // 64) ** -0.5, 1.75, ((0, 32),)),
        "norm_gain": jnp.clip(1.0 + 0.1 * jax.random.normal(key_list[4], (D, 2), jnp.float32), 0.5, 1.5).astype(jnp.bfloat16),
        "norm_shift": bell_draw(key_list[5], (D, 2), 0.5, 3.0, ((0, 32),)),
        "gate_up": bell_draw(key_list[6], (D, 2, FF), D ** -0.5, 0.21875, ((0, 16), (2, 2))),
        "down_weight": bell_draw(key_list[7], (D, FF), FF ** -0.5, 0.109375, ((0, 16), (1, 2))),
        "cotangent": bell_draw(key_list[8], (NSEQ, SEQ, D), 1.0, 6.0, ((0, 16), (1, 2))),
    }


HIGHEST = lax.Precision.HIGHEST
EPSILON = 1e-05
MASKED = -1e+30

@jax.custom_vjp
def low(v):
    return lax.optimization_barrier(v.astype(jnp.bfloat16)).astype(jnp.float32)

@jax.custom_vjp
def low_back(v):
    return v

def low_keep(v):
    return (low(v), None)

def low_pass(kept, grad):
    return (grad,)

def back_keep(v):
    return (v, None)

def back_low(kept, grad):
    return (low(grad),)
low.defvjp(low_keep, low_pass)
low_back.defvjp(back_keep, back_low)

def rotary_tables(segment_row):
    labels = jnp.arange(NDOC + 1, dtype=jnp.int32)
    member = (segment_row[:, None] == labels[None, :]).astype(jnp.int32)
    counts = lax.optimization_barrier(jnp.sum(member, axis=0)).astype(jnp.int32)
    starts = jnp.concatenate([jnp.zeros((1,), jnp.int32), jnp.cumsum(counts)[:-1].astype(jnp.int32)])
    offset = lax.optimization_barrier(jnp.sum(member * starts[None, :], axis=1)).astype(jnp.int32)
    position = (jnp.arange(SEQ, dtype=jnp.int32) - offset).astype(jnp.float32)
    exponent = -2.0 * jnp.arange(HEAD // 2).astype(jnp.float32) / HEAD
    frequency = jnp.power(jnp.float32(1000.0), exponent).astype(jnp.float32)
    angle = position[:, None] * frequency[None, :]
    return (jnp.cos(angle)[:, None, :], jnp.sin(angle)[:, None, :])

def rotate(vector, cosine, sine):
    half = vector.shape[-1] // 2
    first_half = vector[..., :half]
    second_half = vector[..., half:]
    return jnp.concatenate([first_half * cosine - second_half * sine, second_half * cosine + first_half * sine], axis=-1)

def layer_norm(vector, gain, shift):
    center = vector - lax.optimization_barrier(jnp.mean(vector, axis=-1, keepdims=True))
    variance = lax.optimization_barrier(jnp.mean(center * center, axis=-1, keepdims=True))
    return center * lax.rsqrt(variance + EPSILON) * gain + shift

def sequence_layer(params, token_row, segment_row):
    qkv_w, out_w, gains, shifts, gate_up_w, down_w = params
    projected = low_back(jnp.einsum('sd,dke->ske', token_row, qkv_w, precision=HIGHEST))
    cosine, sine = rotary_tables(segment_row)
    head_shape = (SEQ, HEADS, HEAD)
    queries = low(rotate(projected[:, 0].reshape(head_shape), cosine, sine))
    keys = low(rotate(projected[:, 1].reshape(head_shape), cosine, sine))
    values = low(projected[:, 2].reshape(head_shape))
    scores = low_back(jnp.einsum('qhe,khe->hqk', queries, keys, precision=HIGHEST) * HEAD ** (-0.5))
    allowed = segment_row[:, None] == segment_row[None, :]
    masked = jnp.where(allowed[None], scores, MASKED)
    logsum = jax.nn.logsumexp(masked, axis=-1, keepdims=True)
    probs = jnp.exp(masked - logsum)
    context = jnp.einsum('hqk,khe->qhe', low(probs), values, precision=HIGHEST).reshape(SEQ, D)
    context = low(low_back(context))
    attended = low_back(jnp.dot(context, out_w, precision=HIGHEST))
    normed = layer_norm(token_row + attended, gains[:, 0], shifts[:, 0])
    normed_low = low(normed)
    gate_pair = low_back(jnp.einsum('sd,dkf->skf', normed_low, gate_up_w, precision=HIGHEST))
    swiglu = low(jax.nn.silu(gate_pair[:, 0]) * gate_pair[:, 1])
    mlp_out = low_back(jnp.einsum('sf,df->sd', swiglu, down_w, precision=HIGHEST))
    return layer_norm(normed + mlp_out, gains[:, 1], shifts[:, 1])

def reference(tokens, segments, qkv_weight, out_weight, norm_gain, norm_shift, gate_up, down_weight, cotangent):
    params = (qkv_weight.astype(jnp.float32), out_weight.astype(jnp.float32), norm_gain.astype(jnp.float32), norm_shift.astype(jnp.float32), gate_up.astype(jnp.float32), down_weight.astype(jnp.float32))
    layer = jax.checkpoint(sequence_layer)

    def forward(weights, inputs):

        def visit(carry, item):
            return (carry, layer(weights, item[0], item[1]))
        carry_out, outputs = lax.scan(visit, jnp.zeros((), jnp.float32), (inputs, segments))
        return outputs
    outputs, pullback = jax.vjp(forward, params, tokens.astype(jnp.float32))
    weight_grads, input_grad = pullback(cotangent.astype(jnp.float32))
    qkv_grad, out_grad, gain_grad, shift_grad, gate_up_grad, down_grad = weight_grads
    return (outputs.astype(jnp.bfloat16), input_grad, qkv_grad, out_grad, gain_grad, shift_grad, gate_up_grad, down_grad)
```

```python
import jax
import jax.numpy as jnp
from jax import lax
from jax.experimental import pallas as pl
from jax.experimental.pallas import tpu as pltpu
from jax.sharding import PartitionSpec as P

D = 768
HEADS = 12
HEAD = 64
SEQ = 1024
NDOC = 8


EPSILON = 1e-05
MASKED = -1e30


def for_sending(value):
    return jax.tree.map(lambda a: a.astype(jnp.bfloat16) if a.dtype == jnp.float32 else a, value)


def rotary_tables(segment_row):
    labels = jnp.arange(NDOC + 1, dtype=jnp.int32)
    member = (segment_row[:, None] == labels[None, :]).astype(jnp.int32)
    counts = jnp.sum(member, axis=0)
    starts = jnp.concatenate([jnp.zeros((1,), jnp.int32), jnp.cumsum(counts)[:-1]])
    offset = jnp.sum(member * starts[None, :], axis=1)
    position = (jnp.arange(SEQ, dtype=jnp.int32) - offset).astype(jnp.float32)
    exponent = -2.0 * jnp.arange(HEAD // 2).astype(jnp.float32) / HEAD
    frequency = jnp.power(jnp.float32(1000.0), exponent)
    angle = position[:, None] * frequency[None, :]
    return (jnp.cos(angle)[:, None, :], jnp.sin(angle)[:, None, :])


def rotate(vector, cosine, sine):
    half = vector.shape[-1] // 2
    first_half = vector[..., :half]
    second_half = vector[..., half:]
    return jnp.concatenate(
        [first_half * cosine - second_half * sine, second_half * cosine + first_half * sine],
        axis=-1,
    )


def unrotate(gradient, cosine, sine):

    def turned(vector):
        return rotate(vector, cosine, sine)

    _, pullback = jax.vjp(turned, gradient)
    return pullback(gradient)[0]


def layer_norm(vector, gain, shift):
    center = vector - jnp.mean(vector, axis=-1, keepdims=True)
    variance = jnp.mean(center * center, axis=-1, keepdims=True)
    return center * lax.rsqrt(variance + EPSILON) * gain + shift


def swiglu_piece(gate, upper):
    return jax.nn.silu(gate) * upper


def accumulate(total, term):
    if total is None:
        return term
    return tuple((left + right for left, right in zip(total, term)))


def general_device(
    tokens, segments, qkv_weight, out_weight, norm_gain, norm_shift, gate_up, down_weight, cotangent
):
    tensor_size = lax.axis_size("tensor")
    own_rows = SEQ // tensor_size
    row_start = lax.axis_index("tensor") * own_rows
    score_scale = HEAD ** (-0.5)
    qkv_full, out_full, gain_full, shift_full = (
        lax.all_gather(qkv_weight, ("dp", "tensor"), axis=0, tiled=True),
        lax.all_gather(out_weight, ("dp", "tensor"), axis=0, tiled=True),
        lax.all_gather(norm_gain, ("dp", "tensor"), axis=0, tiled=True),
        lax.all_gather(norm_shift, ("dp", "tensor"), axis=0, tiled=True),
    )
    gains = gain_full.astype(jnp.float32)
    shifts = shift_full.astype(jnp.float32)
    gate_up_full, down_full = (
        lax.all_gather(gate_up, "dp", axis=0, tiled=True),
        lax.all_gather(down_weight, "dp", axis=0, tiled=True),
    )
    batches = tokens.shape[0]
    outputs = []
    input_grads = []
    attn_total = None
    mlp_total = None
    for batch_index in range(batches):
        source = tokens[batch_index]
        own_source = lax.dynamic_slice_in_dim(source, row_start, own_rows, 0)
        segment_row = segments[batch_index]
        cosine, sine = rotary_tables(segment_row)
        own_cos = lax.dynamic_slice_in_dim(cosine, row_start, own_rows, 0)
        own_sin = lax.dynamic_slice_in_dim(sine, row_start, own_rows, 0)
        query_proj = jnp.einsum(
            "sd,de->se", own_source, qkv_full[:, 0], preferred_element_type=jnp.float32
        )
        pair_proj = jnp.einsum(
            "sd,dke->ske", source, qkv_full[:, 1:], preferred_element_type=jnp.float32
        )
        keys = rotate(pair_proj[:, 0].reshape(SEQ, HEADS, HEAD), cosine, sine).astype(jnp.bfloat16)
        values = pair_proj[:, 1].reshape(SEQ, HEADS, HEAD).astype(jnp.bfloat16)
        queries = rotate(query_proj.reshape(own_rows, HEADS, HEAD), own_cos, own_sin).astype(
            jnp.bfloat16
        )
        own_segments = lax.dynamic_slice_in_dim(segment_row, row_start, own_rows, 0)
        allowed = (own_segments[:, None] == segment_row[None, :])[None]
        raw_scores = (
            jnp.einsum("qhe,khe->hqk", queries, keys, preferred_element_type=jnp.float32)
            * score_scale
        )
        masked = jnp.where(allowed, raw_scores, MASKED)
        top_score = jnp.max(masked, axis=-1, keepdims=True)
        logsum = top_score + jnp.log(jnp.sum(jnp.exp(masked - top_score), axis=-1, keepdims=True))
        probs_low = jnp.exp(masked - logsum).astype(jnp.bfloat16)
        context = (
            jnp.einsum("hqk,khe->qhe", probs_low, values, preferred_element_type=jnp.float32)
            .reshape(own_rows, D)
            .astype(jnp.bfloat16)
        )
        attended = jnp.dot(context, out_full, preferred_element_type=jnp.float32)
        hidden_in = own_source.astype(jnp.float32) + attended
        normed = layer_norm(hidden_in, gains[:, 0], shifts[:, 0])
        normed_all = lax.all_gather(normed.astype(jnp.bfloat16), "tensor", axis=0, tiled=True)
        gate_pair = jnp.einsum(
            "sd,dkf->skf", normed_all, gate_up_full, preferred_element_type=jnp.float32
        )
        swiglu = swiglu_piece(gate_pair[:, 0], gate_pair[:, 1]).astype(jnp.bfloat16)
        mlp_out = lax.psum_scatter(
            jnp.einsum("sf,df->sd", swiglu, down_full, preferred_element_type=jnp.float32).astype(
                jnp.bfloat16
            ),
            "tensor",
            scatter_dimension=0,
            tiled=True,
        ).astype(jnp.float32)
        resid = normed + mlp_out
        outputs.append(layer_norm(resid, gains[:, 1], shifts[:, 1]).astype(jnp.bfloat16))
        upstream = cotangent[batch_index].astype(jnp.float32)
        _, second_pull = jax.vjp(layer_norm, resid, gains[:, 1], shifts[:, 1])
        resid_grad, gain_two, shift_two = second_pull(upstream)
        mlp_grad = lax.all_gather(resid_grad.astype(jnp.bfloat16), "tensor", axis=0, tiled=True)
        swiglu_grad = jnp.einsum(
            "sd,df->sf", mlp_grad, down_full, preferred_element_type=jnp.float32
        )
        _, glu_pull = jax.vjp(swiglu_piece, gate_pair[:, 0], gate_pair[:, 1])
        gate_grad, upper_grad = glu_pull(swiglu_grad)
        pair_grad = jnp.stack([gate_grad, upper_grad], axis=1).astype(jnp.bfloat16)
        down_term = jnp.einsum("sd,sf->df", mlp_grad, swiglu, preferred_element_type=jnp.float32)
        gate_up_term = jnp.einsum(
            "sd,skf->dkf", normed_all, pair_grad, preferred_element_type=jnp.float32
        )
        normed_grad = resid_grad + lax.psum_scatter(
            jnp.einsum("skf,dkf->sd", pair_grad, gate_up_full, preferred_element_type=jnp.float32),
            "tensor",
            scatter_dimension=0,
            tiled=True,
        )
        _, first_pull = jax.vjp(layer_norm, hidden_in, gains[:, 0], shifts[:, 0])
        hidden_grad, gain_one, shift_one = first_pull(normed_grad)
        attended_grad = hidden_grad.astype(jnp.bfloat16)
        out_term = jnp.einsum(
            "sd,se->de", context, attended_grad, preferred_element_type=jnp.float32
        )
        context_grad = (
            jnp.einsum("se,de->sd", attended_grad, out_full, preferred_element_type=jnp.float32)
            .astype(jnp.bfloat16)
            .reshape(own_rows, HEADS, HEAD)
        )
        probs = jnp.exp(masked - logsum)
        weights_grad = jnp.einsum(
            "qhe,khe->hqk", context_grad, values, preferred_element_type=jnp.float32
        )
        row_delta = jnp.sum(probs * weights_grad, axis=-1, keepdims=True)
        score_grad = (probs * (weights_grad - row_delta)).astype(jnp.bfloat16)
        query_grad = (
            jnp.einsum("hqk,khe->qhe", score_grad, keys, preferred_element_type=jnp.float32)
            * score_scale
        )
        key_part = (
            jnp.einsum("hqk,qhe->khe", score_grad, queries, preferred_element_type=jnp.float32)
            * score_scale
        )
        value_part = jnp.einsum(
            "hqk,qhe->khe", probs_low, context_grad, preferred_element_type=jnp.float32
        )
        key_value = lax.psum_scatter(
            jnp.stack(
                [
                    key_part.reshape(lax.axis_size("tensor") * own_rows, D),
                    value_part.reshape(lax.axis_size("tensor") * own_rows, D),
                ],
                axis=1,
            ).astype(jnp.bfloat16),
            "tensor",
            scatter_dimension=0,
            tiled=True,
        ).astype(jnp.float32)
        query_back = unrotate(query_grad, own_cos, own_sin).reshape(own_rows, D)
        key_back = unrotate(
            key_value[:, 0].reshape(own_rows, HEADS, HEAD), own_cos, own_sin
        ).reshape(own_rows, D)
        proj_grad = jnp.stack([query_back, key_back, key_value[:, 1]], axis=1).astype(jnp.bfloat16)
        input_grads.append(
            hidden_grad
            + jnp.einsum("ske,dke->sd", proj_grad, qkv_full, preferred_element_type=jnp.float32)
        )
        qkv_term = jnp.einsum(
            "sd,ske->dke", own_source, proj_grad, preferred_element_type=jnp.float32
        )
        gain_term = jnp.stack([gain_one, gain_two], axis=1)
        shift_term = jnp.stack([shift_one, shift_two], axis=1)
        attn_terms = (qkv_term, out_term, gain_term, shift_term)
        mlp_terms = (gate_up_term, down_term)
        attn_total = accumulate(attn_total, attn_terms)
        mlp_total = accumulate(mlp_total, mlp_terms)
    attn_final = lax.psum_scatter(attn_total, ("dp", "tensor"), scatter_dimension=0, tiled=True)
    mlp_final = jax.tree.map(
        lambda part: part.astype(jnp.float32),
        lax.psum_scatter(for_sending(mlp_total), "dp", scatter_dimension=0, tiled=True),
    )
    return (
        jnp.stack(outputs, axis=0),
        jnp.stack(input_grads, axis=0),
        attn_final[0],
        attn_final[1],
        attn_final[2],
        attn_final[3],
        mlp_final[0],
        mlp_final[1],
    )


HIDDEN = 1536
WIDE = 3 * HIDDEN
ATTN = 4 * D + 256
PAIRS = HEADS // 2
LANES = 2 * HEAD
BLOCK = 256
NBLOCK = SEQ // BLOCK
ROWS = 256
CHUNK = 512
LOG2E = 1.4426950408889634
F32 = jnp.float32
BF16 = jnp.bfloat16


def across(value, move):
    pairs = []
    for z in range(4):
        for y in range(2):
            for x in range(2):
                for c in range(2):
                    tz, ty, tx, tc = move(z, y, x, c)
                    pairs.append((((z * 2 + y) * 2 + x) * 2 + c, ((tz * 2 + ty) * 2 + tx) * 2 + tc))
    return lax.ppermute(value, ("dp", "tensor"), pairs)


def core_swap(value):
    return across(value, lambda z, y, x, c: (z, y, x, 1 - c))


def first_swap(value):
    return across(value, lambda z, y, x, c: (z, y, 1 - x, c) if c == 0 else (z, 1 - y, x, c))


def second_swap(value):
    return across(value, lambda z, y, x, c: (z, 1 - y, x, c) if c == 0 else (z, y, 1 - x, c))


def depth_shift(value, steps):
    return across(value, lambda z, y, x, c: ((z + steps) % 4, y, x, c))


def slot_blocks(sign, core):
    me = lax.axis_index("dp")
    z, y, x = me // 4, (me // 2) % 2, me % 2
    slot = jnp.arange(16, dtype=jnp.int32)
    second, first, depth = slot // 8, (slot // 4) % 2, slot % 4
    x_bit = jnp.where(core == 0, first, second)
    y_bit = jnp.where(core == 0, second, first)
    return (((z + sign * depth) % 4) * 4 + (y ^ y_bit) * 2 + (x ^ x_bit)).astype(jnp.int32)


def gather_stages(block):
    parts = [block] + [depth_shift(block, k) for k in (1, 2, 3)]
    four = jnp.stack(parts, axis=0)
    eight = jnp.concatenate([four, first_swap(four)], axis=0)
    return eight, second_swap(eight)


def reduce_stages(local):
    once = local[0] + first_swap(local[1])
    twice = once[0] + second_swap(once[1])
    total = twice[0].astype(F32)
    for k in (1, 2, 3):
        total = total + depth_shift(twice[k], k).astype(F32)
    return total


def cost(flops, nbytes, trans=0):
    return pl.CostEstimate(flops=int(flops), bytes_accessed=int(nbytes), transcendentals=int(trans))


def params(vmem_mb, sem=("arbitrary",)):
    return pltpu.CompilerParams(dimension_semantics=sem, vmem_limit_bytes=vmem_mb << 20)


ANY = pl.BlockSpec(memory_space=pl.ANY)


def assemble_attn(own, other, index):
    def body(idx, a, b, c, d, out, sem):
        copies = []
        for i, ref in enumerate((a, b, c, d)):
            for s in range(8):
                copies.append(
                    pltpu.make_async_copy(ref.at[s], out.at[idx[i * 8 + s]], sem.at[i * 8 + s])
                )
        for cp in copies:
            cp.start()
        for cp in copies:
            cp.wait()

    rows = own[0].shape[1]
    return pl.pallas_call(
        body,
        grid_spec=pltpu.PrefetchScalarGridSpec(
            num_scalar_prefetch=1,
            grid=(1,),
            in_specs=[ANY] * 4,
            out_specs=ANY,
            scratch_shapes=[pltpu.SemaphoreType.DMA((32,))],
        ),
        out_shape=jax.ShapeDtypeStruct((32, rows, ATTN), BF16),
        compiler_params=params(16),
        cost_estimate=cost(0, 4 * 32 * rows * ATTN),
        name="assemble",
    )(index, *own, *other)


def turn(vector, cosine, sine):
    lane = lax.broadcasted_iota(jnp.int32, vector.shape, 1)
    swapped = jnp.where(
        lane % HEAD < HEAD // 2,
        pltpu.roll(vector, LANES - HEAD // 2, 1),
        pltpu.roll(vector, HEAD // 2, 1),
    )
    return vector * cosine + swapped * sine


def dot_nn(a, b):
    return lax.dot_general(a, b, (((1,), (0,)), ((), ())), preferred_element_type=F32)


def dot_nt(a, b):
    return lax.dot_general(a, b, (((1,), (1,)), ((), ())), preferred_element_type=F32)


def dot_tn(a, b):
    return lax.dot_general(a, b, (((0,), (0,)), ((), ())), preferred_element_type=F32)


def attn_forward(bounds, source, weights, cosine, sine, seg_col, seg_row):
    def body(bnd, x, wq, wk, wv, cos, sin, sc, sr, q_out, k_out, v_out, ctx_out, lse_out):
        low_lane = lax.broadcasted_iota(jnp.int32, (BLOCK, LANES), 1) < HEAD
        for r in range(NBLOCK):
            rows = pl.ds(r * BLOCK, BLOCK)
            xr, cr, sn = x[rows, :], cos[rows, :], sin[rows, :]
            q = turn(dot_nn(xr, wq[...]), cr, sn).astype(BF16)
            q_out[rows, :] = q * jnp.asarray(HEAD**-0.5, BF16)
            k_out[rows, :] = turn(dot_nn(xr, wk[...]), cr, sn).astype(BF16)
            v_out[rows, :] = dot_nn(xr, wv[...]).astype(BF16)
        for i in range(NBLOCK):
            rows = pl.ds(i * BLOCK, BLOCK)
            q = q_out[rows, :]
            zero = jnp.zeros_like(q)
            heads = (jnp.where(low_lane, q, zero), jnp.where(low_lane, zero, q))
            own_seg = sc[rows, :]

            def step(j, carry):
                tops, sums, acc = carry
                cols = pl.ds(pl.multiple_of(j * BLOCK, BLOCK), BLOCK)
                k, v = k_out[cols, :], v_out[cols, :]
                seen = own_seg == sr[:, cols]
                new_tops, new_sums, alphas, parts = [], [], [], []
                for h in range(2):
                    s = jnp.where(seen, dot_nt(heads[h], k) * LOG2E, MASKED)
                    top = jnp.maximum(tops[h], jnp.max(s, axis=1, keepdims=True))
                    p = jnp.exp2(s - top)
                    alpha = jnp.exp2(tops[h] - top)
                    new_tops.append(top)
                    alphas.append(alpha)
                    new_sums.append(sums[h] * alpha + jnp.sum(p, axis=1, keepdims=True))
                    parts.append(dot_nn(p.astype(BF16), v))
                acc = acc * jnp.where(low_lane, alphas[0], alphas[1]) + jnp.where(
                    low_lane, parts[0], parts[1]
                )
                return tuple(new_tops), tuple(new_sums), acc

            start = jnp.full((BLOCK, 1), MASKED, F32)
            none = jnp.zeros((BLOCK, 1), F32)
            tops, sums, acc = lax.fori_loop(
                bnd[i],
                bnd[NBLOCK + i],
                step,
                ((start, start), (none, none), jnp.zeros((BLOCK, LANES), F32)),
            )
            ctx_out[rows, :] = (acc / jnp.where(low_lane, sums[0], sums[1])).astype(BF16)
            both = jnp.where(
                low_lane, tops[0] + jnp.log2(sums[0]), tops[1] + jnp.log2(sums[1])
            )
            flipped = both.T
            lse_out[0, 0:1, i * BLOCK : (i + 1) * BLOCK] = flipped[0:1]
            lse_out[0, 1:2, i * BLOCK : (i + 1) * BLOCK] = flipped[HEAD : HEAD + 1]

    full = lambda shape: pl.BlockSpec(shape, lambda p, b: (0,) * len(shape))
    column = lambda shift: pl.BlockSpec((D, LANES), lambda p, b: (0, shift * PAIRS + p))
    pair = pl.BlockSpec((SEQ, LANES), lambda p, b: (0, p))
    act = jax.ShapeDtypeStruct((SEQ, D), BF16)
    return pl.pallas_call(
        body,
        grid_spec=pltpu.PrefetchScalarGridSpec(
            num_scalar_prefetch=1,
            grid=(PAIRS,),
            in_specs=[
                full((SEQ, D)),
                column(0),
                column(1),
                column(2),
                full((SEQ, LANES)),
                full((SEQ, LANES)),
                full((SEQ, 1)),
                full((1, SEQ)),
            ],
            out_specs=[pair, pair, pair, pair, pl.BlockSpec((1, 8, SEQ), lambda p, b: (p, 0, 0))],
        ),
        out_shape=[act, act, act, act, jax.ShapeDtypeStruct((PAIRS, 8, SEQ), F32)],
        compiler_params=params(32),
        cost_estimate=cost(2 * SEQ * D * 3 * D + 16 * SEQ * SEQ * D, 16 << 20, HEADS * SEQ * SEQ),
        name="attn_forward",
    )(bounds, source, weights, weights, weights, cosine, sine, seg_col, seg_row)


def attn_backward(bounds, q, k, v, ctx, ctx_grad, lse, cosine, sine, seg_col, seg_row):
    def body(bnd, q, k, v, o, do, lse, cos, sin, sc, sr, out, qm, km, vm, dom, dq, dk, dv, dl):
        low_lane = lax.broadcasted_iota(jnp.int32, (SEQ, LANES), 1) < HEAD
        zero = jnp.zeros((SEQ, LANES), BF16)
        for ref, kept in ((q, qm), (k, km), (v, vm), (do, dom)):
            kept[0] = jnp.where(low_lane, ref[...], zero)
            kept[1] = jnp.where(low_lane, zero, ref[...])
        row = lax.broadcasted_iota(jnp.int32, (8, LANES), 0)
        lane = lax.broadcasted_iota(jnp.int32, (8, LANES), 1)
        pick = jnp.where(row == lane // HEAD, 1.0, 0.0).astype(F32)
        product = do[...].astype(F32) * o[...].astype(F32)
        dl[...] = lax.dot_general(
            pick,
            product,
            (((1,), (1,)), ((), ())),
            preferred_element_type=F32,
            precision=lax.Precision.HIGHEST,
        )
        dk[...] = jnp.zeros_like(dk)
        dv[...] = jnp.zeros_like(dv)
        for i in range(NBLOCK):
            rows = pl.ds(i * BLOCK, BLOCK)
            own_seg = sr[:, rows]
            lses = [lse[0, h : h + 1, i * BLOCK : (i + 1) * BLOCK] for h in range(2)]
            deltas = [dl[h : h + 1, i * BLOCK : (i + 1) * BLOCK] for h in range(2)]

            def step(j, acc):
                cols = pl.ds(pl.multiple_of(j * BLOCK, BLOCK), BLOCK)
                seen = sc[cols, :] == own_seg
                probs, grads = [], []
                for h in range(2):
                    s = dot_nt(km[h, cols, :], q[rows, :]) * LOG2E - lses[h]
                    p = jnp.exp2(jnp.where(seen, s, MASKED))
                    dp = dot_nt(vm[h, cols, :], do[rows, :])
                    probs.append(p.astype(BF16))
                    grads.append((p * (dp - deltas[h])).astype(BF16))
                dv[cols, :] += dot_nn(probs[0], dom[0, rows, :]) + dot_nn(probs[1], dom[1, rows, :])
                dk[cols, :] += dot_nn(grads[0], qm[0, rows, :]) + dot_nn(grads[1], qm[1, rows, :])
                return acc + dot_tn(grads[0], km[0, cols, :]) + dot_tn(grads[1], km[1, cols, :])

            dq[rows, :] = lax.fori_loop(
                bnd[i], bnd[NBLOCK + i], step, jnp.zeros((BLOCK, LANES), F32)
            )
        for r in range(NBLOCK):
            rows = pl.ds(r * BLOCK, BLOCK)
            cr, sn = cos[rows, :], -sin[rows, :]
            out[0, rows, :] = turn(dq[rows, :] * (HEAD**-0.5), cr, sn).astype(BF16)
            out[1, rows, :] = turn(dk[rows, :], cr, sn).astype(BF16)
            out[2, rows, :] = dv[rows, :].astype(BF16)

    full = lambda shape: pl.BlockSpec(shape, lambda p, b: (0,) * len(shape))
    pair = pl.BlockSpec((SEQ, LANES), lambda p, b: (0, p))
    low2 = pltpu.VMEM((2, SEQ, LANES), BF16)
    wide = pltpu.VMEM((SEQ, LANES), F32)
    return pl.pallas_call(
        body,
        grid_spec=pltpu.PrefetchScalarGridSpec(
            num_scalar_prefetch=1,
            grid=(PAIRS,),
            in_specs=[
                pair,
                pair,
                pair,
                pair,
                pair,
                pl.BlockSpec((1, 8, SEQ), lambda p, b: (p, 0, 0)),
                full((SEQ, LANES)),
                full((SEQ, LANES)),
                full((SEQ, 1)),
                full((1, SEQ)),
            ],
            out_specs=pl.BlockSpec((3, SEQ, LANES), lambda p, b: (0, 0, p)),
            scratch_shapes=[low2, low2, low2, low2, wide, wide, wide, pltpu.VMEM((8, SEQ), F32)],
        ),
        out_shape=jax.ShapeDtypeStruct((3, SEQ, D), BF16),
        compiler_params=params(32),
        cost_estimate=cost(40 * SEQ * SEQ * D, 16 << 20, HEADS * SEQ * SEQ),
        name="attn_backward",
    )(bounds, q, k, v, ctx, ctx_grad, lse, cosine, sine, seg_col, seg_row)


def middle(index, source, ctx, cot, out_weight, norms, own, other):
    def norm(v):
        center = v - jnp.mean(v, axis=1, keepdims=True)
        scale = lax.rsqrt(jnp.mean(center * center, axis=1, keepdims=True) + EPSILON)
        return center * scale, scale

    def norm_back(u, hat, scale, gain):
        g = u * gain
        return scale * (
            g - jnp.mean(g, axis=1, keepdims=True) - hat * jnp.mean(g * hat, axis=1, keepdims=True)
        )

    def body(
        idx, x, ctx, cot, wo, nrm, a, b, c, d,
        out, normed_out, mlp_out, att_out, ctxg_out, hid_out, gu0, gu1, sw0, sw1, sums,
        w, gate_s, up_s, sem,
    ):
        step = pl.program_id(0)

        @pl.when(step == 0)
        def _():
            copies = []
            for i, ref in enumerate((a, b, c, d)):
                for s in range(8):
                    n = i * 8 + s
                    place = pl.ds(pl.multiple_of(idx[n] * 48, 16), 48)
                    copies.append(
                        pltpu.make_async_copy(ref.at[s], w.at[i // 2, place, :], sem.at[n])
                    )
            for cp in copies:
                cp.start()
            for cp in copies:
                cp.wait()
            sums[...] = jnp.zeros_like(sums)

        gain1, gain2, shift1, shift2 = (nrm[i : i + 1, :] for i in range(4))
        hidden_in = x[...].astype(F32) + dot_nn(ctx[...], wo[...])
        hat1, scale1 = norm(hidden_in)
        normed = hat1 * gain1 + shift1
        low = normed.astype(BF16)
        normed_out[...] = low
        total = normed
        for half in range(2):
            sw = (sw0, sw1)[half]
            for n in range(HIDDEN // CHUNK):
                g_at, u_at, d_at = (pl.ds(p * HIDDEN + n * CHUNK, CHUNK) for p in range(3))
                gate = dot_nn(low, w[half, :, g_at])
                up = dot_nn(low, w[half, :, u_at])
                gate_s[half, :, g_at] = gate
                up_s[half, :, g_at] = up
                act = (gate * jax.nn.sigmoid(gate) * up).astype(BF16)
                sw[:, g_at] = act
                total = total + dot_nt(act, w[half, :, d_at])
        hat2, scale2 = norm(total)
        out[...] = (hat2 * gain2 + shift2).astype(BF16)
        u2 = cot[...].astype(F32)
        resid = norm_back(u2, hat2, scale2, gain2)
        mlp = resid.astype(BF16)
        mlp_out[...] = mlp
        back = resid
        for half in range(2):
            gu = (gu0, gu1)[half]
            for n in range(HIDDEN // CHUNK):
                g_at, u_at, d_at = (pl.ds(p * HIDDEN + n * CHUNK, CHUNK) for p in range(3))
                grad = dot_nn(mlp, w[half, :, d_at])
                gate, up = gate_s[half, :, g_at], up_s[half, :, g_at]
                s = jax.nn.sigmoid(gate)
                gate_grad = (grad * up * (s * (1.0 + gate * (1.0 - s)))).astype(BF16)
                up_grad = (grad * (gate * s)).astype(BF16)
                gu[:, g_at] = gate_grad
                gu[:, u_at] = up_grad
                back = back + dot_nt(gate_grad, w[half, :, g_at])
                back = back + dot_nt(up_grad, w[half, :, u_at])
        hidden_grad = norm_back(back, hat1, scale1, gain1)
        hid_out[...] = hidden_grad
        att = hidden_grad.astype(BF16)
        att_out[...] = att
        ctxg_out[...] = dot_nt(att, wo[...]).astype(BF16)
        for i, v in enumerate((back * hat1, u2 * hat2, back, u2)):
            sums[i : i + 1, :] += jnp.sum(v, axis=0, keepdims=True)

    row = pl.BlockSpec((ROWS, D), lambda r, i: (r, 0))
    wide = lambda n: pl.BlockSpec((ROWS, n), lambda r, i: (r, 0))
    whole = lambda shape: pl.BlockSpec(shape, lambda r, i: (0,) * len(shape))
    act = lambda n, t=BF16: jax.ShapeDtypeStruct((SEQ, n), t)
    return pl.pallas_call(
        body,
        grid_spec=pltpu.PrefetchScalarGridSpec(
            num_scalar_prefetch=1,
            grid=(SEQ // ROWS,),
            in_specs=[row, row, row, whole((D, D)), whole((8, D)), ANY, ANY, ANY, ANY],
            out_specs=[row] * 6
            + [wide(2 * HIDDEN)] * 2
            + [wide(HIDDEN)] * 2
            + [whole((8, D))],
            scratch_shapes=[
                pltpu.VMEM((2, D, WIDE), BF16),
                pltpu.VMEM((2, ROWS, HIDDEN), F32),
                pltpu.VMEM((2, ROWS, HIDDEN), F32),
                pltpu.SemaphoreType.DMA((32,)),
            ],
        ),
        out_shape=[
            act(D),
            act(D),
            act(D),
            act(D),
            act(D),
            act(D, F32),
            act(2 * HIDDEN),
            act(2 * HIDDEN),
            act(HIDDEN),
            act(HIDDEN),
            jax.ShapeDtypeStruct((8, D), F32),
        ],
        compiler_params=params(56),
        cost_estimate=cost(12 * SEQ * D * 2 * HIDDEN + 4 * SEQ * D * D, 60 << 20, 4 * SEQ * HIDDEN),
        name="middle",
    )(index, source, ctx, cot, out_weight, norms, *own, *other)


def join_mlp(index, gu, gu_there, down, down_there):
    def body(idx, a, b, c, d, out):
        add = lambda p, q: (p[...].astype(F32) + q[...].astype(F32)).astype(BF16)
        out[0, :, : 2 * HIDDEN] = add(a, b)
        out[0, :, 2 * HIDDEN :] = add(c, d)

    rows = D // 16
    pick = lambda n: pl.BlockSpec((rows, n), lambda s, i: (i[s], 0))
    return pl.pallas_call(
        body,
        grid_spec=pltpu.PrefetchScalarGridSpec(
            num_scalar_prefetch=1,
            grid=(16,),
            in_specs=[pick(2 * HIDDEN), pick(2 * HIDDEN), pick(HIDDEN), pick(HIDDEN)],
            out_specs=pl.BlockSpec((1, rows, WIDE), lambda s, i: (s, 0, 0)),
        ),
        out_shape=jax.ShapeDtypeStruct((16, rows, WIDE), BF16),
        compiler_params=params(32),
        cost_estimate=cost(D * WIDE, 6 * D * WIDE),
        name="join_mlp",
    )(index, gu, gu_there, down, down_there)


def join_attn(index, grads, there):
    def body(idx, a, b, out):
        out[...] = (a[...].astype(F32) + b[...].astype(F32)).astype(BF16)

    rows = D // 32
    block = (1, rows, ATTN)
    return pl.pallas_call(
        body,
        grid_spec=pltpu.PrefetchScalarGridSpec(
            num_scalar_prefetch=1,
            grid=(16,),
            in_specs=[
                pl.BlockSpec(block, lambda s, i: (i[s] * 2 + i[16], 0, 0)),
                pl.BlockSpec(block, lambda s, i: (i[s], 0, 0)),
            ],
            out_specs=pl.BlockSpec(block, lambda s, i: (s, 0, 0)),
        ),
        out_shape=jax.ShapeDtypeStruct((16, rows, ATTN), BF16),
        compiler_params=params(32),
        cost_estimate=cost(D * ATTN // 2, 3 * D * ATTN),
        name="join_attn",
    )(index, grads, there)


def rotary_lanes(segment_row):
    labels = jnp.arange(NDOC + 1, dtype=jnp.int32)
    before = jnp.sum((segment_row[None, :] < labels[:, None]).astype(jnp.int32), axis=1)
    member = segment_row[:, None] == labels[None, :]
    first = jnp.sum(jnp.where(member, before[None, :], 0), axis=1)
    position = (jnp.arange(SEQ, dtype=jnp.int32) - first).astype(F32)
    lane = jnp.arange(LANES) % (HEAD // 2)
    frequency = jnp.power(F32(1000.0), -2.0 * lane.astype(F32) / HEAD)
    angle = position[:, None] * frequency[None, :]
    sign = jnp.where(jnp.arange(LANES) % HEAD < HEAD // 2, -1.0, 1.0)
    ends = jnp.concatenate([before[1:], jnp.full((1,), SEQ, jnp.int32)])
    heads = segment_row[::BLOCK]
    tails = segment_row[BLOCK - 1 :: BLOCK]
    low = jnp.sum(jnp.where(heads[:, None] == labels[None, :], before[None, :], 0), axis=1)
    high = jnp.sum(jnp.where(tails[:, None] == labels[None, :], ends[None, :], 0), axis=1)
    bounds = jnp.concatenate([low // BLOCK, (high + BLOCK - 1) // BLOCK]).astype(jnp.int32)
    return jnp.cos(angle), jnp.sin(angle) * sign[None, :], bounds


def sequence_device(
    tokens, segments, qkv_weight, out_weight, norm_gain, norm_shift, gate_up, down_weight, cotangent
):
    core = lax.axis_index("tensor")
    half = SEQ // 2

    def ordered(mine, theirs):
        return jnp.where(
            core == 0, jnp.stack([mine, theirs], axis=0), jnp.stack([theirs, mine], axis=0)
        )

    pick = lambda a, i: lax.dynamic_index_in_dim(a, i, 0, keepdims=False)
    source = pick(tokens, core)
    segment_row = pick(segments, core)

    attn_block = jnp.concatenate(
        [
            qkv_weight.reshape(-1, 3 * D),
            out_weight,
            norm_gain,
            norm_shift,
            jnp.zeros((out_weight.shape[0], 252), BF16),
        ],
        axis=1,
    )
    mlp_block = jnp.concatenate([gate_up.reshape(-1, 2 * HIDDEN), down_weight], axis=1)

    from_here, from_there = slot_blocks(-1, core), slot_blocks(-1, 1 - core)
    attn_own = gather_stages(attn_block)
    attn_other = tuple(core_swap(part) for part in attn_own)
    index = jnp.concatenate([from_here * 2 + core, from_there * 2 + 1 - core]).astype(jnp.int32)
    weights = assemble_attn(attn_own, attn_other, index).reshape(D, ATTN)

    mlp_own = gather_stages(mlp_block)
    mlp_other = tuple(core_swap(part) for part in mlp_own)

    cot = ordered(pick(cotangent, core), core_swap(pick(cotangent, 1 - core))).reshape(SEQ, D)
    cosine, sine, bounds = rotary_lanes(segment_row)
    seg_col, seg_row = segment_row[:, None], segment_row[None, :]

    q, k, v, ctx, lse = attn_forward(bounds, source, weights, cosine, sine, seg_col, seg_row)
    norms = weights[:, 4 * D : 4 * D + 8].astype(F32).T
    norms = jnp.stack([norms[0], norms[1], norms[2], norms[3]] + [norms[4]] * 4, axis=0)
    out_full = weights[:, 3 * D : 4 * D]
    (out, normed, mlp_grad, att_grad, ctx_grad, hidden_grad, gu0, gu1, sw0, sw1, sums) = middle(
        jnp.concatenate([from_here, from_there]), source, ctx, cot, out_full, norms, mlp_own, mlp_other
    )

    wgrad = lambda a, b: lax.dot_general(
        a, b, (((0,), (0,)), ((), ())), preferred_element_type=F32
    ).astype(BF16)
    to_here = slot_blocks(1, core).reshape(2, 2, 4).transpose(1, 0, 2).reshape(16)
    down_mine, down_theirs = wgrad(mlp_grad, sw0), wgrad(mlp_grad, sw1)
    gu_mine, gu_theirs = wgrad(normed, gu0), wgrad(normed, gu1)
    joined = join_mlp(to_here, gu_mine, core_swap(gu_theirs), down_mine, core_swap(down_theirs))
    mlp_total = reduce_stages(joined.reshape(2, 2, 4, D // 16, WIDE))

    projected = attn_backward(bounds, q, k, v, ctx, ctx_grad, lse, cosine, sine, seg_col, seg_row)
    qkv_term = [wgrad(source, projected[i]) for i in range(3)]
    out_term = wgrad(ctx, att_grad)
    norm_term = jnp.pad(sums[:4].T, ((0, 0), (0, 252))).astype(BF16)
    grads = jnp.concatenate(qkv_term + [out_term, norm_term], axis=1).reshape(16, 2, D // 32, ATTN)
    leaving = lax.dynamic_index_in_dim(grads, 1 - core, 1, keepdims=False)
    where = jnp.concatenate([to_here, core[None]]).astype(jnp.int32)
    joined = join_attn(where, grads.reshape(32, D // 32, ATTN), core_swap(leaving))
    attn_total = reduce_stages(joined.reshape(2, 2, 4, D // 32, ATTN))

    input_grad = hidden_grad
    for i in range(3):
        input_grad = input_grad + lax.dot_general(
            projected[i],
            weights[:, i * D : (i + 1) * D],
            (((1,), (1,)), ((), ())),
            preferred_element_type=F32,
        )

    def spread(whole):
        parts = whole.reshape(2, half, D)
        return ordered(pick(parts, core), core_swap(pick(parts, 1 - core)))

    return (
        spread(out),
        spread(input_grad),
        attn_total[:, : 3 * D].reshape(-1, 3, D),
        attn_total[:, 3 * D : 4 * D],
        attn_total[:, 4 * D : 4 * D + 2],
        attn_total[:, 4 * D + 2 : 4 * D + 4],
        mlp_total[:, : 2 * HIDDEN].reshape(-1, 2, HIDDEN),
        mlp_total[:, 2 * HIDDEN :],
    )


def solution(mesh):
    in_specs = (
        P("dp", None, None),
        P("dp", None),
        P(("dp", "tensor"), None, None),
        P(("dp", "tensor"), None),
        P(("dp", "tensor"), None),
        P(("dp", "tensor"), None),
        P("dp", None, "tensor"),
        P("dp", "tensor"),
        P("dp", "tensor", None),
    )
    out_specs = (
        P("dp", "tensor", None),
        P("dp", "tensor", None),
        P(("dp", "tensor"), None, None),
        P(("dp", "tensor"), None),
        P(("dp", "tensor"), None),
        P(("dp", "tensor"), None),
        P("dp", None, "tensor"),
        P("dp", "tensor"),
    )
    sizes = dict(mesh.shape)

    def per_device(tokens, *others):
        if sizes["dp"] == 16 and sizes["tensor"] == 2 and tokens.shape[0] == 2:
            return sequence_device(tokens, *others)
        return general_device(tokens, *others)

    return jax.shard_map(
        per_device, mesh=mesh, in_specs=in_specs, out_specs=out_specs, check_vma=False
    )
```

```python
import jax
import jax.numpy as jnp
from jax import lax
from jax.experimental import pallas as pl
from jax.experimental.pallas import tpu as pltpu
from jax.sharding import PartitionSpec as P

D = 768
HEADS = 12
HEAD = 64
SEQ = 1024
NDOC = 8


EPSILON = 1e-05
MASKED = -1e30


def for_sending(value):
    return jax.tree.map(lambda a: a.astype(jnp.bfloat16) if a.dtype == jnp.float32 else a, value)


def rotary_tables(segment_row):
    labels = jnp.arange(NDOC + 1, dtype=jnp.int32)
    member = (segment_row[:, None] == labels[None, :]).astype(jnp.int32)
    counts = jnp.sum(member, axis=0)
    starts = jnp.concatenate([jnp.zeros((1,), jnp.int32), jnp.cumsum(counts)[:-1]])
    offset = jnp.sum(member * starts[None, :], axis=1)
    position = (jnp.arange(SEQ, dtype=jnp.int32) - offset).astype(jnp.float32)
    exponent = -2.0 * jnp.arange(HEAD // 2).astype(jnp.float32) / HEAD
    frequency = jnp.power(jnp.float32(1000.0), exponent)
    angle = position[:, None] * frequency[None, :]
    return (jnp.cos(angle)[:, None, :], jnp.sin(angle)[:, None, :])


def rotate(vector, cosine, sine):
    half = vector.shape[-1] // 2
    first_half = vector[..., :half]
    second_half = vector[..., half:]
    return jnp.concatenate(
        [first_half * cosine - second_half * sine, second_half * cosine + first_half * sine],
        axis=-1,
    )


def unrotate(gradient, cosine, sine):

    def turned(vector):
        return rotate(vector, cosine, sine)

    _, pullback = jax.vjp(turned, gradient)
    return pullback(gradient)[0]


def layer_norm(vector, gain, shift):
    center = vector - jnp.mean(vector, axis=-1, keepdims=True)
    variance = jnp.mean(center * center, axis=-1, keepdims=True)
    return center * lax.rsqrt(variance + EPSILON) * gain + shift


def swiglu_piece(gate, upper):
    return jax.nn.silu(gate) * upper


def accumulate(total, term):
    if total is None:
        return term
    return tuple((left + right for left, right in zip(total, term)))


def general_device(
    tokens, segments, qkv_weight, out_weight, norm_gain, norm_shift, gate_up, down_weight, cotangent
):
    tensor_size = lax.axis_size("tensor")
    own_rows = SEQ // tensor_size
    row_start = lax.axis_index("tensor") * own_rows
    score_scale = HEAD ** (-0.5)
    qkv_full, out_full, gain_full, shift_full = (
        lax.all_gather(qkv_weight, ("dp", "tensor"), axis=0, tiled=True),
        lax.all_gather(out_weight, ("dp", "tensor"), axis=0, tiled=True),
        lax.all_gather(norm_gain, ("dp", "tensor"), axis=0, tiled=True),
        lax.all_gather(norm_shift, ("dp", "tensor"), axis=0, tiled=True),
    )
    gains = gain_full.astype(jnp.float32)
    shifts = shift_full.astype(jnp.float32)
    gate_up_full, down_full = (
        lax.all_gather(gate_up, "dp", axis=0, tiled=True),
        lax.all_gather(down_weight, "dp", axis=0, tiled=True),
    )
    batches = tokens.shape[0]
    outputs = []
    input_grads = []
    attn_total = None
    mlp_total = None
    for batch_index in range(batches):
        source = tokens[batch_index]
        own_source = lax.dynamic_slice_in_dim(source, row_start, own_rows, 0)
        segment_row = segments[batch_index]
        cosine, sine = rotary_tables(segment_row)
        own_cos = lax.dynamic_slice_in_dim(cosine, row_start, own_rows, 0)
        own_sin = lax.dynamic_slice_in_dim(sine, row_start, own_rows, 0)
        query_proj = jnp.einsum(
            "sd,de->se", own_source, qkv_full[:, 0], preferred_element_type=jnp.float32
        )
        pair_proj = jnp.einsum(
            "sd,dke->ske", source, qkv_full[:, 1:], preferred_element_type=jnp.float32
        )
        keys = rotate(pair_proj[:, 0].reshape(SEQ, HEADS, HEAD), cosine, sine).astype(jnp.bfloat16)
        values = pair_proj[:, 1].reshape(SEQ, HEADS, HEAD).astype(jnp.bfloat16)
        queries = rotate(query_proj.reshape(own_rows, HEADS, HEAD), own_cos, own_sin).astype(
            jnp.bfloat16
        )
        own_segments = lax.dynamic_slice_in_dim(segment_row, row_start, own_rows, 0)
        allowed = (own_segments[:, None] == segment_row[None, :])[None]
        raw_scores = (
            jnp.einsum("qhe,khe->hqk", queries, keys, preferred_element_type=jnp.float32)
            * score_scale
        )
        masked = jnp.where(allowed, raw_scores, MASKED)
        top_score = jnp.max(masked, axis=-1, keepdims=True)
        logsum = top_score + jnp.log(jnp.sum(jnp.exp(masked - top_score), axis=-1, keepdims=True))
        probs_low = jnp.exp(masked - logsum).astype(jnp.bfloat16)
        context = (
            jnp.einsum("hqk,khe->qhe", probs_low, values, preferred_element_type=jnp.float32)
            .reshape(own_rows, D)
            .astype(jnp.bfloat16)
        )
        attended = jnp.dot(context, out_full, preferred_element_type=jnp.float32)
        hidden_in = own_source.astype(jnp.float32) + attended
        normed = layer_norm(hidden_in, gains[:, 0], shifts[:, 0])
        normed_all = lax.all_gather(normed.astype(jnp.bfloat16), "tensor", axis=0, tiled=True)
        gate_pair = jnp.einsum(
            "sd,dkf->skf", normed_all, gate_up_full, preferred_element_type=jnp.float32
        )
        swiglu = swiglu_piece(gate_pair[:, 0], gate_pair[:, 1]).astype(jnp.bfloat16)
        mlp_out = lax.psum_scatter(
            jnp.einsum("sf,df->sd", swiglu, down_full, preferred_element_type=jnp.float32).astype(
                jnp.bfloat16
            ),
            "tensor",
            scatter_dimension=0,
            tiled=True,
        ).astype(jnp.float32)
        resid = normed + mlp_out
        outputs.append(layer_norm(resid, gains[:, 1], shifts[:, 1]).astype(jnp.bfloat16))
        upstream = cotangent[batch_index].astype(jnp.float32)
        _, second_pull = jax.vjp(layer_norm, resid, gains[:, 1], shifts[:, 1])
        resid_grad, gain_two, shift_two = second_pull(upstream)
        mlp_grad = lax.all_gather(resid_grad.astype(jnp.bfloat16), "tensor", axis=0, tiled=True)
        swiglu_grad = jnp.einsum(
            "sd,df->sf", mlp_grad, down_full, preferred_element_type=jnp.float32
        )
        _, glu_pull = jax.vjp(swiglu_piece, gate_pair[:, 0], gate_pair[:, 1])
        gate_grad, upper_grad = glu_pull(swiglu_grad)
        pair_grad = jnp.stack([gate_grad, upper_grad], axis=1).astype(jnp.bfloat16)
        down_term = jnp.einsum("sd,sf->df", mlp_grad, swiglu, preferred_element_type=jnp.float32)
        gate_up_term = jnp.einsum(
            "sd,skf->dkf", normed_all, pair_grad, preferred_element_type=jnp.float32
        )
        normed_grad = resid_grad + lax.psum_scatter(
            jnp.einsum("skf,dkf->sd", pair_grad, gate_up_full, preferred_element_type=jnp.float32),
            "tensor",
            scatter_dimension=0,
            tiled=True,
        )
        _, first_pull = jax.vjp(layer_norm, hidden_in, gains[:, 0], shifts[:, 0])
        hidden_grad, gain_one, shift_one = first_pull(normed_grad)
        attended_grad = hidden_grad.astype(jnp.bfloat16)
        out_term = jnp.einsum(
            "sd,se->de", context, attended_grad, preferred_element_type=jnp.float32
        )
        context_grad = (
            jnp.einsum("se,de->sd", attended_grad, out_full, preferred_element_type=jnp.float32)
            .astype(jnp.bfloat16)
            .reshape(own_rows, HEADS, HEAD)
        )
        probs = jnp.exp(masked - logsum)
        weights_grad = jnp.einsum(
            "qhe,khe->hqk", context_grad, values, preferred_element_type=jnp.float32
        )
        row_delta = jnp.sum(probs * weights_grad, axis=-1, keepdims=True)
        score_grad = (probs * (weights_grad - row_delta)).astype(jnp.bfloat16)
        query_grad = (
            jnp.einsum("hqk,khe->qhe", score_grad, keys, preferred_element_type=jnp.float32)
            * score_scale
        )
        key_part = (
            jnp.einsum("hqk,qhe->khe", score_grad, queries, preferred_element_type=jnp.float32)
            * score_scale
        )
        value_part = jnp.einsum(
            "hqk,qhe->khe", probs_low, context_grad, preferred_element_type=jnp.float32
        )
        key_value = lax.psum_scatter(
            jnp.stack(
                [
                    key_part.reshape(lax.axis_size("tensor") * own_rows, D),
                    value_part.reshape(lax.axis_size("tensor") * own_rows, D),
                ],
                axis=1,
            ).astype(jnp.bfloat16),
            "tensor",
            scatter_dimension=0,
            tiled=True,
        ).astype(jnp.float32)
        query_back = unrotate(query_grad, own_cos, own_sin).reshape(own_rows, D)
        key_back = unrotate(
            key_value[:, 0].reshape(own_rows, HEADS, HEAD), own_cos, own_sin
        ).reshape(own_rows, D)
        proj_grad = jnp.stack([query_back, key_back, key_value[:, 1]], axis=1).astype(jnp.bfloat16)
        input_grads.append(
            hidden_grad
            + jnp.einsum("ske,dke->sd", proj_grad, qkv_full, preferred_element_type=jnp.float32)
        )
        qkv_term = jnp.einsum(
            "sd,ske->dke", own_source, proj_grad, preferred_element_type=jnp.float32
        )
        gain_term = jnp.stack([gain_one, gain_two], axis=1)
        shift_term = jnp.stack([shift_one, shift_two], axis=1)
        attn_terms = (qkv_term, out_term, gain_term, shift_term)
        mlp_terms = (gate_up_term, down_term)
        attn_total = accumulate(attn_total, attn_terms)
        mlp_total = accumulate(mlp_total, mlp_terms)
    attn_final = lax.psum_scatter(attn_total, ("dp", "tensor"), scatter_dimension=0, tiled=True)
    mlp_final = jax.tree.map(
        lambda part: part.astype(jnp.float32),
        lax.psum_scatter(for_sending(mlp_total), "dp", scatter_dimension=0, tiled=True),
    )
    return (
        jnp.stack(outputs, axis=0),
        jnp.stack(input_grads, axis=0),
        attn_final[0],
        attn_final[1],
        attn_final[2],
        attn_final[3],
        mlp_final[0],
        mlp_final[1],
    )


HIDDEN = 1536
WIDE = 3 * HIDDEN
REST = 512
TAIL = 2 * REST
GROUP = 4 * HEAD
GROUPS = D // GROUP
KEYS = 128
LANES = 2 * HEAD
BLOCK = 256
NBLOCK = SEQ // BLOCK
ROWS = 256
CHUNK = 512
LOG2E = 1.4426950408889634
F32 = jnp.float32
BF16 = jnp.bfloat16


def across(value, move):
    pairs = []
    for z in range(4):
        for y in range(2):
            for x in range(2):
                for c in range(2):
                    tz, ty, tx, tc = move(z, y, x, c)
                    pairs.append((((z * 2 + y) * 2 + x) * 2 + c, ((tz * 2 + ty) * 2 + tx) * 2 + tc))
    return lax.ppermute(value, ("dp", "tensor"), pairs)


def core_swap(value):
    return across(value, lambda z, y, x, c: (z, y, x, 1 - c))


def first_swap(value):
    return across(value, lambda z, y, x, c: (z, y, 1 - x, c) if c == 0 else (z, 1 - y, x, c))


def second_swap(value):
    return across(value, lambda z, y, x, c: (z, 1 - y, x, c) if c == 0 else (z, y, 1 - x, c))


def depth_shift(value, steps):
    return across(value, lambda z, y, x, c: ((z + steps) % 4, y, x, c))


def slot_blocks(sign, core):
    me = lax.axis_index("dp")
    z, y, x = me // 4, (me // 2) % 2, me % 2
    slot = jnp.arange(16, dtype=jnp.int32)
    second, first, depth = slot // 8, (slot // 4) % 2, slot % 4
    x_bit = jnp.where(core == 0, first, second)
    y_bit = jnp.where(core == 0, second, first)
    return (((z + sign * depth) % 4) * 4 + (y ^ y_bit) * 2 + (x ^ x_bit)).astype(jnp.int32)


def depth_parts(block):
    return [block] + [depth_shift(block, k) for k in (1, 2, 3)]


def depth_sum(parts):
    total = parts[0].astype(F32)
    for k in (1, 2, 3):
        total = total + depth_shift(parts[k], k).astype(F32)
    return total


def cost(flops, nbytes, trans=0):
    return pl.CostEstimate(flops=int(flops), bytes_accessed=int(nbytes), transcendentals=int(trans))


def params(vmem_mb, sem=("arbitrary",)):
    return pltpu.CompilerParams(dimension_semantics=sem, vmem_limit_bytes=vmem_mb << 20)


ANY = pl.BlockSpec(memory_space=pl.ANY)


def pile(parts, deps=()):
    spans, start = [], 0
    for part in parts:
        spans.append((start, part.shape[0]))
        start += part.shape[0]

    def body(*refs):
        ins, out, sem = refs[: len(parts)], refs[-2], refs[-1]
        copies = [
            pltpu.make_async_copy(ref, out.at[pl.ds(at, n)], sem.at[i])
            for i, (ref, (at, n)) in enumerate(zip(ins, spans))
        ]
        for cp in copies:
            cp.start()
        for cp in copies:
            cp.wait()

    shape = (start,) + parts[0].shape[1:]
    return pl.pallas_call(
        body,
        in_specs=[ANY] * (len(parts) + len(deps)),
        out_specs=ANY,
        out_shape=jax.ShapeDtypeStruct(shape, parts[0].dtype),
        scratch_shapes=[pltpu.SemaphoreType.DMA((len(parts),))],
        compiler_params=params(16, None),
        cost_estimate=cost(0, 4 * start * shape[1] * shape[2]),
        name="pile",
    )(*parts, *deps)


def place(core, mine, there):
    def body(c, a, b, out, sem):
        first = pltpu.make_async_copy(a, out.at[c[0]], sem.at[0])
        second = pltpu.make_async_copy(b, out.at[1 - c[0]], sem.at[1])
        first.start()
        second.start()
        first.wait()
        second.wait()

    return pl.pallas_call(
        body,
        grid_spec=pltpu.PrefetchScalarGridSpec(
            num_scalar_prefetch=1,
            grid=(1,),
            in_specs=[ANY, ANY],
            out_specs=ANY,
            scratch_shapes=[pltpu.SemaphoreType.DMA((2,))],
        ),
        out_shape=jax.ShapeDtypeStruct((2,) + mine.shape, mine.dtype),
        compiler_params=params(16),
        cost_estimate=cost(0, 4 * mine.size),
        name="place",
    )(core[None], mine, there)


def assemble(own, other, index):
    def body(idx, a, b, c, d, out, sem):
        copies = []
        for i, ref in enumerate((a, b, c, d)):
            for s in range(8):
                copies.append(
                    pltpu.make_async_copy(ref.at[s], out.at[idx[i * 8 + s]], sem.at[i * 8 + s])
                )
        for cp in copies:
            cp.start()
        for cp in copies:
            cp.wait()

    rows, wide = own[0].shape[1:]
    return pl.pallas_call(
        body,
        grid_spec=pltpu.PrefetchScalarGridSpec(
            num_scalar_prefetch=1,
            grid=(1,),
            in_specs=[ANY] * 4,
            out_specs=ANY,
            scratch_shapes=[pltpu.SemaphoreType.DMA((32,))],
        ),
        out_shape=jax.ShapeDtypeStruct((32, rows, wide), BF16),
        compiler_params=params(16),
        cost_estimate=cost(0, 4 * 32 * rows * wide),
        name="assemble",
    )(index, *own, *other)


def turn(vector, cosine, sine):
    lane = lax.broadcasted_iota(jnp.int32, vector.shape, 1)
    swapped = jnp.where(
        lane % HEAD < HEAD // 2,
        pltpu.roll(vector, LANES - HEAD // 2, 1),
        pltpu.roll(vector, HEAD // 2, 1),
    )
    return vector * cosine + swapped * sine


def dot_nn(a, b):
    return lax.dot_general(a, b, (((1,), (0,)), ((), ())), preferred_element_type=F32)


def dot_nt(a, b):
    return lax.dot_general(a, b, (((1,), (1,)), ((), ())), preferred_element_type=F32)


def dot_tn(a, b):
    return lax.dot_general(a, b, (((0,), (0,)), ((), ())), preferred_element_type=F32)


def stacked(low_lane, pair):
    zero = jnp.zeros_like(pair)
    return jnp.concatenate(
        [jnp.where(low_lane, pair, zero), jnp.where(low_lane, zero, pair)], axis=0
    )


def windows(bnd, i, work):
    blocks = (bnd[NBLOCK + i] - bnd[i] + BLOCK // KEYS - 1) // (BLOCK // KEYS)
    for width in range(1, NBLOCK + 1):

        @pl.when(blocks == width)
        def _():
            low = jnp.minimum(bnd[i], (SEQ - width * BLOCK) // KEYS)
            work(pl.ds(pl.multiple_of(low * KEYS, KEYS), width * BLOCK))


def attn_forward(first, count, bounds, source, weights, cosine, sine, seg_col, seg_row, deps=()):
    def body(bnd, x, wq, wk, wv, cos, sin, sc, sr, *rest):
        q_out, k_out, v_out, ctx_out, lse_out, qm = rest[len(deps) :]
        low_lane = lax.broadcasted_iota(jnp.int32, (BLOCK, LANES), 1) < HEAD

        @pl.loop(0, NBLOCK)
        def _(r):
            rows = pl.ds(pl.multiple_of(r * BLOCK, BLOCK), BLOCK)
            xr, cr, sn = x[rows, :], cos[rows, :], sin[rows, :]
            q_proj, k_proj = dot_nn(xr, wq[...]), dot_nn(xr, wk[...])
            v_out[rows, :] = dot_nn(xr, wv[...]).astype(BF16)
            for p in range(GROUP // LANES):
                ln = slice(p * LANES, (p + 1) * LANES)
                q = turn(q_proj[:, ln], cr, sn).astype(BF16) * jnp.asarray(HEAD**-0.5, BF16)
                q_out[rows, ln] = q
                qm[p, r] = stacked(low_lane, q)
                k_out[rows, ln] = turn(k_proj[:, ln], cr, sn).astype(BF16)

        def block(i, _):
            rows = pl.ds(pl.multiple_of(i * BLOCK, BLOCK), BLOCK)
            own = jnp.concatenate([sc[rows, :], sc[rows, :]], axis=0)

            def work(cols):
                seen = own == sr[:, cols]
                for p in range(GROUP // LANES):
                    ln = slice(p * LANES, (p + 1) * LANES)
                    s = jnp.where(seen, dot_nt(qm[p, i], k_out[cols, ln]) * LOG2E, MASKED)
                    top = jnp.max(s, axis=1, keepdims=True)
                    e = jnp.exp2(s - top)
                    total = jnp.sum(e, axis=1, keepdims=True)
                    mixed = dot_nn(e.astype(BF16), v_out[cols, ln]) / total
                    ctx_out[rows, ln] = jnp.where(low_lane, mixed[:BLOCK], mixed[BLOCK:]).astype(BF16)
                    logs = top + jnp.log2(total)
                    flipped = jnp.where(low_lane, logs[:BLOCK], logs[BLOCK:]).T
                    lse_out[0, 2 * p : 2 * p + 1, rows] = flipped[0:1]
                    lse_out[0, 2 * p + 1 : 2 * p + 2, rows] = flipped[HEAD : HEAD + 1]

            windows(bnd, i, work)
            return 0

        lax.fori_loop(0, NBLOCK, block, 0)

    full = lambda shape: pl.BlockSpec(shape, lambda p, b: (0,) * len(shape))
    column = lambda shift: pl.BlockSpec((D, GROUP), lambda p, b: (0, shift * GROUPS + first + p))
    part = pl.BlockSpec((SEQ, GROUP), lambda p, b: (0, p))
    act = jax.ShapeDtypeStruct((SEQ, count * GROUP), BF16)
    return pl.pallas_call(
        body,
        grid_spec=pltpu.PrefetchScalarGridSpec(
            num_scalar_prefetch=1,
            grid=(count,),
            in_specs=[
                full((SEQ, D)),
                column(0),
                column(1),
                column(2),
                full((SEQ, LANES)),
                full((SEQ, LANES)),
                full((SEQ, 1)),
                full((1, SEQ)),
            ]
            + [ANY] * len(deps),
            out_specs=[part] * 4 + [pl.BlockSpec((1, 8, SEQ), lambda p, b: (p, 0, 0))],
            scratch_shapes=[pltpu.VMEM((GROUP // LANES, NBLOCK, 2 * BLOCK, LANES), BF16)],
        ),
        out_shape=[act] * 4 + [jax.ShapeDtypeStruct((count, 8, SEQ), F32)],
        compiler_params=params(48),
        cost_estimate=cost(
            count * GROUP * (6 * SEQ * D + 16 * SEQ * SEQ), 8 << 20, count * 4 * SEQ * SEQ
        ),
        name="attn_forward",
    )(bounds, source, weights, weights, weights, cosine, sine, seg_col, seg_row, *deps)


def deal(core, whole, mine, theirs, columns):
    parts = whole.reshape(16, 2, D // 32, whole.shape[1])
    first, second = parts[:, 0], parts[:, 1]
    mine[:, :, columns] = jnp.where(core == 0, first, second).astype(BF16)
    theirs[:, :, columns] = jnp.where(core == 0, second, first).astype(BF16)


def attn_backward(at, grad_at, bounds, saved, ctx_grad, source, cosine, sine, seg_col, seg_row, deps=()):
    def body(bnd, q, k, v, o, do, lse, x, cos, sin, sc, sr, *rest):
        core = bnd[2 * NBLOCK]
        out, mine, theirs, qm, dm, dq, dk, dv, dl = rest[len(deps) :]
        low_lane = lax.broadcasted_iota(jnp.int32, (BLOCK, LANES), 1) < HEAD
        row = lax.broadcasted_iota(jnp.int32, (8, LANES), 0)
        lane = lax.broadcasted_iota(jnp.int32, (8, LANES), 1)
        pick = jnp.where(row == lane // HEAD, 1.0, 0.0).astype(F32)
        for p in range(GROUP // LANES):
            ln = slice(p * LANES, (p + 1) * LANES)

            @pl.loop(0, NBLOCK)
            def _(i):
                rows = pl.ds(pl.multiple_of(i * BLOCK, BLOCK), BLOCK)
                qm[p, i] = stacked(low_lane, q[rows, ln])
                dm[p, i] = stacked(low_lane, do[rows, ln])

            dl[p] = lax.dot_general(
                pick,
                do[:, ln].astype(F32) * o[:, ln].astype(F32),
                (((1,), (1,)), ((), ())),
                preferred_element_type=F32,
                precision=lax.Precision.HIGHEST,
            )
        dk[...] = jnp.zeros_like(dk)
        dv[...] = jnp.zeros_like(dv)

        def block(i, _):
            rows = pl.ds(pl.multiple_of(i * BLOCK, BLOCK), BLOCK)
            own = jnp.concatenate([sr[:, rows], sr[:, rows]], axis=1)

            def work(cols):
                seen = sc[cols, :] == own
                for p in range(GROUP // LANES):
                    ln = slice(p * LANES, (p + 1) * LANES)
                    keys, values, qq, dd = k[cols, ln], v[cols, ln], qm[p, i], dm[p, i]
                    logs = jnp.concatenate(
                        [lse[0, 2 * p : 2 * p + 1, rows], lse[0, 2 * p + 1 : 2 * p + 2, rows]], axis=1
                    )
                    deltas = jnp.concatenate([dl[p, 0:1, rows], dl[p, 1:2, rows]], axis=1)
                    s = dot_nt(keys, qq) * LOG2E - logs
                    probs = jnp.exp2(jnp.where(seen, s, MASKED))
                    g = (probs * (dot_nt(values, dd) - deltas)).astype(BF16)
                    dv[cols, ln] += dot_nn(probs.astype(BF16), dd)
                    dk[cols, ln] += dot_nn(g, qq)
                    both = dot_tn(g, keys)
                    dq[rows, ln] = jnp.where(low_lane, both[:BLOCK], both[BLOCK:])

            windows(bnd, i, work)
            return 0

        lax.fori_loop(0, NBLOCK, block, 0)

        @pl.loop(0, NBLOCK)
        def _(r):
            rows = pl.ds(pl.multiple_of(r * BLOCK, BLOCK), BLOCK)
            cr, sn = cos[rows, :], -sin[rows, :]
            for p in range(GROUP // LANES):
                ln = slice(p * LANES, (p + 1) * LANES)
                out[0, rows, ln] = turn(dq[rows, ln] * (HEAD**-0.5), cr, sn).astype(BF16)
                out[1, rows, ln] = turn(dk[rows, ln], cr, sn).astype(BF16)
                out[2, rows, ln] = dv[rows, ln].astype(BF16)

        for i in range(3):
            deal(core, dot_tn(x[...], out[i]), mine, theirs, slice(i * GROUP, (i + 1) * GROUP))

    full = lambda shape: pl.BlockSpec(shape, lambda p, b: (0,) * len(shape))
    part = pl.BlockSpec((SEQ, GROUP), lambda p, b: (0, at))
    low2 = pltpu.VMEM((GROUP // LANES, NBLOCK, 2 * BLOCK, LANES), BF16)
    wide = pltpu.VMEM((SEQ, GROUP), F32)
    dealt = (16, D // 32, 3 * GROUP)
    return pl.pallas_call(
        body,
        grid_spec=pltpu.PrefetchScalarGridSpec(
            num_scalar_prefetch=1,
            grid=(1,),
            in_specs=[part] * 4
            + [
                pl.BlockSpec((SEQ, GROUP), lambda p, b: (0, grad_at)),
                pl.BlockSpec((1, 8, SEQ), lambda p, b: (at, 0, 0)),
                full((SEQ, D)),
                full((SEQ, LANES)),
                full((SEQ, LANES)),
                full((SEQ, 1)),
                full((1, SEQ)),
            ]
            + [ANY] * len(deps),
            out_specs=[full((3, SEQ, GROUP)), full(dealt), full(dealt)],
            scratch_shapes=[
                low2,
                low2,
                wide,
                wide,
                wide,
                pltpu.VMEM((GROUP // LANES, 8, SEQ), F32),
            ],
        ),
        out_shape=[
            jax.ShapeDtypeStruct((3, SEQ, GROUP), BF16),
            jax.ShapeDtypeStruct(dealt, BF16),
            jax.ShapeDtypeStruct(dealt, BF16),
        ],
        compiler_params=params(48),
        cost_estimate=cost(GROUP * (40 * SEQ * SEQ + 6 * SEQ * D), 10 << 20, 4 * SEQ * SEQ),
        name="attn_backward",
    )(bounds, *saved[:4], ctx_grad, saved[4], source, cosine, sine, seg_col, seg_row, *deps)


def weight_grad(left, right, columns=512):
    wide = right.shape[1]

    def body(a, b, out, flipped):
        @pl.when(pl.program_id(0) == 0)
        def _():
            flipped[...] = a[...].T

        out[...] = dot_nn(flipped[...], b[...]).astype(BF16)

    return pl.pallas_call(
        body,
        grid=(wide // columns,),
        in_specs=[
            pl.BlockSpec((SEQ, D), lambda n: (0, 0)),
            pl.BlockSpec((SEQ, columns), lambda n: (0, n)),
        ],
        out_specs=pl.BlockSpec((D, columns), lambda n: (0, n)),
        out_shape=jax.ShapeDtypeStruct((D, wide), BF16),
        scratch_shapes=[pltpu.VMEM((D, SEQ), BF16)],
        compiler_params=params(32),
        cost_estimate=cost(2 * SEQ * D * wide, 2 * (SEQ * D + SEQ * wide + D * wide)),
        name="weight_grad",
    )(left, right)


def weight_grad_join(index, left, right, there, columns=512):
    wide = right.shape[1]
    rows = D // 16

    def body(idx, a, b, other, keep, send, flipped, total):
        @pl.when(pl.program_id(0) == 0)
        def _():
            flipped[...] = a[...].T

        total[...] = dot_nn(flipped[...], b[...]) + other[...].astype(F32)
        for s in range(16):
            at = pl.ds(pl.multiple_of(idx[s] * rows, 16), rows)
            (keep, send)[s // 8][s % 8] = total[at, :].astype(BF16)

    half = pl.BlockSpec((8, rows, columns), lambda n, i: (0, 0, n))
    shape = jax.ShapeDtypeStruct((8, rows, wide), BF16)
    return pl.pallas_call(
        body,
        grid_spec=pltpu.PrefetchScalarGridSpec(
            num_scalar_prefetch=1,
            grid=(wide // columns,),
            in_specs=[
                pl.BlockSpec((SEQ, D), lambda n, i: (0, 0)),
                pl.BlockSpec((SEQ, columns), lambda n, i: (0, n)),
                pl.BlockSpec((D, columns), lambda n, i: (0, n)),
            ],
            out_specs=[half, half],
            scratch_shapes=[pltpu.VMEM((D, SEQ), BF16), pltpu.VMEM((D, columns), F32)],
        ),
        out_shape=[shape, shape],
        compiler_params=params(32),
        cost_estimate=cost(2 * SEQ * D * wide, 2 * (SEQ * D + SEQ * wide + 2 * D * wide)),
        name="weight_grad_join",
    )(index, left, right, there)


def out_grad(core, ctx, right, norms):
    def body(c, a, b, d, nrm, mine, theirs):
        whole = jnp.concatenate([dot_tn(p[...], b[...]) for p in (a, d)], axis=0)
        deal(c[0], whole, mine, theirs, slice(0, D))
        flipped = jnp.concatenate([nrm[...], jnp.zeros((LANES - 8, D), F32)], axis=0).T
        filled = jnp.concatenate([flipped, jnp.zeros((D, LANES), F32)], axis=1)
        deal(c[0], filled, mine, theirs, slice(D, TAIL))

    full = lambda shape: pl.BlockSpec(shape, lambda p, b: (0,) * len(shape))
    dealt = (16, D // 32, TAIL)
    return pl.pallas_call(
        body,
        grid_spec=pltpu.PrefetchScalarGridSpec(
            num_scalar_prefetch=1,
            grid=(1,),
            in_specs=[full((SEQ, GROUP)), full((SEQ, D)), full((SEQ, D - GROUP)), full((8, D))],
            out_specs=[full(dealt), full(dealt)],
        ),
        out_shape=[jax.ShapeDtypeStruct(dealt, BF16)] * 2,
        compiler_params=params(32),
        cost_estimate=cost(2 * SEQ * D * D, 8 << 20),
        name="out_grad",
    )(core[None], ctx[0], right, ctx[1], norms)


def join_dealt(index, mine, there):
    widths = [m.shape[2] for m in mine]
    wide, rows, count = sum(widths), D // 32, len(mine)

    def body(idx, *refs):
        ours, others, keep, send = refs[:count], refs[count : 2 * count], refs[-2], refs[-1]
        for s in range(16):
            start = 0
            for a, b, n in zip(ours, others, widths):
                total = a[idx[s]].astype(F32) + b[idx[s]].astype(F32)
                (keep, send)[s // 8][s % 8, :, start : start + n] = total.astype(BF16)
                start += n

    full = lambda shape: pl.BlockSpec(shape, lambda p, b: (0,) * len(shape))
    half = (8, rows, wide)
    return pl.pallas_call(
        body,
        grid_spec=pltpu.PrefetchScalarGridSpec(
            num_scalar_prefetch=1,
            grid=(1,),
            in_specs=[full((16, rows, n)) for n in widths] * 2,
            out_specs=[full(half), full(half)],
        ),
        out_shape=[jax.ShapeDtypeStruct(half, BF16)] * 2,
        compiler_params=params(48),
        cost_estimate=cost(D * wide // 2, 3 * D * wide),
        name="join_dealt",
    )(index, *mine, *there)


def fold(keep, there, deps=()):
    rows, wide = keep.shape[1:]

    def body(a, b, c, d, *rest):
        rest[-2][...] = (a[...].astype(F32) + c[...].astype(F32)).astype(BF16)
        rest[-1][...] = (b[...].astype(F32) + d[...].astype(F32)).astype(BF16)

    low = pl.BlockSpec((1, rows, wide), lambda i: (i, 0, 0))
    high = pl.BlockSpec((1, rows, wide), lambda i: (4 + i, 0, 0))
    shape = jax.ShapeDtypeStruct((4, rows, wide), BF16)
    return pl.pallas_call(
        body,
        grid=(4,),
        in_specs=[low, high, low, high] + [ANY] * len(deps),
        out_specs=[low, low],
        out_shape=[shape, shape],
        compiler_params=params(32),
        cost_estimate=cost(8 * rows * wide, 48 * rows * wide),
        name="fold",
    )(keep, keep, there, there, *deps)


def input_back(core, hidden_grad, projected, weights):
    half = SEQ // 2 // BLOCK

    def body(c, hid, a, b, d, w, mine, leave):
        total = hid[...]
        for g, ref in enumerate((a, b, d)):
            for i in range(3):
                at = i * D + g * GROUP
                total = total + dot_nt(ref[i], w[:, at : at + GROUP])
        own = pl.program_id(0) // half == c[0]

        @pl.when(own)
        def _():
            mine[...] = total

        @pl.when(jnp.logical_not(own))
        def _():
            leave[...] = total

    row = pl.BlockSpec((BLOCK, D), lambda r, c: (r, 0))
    shape = jax.ShapeDtypeStruct((SEQ // 2, D), F32)
    return pl.pallas_call(
        body,
        grid_spec=pltpu.PrefetchScalarGridSpec(
            num_scalar_prefetch=1,
            grid=(SEQ // BLOCK,),
            in_specs=[row]
            + [pl.BlockSpec((3, BLOCK, GROUP), lambda r, c: (0, r, 0))] * 3
            + [pl.BlockSpec((D, 3 * D), lambda r, c: (0, 0))],
            out_specs=[
                pl.BlockSpec((BLOCK, D), lambda r, c: (jnp.clip(r - half * c[0], 0, half - 1), 0)),
                pl.BlockSpec(
                    (BLOCK, D), lambda r, c: (jnp.clip(r - half * (1 - c[0]), 0, half - 1), 0)
                ),
            ],
        ),
        out_shape=[shape, shape],
        compiler_params=params(32),
        cost_estimate=cost(6 * SEQ * D * D, 16 << 20),
        name="input_back",
    )(core[None], hidden_grad, *projected, weights)


def middle(index, source, ctx, cot, pieces):
    def norm(v):
        center = v - jnp.mean(v, axis=1, keepdims=True)
        scale = lax.rsqrt(jnp.mean(center * center, axis=1, keepdims=True) + EPSILON)
        return center * scale, scale

    def norm_back(u, hat, scale, gain):
        g = u * gain
        return scale * (
            g - jnp.mean(g, axis=1, keepdims=True) - hat * jnp.mean(g * hat, axis=1, keepdims=True)
        )

    def body(
        idx, x, ctx0, ctx1, cot, *refs
    ):
        pieces, refs = refs[:8], refs[8:]
        out, out_leave, normed_out, mlp_out, att_out, ctxg_out, hid_out, gu0, gu1, sw0, sw1, sums = refs[:12]
        w, wo, tail, nrm, sem = refs[12:]
        step = pl.program_id(0)
        core = idx[32]
        rows = D // 32

        @pl.when(step == 0)
        def _():
            copies = []
            for i, ref in enumerate(pieces):
                which, rest = i // 4, i % 4
                for s in range(8):
                    block = idx[rest * 8 + s]
                    at = pl.ds(pl.multiple_of(block * 48, 16), 48)
                    owner = core if rest < 2 else 1 - core
                    n = i * 8 + s
                    if which == 0:
                        copies.append(
                            pltpu.make_async_copy(
                                ref.at[s], w.at[rest // 2, at, pl.ds(0, 2 * HIDDEN)], sem.at[n]
                            )
                        )
                        continue
                    copies.append(
                        pltpu.make_async_copy(
                            ref.at[s, :, pl.ds(0, HIDDEN)],
                            w.at[rest // 2, at, pl.ds(2 * HIDDEN, HIDDEN)],
                            sem.at[n],
                        )
                    )
                    for part in range(2):
                        copies.append(
                            pltpu.make_async_copy(
                                ref.at[s, pl.ds(part * rows, rows), pl.ds(HIDDEN, REST)],
                                tail.at[part, block * 2 + owner],
                                sem.at[32 + n + 32 * part],
                            )
                        )
            for cp in copies:
                cp.start()
            for cp in copies:
                cp.wait()
            joined = jnp.concatenate(
                [tail[0].reshape(D, REST), tail[1].reshape(D, REST)], axis=1
            )
            wo[...] = joined[:, :D]
            nrm[...] = joined[:, D : D + LANES].astype(F32).T[:8]
            sums[...] = jnp.zeros_like(sums)

        gain1, gain2, shift1, shift2 = (nrm[i : i + 1, :] for i in range(4))
        hidden_in = x[...].astype(F32) + dot_nn(ctx0[...], wo[:GROUP, :]) + dot_nn(ctx1[...], wo[GROUP:, :])
        hat1, scale1 = norm(hidden_in)
        normed = hat1 * gain1 + shift1
        low = normed.astype(BF16)
        normed_out[...] = low
        total = normed
        for half in range(2):
            sw, gu = (sw0, sw1)[half], (gu0, gu1)[half]
            for n in range(HIDDEN // CHUNK):
                g_at, u_at, d_at = (pl.ds(p * HIDDEN + n * CHUNK, CHUNK) for p in range(3))
                gate = dot_nn(low, w[half, :, g_at])
                up = dot_nn(low, w[half, :, u_at])
                s = jax.nn.sigmoid(gate)
                silu = gate * s
                act = (silu * up).astype(BF16)
                gu[:, g_at] = (up * (s * (1.0 + gate * (1.0 - s)))).astype(BF16)
                gu[:, u_at] = silu.astype(BF16)
                sw[:, g_at] = act
                total = total + dot_nt(act, w[half, :, d_at])
        hat2, scale2 = norm(total)
        result = (hat2 * gain2 + shift2).astype(BF16)
        own = step // (SEQ // 2 // ROWS) == core

        @pl.when(own)
        def _():
            out[...] = result

        @pl.when(jnp.logical_not(own))
        def _():
            out_leave[...] = result

        u2 = cot[...].astype(F32)
        resid = norm_back(u2, hat2, scale2, gain2)
        mlp = resid.astype(BF16)
        mlp_out[...] = mlp
        back = resid
        for half in range(2):
            gu = (gu0, gu1)[half]
            for n in range(HIDDEN // CHUNK):
                g_at, u_at, d_at = (pl.ds(p * HIDDEN + n * CHUNK, CHUNK) for p in range(3))
                grad = dot_nn(mlp, w[half, :, d_at])
                gate_grad = (grad * gu[:, g_at].astype(F32)).astype(BF16)
                up_grad = (grad * gu[:, u_at].astype(F32)).astype(BF16)
                gu[:, g_at] = gate_grad
                gu[:, u_at] = up_grad
                back = back + dot_nt(gate_grad, w[half, :, g_at])
                back = back + dot_nt(up_grad, w[half, :, u_at])
        hidden_grad = norm_back(back, hat1, scale1, gain1)
        hid_out[...] = hidden_grad
        att = hidden_grad.astype(BF16)
        att_out[...] = att
        ctxg_out[...] = dot_nt(att, wo[...]).astype(BF16)
        for i, v in enumerate((back * hat1, u2 * hat2, back, u2)):
            sums[i : i + 1, :] += jnp.sum(v, axis=0, keepdims=True)

    row = pl.BlockSpec((ROWS, D), lambda r, i: (r, 0))
    wide = lambda n: pl.BlockSpec((ROWS, n), lambda r, i: (r, 0))
    whole = lambda shape: pl.BlockSpec(shape, lambda r, i: (0,) * len(shape))
    act = lambda n, t=BF16: jax.ShapeDtypeStruct((SEQ, n), t)
    half = SEQ // 2 // ROWS
    mine = pl.BlockSpec((ROWS, D), lambda r, i: (jnp.clip(r - half * i[32], 0, half - 1), 0))
    leave = pl.BlockSpec((ROWS, D), lambda r, i: (jnp.clip(r - half * (1 - i[32]), 0, half - 1), 0))
    return pl.pallas_call(
        body,
        grid_spec=pltpu.PrefetchScalarGridSpec(
            num_scalar_prefetch=1,
            grid=(SEQ // ROWS,),
            in_specs=[row, wide(GROUP), wide(D - GROUP), row] + [ANY] * 8,
            out_specs=[mine, leave]
            + [row] * 5
            + [wide(2 * HIDDEN)] * 2
            + [wide(HIDDEN)] * 2
            + [whole((8, D))],
            scratch_shapes=[
                pltpu.VMEM((2, D, WIDE), BF16),
                pltpu.VMEM((D, D), BF16),
                pltpu.VMEM((2, 32, D // 32, REST), BF16),
                pltpu.VMEM((8, D), F32),
                pltpu.SemaphoreType.DMA((128,)),
            ],
        ),
        out_shape=[
            jax.ShapeDtypeStruct((SEQ // 2, D), BF16),
            jax.ShapeDtypeStruct((SEQ // 2, D), BF16),
            act(D),
            act(D),
            act(D),
            act(D),
            act(D, F32),
            act(2 * HIDDEN),
            act(2 * HIDDEN),
            act(HIDDEN),
            act(HIDDEN),
            jax.ShapeDtypeStruct((8, D), F32),
        ],
        compiler_params=params(56),
        cost_estimate=cost(12 * SEQ * D * 2 * HIDDEN + 4 * SEQ * D * D, 60 << 20, 4 * SEQ * HIDDEN),
        name="middle",
    )(index, source, *ctx, cot, *pieces)


def rotary_lanes(segment_row):
    labels = jnp.arange(NDOC + 1, dtype=jnp.int32)
    before = jnp.sum((segment_row[None, :] < labels[:, None]).astype(jnp.int32), axis=1)
    member = segment_row[:, None] == labels[None, :]
    first = jnp.sum(jnp.where(member, before[None, :], 0), axis=1)
    position = (jnp.arange(SEQ, dtype=jnp.int32) - first).astype(F32)
    lane = jnp.arange(LANES) % (HEAD // 2)
    frequency = jnp.power(F32(1000.0), -2.0 * lane.astype(F32) / HEAD)
    angle = position[:, None] * frequency[None, :]
    sign = jnp.where(jnp.arange(LANES) % HEAD < HEAD // 2, -1.0, 1.0)
    ends = jnp.concatenate([before[1:], jnp.full((1,), SEQ, jnp.int32)])
    heads = segment_row[::BLOCK]
    tails = segment_row[BLOCK - 1 :: BLOCK]
    low = jnp.sum(jnp.where(heads[:, None] == labels[None, :], before[None, :], 0), axis=1)
    high = jnp.sum(jnp.where(tails[:, None] == labels[None, :], ends[None, :], 0), axis=1)
    bounds = jnp.concatenate([low // KEYS, (high + KEYS - 1) // KEYS]).astype(jnp.int32)
    return jnp.cos(angle), jnp.sin(angle) * sign[None, :], bounds


def sequence_device(
    tokens, segments, qkv_weight, out_weight, norm_gain, norm_shift, gate_up, down_weight, cotangent
):
    core = lax.axis_index("tensor")
    def ordered(mine, theirs):
        return jnp.where(
            core == 0, jnp.stack([mine, theirs], axis=0), jnp.stack([theirs, mine], axis=0)
        )

    pick = lambda a, i: lax.dynamic_index_in_dim(a, i, 0, keepdims=False)
    source = pick(tokens, core)
    segment_row = pick(segments, core)

    attn_block = qkv_weight.reshape(-1, 3 * D)
    gate_block = gate_up.reshape(-1, 2 * HIDDEN)
    tail_block = jnp.concatenate(
        [out_weight, norm_gain, norm_shift, jnp.zeros((D // 32, TAIL - D - 4), BF16)], axis=1
    )
    down_block = jnp.concatenate(
        [down_weight, jnp.concatenate([tail_block[:, :REST], tail_block[:, REST:]], axis=0)], axis=1
    )
    from_here, from_there = slot_blocks(-1, core), slot_blocks(-1, 1 - core)
    to_here = slot_blocks(1, core).reshape(2, 2, 4).transpose(1, 0, 2).reshape(16)

    cot = ordered(pick(cotangent, core), core_swap(pick(cotangent, 1 - core))).reshape(SEQ, D)
    cosine, sine, bounds = rotary_lanes(segment_row)
    bounds = jnp.concatenate([bounds, core[None]]).astype(jnp.int32)
    tables = (cosine, sine, segment_row[:, None], segment_row[None, :])

    ahead = lambda parts: [part[None] for part in parts]
    attn_four = pile(ahead(depth_parts(attn_block)))
    gate_block = pile([gate_block[None]], deps=(attn_four,))[0]
    gate_parts = ahead(depth_parts(gate_block))
    attn_eight = pile([attn_four, first_swap(attn_four)])
    attn_last = second_swap(attn_eight)
    index = jnp.concatenate([from_here * 2 + core, from_there * 2 + 1 - core]).astype(jnp.int32)
    weights = assemble(
        (attn_eight, attn_last), (core_swap(attn_eight), core_swap(attn_last)), index
    ).reshape(D, 3 * D)

    gate_four = pile(gate_parts, deps=(attn_last,))
    down_block = pile([down_block[None]], deps=(gate_four,))[0]
    down_parts = ahead(depth_parts(down_block))
    saved0 = attn_forward(0, 1, bounds, source, weights, *tables, deps=(gate_four, down_block))
    gate_eight = pile([gate_four, first_swap(gate_four)], deps=(saved0[4],))
    gate_last = second_swap(gate_eight)
    down_four = pile(down_parts, deps=(gate_eight,))
    saved1 = attn_forward(1, 2, bounds, source, weights, *tables, deps=(down_four,))
    down_eight = pile([down_four, first_swap(down_four)], deps=(saved1[4],))
    down_last = second_swap(down_eight)
    pieces = (gate_eight, gate_last, core_swap(gate_eight), core_swap(gate_last))
    pieces += (down_eight, down_last, core_swap(down_eight), core_swap(down_last))

    index = jnp.concatenate([from_here, from_there, core[None]]).astype(jnp.int32)
    ctx = (saved0[3], saved1[3])
    (out, out_leave, normed, mlp_grad, att_grad, ctx_grad, hidden_grad, gu0, gu1, sw0, sw1, sums) = middle(
        index, source, ctx, cot, pieces
    )

    down_there = core_swap(weight_grad(mlp_grad, sw1))
    gu_there = core_swap(weight_grad(normed, gu1))
    down_keep, down_send = weight_grad_join(to_here, mlp_grad, sw0, down_there)
    tail_mine, tail_theirs = out_grad(core, ctx, att_grad, sums)
    gu_keep, gu_send = weight_grad_join(to_here, normed, gu0, gu_there)
    down_first = first_swap(down_send)
    gu_first = first_swap(gu_send)

    common = (source,) + tables
    back0 = attn_backward(0, 0, bounds, saved0, ctx_grad, *common, deps=(gu_send, down_send))
    down_keep, down_send = fold(down_keep, down_first, deps=(back0[1],))
    down_second = second_swap(down_send)
    back1 = attn_backward(0, 1, bounds, saved1, ctx_grad, *common, deps=(down_send,))
    gu_keep, gu_send = fold(gu_keep, gu_first, deps=(back1[1],))
    gu_second = second_swap(gu_send)
    early_keep, early_send = join_dealt(
        to_here,
        (back0[1], back1[1], tail_mine),
        (core_swap(back0[2]), core_swap(back1[2]), core_swap(tail_theirs)),
    )
    early_first = first_swap(early_send)
    back2 = attn_backward(1, 2, bounds, saved1, ctx_grad, *common, deps=(gu_send, early_send))

    late_keep, late_send = join_dealt(to_here, (back2[1],), (core_swap(back2[2]),))
    late_keep, late_send = fold(late_keep, first_swap(late_send))
    early_keep, early_send = fold(early_keep, early_first)
    early_total = depth_sum(early_keep + second_swap(early_send))
    late_total = depth_sum(late_keep + second_swap(late_send))
    down_total = depth_sum(down_keep + down_second)
    gu_total = depth_sum(gu_keep + gu_second)

    rows = D // 32
    qkv_total = jnp.concatenate([early_total[:, : 6 * GROUP], late_total], axis=1)
    qkv_total = qkv_total.reshape(rows, GROUPS, 3, GROUP).transpose(0, 2, 1, 3).reshape(rows, 3, D)
    rest = early_total[:, 6 * GROUP :]
    grad, grad_leave = input_back(core, hidden_grad, (back0[0], back1[0], back2[0]), weights)

    return (
        place(core, out, core_swap(out_leave)),
        place(core, grad, core_swap(grad_leave)),
        qkv_total,
        rest[:, :D],
        rest[:, D : D + 2],
        rest[:, D + 2 : D + 4],
        gu_total.reshape(-1, 2, HIDDEN),
        down_total,
    )


def solution(mesh):
    in_specs = (
        P("dp", None, None),
        P("dp", None),
        P(("dp", "tensor"), None, None),
        P(("dp", "tensor"), None),
        P(("dp", "tensor"), None),
        P(("dp", "tensor"), None),
        P("dp", None, "tensor"),
        P("dp", "tensor"),
        P("dp", "tensor", None),
    )
    out_specs = (
        P("dp", "tensor", None),
        P("dp", "tensor", None),
        P(("dp", "tensor"), None, None),
        P(("dp", "tensor"), None),
        P(("dp", "tensor"), None),
        P(("dp", "tensor"), None),
        P("dp", None, "tensor"),
        P("dp", "tensor"),
    )
    sizes = dict(mesh.shape)

    def per_device(tokens, *others):
        if sizes["dp"] == 16 and sizes["tensor"] == 2 and tokens.shape[0] == 2:
            return sequence_device(tokens, *others)
        return general_device(tokens, *others)

    return jax.shard_map(
        per_device, mesh=mesh, in_specs=in_specs, out_specs=out_specs, check_vma=False
    )
```

```python
import jax
import jax.numpy as jnp
from jax import lax
from jax.experimental import pallas as pl
from jax.experimental.pallas import tpu as pltpu
from jax.sharding import PartitionSpec as P

D = 768
HEADS = 12
HEAD = 64
SEQ = 1024
NDOC = 8


EPSILON = 1e-05
MASKED = -1e30


def for_sending(value):
    return jax.tree.map(lambda a: a.astype(jnp.bfloat16) if a.dtype == jnp.float32 else a, value)


def rotary_tables(segment_row):
    labels = jnp.arange(NDOC + 1, dtype=jnp.int32)
    member = (segment_row[:, None] == labels[None, :]).astype(jnp.int32)
    counts = jnp.sum(member, axis=0)
    starts = jnp.concatenate([jnp.zeros((1,), jnp.int32), jnp.cumsum(counts)[:-1]])
    offset = jnp.sum(member * starts[None, :], axis=1)
    position = (jnp.arange(SEQ, dtype=jnp.int32) - offset).astype(jnp.float32)
    exponent = -2.0 * jnp.arange(HEAD // 2).astype(jnp.float32) / HEAD
    frequency = jnp.power(jnp.float32(1000.0), exponent)
    angle = position[:, None] * frequency[None, :]
    return (jnp.cos(angle)[:, None, :], jnp.sin(angle)[:, None, :])


def rotate(vector, cosine, sine):
    half = vector.shape[-1] // 2
    first_half = vector[..., :half]
    second_half = vector[..., half:]
    return jnp.concatenate(
        [first_half * cosine - second_half * sine, second_half * cosine + first_half * sine],
        axis=-1,
    )


def unrotate(gradient, cosine, sine):

    def turned(vector):
        return rotate(vector, cosine, sine)

    _, pullback = jax.vjp(turned, gradient)
    return pullback(gradient)[0]


def layer_norm(vector, gain, shift):
    center = vector - jnp.mean(vector, axis=-1, keepdims=True)
    variance = jnp.mean(center * center, axis=-1, keepdims=True)
    return center * lax.rsqrt(variance + EPSILON) * gain + shift


def swiglu_piece(gate, upper):
    return jax.nn.silu(gate) * upper


def accumulate(total, term):
    if total is None:
        return term
    return tuple((left + right for left, right in zip(total, term)))


def general_device(
    tokens, segments, qkv_weight, out_weight, norm_gain, norm_shift, gate_up, down_weight, cotangent
):
    tensor_size = lax.axis_size("tensor")
    own_rows = SEQ // tensor_size
    row_start = lax.axis_index("tensor") * own_rows
    score_scale = HEAD ** (-0.5)
    qkv_full, out_full, gain_full, shift_full = (
        lax.all_gather(qkv_weight, ("dp", "tensor"), axis=0, tiled=True),
        lax.all_gather(out_weight, ("dp", "tensor"), axis=0, tiled=True),
        lax.all_gather(norm_gain, ("dp", "tensor"), axis=0, tiled=True),
        lax.all_gather(norm_shift, ("dp", "tensor"), axis=0, tiled=True),
    )
    gains = gain_full.astype(jnp.float32)
    shifts = shift_full.astype(jnp.float32)
    gate_up_full, down_full = (
        lax.all_gather(gate_up, "dp", axis=0, tiled=True),
        lax.all_gather(down_weight, "dp", axis=0, tiled=True),
    )
    batches = tokens.shape[0]
    outputs = []
    input_grads = []
    attn_total = None
    mlp_total = None
    for batch_index in range(batches):
        source = tokens[batch_index]
        own_source = lax.dynamic_slice_in_dim(source, row_start, own_rows, 0)
        segment_row = segments[batch_index]
        cosine, sine = rotary_tables(segment_row)
        own_cos = lax.dynamic_slice_in_dim(cosine, row_start, own_rows, 0)
        own_sin = lax.dynamic_slice_in_dim(sine, row_start, own_rows, 0)
        query_proj = jnp.einsum(
            "sd,de->se", own_source, qkv_full[:, 0], preferred_element_type=jnp.float32
        )
        pair_proj = jnp.einsum(
            "sd,dke->ske", source, qkv_full[:, 1:], preferred_element_type=jnp.float32
        )
        keys = rotate(pair_proj[:, 0].reshape(SEQ, HEADS, HEAD), cosine, sine).astype(jnp.bfloat16)
        values = pair_proj[:, 1].reshape(SEQ, HEADS, HEAD).astype(jnp.bfloat16)
        queries = rotate(query_proj.reshape(own_rows, HEADS, HEAD), own_cos, own_sin).astype(
            jnp.bfloat16
        )
        own_segments = lax.dynamic_slice_in_dim(segment_row, row_start, own_rows, 0)
        allowed = (own_segments[:, None] == segment_row[None, :])[None]
        raw_scores = (
            jnp.einsum("qhe,khe->hqk", queries, keys, preferred_element_type=jnp.float32)
            * score_scale
        )
        masked = jnp.where(allowed, raw_scores, MASKED)
        top_score = jnp.max(masked, axis=-1, keepdims=True)
        logsum = top_score + jnp.log(jnp.sum(jnp.exp(masked - top_score), axis=-1, keepdims=True))
        probs_low = jnp.exp(masked - logsum).astype(jnp.bfloat16)
        context = (
            jnp.einsum("hqk,khe->qhe", probs_low, values, preferred_element_type=jnp.float32)
            .reshape(own_rows, D)
            .astype(jnp.bfloat16)
        )
        attended = jnp.dot(context, out_full, preferred_element_type=jnp.float32)
        hidden_in = own_source.astype(jnp.float32) + attended
        normed = layer_norm(hidden_in, gains[:, 0], shifts[:, 0])
        normed_all = lax.all_gather(normed.astype(jnp.bfloat16), "tensor", axis=0, tiled=True)
        gate_pair = jnp.einsum(
            "sd,dkf->skf", normed_all, gate_up_full, preferred_element_type=jnp.float32
        )
        swiglu = swiglu_piece(gate_pair[:, 0], gate_pair[:, 1]).astype(jnp.bfloat16)
        mlp_out = lax.psum_scatter(
            jnp.einsum("sf,df->sd", swiglu, down_full, preferred_element_type=jnp.float32).astype(
                jnp.bfloat16
            ),
            "tensor",
            scatter_dimension=0,
            tiled=True,
        ).astype(jnp.float32)
        resid = normed + mlp_out
        outputs.append(layer_norm(resid, gains[:, 1], shifts[:, 1]).astype(jnp.bfloat16))
        upstream = cotangent[batch_index].astype(jnp.float32)
        _, second_pull = jax.vjp(layer_norm, resid, gains[:, 1], shifts[:, 1])
        resid_grad, gain_two, shift_two = second_pull(upstream)
        mlp_grad = lax.all_gather(resid_grad.astype(jnp.bfloat16), "tensor", axis=0, tiled=True)
        swiglu_grad = jnp.einsum(
            "sd,df->sf", mlp_grad, down_full, preferred_element_type=jnp.float32
        )
        _, glu_pull = jax.vjp(swiglu_piece, gate_pair[:, 0], gate_pair[:, 1])
        gate_grad, upper_grad = glu_pull(swiglu_grad)
        pair_grad = jnp.stack([gate_grad, upper_grad], axis=1).astype(jnp.bfloat16)
        down_term = jnp.einsum("sd,sf->df", mlp_grad, swiglu, preferred_element_type=jnp.float32)
        gate_up_term = jnp.einsum(
            "sd,skf->dkf", normed_all, pair_grad, preferred_element_type=jnp.float32
        )
        normed_grad = resid_grad + lax.psum_scatter(
            jnp.einsum("skf,dkf->sd", pair_grad, gate_up_full, preferred_element_type=jnp.float32),
            "tensor",
            scatter_dimension=0,
            tiled=True,
        )
        _, first_pull = jax.vjp(layer_norm, hidden_in, gains[:, 0], shifts[:, 0])
        hidden_grad, gain_one, shift_one = first_pull(normed_grad)
        attended_grad = hidden_grad.astype(jnp.bfloat16)
        out_term = jnp.einsum(
            "sd,se->de", context, attended_grad, preferred_element_type=jnp.float32
        )
        context_grad = (
            jnp.einsum("se,de->sd", attended_grad, out_full, preferred_element_type=jnp.float32)
            .astype(jnp.bfloat16)
            .reshape(own_rows, HEADS, HEAD)
        )
        probs = jnp.exp(masked - logsum)
        weights_grad = jnp.einsum(
            "qhe,khe->hqk", context_grad, values, preferred_element_type=jnp.float32
        )
        row_delta = jnp.sum(probs * weights_grad, axis=-1, keepdims=True)
        score_grad = (probs * (weights_grad - row_delta)).astype(jnp.bfloat16)
        query_grad = (
            jnp.einsum("hqk,khe->qhe", score_grad, keys, preferred_element_type=jnp.float32)
            * score_scale
        )
        key_part = (
            jnp.einsum("hqk,qhe->khe", score_grad, queries, preferred_element_type=jnp.float32)
            * score_scale
        )
        value_part = jnp.einsum(
            "hqk,qhe->khe", probs_low, context_grad, preferred_element_type=jnp.float32
        )
        key_value = lax.psum_scatter(
            jnp.stack(
                [
                    key_part.reshape(lax.axis_size("tensor") * own_rows, D),
                    value_part.reshape(lax.axis_size("tensor") * own_rows, D),
                ],
                axis=1,
            ).astype(jnp.bfloat16),
            "tensor",
            scatter_dimension=0,
            tiled=True,
        ).astype(jnp.float32)
        query_back = unrotate(query_grad, own_cos, own_sin).reshape(own_rows, D)
        key_back = unrotate(
            key_value[:, 0].reshape(own_rows, HEADS, HEAD), own_cos, own_sin
        ).reshape(own_rows, D)
        proj_grad = jnp.stack([query_back, key_back, key_value[:, 1]], axis=1).astype(jnp.bfloat16)
        input_grads.append(
            hidden_grad
            + jnp.einsum("ske,dke->sd", proj_grad, qkv_full, preferred_element_type=jnp.float32)
        )
        qkv_term = jnp.einsum(
            "sd,ske->dke", own_source, proj_grad, preferred_element_type=jnp.float32
        )
        gain_term = jnp.stack([gain_one, gain_two], axis=1)
        shift_term = jnp.stack([shift_one, shift_two], axis=1)
        attn_terms = (qkv_term, out_term, gain_term, shift_term)
        mlp_terms = (gate_up_term, down_term)
        attn_total = accumulate(attn_total, attn_terms)
        mlp_total = accumulate(mlp_total, mlp_terms)
    attn_final = lax.psum_scatter(attn_total, ("dp", "tensor"), scatter_dimension=0, tiled=True)
    mlp_final = jax.tree.map(
        lambda part: part.astype(jnp.float32),
        lax.psum_scatter(for_sending(mlp_total), "dp", scatter_dimension=0, tiled=True),
    )
    return (
        jnp.stack(outputs, axis=0),
        jnp.stack(input_grads, axis=0),
        attn_final[0],
        attn_final[1],
        attn_final[2],
        attn_final[3],
        mlp_final[0],
        mlp_final[1],
    )


HIDDEN = 1536
WIDE = 3 * HIDDEN
REST = 512
TAIL = 2 * REST
GROUP = 4 * HEAD
GROUPS = D // GROUP
KEYS = 128
LANES = 2 * HEAD
BLOCK = 256
NBLOCK = SEQ // BLOCK
ROWS = 256
CHUNK = 512
LOG2E = 1.4426950408889634
F32 = jnp.float32
BF16 = jnp.bfloat16


def across(value, move):
    pairs = []
    for z in range(4):
        for y in range(2):
            for x in range(2):
                for c in range(2):
                    tz, ty, tx, tc = move(z, y, x, c)
                    pairs.append((((z * 2 + y) * 2 + x) * 2 + c, ((tz * 2 + ty) * 2 + tx) * 2 + tc))
    return lax.ppermute(value, ("dp", "tensor"), pairs)


def core_swap(value):
    return across(value, lambda z, y, x, c: (z, y, x, 1 - c))


def first_swap(value):
    return across(value, lambda z, y, x, c: (z, y, 1 - x, c) if c == 0 else (z, 1 - y, x, c))


def second_swap(value):
    return across(value, lambda z, y, x, c: (z, 1 - y, x, c) if c == 0 else (z, y, 1 - x, c))


def depth_shift(value, steps):
    return across(value, lambda z, y, x, c: ((z + steps) % 4, y, x, c))


def slot_blocks(sign, core):
    me = lax.axis_index("dp")
    z, y, x = me // 4, (me // 2) % 2, me % 2
    slot = jnp.arange(16, dtype=jnp.int32)
    second, first, depth = slot // 8, (slot // 4) % 2, slot % 4
    x_bit = jnp.where(core == 0, first, second)
    y_bit = jnp.where(core == 0, second, first)
    return (((z + sign * depth) % 4) * 4 + (y ^ y_bit) * 2 + (x ^ x_bit)).astype(jnp.int32)


def depth_parts(block):
    return [block] + [depth_shift(block, k) for k in (1, 2, 3)]


def depth_ring(block):
    parts = [block]
    for _ in range(3):
        parts.append(depth_shift(parts[-1], 1))
    return parts


def cost(flops, nbytes, trans=0):
    return pl.CostEstimate(flops=int(flops), bytes_accessed=int(nbytes), transcendentals=int(trans))


def params(vmem_mb, sem=("arbitrary",)):
    return pltpu.CompilerParams(dimension_semantics=sem, vmem_limit_bytes=vmem_mb << 20)


ANY = pl.BlockSpec(memory_space=pl.ANY)


def pile(parts, deps=()):
    spans, start = [], 0
    for part in parts:
        spans.append((start, part.shape[0]))
        start += part.shape[0]

    def body(*refs):
        ins, out, sem = refs[: len(parts)], refs[-2], refs[-1]
        copies = [
            pltpu.make_async_copy(ref, out.at[pl.ds(at, n)], sem.at[i])
            for i, (ref, (at, n)) in enumerate(zip(ins, spans))
        ]
        for cp in copies:
            cp.start()
        for cp in copies:
            cp.wait()

    shape = (start,) + parts[0].shape[1:]
    return pl.pallas_call(
        body,
        in_specs=[ANY] * (len(parts) + len(deps)),
        out_specs=ANY,
        out_shape=jax.ShapeDtypeStruct(shape, parts[0].dtype),
        scratch_shapes=[pltpu.SemaphoreType.DMA((len(parts),))],
        compiler_params=params(60, None),
        cost_estimate=cost(0, 4 * start * shape[1] * shape[2]),
        name="pile",
    )(*parts, *deps)


def place(core, mine, there):
    def body(c, a, b, out, sem):
        first = pltpu.make_async_copy(a, out.at[c[0]], sem.at[0])
        second = pltpu.make_async_copy(b, out.at[1 - c[0]], sem.at[1])
        first.start()
        second.start()
        first.wait()
        second.wait()

    return pl.pallas_call(
        body,
        grid_spec=pltpu.PrefetchScalarGridSpec(
            num_scalar_prefetch=1,
            grid=(1,),
            in_specs=[ANY, ANY],
            out_specs=ANY,
            scratch_shapes=[pltpu.SemaphoreType.DMA((2,))],
        ),
        out_shape=jax.ShapeDtypeStruct((2,) + mine.shape, mine.dtype),
        compiler_params=params(60),
        cost_estimate=cost(0, 4 * mine.size),
        name="place",
    )(core[None], mine, there)


def assemble(own, other, index, deps=()):
    def body(idx, a, b, c, d, *rest):
        out, sem = rest[-2:]
        copies = []
        for i, ref in enumerate((a, b, c, d)):
            for s in range(8):
                copies.append(
                    pltpu.make_async_copy(ref.at[s], out.at[idx[i * 8 + s]], sem.at[i * 8 + s])
                )
        for cp in copies:
            cp.start()
        for cp in copies:
            cp.wait()

    rows, wide = own[0].shape[1:]
    return pl.pallas_call(
        body,
        grid_spec=pltpu.PrefetchScalarGridSpec(
            num_scalar_prefetch=1,
            grid=(1,),
            in_specs=[ANY] * (4 + len(deps)),
            out_specs=ANY,
            scratch_shapes=[pltpu.SemaphoreType.DMA((32,))],
        ),
        out_shape=jax.ShapeDtypeStruct((32, rows, wide), BF16),
        compiler_params=params(60),
        cost_estimate=cost(0, 4 * 32 * rows * wide),
        name="assemble",
    )(index, *own, *other, *deps)


def turn(vector, cosine, sine):
    lane = lax.broadcasted_iota(jnp.int32, vector.shape, 1)
    swapped = jnp.where(
        lane % HEAD < HEAD // 2,
        pltpu.roll(vector, LANES - HEAD // 2, 1),
        pltpu.roll(vector, HEAD // 2, 1),
    )
    return vector * cosine + swapped * sine


def dot_nn(a, b):
    return lax.dot_general(a, b, (((1,), (0,)), ((), ())), preferred_element_type=F32)


def dot_nt(a, b):
    return lax.dot_general(a, b, (((1,), (1,)), ((), ())), preferred_element_type=F32)


def dot_tn(a, b):
    return lax.dot_general(a, b, (((0,), (0,)), ((), ())), preferred_element_type=F32)


def stacked(low_lane, pair):
    zero = jnp.zeros_like(pair)
    return jnp.concatenate(
        [jnp.where(low_lane, pair, zero), jnp.where(low_lane, zero, pair)], axis=0
    )


def windows(bnd, i, work):
    blocks = (bnd[NBLOCK + i] - bnd[i] + BLOCK // KEYS - 1) // (BLOCK // KEYS)
    for width in range(1, NBLOCK + 1):

        @pl.when(blocks == width)
        def _():
            low = jnp.minimum(bnd[i], (SEQ - width * BLOCK) // KEYS)
            work(pl.ds(pl.multiple_of(low * KEYS, KEYS), width * BLOCK))


def attn_forward(first, count, bounds, source, weights, cosine, sine, seg_col, seg_row, deps=()):
    def body(bnd, x, wq, wk, wv, cos, sin, sc, sr, *rest):
        q_out, k_out, v_out, ctx_out, lse_out, qm = rest[len(deps) :]
        low_lane = lax.broadcasted_iota(jnp.int32, (BLOCK, LANES), 1) < HEAD

        @pl.loop(0, NBLOCK)
        def _(r):
            rows = pl.ds(pl.multiple_of(r * BLOCK, BLOCK), BLOCK)
            xr, cr, sn = x[rows, :], cos[rows, :], sin[rows, :]
            q_proj, k_proj = dot_nn(xr, wq[...]), dot_nn(xr, wk[...])
            v_out[rows, :] = dot_nn(xr, wv[...]).astype(BF16)
            for p in range(GROUP // LANES):
                ln = slice(p * LANES, (p + 1) * LANES)
                q = turn(q_proj[:, ln], cr, sn).astype(BF16) * jnp.asarray(HEAD**-0.5, BF16)
                q_out[rows, ln] = q
                qm[p, r] = stacked(low_lane, q)
                k_out[rows, ln] = turn(k_proj[:, ln], cr, sn).astype(BF16)

        def block(i, _):
            rows = pl.ds(pl.multiple_of(i * BLOCK, BLOCK), BLOCK)
            own = jnp.concatenate([sc[rows, :], sc[rows, :]], axis=0)

            def work(cols):
                seen = own == sr[:, cols]
                for p in range(GROUP // LANES):
                    ln = slice(p * LANES, (p + 1) * LANES)
                    s = jnp.where(seen, dot_nt(qm[p, i], k_out[cols, ln]) * LOG2E, MASKED)
                    top = jnp.max(s, axis=1, keepdims=True)
                    e = jnp.exp2(s - top)
                    total = jnp.sum(e, axis=1, keepdims=True)
                    mixed = dot_nn(e.astype(BF16), v_out[cols, ln]) / total
                    ctx_out[rows, ln] = jnp.where(low_lane, mixed[:BLOCK], mixed[BLOCK:]).astype(BF16)
                    logs = top + jnp.log2(total)
                    flipped = jnp.where(low_lane, logs[:BLOCK], logs[BLOCK:]).T
                    lse_out[0, 2 * p : 2 * p + 1, rows] = flipped[0:1]
                    lse_out[0, 2 * p + 1 : 2 * p + 2, rows] = flipped[HEAD : HEAD + 1]

            windows(bnd, i, work)
            return 0

        lax.fori_loop(0, NBLOCK, block, 0)

    full = lambda shape: pl.BlockSpec(shape, lambda p, b: (0,) * len(shape))
    column = lambda shift: pl.BlockSpec((D, GROUP), lambda p, b: (0, shift * GROUPS + first + p))
    part = pl.BlockSpec((SEQ, GROUP), lambda p, b: (0, p))
    act = jax.ShapeDtypeStruct((SEQ, count * GROUP), BF16)
    return pl.pallas_call(
        body,
        grid_spec=pltpu.PrefetchScalarGridSpec(
            num_scalar_prefetch=1,
            grid=(count,),
            in_specs=[
                full((SEQ, D)),
                column(0),
                column(1),
                column(2),
                full((SEQ, LANES)),
                full((SEQ, LANES)),
                full((SEQ, 1)),
                full((1, SEQ)),
            ]
            + [ANY] * len(deps),
            out_specs=[part] * 4 + [pl.BlockSpec((1, 8, SEQ), lambda p, b: (p, 0, 0))],
            scratch_shapes=[pltpu.VMEM((GROUP // LANES, NBLOCK, 2 * BLOCK, LANES), BF16)],
        ),
        out_shape=[act] * 4 + [jax.ShapeDtypeStruct((count, 8, SEQ), F32)],
        compiler_params=params(60),
        cost_estimate=cost(
            count * GROUP * (6 * SEQ * D + 16 * SEQ * SEQ), 8 << 20, count * 4 * SEQ * SEQ
        ),
        name="attn_forward",
    )(bounds, source, weights, weights, weights, cosine, sine, seg_col, seg_row, *deps)


def deal(core, whole, mine, theirs, columns):
    parts = whole.reshape(16, 2, D // 32, whole.shape[1])
    first, second = parts[:, 0], parts[:, 1]
    mine[:, :, columns] = jnp.where(core == 0, first, second).astype(BF16)
    theirs[:, :, columns] = jnp.where(core == 0, second, first).astype(BF16)


def attn_backward(at, grad_at, bounds, saved, ctx_grad, source, cosine, sine, seg_col, seg_row, deps=()):
    def body(bnd, q, k, v, o, do, lse, x, cos, sin, sc, sr, *rest):
        core = bnd[2 * NBLOCK]
        out, mine, theirs, qm, dm, dq, dk, dv, dl = rest[len(deps) :]
        low_lane = lax.broadcasted_iota(jnp.int32, (BLOCK, LANES), 1) < HEAD
        row = lax.broadcasted_iota(jnp.int32, (8, LANES), 0)
        lane = lax.broadcasted_iota(jnp.int32, (8, LANES), 1)
        pick = jnp.where(row == lane // HEAD, 1.0, 0.0).astype(F32)
        for p in range(GROUP // LANES):
            ln = slice(p * LANES, (p + 1) * LANES)

            @pl.loop(0, NBLOCK)
            def _(i):
                rows = pl.ds(pl.multiple_of(i * BLOCK, BLOCK), BLOCK)
                qm[p, i] = stacked(low_lane, q[rows, ln])
                dm[p, i] = stacked(low_lane, do[rows, ln])

            dl[p] = lax.dot_general(
                pick,
                do[:, ln].astype(F32) * o[:, ln].astype(F32),
                (((1,), (1,)), ((), ())),
                preferred_element_type=F32,
                precision=lax.Precision.HIGHEST,
            )
        dk[...] = jnp.zeros_like(dk)
        dv[...] = jnp.zeros_like(dv)

        def block(i, _):
            rows = pl.ds(pl.multiple_of(i * BLOCK, BLOCK), BLOCK)
            own = jnp.concatenate([sr[:, rows], sr[:, rows]], axis=1)

            def work(cols):
                seen = sc[cols, :] == own
                for p in range(GROUP // LANES):
                    ln = slice(p * LANES, (p + 1) * LANES)
                    keys, values, qq, dd = k[cols, ln], v[cols, ln], qm[p, i], dm[p, i]
                    logs = jnp.concatenate(
                        [lse[0, 2 * p : 2 * p + 1, rows], lse[0, 2 * p + 1 : 2 * p + 2, rows]], axis=1
                    )
                    deltas = jnp.concatenate([dl[p, 0:1, rows], dl[p, 1:2, rows]], axis=1)
                    s = dot_nt(keys, qq) * LOG2E - logs
                    probs = jnp.exp2(jnp.where(seen, s, MASKED))
                    g = (probs * (dot_nt(values, dd) - deltas)).astype(BF16)
                    dv[cols, ln] += dot_nn(probs.astype(BF16), dd)
                    dk[cols, ln] += dot_nn(g, qq)
                    both = dot_tn(g, keys)
                    dq[rows, ln] = jnp.where(low_lane, both[:BLOCK], both[BLOCK:])

            windows(bnd, i, work)
            return 0

        lax.fori_loop(0, NBLOCK, block, 0)

        @pl.loop(0, NBLOCK)
        def _(r):
            rows = pl.ds(pl.multiple_of(r * BLOCK, BLOCK), BLOCK)
            cr, sn = cos[rows, :], -sin[rows, :]
            for p in range(GROUP // LANES):
                ln = slice(p * LANES, (p + 1) * LANES)
                out[0, rows, ln] = turn(dq[rows, ln] * (HEAD**-0.5), cr, sn).astype(BF16)
                out[1, rows, ln] = turn(dk[rows, ln], cr, sn).astype(BF16)
                out[2, rows, ln] = dv[rows, ln].astype(BF16)

        for i in range(3):
            deal(core, dot_tn(x[...], out[i]), mine, theirs, slice(i * GROUP, (i + 1) * GROUP))

    full = lambda shape: pl.BlockSpec(shape, lambda p, b: (0,) * len(shape))
    part = pl.BlockSpec((SEQ, GROUP), lambda p, b: (0, at))
    low2 = pltpu.VMEM((GROUP // LANES, NBLOCK, 2 * BLOCK, LANES), BF16)
    wide = pltpu.VMEM((SEQ, GROUP), F32)
    dealt = (16, D // 32, 3 * GROUP)
    return pl.pallas_call(
        body,
        grid_spec=pltpu.PrefetchScalarGridSpec(
            num_scalar_prefetch=1,
            grid=(1,),
            in_specs=[part] * 4
            + [
                pl.BlockSpec((SEQ, GROUP), lambda p, b: (0, grad_at)),
                pl.BlockSpec((1, 8, SEQ), lambda p, b: (at, 0, 0)),
                full((SEQ, D)),
                full((SEQ, LANES)),
                full((SEQ, LANES)),
                full((SEQ, 1)),
                full((1, SEQ)),
            ]
            + [ANY] * len(deps),
            out_specs=[full((3, SEQ, GROUP)), full(dealt), full(dealt)],
            scratch_shapes=[
                low2,
                low2,
                wide,
                wide,
                wide,
                pltpu.VMEM((GROUP // LANES, 8, SEQ), F32),
            ],
        ),
        out_shape=[
            jax.ShapeDtypeStruct((3, SEQ, GROUP), BF16),
            jax.ShapeDtypeStruct(dealt, BF16),
            jax.ShapeDtypeStruct(dealt, BF16),
        ],
        compiler_params=params(60),
        cost_estimate=cost(GROUP * (40 * SEQ * SEQ + 6 * SEQ * D), 10 << 20, 4 * SEQ * SEQ),
        name="attn_backward",
    )(bounds, *saved[:4], ctx_grad, saved[4], source, cosine, sine, seg_col, seg_row, *deps)


def weight_grad(left, right, columns=512):
    wide = right.shape[1]

    def body(a, b, out, flipped):
        @pl.when(pl.program_id(0) == 0)
        def _():
            flipped[...] = a[...].T

        out[...] = dot_nn(flipped[...], b[...]).astype(BF16)

    return pl.pallas_call(
        body,
        grid=(wide // columns,),
        in_specs=[
            pl.BlockSpec((SEQ, D), lambda n: (0, 0)),
            pl.BlockSpec((SEQ, columns), lambda n: (0, n)),
        ],
        out_specs=pl.BlockSpec((D, columns), lambda n: (0, n)),
        out_shape=jax.ShapeDtypeStruct((D, wide), BF16),
        scratch_shapes=[pltpu.VMEM((D, SEQ), BF16)],
        compiler_params=params(60),
        cost_estimate=cost(2 * SEQ * D * wide, 2 * (SEQ * D + SEQ * wide + D * wide)),
        name="weight_grad",
    )(left, right)


def weight_grad_join(index, left, right, there, count, columns=512):
    wide = right.shape[1]
    rows = D // 16
    each = 16 // count

    def body(idx, a, b, other, *refs):
        outs, (flipped, total) = refs[:count], refs[count:]

        @pl.when(pl.program_id(0) == 0)
        def _():
            flipped[...] = a[...].T

        total[...] = dot_nn(flipped[...], b[...]) + other[...].astype(F32)
        for s in range(16):
            at = pl.ds(pl.multiple_of(idx[s] * rows, 16), rows)
            outs[s // each][s % each] = total[at, :].astype(BF16)

    part = pl.BlockSpec((each, rows, columns), lambda n, i: (0, 0, n))
    shape = jax.ShapeDtypeStruct((each, rows, wide), BF16)
    return pl.pallas_call(
        body,
        grid_spec=pltpu.PrefetchScalarGridSpec(
            num_scalar_prefetch=1,
            grid=(wide // columns,),
            in_specs=[
                pl.BlockSpec((SEQ, D), lambda n, i: (0, 0)),
                pl.BlockSpec((SEQ, columns), lambda n, i: (0, n)),
                pl.BlockSpec((D, columns), lambda n, i: (0, n)),
            ],
            out_specs=[part] * count,
            scratch_shapes=[pltpu.VMEM((D, SEQ), BF16), pltpu.VMEM((D, columns), F32)],
        ),
        out_shape=[shape] * count,
        compiler_params=params(60),
        cost_estimate=cost(2 * SEQ * D * wide, 2 * (SEQ * D + SEQ * wide + 2 * D * wide)),
        name="weight_grad_join",
    )(index, left, right, there)


def out_grad(core, ctx, right, norms):
    def body(c, a, b, d, nrm, mine, theirs):
        whole = jnp.concatenate([dot_tn(p[...], b[...]) for p in (a, d)], axis=0)
        deal(c[0], whole, mine, theirs, slice(0, D))
        flipped = jnp.concatenate([nrm[...], jnp.zeros((LANES - 8, D), F32)], axis=0).T
        filled = jnp.concatenate([flipped, jnp.zeros((D, LANES), F32)], axis=1)
        deal(c[0], filled, mine, theirs, slice(D, TAIL))

    full = lambda shape: pl.BlockSpec(shape, lambda p, b: (0,) * len(shape))
    dealt = (16, D // 32, TAIL)
    return pl.pallas_call(
        body,
        grid_spec=pltpu.PrefetchScalarGridSpec(
            num_scalar_prefetch=1,
            grid=(1,),
            in_specs=[full((SEQ, GROUP)), full((SEQ, D)), full((SEQ, D - GROUP)), full((8, D))],
            out_specs=[full(dealt), full(dealt)],
        ),
        out_shape=[jax.ShapeDtypeStruct(dealt, BF16)] * 2,
        compiler_params=params(60),
        cost_estimate=cost(2 * SEQ * D * D, 8 << 20),
        name="out_grad",
    )(core[None], ctx[0], right, ctx[1], norms)


def join_dealt(index, mine, there, deps=()):
    widths = [m.shape[2] for m in mine]
    wide, rows, count = sum(widths), D // 32, len(mine)

    def body(idx, *refs):
        ours, others, keep, send = refs[:count], refs[count : 2 * count], refs[-2], refs[-1]
        for s in range(16):
            start = 0
            for a, b, n in zip(ours, others, widths):
                total = a[idx[s]].astype(F32) + b[idx[s]].astype(F32)
                (keep, send)[s // 8][s % 8, :, start : start + n] = total.astype(BF16)
                start += n

    full = lambda shape: pl.BlockSpec(shape, lambda p, b: (0,) * len(shape))
    half = (8, rows, wide)
    return pl.pallas_call(
        body,
        grid_spec=pltpu.PrefetchScalarGridSpec(
            num_scalar_prefetch=1,
            grid=(1,),
            in_specs=[full((16, rows, n)) for n in widths] * 2 + [ANY] * len(deps),
            out_specs=[full(half), full(half)],
        ),
        out_shape=[jax.ShapeDtypeStruct(half, BF16)] * 2,
        compiler_params=params(60),
        cost_estimate=cost(D * wide // 2, 3 * D * wide),
        name="join_dealt",
    )(index, *mine, *there, *deps)


def fold(keep, there, count, dtype=BF16, deps=()):
    blocks, rows, wide = keep.shape
    each = blocks // count

    def body(a, b, *rest):
        for n, out in enumerate(rest[len(deps) :]):
            at = slice(n * each, (n + 1) * each)
            out[...] = (a[at].astype(F32) + b[at].astype(F32)).astype(dtype)

    columns = wide // 2
    part = pl.BlockSpec((blocks, rows, columns), lambda i: (0, 0, i))
    return pl.pallas_call(
        body,
        grid=(2,),
        in_specs=[part, part] + [ANY] * len(deps),
        out_specs=[pl.BlockSpec((each, rows, columns), lambda i: (0, 0, i))] * count,
        out_shape=[jax.ShapeDtypeStruct((each, rows, wide), dtype)] * count,
        compiler_params=params(60),
        cost_estimate=cost(blocks * rows * wide, 6 * blocks * rows * wide),
        name="fold",
    )(keep, there, *deps)


def total4(parts, count, dtype, deps=()):
    blocks, rows, wide = parts[0].shape
    each = blocks // count

    def body(a, b, c, d, *rest):
        total = a[...].astype(F32) + b[...].astype(F32) + c[...].astype(F32) + d[...].astype(F32)
        for n, out in enumerate(rest[len(deps) :]):
            out[...] = total[n * each : (n + 1) * each].astype(dtype)

    columns = wide // 2
    part = pl.BlockSpec((blocks, rows, columns), lambda i: (0, 0, i))
    return pl.pallas_call(
        body,
        grid=(2,),
        in_specs=[part] * 4 + [ANY] * len(deps),
        out_specs=[pl.BlockSpec((each, rows, columns), lambda i: (0, 0, i))] * count,
        out_shape=[jax.ShapeDtypeStruct((each, rows, wide), dtype)] * count,
        compiler_params=params(60),
        cost_estimate=cost(4 * blocks * rows * wide, 10 * blocks * rows * wide),
        name="total",
    )(*parts, *deps)


def input_back(core, hidden_grad, projected, weights, deps=()):
    half = SEQ // 2 // BLOCK

    def body(c, hid, a, b, d, w, *rest):
        mine, leave = rest[-2:]
        total = hid[...]
        for g, ref in enumerate((a, b, d)):
            for i in range(3):
                at = i * D + g * GROUP
                total = total + dot_nt(ref[i], w[:, at : at + GROUP])
        own = pl.program_id(0) // half == c[0]

        @pl.when(own)
        def _():
            mine[...] = total

        @pl.when(jnp.logical_not(own))
        def _():
            leave[...] = total

    row = pl.BlockSpec((BLOCK, D), lambda r, c: (r, 0))
    shape = jax.ShapeDtypeStruct((SEQ // 2, D), F32)
    return pl.pallas_call(
        body,
        grid_spec=pltpu.PrefetchScalarGridSpec(
            num_scalar_prefetch=1,
            grid=(SEQ // BLOCK,),
            in_specs=[row]
            + [pl.BlockSpec((3, BLOCK, GROUP), lambda r, c: (0, r, 0))] * 3
            + [pl.BlockSpec((D, 3 * D), lambda r, c: (0, 0))]
            + [ANY] * len(deps),
            out_specs=[
                pl.BlockSpec((BLOCK, D), lambda r, c: (jnp.clip(r - half * c[0], 0, half - 1), 0)),
                pl.BlockSpec(
                    (BLOCK, D), lambda r, c: (jnp.clip(r - half * (1 - c[0]), 0, half - 1), 0)
                ),
            ],
        ),
        out_shape=[shape, shape],
        compiler_params=params(60),
        cost_estimate=cost(6 * SEQ * D * D, 16 << 20),
        name="input_back",
    )(core[None], hidden_grad, *projected, weights, *deps)


def middle(index, source, ctx, cot, pieces):
    def norm(v):
        center = v - jnp.mean(v, axis=1, keepdims=True)
        scale = lax.rsqrt(jnp.mean(center * center, axis=1, keepdims=True) + EPSILON)
        return center * scale, scale

    def norm_back(u, hat, scale, gain):
        g = u * gain
        return scale * (
            g - jnp.mean(g, axis=1, keepdims=True) - hat * jnp.mean(g * hat, axis=1, keepdims=True)
        )

    def body(
        idx, x, ctx0, ctx1, cot, *refs
    ):
        pieces, refs = refs[:8], refs[8:]
        out, out_leave, normed_out, mlp_out, att_out, ctxg_out, hid_out, gu0, gu1, sw0, sw1, sums = refs[:12]
        w, wo, tail, nrm, sem = refs[12:]
        step = pl.program_id(0)
        core = idx[32]
        rows = D // 32

        @pl.when(step == 0)
        def _():
            copies = []
            for i, ref in enumerate(pieces):
                which, rest = i // 4, i % 4
                for s in range(8):
                    block = idx[rest * 8 + s]
                    at = pl.ds(pl.multiple_of(block * 48, 16), 48)
                    owner = core if rest < 2 else 1 - core
                    n = i * 8 + s
                    if which == 0:
                        copies.append(
                            pltpu.make_async_copy(
                                ref.at[s], w.at[rest // 2, at, pl.ds(0, 2 * HIDDEN)], sem.at[n]
                            )
                        )
                        continue
                    copies.append(
                        pltpu.make_async_copy(
                            ref.at[s, :, pl.ds(0, HIDDEN)],
                            w.at[rest // 2, at, pl.ds(2 * HIDDEN, HIDDEN)],
                            sem.at[n],
                        )
                    )
                    for part in range(2):
                        copies.append(
                            pltpu.make_async_copy(
                                ref.at[s, pl.ds(part * rows, rows), pl.ds(HIDDEN, REST)],
                                tail.at[part, block * 2 + owner],
                                sem.at[32 + n + 32 * part],
                            )
                        )
            for cp in copies:
                cp.start()
            for cp in copies:
                cp.wait()
            joined = jnp.concatenate(
                [tail[0].reshape(D, REST), tail[1].reshape(D, REST)], axis=1
            )
            wo[...] = joined[:, :D]
            nrm[...] = joined[:, D : D + LANES].astype(F32).T[:8]
            sums[...] = jnp.zeros_like(sums)

        gain1, gain2, shift1, shift2 = (nrm[i : i + 1, :] for i in range(4))
        hidden_in = x[...].astype(F32) + dot_nn(ctx0[...], wo[:GROUP, :]) + dot_nn(ctx1[...], wo[GROUP:, :])
        hat1, scale1 = norm(hidden_in)
        normed = hat1 * gain1 + shift1
        low = normed.astype(BF16)
        normed_out[...] = low
        total = normed
        for half in range(2):
            sw, gu = (sw0, sw1)[half], (gu0, gu1)[half]
            for n in range(HIDDEN // CHUNK):
                g_at, u_at, d_at = (pl.ds(p * HIDDEN + n * CHUNK, CHUNK) for p in range(3))
                gate = dot_nn(low, w[half, :, g_at])
                up = dot_nn(low, w[half, :, u_at])
                s = jax.nn.sigmoid(gate)
                silu = gate * s
                act = (silu * up).astype(BF16)
                gu[:, g_at] = (up * (s * (1.0 + gate * (1.0 - s)))).astype(BF16)
                gu[:, u_at] = silu.astype(BF16)
                sw[:, g_at] = act
                total = total + dot_nt(act, w[half, :, d_at])
        hat2, scale2 = norm(total)
        result = (hat2 * gain2 + shift2).astype(BF16)
        own = step // (SEQ // 2 // ROWS) == core

        @pl.when(own)
        def _():
            out[...] = result

        @pl.when(jnp.logical_not(own))
        def _():
            out_leave[...] = result

        u2 = cot[...].astype(F32)
        resid = norm_back(u2, hat2, scale2, gain2)
        mlp = resid.astype(BF16)
        mlp_out[...] = mlp
        back = resid
        for half in range(2):
            gu = (gu0, gu1)[half]
            for n in range(HIDDEN // CHUNK):
                g_at, u_at, d_at = (pl.ds(p * HIDDEN + n * CHUNK, CHUNK) for p in range(3))
                grad = dot_nn(mlp, w[half, :, d_at])
                gate_grad = (grad * gu[:, g_at].astype(F32)).astype(BF16)
                up_grad = (grad * gu[:, u_at].astype(F32)).astype(BF16)
                gu[:, g_at] = gate_grad
                gu[:, u_at] = up_grad
                back = back + dot_nt(gate_grad, w[half, :, g_at])
                back = back + dot_nt(up_grad, w[half, :, u_at])
        hidden_grad = norm_back(back, hat1, scale1, gain1)
        hid_out[...] = hidden_grad
        att = hidden_grad.astype(BF16)
        att_out[...] = att
        ctxg_out[...] = dot_nt(att, wo[...]).astype(BF16)
        for i, v in enumerate((back * hat1, u2 * hat2, back, u2)):
            sums[i : i + 1, :] += jnp.sum(v, axis=0, keepdims=True)

    row = pl.BlockSpec((ROWS, D), lambda r, i: (r, 0))
    wide = lambda n: pl.BlockSpec((ROWS, n), lambda r, i: (r, 0))
    whole = lambda shape: pl.BlockSpec(shape, lambda r, i: (0,) * len(shape))
    act = lambda n, t=BF16: jax.ShapeDtypeStruct((SEQ, n), t)
    half = SEQ // 2 // ROWS
    mine = pl.BlockSpec((ROWS, D), lambda r, i: (jnp.clip(r - half * i[32], 0, half - 1), 0))
    leave = pl.BlockSpec((ROWS, D), lambda r, i: (jnp.clip(r - half * (1 - i[32]), 0, half - 1), 0))
    return pl.pallas_call(
        body,
        grid_spec=pltpu.PrefetchScalarGridSpec(
            num_scalar_prefetch=1,
            grid=(SEQ // ROWS,),
            in_specs=[row, wide(GROUP), wide(D - GROUP), row] + [ANY] * 8,
            out_specs=[mine, leave]
            + [row] * 5
            + [wide(2 * HIDDEN)] * 2
            + [wide(HIDDEN)] * 2
            + [whole((8, D))],
            scratch_shapes=[
                pltpu.VMEM((2, D, WIDE), BF16),
                pltpu.VMEM((D, D), BF16),
                pltpu.VMEM((2, 32, D // 32, REST), BF16),
                pltpu.VMEM((8, D), F32),
                pltpu.SemaphoreType.DMA((128,)),
            ],
        ),
        out_shape=[
            jax.ShapeDtypeStruct((SEQ // 2, D), BF16),
            jax.ShapeDtypeStruct((SEQ // 2, D), BF16),
            act(D),
            act(D),
            act(D),
            act(D),
            act(D, F32),
            act(2 * HIDDEN),
            act(2 * HIDDEN),
            act(HIDDEN),
            act(HIDDEN),
            jax.ShapeDtypeStruct((8, D), F32),
        ],
        compiler_params=params(60),
        cost_estimate=cost(12 * SEQ * D * 2 * HIDDEN + 4 * SEQ * D * D, 60 << 20, 4 * SEQ * HIDDEN),
        name="middle",
    )(index, source, *ctx, cot, *pieces)


def rotary_lanes(segment_row):
    labels = jnp.arange(NDOC + 1, dtype=jnp.int32)
    before = jnp.sum((segment_row[None, :] < labels[:, None]).astype(jnp.int32), axis=1)
    member = segment_row[:, None] == labels[None, :]
    first = jnp.sum(jnp.where(member, before[None, :], 0), axis=1)
    position = (jnp.arange(SEQ, dtype=jnp.int32) - first).astype(F32)
    lane = jnp.arange(LANES) % (HEAD // 2)
    frequency = jnp.power(F32(1000.0), -2.0 * lane.astype(F32) / HEAD)
    angle = position[:, None] * frequency[None, :]
    sign = jnp.where(jnp.arange(LANES) % HEAD < HEAD // 2, -1.0, 1.0)
    ends = jnp.concatenate([before[1:], jnp.full((1,), SEQ, jnp.int32)])
    heads = segment_row[::BLOCK]
    tails = segment_row[BLOCK - 1 :: BLOCK]
    low = jnp.sum(jnp.where(heads[:, None] == labels[None, :], before[None, :], 0), axis=1)
    high = jnp.sum(jnp.where(tails[:, None] == labels[None, :], ends[None, :], 0), axis=1)
    bounds = jnp.concatenate([low // KEYS, (high + KEYS - 1) // KEYS]).astype(jnp.int32)
    return jnp.cos(angle), jnp.sin(angle) * sign[None, :], bounds


def sequence_device(
    tokens, segments, qkv_weight, out_weight, norm_gain, norm_shift, gate_up, down_weight, cotangent
):
    core = lax.axis_index("tensor")
    def ordered(mine, theirs):
        return jnp.where(
            core == 0, jnp.stack([mine, theirs], axis=0), jnp.stack([theirs, mine], axis=0)
        )

    pick = lambda a, i: lax.dynamic_index_in_dim(a, i, 0, keepdims=False)
    source = pick(tokens, core)
    segment_row = pick(segments, core)

    attn_block = qkv_weight.reshape(-1, 3 * D)
    gate_block = gate_up.reshape(-1, 2 * HIDDEN)
    tail_block = jnp.concatenate(
        [out_weight, norm_gain, norm_shift, jnp.zeros((D // 32, TAIL - D - 4), BF16)], axis=1
    )
    down_block = jnp.concatenate(
        [down_weight, jnp.concatenate([tail_block[:, :REST], tail_block[:, REST:]], axis=0)], axis=1
    )
    from_here, from_there = slot_blocks(-1, core), slot_blocks(-1, 1 - core)
    there_blocks = slot_blocks(1, core).reshape(2, 2, 4)
    to_here = there_blocks.transpose(1, 0, 2).reshape(16)
    deep_first = there_blocks.transpose(2, 1, 0).reshape(16)

    cot = ordered(pick(cotangent, core), core_swap(pick(cotangent, 1 - core))).reshape(SEQ, D)
    cosine, sine, bounds = rotary_lanes(segment_row)
    bounds = jnp.concatenate([bounds, core[None]]).astype(jnp.int32)
    tables = (cosine, sine, segment_row[:, None], segment_row[None, :])

    ahead = lambda parts: [part[None] for part in parts]
    attn_four = pile(ahead(depth_parts(attn_block)))
    gate_block = pile([gate_block[None]], deps=(attn_four,))[0]
    gate_parts = depth_ring(gate_block)
    gate_four = pile(ahead(gate_parts))
    attn_eight = pile([attn_four, first_swap(attn_four)], deps=(gate_parts[1],))
    attn_last = second_swap(attn_eight)
    index = jnp.concatenate([from_here * 2 + core, from_there * 2 + 1 - core]).astype(jnp.int32)
    weights = assemble(
        (attn_eight, attn_last),
        (core_swap(attn_eight), core_swap(attn_last)),
        index,
        deps=(gate_four,),
    ).reshape(D, 3 * D)

    down_block = pile([down_block[None]], deps=(gate_four,))[0]
    saved0 = attn_forward(0, 1, bounds, source, weights, *tables)
    gate_eight = pile([gate_four, first_swap(gate_four)], deps=(saved0[4],))
    gate_last = second_swap(gate_eight)
    down_four = pile(ahead(depth_parts(down_block)), deps=(gate_eight,))
    saved1 = attn_forward(1, 2, bounds, source, weights, *tables, deps=(down_four,))
    down_eight = pile([down_four, first_swap(down_four)], deps=(saved1[4], gate_last))
    down_last = second_swap(down_eight)
    pieces = (gate_eight, gate_last, core_swap(gate_eight), core_swap(gate_last))
    pieces += (down_eight, down_last, core_swap(down_eight), core_swap(down_last))

    index = jnp.concatenate([from_here, from_there, core[None]]).astype(jnp.int32)
    ctx = (saved0[3], saved1[3])
    (out, out_leave, normed, mlp_grad, att_grad, ctx_grad, hidden_grad, gu0, gu1, sw0, sw1, sums) = middle(
        index, source, ctx, cot, pieces
    )

    gu_there = core_swap(weight_grad(normed, gu1))
    down_there = core_swap(weight_grad(mlp_grad, sw1))
    tail_mine, tail_theirs = out_grad(core, ctx, att_grad, sums)
    gu_keep, gu_send = weight_grad_join(to_here, normed, gu0, gu_there, 2)
    gu_first = first_swap(gu_send)
    down_parts = weight_grad_join(deep_first, mlp_grad, sw0, down_there, 4)
    passing = depth_shift(down_parts[3], 1)

    common = (source,) + tables
    back0 = attn_backward(0, 0, bounds, saved0, ctx_grad, *common, deps=(gu_send, down_parts[0]))
    (passing,) = fold(passing, down_parts[2], 1, deps=(back0[1],))
    back1 = attn_backward(0, 1, bounds, saved1, ctx_grad, *common, deps=(passing,))
    passing = depth_shift(passing, 1)
    (passing,) = fold(passing, down_parts[1], 1, deps=(back1[1],))
    gu_keep, gu_send = fold(gu_keep, gu_first, 2, deps=(back1[1],))
    gu_second = second_swap(gu_send)
    early_keep, early_send = join_dealt(
        to_here,
        (back0[1], back1[1], tail_mine),
        (core_swap(back0[2]), core_swap(back1[2]), core_swap(tail_theirs)),
    )
    early_first = first_swap(early_send)
    back2 = attn_backward(1, 2, bounds, saved1, ctx_grad, *common, deps=(gu_send, early_send, passing))

    deep = lambda parts: [parts[0]] + [depth_shift(parts[k], k) for k in (1, 2, 3)]
    passing = depth_shift(passing, 1)
    gu_parts = fold(gu_keep, gu_second, 4, deps=(back2[1],))
    gu_total = gu_parts[3]
    for k in (2, 1):
        (gu_total,) = fold(depth_shift(gu_total, 1), gu_parts[k], 1)
    down_keep, down_send = fold(passing, down_parts[0], 2, deps=(gu_parts[0],))
    down_keep, down_send = fold(down_keep, first_swap(down_send), 2)
    down_second = second_swap(down_send)
    early_keep, early_send = fold(early_keep, early_first, 2, deps=(gu_parts[0],))
    early_second = second_swap(early_send)
    late_keep, late_send = join_dealt(
        to_here, (back2[1],), (core_swap(back2[2]),), deps=(early_send, down_keep)
    )
    grad, grad_leave = input_back(
        core, hidden_grad, (back0[0], back1[0], back2[0]), weights, deps=(late_send,)
    )
    late_keep, late_send = fold(late_keep, first_swap(late_send), 2, deps=(grad,))
    late_second = second_swap(late_send)
    (gu_total,) = fold(depth_shift(gu_total, 1), gu_parts[0], 1, F32, deps=(late_send,))
    early_parts = deep(fold(early_keep, early_second, 4, deps=(gu_total,)))
    late_parts = deep(fold(late_keep, late_second, 4, deps=(early_parts[0],)))
    down_total = (down_keep.astype(F32) + down_second.astype(F32))[0]
    (early_total,) = total4(early_parts, 1, F32)
    (late_total,) = total4(late_parts, 1, F32)
    gu_total, early_total, late_total = gu_total[0], early_total[0], late_total[0]

    rows = D // 32
    qkv_total = jnp.concatenate([early_total[:, : 6 * GROUP], late_total], axis=1)
    qkv_total = qkv_total.reshape(rows, GROUPS, 3, GROUP).transpose(0, 2, 1, 3).reshape(rows, 3, D)
    rest = early_total[:, 6 * GROUP :]

    return (
        place(core, out, core_swap(out_leave)),
        place(core, grad, core_swap(grad_leave)),
        qkv_total,
        rest[:, :D],
        rest[:, D : D + 2],
        rest[:, D + 2 : D + 4],
        gu_total.reshape(-1, 2, HIDDEN),
        down_total,
    )


def solution(mesh):
    in_specs = (
        P("dp", None, None),
        P("dp", None),
        P(("dp", "tensor"), None, None),
        P(("dp", "tensor"), None),
        P(("dp", "tensor"), None),
        P(("dp", "tensor"), None),
        P("dp", None, "tensor"),
        P("dp", "tensor"),
        P("dp", "tensor", None),
    )
    out_specs = (
        P("dp", "tensor", None),
        P("dp", "tensor", None),
        P(("dp", "tensor"), None, None),
        P(("dp", "tensor"), None),
        P(("dp", "tensor"), None),
        P(("dp", "tensor"), None),
        P("dp", None, "tensor"),
        P("dp", "tensor"),
    )
    sizes = dict(mesh.shape)

    def per_device(tokens, *others):
        if sizes["dp"] == 16 and sizes["tensor"] == 2 and tokens.shape[0] == 2:
            return sequence_device(tokens, *others)
        return general_device(tokens, *others)

    return jax.shard_map(
        per_device, mesh=mesh, in_specs=in_specs, out_specs=out_specs, check_vma=False
    )
```

```python
import jax
import jax.numpy as jnp
from jax import lax
from jax.experimental import pallas as pl
from jax.experimental.pallas import tpu as pltpu
from jax.sharding import PartitionSpec as P

D = 768
HEADS = 12
HEAD = 64
SEQ = 1024
NDOC = 8


EPSILON = 1e-05
MASKED = -1e30


def for_sending(value):
    return jax.tree.map(lambda a: a.astype(jnp.bfloat16) if a.dtype == jnp.float32 else a, value)


def rotary_tables(segment_row):
    labels = jnp.arange(NDOC + 1, dtype=jnp.int32)
    member = (segment_row[:, None] == labels[None, :]).astype(jnp.int32)
    counts = jnp.sum(member, axis=0)
    starts = jnp.concatenate([jnp.zeros((1,), jnp.int32), jnp.cumsum(counts)[:-1]])
    offset = jnp.sum(member * starts[None, :], axis=1)
    position = (jnp.arange(SEQ, dtype=jnp.int32) - offset).astype(jnp.float32)
    exponent = -2.0 * jnp.arange(HEAD // 2).astype(jnp.float32) / HEAD
    frequency = jnp.power(jnp.float32(1000.0), exponent)
    angle = position[:, None] * frequency[None, :]
    return (jnp.cos(angle)[:, None, :], jnp.sin(angle)[:, None, :])


def rotate(vector, cosine, sine):
    half = vector.shape[-1] // 2
    first_half = vector[..., :half]
    second_half = vector[..., half:]
    return jnp.concatenate(
        [first_half * cosine - second_half * sine, second_half * cosine + first_half * sine],
        axis=-1,
    )


def unrotate(gradient, cosine, sine):

    def turned(vector):
        return rotate(vector, cosine, sine)

    _, pullback = jax.vjp(turned, gradient)
    return pullback(gradient)[0]


def layer_norm(vector, gain, shift):
    center = vector - jnp.mean(vector, axis=-1, keepdims=True)
    variance = jnp.mean(center * center, axis=-1, keepdims=True)
    return center * lax.rsqrt(variance + EPSILON) * gain + shift


def swiglu_piece(gate, upper):
    return jax.nn.silu(gate) * upper


def accumulate(total, term):
    if total is None:
        return term
    return tuple((left + right for left, right in zip(total, term)))


def general_device(
    tokens, segments, qkv_weight, out_weight, norm_gain, norm_shift, gate_up, down_weight, cotangent
):
    tensor_size = lax.axis_size("tensor")
    own_rows = SEQ // tensor_size
    row_start = lax.axis_index("tensor") * own_rows
    score_scale = HEAD ** (-0.5)
    qkv_full, out_full, gain_full, shift_full = (
        lax.all_gather(qkv_weight, ("dp", "tensor"), axis=0, tiled=True),
        lax.all_gather(out_weight, ("dp", "tensor"), axis=0, tiled=True),
        lax.all_gather(norm_gain, ("dp", "tensor"), axis=0, tiled=True),
        lax.all_gather(norm_shift, ("dp", "tensor"), axis=0, tiled=True),
    )
    gains = gain_full.astype(jnp.float32)
    shifts = shift_full.astype(jnp.float32)
    gate_up_full, down_full = (
        lax.all_gather(gate_up, "dp", axis=0, tiled=True),
        lax.all_gather(down_weight, "dp", axis=0, tiled=True),
    )
    batches = tokens.shape[0]
    outputs = []
    input_grads = []
    attn_total = None
    mlp_total = None
    for batch_index in range(batches):
        source = tokens[batch_index]
        own_source = lax.dynamic_slice_in_dim(source, row_start, own_rows, 0)
        segment_row = segments[batch_index]
        cosine, sine = rotary_tables(segment_row)
        own_cos = lax.dynamic_slice_in_dim(cosine, row_start, own_rows, 0)
        own_sin = lax.dynamic_slice_in_dim(sine, row_start, own_rows, 0)
        query_proj = jnp.einsum(
            "sd,de->se", own_source, qkv_full[:, 0], preferred_element_type=jnp.float32
        )
        pair_proj = jnp.einsum(
            "sd,dke->ske", source, qkv_full[:, 1:], preferred_element_type=jnp.float32
        )
        keys = rotate(pair_proj[:, 0].reshape(SEQ, HEADS, HEAD), cosine, sine).astype(jnp.bfloat16)
        values = pair_proj[:, 1].reshape(SEQ, HEADS, HEAD).astype(jnp.bfloat16)
        queries = rotate(query_proj.reshape(own_rows, HEADS, HEAD), own_cos, own_sin).astype(
            jnp.bfloat16
        )
        own_segments = lax.dynamic_slice_in_dim(segment_row, row_start, own_rows, 0)
        allowed = (own_segments[:, None] == segment_row[None, :])[None]
        raw_scores = (
            jnp.einsum("qhe,khe->hqk", queries, keys, preferred_element_type=jnp.float32)
            * score_scale
        )
        masked = jnp.where(allowed, raw_scores, MASKED)
        top_score = jnp.max(masked, axis=-1, keepdims=True)
        logsum = top_score + jnp.log(jnp.sum(jnp.exp(masked - top_score), axis=-1, keepdims=True))
        probs_low = jnp.exp(masked - logsum).astype(jnp.bfloat16)
        context = (
            jnp.einsum("hqk,khe->qhe", probs_low, values, preferred_element_type=jnp.float32)
            .reshape(own_rows, D)
            .astype(jnp.bfloat16)
        )
        attended = jnp.dot(context, out_full, preferred_element_type=jnp.float32)
        hidden_in = own_source.astype(jnp.float32) + attended
        normed = layer_norm(hidden_in, gains[:, 0], shifts[:, 0])
        normed_all = lax.all_gather(normed.astype(jnp.bfloat16), "tensor", axis=0, tiled=True)
        gate_pair = jnp.einsum(
            "sd,dkf->skf", normed_all, gate_up_full, preferred_element_type=jnp.float32
        )
        swiglu = swiglu_piece(gate_pair[:, 0], gate_pair[:, 1]).astype(jnp.bfloat16)
        mlp_out = lax.psum_scatter(
            jnp.einsum("sf,df->sd", swiglu, down_full, preferred_element_type=jnp.float32).astype(
                jnp.bfloat16
            ),
            "tensor",
            scatter_dimension=0,
            tiled=True,
        ).astype(jnp.float32)
        resid = normed + mlp_out
        outputs.append(layer_norm(resid, gains[:, 1], shifts[:, 1]).astype(jnp.bfloat16))
        upstream = cotangent[batch_index].astype(jnp.float32)
        _, second_pull = jax.vjp(layer_norm, resid, gains[:, 1], shifts[:, 1])
        resid_grad, gain_two, shift_two = second_pull(upstream)
        mlp_grad = lax.all_gather(resid_grad.astype(jnp.bfloat16), "tensor", axis=0, tiled=True)
        swiglu_grad = jnp.einsum(
            "sd,df->sf", mlp_grad, down_full, preferred_element_type=jnp.float32
        )
        _, glu_pull = jax.vjp(swiglu_piece, gate_pair[:, 0], gate_pair[:, 1])
        gate_grad, upper_grad = glu_pull(swiglu_grad)
        pair_grad = jnp.stack([gate_grad, upper_grad], axis=1).astype(jnp.bfloat16)
        down_term = jnp.einsum("sd,sf->df", mlp_grad, swiglu, preferred_element_type=jnp.float32)
        gate_up_term = jnp.einsum(
            "sd,skf->dkf", normed_all, pair_grad, preferred_element_type=jnp.float32
        )
        normed_grad = resid_grad + lax.psum_scatter(
            jnp.einsum("skf,dkf->sd", pair_grad, gate_up_full, preferred_element_type=jnp.float32),
            "tensor",
            scatter_dimension=0,
            tiled=True,
        )
        _, first_pull = jax.vjp(layer_norm, hidden_in, gains[:, 0], shifts[:, 0])
        hidden_grad, gain_one, shift_one = first_pull(normed_grad)
        attended_grad = hidden_grad.astype(jnp.bfloat16)
        out_term = jnp.einsum(
            "sd,se->de", context, attended_grad, preferred_element_type=jnp.float32
        )
        context_grad = (
            jnp.einsum("se,de->sd", attended_grad, out_full, preferred_element_type=jnp.float32)
            .astype(jnp.bfloat16)
            .reshape(own_rows, HEADS, HEAD)
        )
        probs = jnp.exp(masked - logsum)
        weights_grad = jnp.einsum(
            "qhe,khe->hqk", context_grad, values, preferred_element_type=jnp.float32
        )
        row_delta = jnp.sum(probs * weights_grad, axis=-1, keepdims=True)
        score_grad = (probs * (weights_grad - row_delta)).astype(jnp.bfloat16)
        query_grad = (
            jnp.einsum("hqk,khe->qhe", score_grad, keys, preferred_element_type=jnp.float32)
            * score_scale
        )
        key_part = (
            jnp.einsum("hqk,qhe->khe", score_grad, queries, preferred_element_type=jnp.float32)
            * score_scale
        )
        value_part = jnp.einsum(
            "hqk,qhe->khe", probs_low, context_grad, preferred_element_type=jnp.float32
        )
        key_value = lax.psum_scatter(
            jnp.stack(
                [
                    key_part.reshape(lax.axis_size("tensor") * own_rows, D),
                    value_part.reshape(lax.axis_size("tensor") * own_rows, D),
                ],
                axis=1,
            ).astype(jnp.bfloat16),
            "tensor",
            scatter_dimension=0,
            tiled=True,
        ).astype(jnp.float32)
        query_back = unrotate(query_grad, own_cos, own_sin).reshape(own_rows, D)
        key_back = unrotate(
            key_value[:, 0].reshape(own_rows, HEADS, HEAD), own_cos, own_sin
        ).reshape(own_rows, D)
        proj_grad = jnp.stack([query_back, key_back, key_value[:, 1]], axis=1).astype(jnp.bfloat16)
        input_grads.append(
            hidden_grad
            + jnp.einsum("ske,dke->sd", proj_grad, qkv_full, preferred_element_type=jnp.float32)
        )
        qkv_term = jnp.einsum(
            "sd,ske->dke", own_source, proj_grad, preferred_element_type=jnp.float32
        )
        gain_term = jnp.stack([gain_one, gain_two], axis=1)
        shift_term = jnp.stack([shift_one, shift_two], axis=1)
        attn_terms = (qkv_term, out_term, gain_term, shift_term)
        mlp_terms = (gate_up_term, down_term)
        attn_total = accumulate(attn_total, attn_terms)
        mlp_total = accumulate(mlp_total, mlp_terms)
    attn_final = lax.psum_scatter(attn_total, ("dp", "tensor"), scatter_dimension=0, tiled=True)
    mlp_final = jax.tree.map(
        lambda part: part.astype(jnp.float32),
        lax.psum_scatter(for_sending(mlp_total), "dp", scatter_dimension=0, tiled=True),
    )
    return (
        jnp.stack(outputs, axis=0),
        jnp.stack(input_grads, axis=0),
        attn_final[0],
        attn_final[1],
        attn_final[2],
        attn_final[3],
        mlp_final[0],
        mlp_final[1],
    )


HIDDEN = 1536
WIDE = 3 * HIDDEN
REST = 512
TAIL = 2 * REST
GROUP = 4 * HEAD
GROUPS = D // GROUP
KEYS = 128
LANES = 2 * HEAD
BLOCK = 256
NBLOCK = SEQ // BLOCK
ROWS = 256
STEPS = SEQ // ROWS
CHUNK = 512
PIECE = 256
PIECES = 2 * HIDDEN // PIECE
LOG2E = 1.4426950408889634
F32 = jnp.float32
BF16 = jnp.bfloat16


def across(value, move):
    pairs = []
    for z in range(4):
        for y in range(2):
            for x in range(2):
                for c in range(2):
                    tz, ty, tx, tc = move(z, y, x, c)
                    pairs.append((((z * 2 + y) * 2 + x) * 2 + c, ((tz * 2 + ty) * 2 + tx) * 2 + tc))
    return lax.ppermute(value, ("dp", "tensor"), pairs)


def core_swap(value):
    return across(value, lambda z, y, x, c: (z, y, x, 1 - c))


def first_swap(value):
    return across(value, lambda z, y, x, c: (z, y, 1 - x, c) if c == 0 else (z, 1 - y, x, c))


def second_swap(value):
    return across(value, lambda z, y, x, c: (z, 1 - y, x, c) if c == 0 else (z, y, 1 - x, c))


def depth_shift(value, steps):
    return across(value, lambda z, y, x, c: ((z + steps) % 4, y, x, c))


def slot_blocks(sign, core):
    me = lax.axis_index("dp")
    z, y, x = me // 4, (me // 2) % 2, me % 2
    slot = jnp.arange(16, dtype=jnp.int32)
    second, first, depth = slot // 8, (slot // 4) % 2, slot % 4
    x_bit = jnp.where(core == 0, first, second)
    y_bit = jnp.where(core == 0, second, first)
    return (((z + sign * depth) % 4) * 4 + (y ^ y_bit) * 2 + (x ^ x_bit)).astype(jnp.int32)


def depth_parts(block):
    return [block] + [depth_shift(block, k) for k in (1, 2, 3)]


def depth_ring(block):
    parts = [block]
    for _ in range(3):
        parts.append(depth_shift(parts[-1], 1))
    return parts


def cost(flops, nbytes, trans=0):
    return pl.CostEstimate(flops=int(flops), bytes_accessed=int(nbytes), transcendentals=int(trans))


def params(vmem_mb, sem=("arbitrary",)):
    return pltpu.CompilerParams(dimension_semantics=sem, vmem_limit_bytes=vmem_mb << 20)


ANY = pl.BlockSpec(memory_space=pl.ANY)


def pile(parts, deps=()):
    spans, start = [], 0
    for part in parts:
        spans.append((start, part.shape[0]))
        start += part.shape[0]

    def body(*refs):
        ins, out, sem = refs[: len(parts)], refs[-2], refs[-1]
        copies = [
            pltpu.make_async_copy(ref, out.at[pl.ds(at, n)], sem.at[i])
            for i, (ref, (at, n)) in enumerate(zip(ins, spans))
        ]
        for cp in copies:
            cp.start()
        for cp in copies:
            cp.wait()

    shape = (start,) + parts[0].shape[1:]
    return pl.pallas_call(
        body,
        in_specs=[ANY] * (len(parts) + len(deps)),
        out_specs=pl.BlockSpec(memory_space=pltpu.VMEM),
        out_shape=jax.ShapeDtypeStruct(shape, parts[0].dtype),
        scratch_shapes=[pltpu.SemaphoreType.DMA((len(parts),))],
        compiler_params=params(60, None),
        cost_estimate=cost(0, 4 * start * shape[1] * shape[2]),
        name="pile",
    )(*parts, *deps)


def place(core, mine, there):
    def body(c, a, b, out, sem):
        first = pltpu.make_async_copy(a, out.at[c[0]], sem.at[0])
        second = pltpu.make_async_copy(b, out.at[1 - c[0]], sem.at[1])
        first.start()
        second.start()
        first.wait()
        second.wait()

    return pl.pallas_call(
        body,
        grid_spec=pltpu.PrefetchScalarGridSpec(
            num_scalar_prefetch=1,
            grid=(1,),
            in_specs=[ANY, ANY],
            out_specs=pl.BlockSpec((2,) + mine.shape, lambda i, c: (0, 0, 0)),
            scratch_shapes=[pltpu.SemaphoreType.DMA((2,))],
        ),
        out_shape=jax.ShapeDtypeStruct((2,) + mine.shape, mine.dtype),
        compiler_params=params(60),
        cost_estimate=cost(0, 4 * mine.size),
        name="place",
    )(core[None], mine, there)


def assemble(own, other, index, deps=()):
    def body(idx, a, b, c, d, *rest):
        out, sem = rest[-2:]
        copies = []
        for i, ref in enumerate((a, b, c, d)):
            for s in range(8):
                copies.append(
                    pltpu.make_async_copy(ref.at[s], out.at[idx[i * 8 + s]], sem.at[i * 8 + s])
                )
        for cp in copies:
            cp.start()
        for cp in copies:
            cp.wait()

    rows, wide = own[0].shape[1:]
    return pl.pallas_call(
        body,
        grid_spec=pltpu.PrefetchScalarGridSpec(
            num_scalar_prefetch=1,
            grid=(1,),
            in_specs=[ANY] * (4 + len(deps)),
            out_specs=pl.BlockSpec((32, rows, wide), lambda i, c: (0, 0, 0)),
            scratch_shapes=[pltpu.SemaphoreType.DMA((32,))],
        ),
        out_shape=jax.ShapeDtypeStruct((32, rows, wide), BF16),
        compiler_params=params(60),
        cost_estimate=cost(0, 4 * 32 * rows * wide),
        name="assemble",
    )(index, *own, *other, *deps)


def turn(vector, cosine, sine):
    lane = lax.broadcasted_iota(jnp.int32, vector.shape, 1)
    swapped = jnp.where(
        lane % HEAD < HEAD // 2,
        pltpu.roll(vector, LANES - HEAD // 2, 1),
        pltpu.roll(vector, HEAD // 2, 1),
    )
    return vector * cosine + swapped * sine


def dot_nn(a, b):
    return lax.dot_general(a, b, (((1,), (0,)), ((), ())), preferred_element_type=F32)


def dot_nt(a, b):
    return lax.dot_general(a, b, (((1,), (1,)), ((), ())), preferred_element_type=F32)


def dot_tn(a, b):
    return lax.dot_general(a, b, (((0,), (0,)), ((), ())), preferred_element_type=F32)


def stacked(low_lane, pair):
    zero = jnp.zeros_like(pair)
    return jnp.concatenate(
        [jnp.where(low_lane, pair, zero), jnp.where(low_lane, zero, pair)], axis=0
    )


def windows(bnd, i, work):
    blocks = (bnd[NBLOCK + i] - bnd[i] + BLOCK // KEYS - 1) // (BLOCK // KEYS)
    for width in range(1, NBLOCK + 1):

        @pl.when(blocks == width)
        def _():
            low = jnp.minimum(bnd[i], (SEQ - width * BLOCK) // KEYS)
            work(pl.ds(pl.multiple_of(low * KEYS, KEYS), width * BLOCK))


def attn_forward(first, count, bounds, source, weights, cosine, sine, seg_col, seg_row, deps=()):
    def body(bnd, x, wq, wk, wv, cos, sin, sc, sr, *rest):
        q_out, k_out, v_out, ctx_out, lse_out, qm = rest[len(deps) :]
        low_lane = lax.broadcasted_iota(jnp.int32, (BLOCK, LANES), 1) < HEAD

        @pl.loop(0, NBLOCK)
        def _(r):
            rows = pl.ds(pl.multiple_of(r * BLOCK, BLOCK), BLOCK)
            xr, cr, sn = x[rows, :], cos[rows, :], sin[rows, :]
            q_proj, k_proj = dot_nn(xr, wq[...]), dot_nn(xr, wk[...])
            v_out[rows, :] = dot_nn(xr, wv[...]).astype(BF16)
            for p in range(GROUP // LANES):
                ln = slice(p * LANES, (p + 1) * LANES)
                q = turn(q_proj[:, ln], cr, sn).astype(BF16) * jnp.asarray(HEAD**-0.5, BF16)
                q_out[rows, ln] = q
                qm[p, r] = stacked(low_lane, q)
                k_out[rows, ln] = turn(k_proj[:, ln], cr, sn).astype(BF16)

        def block(i, _):
            rows = pl.ds(pl.multiple_of(i * BLOCK, BLOCK), BLOCK)
            own = jnp.concatenate([sc[rows, :], sc[rows, :]], axis=0)

            def work(cols):
                seen = own == sr[:, cols]
                for p in range(GROUP // LANES):
                    ln = slice(p * LANES, (p + 1) * LANES)
                    s = jnp.where(seen, dot_nt(qm[p, i], k_out[cols, ln]) * LOG2E, MASKED)
                    top = jnp.max(s, axis=1, keepdims=True)
                    e = jnp.exp2(s - top)
                    total = jnp.sum(e, axis=1, keepdims=True)
                    mixed = dot_nn(e.astype(BF16), v_out[cols, ln]) / total
                    ctx_out[rows, ln] = jnp.where(low_lane, mixed[:BLOCK], mixed[BLOCK:]).astype(BF16)
                    logs = top + jnp.log2(total)
                    flipped = jnp.where(low_lane, logs[:BLOCK], logs[BLOCK:]).T
                    lse_out[0, 2 * p : 2 * p + 1, rows] = flipped[0:1]
                    lse_out[0, 2 * p + 1 : 2 * p + 2, rows] = flipped[HEAD : HEAD + 1]

            windows(bnd, i, work)
            return 0

        lax.fori_loop(0, NBLOCK, block, 0)

    full = lambda shape: pl.BlockSpec(shape, lambda p, b: (0,) * len(shape))
    column = lambda shift: pl.BlockSpec((D, GROUP), lambda p, b: (0, shift * GROUPS + first + p))
    part = pl.BlockSpec((SEQ, GROUP), lambda p, b: (0, p))
    act = jax.ShapeDtypeStruct((SEQ, count * GROUP), BF16)
    return pl.pallas_call(
        body,
        grid_spec=pltpu.PrefetchScalarGridSpec(
            num_scalar_prefetch=1,
            grid=(count,),
            in_specs=[
                full((SEQ, D)),
                column(0),
                column(1),
                column(2),
                full((SEQ, LANES)),
                full((SEQ, LANES)),
                full((SEQ, 1)),
                full((1, SEQ)),
            ]
            + [ANY] * len(deps),
            out_specs=[part] * 4 + [pl.BlockSpec((1, 8, SEQ), lambda p, b: (p, 0, 0))],
            scratch_shapes=[pltpu.VMEM((GROUP // LANES, NBLOCK, 2 * BLOCK, LANES), BF16)],
        ),
        out_shape=[act] * 4 + [jax.ShapeDtypeStruct((count, 8, SEQ), F32)],
        compiler_params=params(60),
        cost_estimate=cost(
            count * GROUP * (6 * SEQ * D + 16 * SEQ * SEQ), 8 << 20, count * 4 * SEQ * SEQ
        ),
        name="attn_forward",
    )(bounds, source, weights, weights, weights, cosine, sine, seg_col, seg_row, *deps)


def deal(core, whole, mine, theirs, columns):
    parts = whole.reshape(16, 2, D // 32, whole.shape[1])
    first, second = parts[:, 0], parts[:, 1]
    mine[:, :, columns] = jnp.where(core == 0, first, second).astype(BF16)
    theirs[:, :, columns] = jnp.where(core == 0, second, first).astype(BF16)


def attn_backward(at, grad_at, bounds, saved, ctx_grad, source, cosine, sine, seg_col, seg_row, deps=()):
    def body(bnd, q, k, v, o, do, lse, x, cos, sin, sc, sr, *rest):
        core = bnd[2 * NBLOCK]
        out, mine, theirs, qm, dm, dq, dk, dv, dl = rest[len(deps) :]
        low_lane = lax.broadcasted_iota(jnp.int32, (BLOCK, LANES), 1) < HEAD
        row = lax.broadcasted_iota(jnp.int32, (8, LANES), 0)
        lane = lax.broadcasted_iota(jnp.int32, (8, LANES), 1)
        pick = jnp.where(row == lane // HEAD, 1.0, 0.0).astype(F32)
        for p in range(GROUP // LANES):
            ln = slice(p * LANES, (p + 1) * LANES)

            @pl.loop(0, NBLOCK)
            def _(i):
                rows = pl.ds(pl.multiple_of(i * BLOCK, BLOCK), BLOCK)
                qm[p, i] = stacked(low_lane, q[rows, ln])
                dm[p, i] = stacked(low_lane, do[rows, ln])

            dl[p] = lax.dot_general(
                pick,
                do[:, ln].astype(F32) * o[:, ln].astype(F32),
                (((1,), (1,)), ((), ())),
                preferred_element_type=F32,
                precision=lax.Precision.HIGHEST,
            )
        dk[...] = jnp.zeros_like(dk)
        dv[...] = jnp.zeros_like(dv)

        def block(i, _):
            rows = pl.ds(pl.multiple_of(i * BLOCK, BLOCK), BLOCK)
            own = jnp.concatenate([sr[:, rows], sr[:, rows]], axis=1)

            def work(cols):
                seen = sc[cols, :] == own
                for p in range(GROUP // LANES):
                    ln = slice(p * LANES, (p + 1) * LANES)
                    keys, values, qq, dd = k[cols, ln], v[cols, ln], qm[p, i], dm[p, i]
                    logs = jnp.concatenate(
                        [lse[0, 2 * p : 2 * p + 1, rows], lse[0, 2 * p + 1 : 2 * p + 2, rows]], axis=1
                    )
                    deltas = jnp.concatenate([dl[p, 0:1, rows], dl[p, 1:2, rows]], axis=1)
                    s = dot_nt(keys, qq) * LOG2E - logs
                    probs = jnp.exp2(jnp.where(seen, s, MASKED))
                    g = (probs * (dot_nt(values, dd) - deltas)).astype(BF16)
                    dv[cols, ln] += dot_nn(probs.astype(BF16), dd)
                    dk[cols, ln] += dot_nn(g, qq)
                    both = dot_tn(g, keys)
                    dq[rows, ln] = jnp.where(low_lane, both[:BLOCK], both[BLOCK:])

            windows(bnd, i, work)
            return 0

        lax.fori_loop(0, NBLOCK, block, 0)

        @pl.loop(0, NBLOCK)
        def _(r):
            rows = pl.ds(pl.multiple_of(r * BLOCK, BLOCK), BLOCK)
            cr, sn = cos[rows, :], -sin[rows, :]
            for p in range(GROUP // LANES):
                ln = slice(p * LANES, (p + 1) * LANES)
                out[0, rows, ln] = turn(dq[rows, ln] * (HEAD**-0.5), cr, sn).astype(BF16)
                out[1, rows, ln] = turn(dk[rows, ln], cr, sn).astype(BF16)
                out[2, rows, ln] = dv[rows, ln].astype(BF16)

        for i in range(3):
            deal(core, dot_tn(x[...], out[i]), mine, theirs, slice(i * GROUP, (i + 1) * GROUP))

    full = lambda shape: pl.BlockSpec(shape, lambda p, b: (0,) * len(shape))
    part = pl.BlockSpec((SEQ, GROUP), lambda p, b: (0, at))
    low2 = pltpu.VMEM((GROUP // LANES, NBLOCK, 2 * BLOCK, LANES), BF16)
    wide = pltpu.VMEM((SEQ, GROUP), F32)
    dealt = (16, D // 32, 3 * GROUP)
    return pl.pallas_call(
        body,
        grid_spec=pltpu.PrefetchScalarGridSpec(
            num_scalar_prefetch=1,
            grid=(1,),
            in_specs=[part] * 4
            + [
                pl.BlockSpec((SEQ, GROUP), lambda p, b: (0, grad_at)),
                pl.BlockSpec((1, 8, SEQ), lambda p, b: (at, 0, 0)),
                full((SEQ, D)),
                full((SEQ, LANES)),
                full((SEQ, LANES)),
                full((SEQ, 1)),
                full((1, SEQ)),
            ]
            + [ANY] * len(deps),
            out_specs=[full((3, SEQ, GROUP)), full(dealt), full(dealt)],
            scratch_shapes=[
                low2,
                low2,
                wide,
                wide,
                wide,
                pltpu.VMEM((GROUP // LANES, 8, SEQ), F32),
            ],
        ),
        out_shape=[
            jax.ShapeDtypeStruct((3, SEQ, GROUP), BF16),
            jax.ShapeDtypeStruct(dealt, BF16),
            jax.ShapeDtypeStruct(dealt, BF16),
        ],
        compiler_params=params(60),
        cost_estimate=cost(GROUP * (40 * SEQ * SEQ + 6 * SEQ * D), 10 << 20, 4 * SEQ * SEQ),
        name="attn_backward",
    )(bounds, *saved[:4], ctx_grad, saved[4], source, cosine, sine, seg_col, seg_row, *deps)


def join_rows(index, here, there, count, columns=512):
    lead, _, wide = here.shape
    rows = D // 16
    each = 16 // count
    steps = wide // columns

    def body(idx, a, b, *outs):
        for s in range(16):
            at = pl.ds(pl.multiple_of(idx[s] * rows, 16), rows)
            total = a[0, at, :].astype(F32) + b[0, at, :].astype(F32)
            outs[s // each][s % each] = total.astype(BF16)

    whole = pl.BlockSpec((1, D, columns), lambda l, n, i: (l, 0, n))
    part = pl.BlockSpec((each, rows, columns), lambda l, n, i: (0, 0, l * steps + n))
    return pl.pallas_call(
        body,
        grid_spec=pltpu.PrefetchScalarGridSpec(
            num_scalar_prefetch=1,
            grid=(lead, steps),
            in_specs=[whole, whole],
            out_specs=[part] * count,
        ),
        out_shape=[jax.ShapeDtypeStruct((each, rows, lead * wide), BF16)] * count,
        compiler_params=params(60, ("arbitrary", "arbitrary")),
        cost_estimate=cost(D * wide * lead, 6 * D * wide * lead),
        name="join_rows",
    )(index, here, there)


def out_grad(core, ctx, right, norms):
    def body(c, *refs):
        parts, (b, nrm, mine, theirs) = refs[:GROUPS], refs[GROUPS:]
        whole = jnp.concatenate([dot_tn(p[...], b[...]) for p in parts], axis=0)
        deal(c[0], whole, mine, theirs, slice(0, D))
        flipped = jnp.concatenate([nrm[...], jnp.zeros((LANES - 8, D), F32)], axis=0).T
        filled = jnp.concatenate([flipped, jnp.zeros((D, LANES), F32)], axis=1)
        deal(c[0], filled, mine, theirs, slice(D, TAIL))

    full = lambda shape: pl.BlockSpec(shape, lambda p, b: (0,) * len(shape))
    dealt = (16, D // 32, TAIL)
    return pl.pallas_call(
        body,
        grid_spec=pltpu.PrefetchScalarGridSpec(
            num_scalar_prefetch=1,
            grid=(1,),
            in_specs=[full((SEQ, GROUP))] * GROUPS + [full((SEQ, D)), full((8, D))],
            out_specs=[full(dealt), full(dealt)],
        ),
        out_shape=[jax.ShapeDtypeStruct(dealt, BF16)] * 2,
        compiler_params=params(60),
        cost_estimate=cost(2 * SEQ * D * D, 8 << 20),
        name="out_grad",
    )(core[None], *ctx, right, norms)


def join_dealt(index, mine, there, deps=()):
    widths = [m.shape[2] for m in mine]
    wide, rows, count = sum(widths), D // 32, len(mine)

    def body(idx, *refs):
        ours, others, keep, send = refs[:count], refs[count : 2 * count], refs[-2], refs[-1]
        for s in range(16):
            start = 0
            for a, b, n in zip(ours, others, widths):
                total = a[idx[s]].astype(F32) + b[idx[s]].astype(F32)
                (keep, send)[s // 8][s % 8, :, start : start + n] = total.astype(BF16)
                start += n

    full = lambda shape: pl.BlockSpec(shape, lambda p, b: (0,) * len(shape))
    half = (8, rows, wide)
    return pl.pallas_call(
        body,
        grid_spec=pltpu.PrefetchScalarGridSpec(
            num_scalar_prefetch=1,
            grid=(1,),
            in_specs=[full((16, rows, n)) for n in widths] * 2 + [ANY] * len(deps),
            out_specs=[full(half), full(half)],
        ),
        out_shape=[jax.ShapeDtypeStruct(half, BF16)] * 2,
        compiler_params=params(60),
        cost_estimate=cost(D * wide // 2, 3 * D * wide),
        name="join_dealt",
    )(index, *mine, *there, *deps)


def fold(keep, there, count, dtype=BF16, deps=()):
    blocks, rows, wide = keep.shape
    each = blocks // count

    def body(a, b, *rest):
        for n, out in enumerate(rest[len(deps) :]):
            at = slice(n * each, (n + 1) * each)
            out[...] = (a[at].astype(F32) + b[at].astype(F32)).astype(dtype)

    columns = wide // 2
    part = pl.BlockSpec((blocks, rows, columns), lambda i: (0, 0, i))
    return pl.pallas_call(
        body,
        grid=(2,),
        in_specs=[part, part] + [ANY] * len(deps),
        out_specs=[pl.BlockSpec((each, rows, columns), lambda i: (0, 0, i))] * count,
        out_shape=[jax.ShapeDtypeStruct((each, rows, wide), dtype)] * count,
        compiler_params=params(60),
        cost_estimate=cost(blocks * rows * wide, 6 * blocks * rows * wide),
        name="fold",
    )(keep, there, *deps)


def total4(parts, count, dtype, deps=()):
    blocks, rows, wide = parts[0].shape
    each = blocks // count

    def body(a, b, c, d, *rest):
        total = a[...].astype(F32) + b[...].astype(F32) + c[...].astype(F32) + d[...].astype(F32)
        for n, out in enumerate(rest[len(deps) :]):
            out[...] = total[n * each : (n + 1) * each].astype(dtype)

    columns = wide // 2
    part = pl.BlockSpec((blocks, rows, columns), lambda i: (0, 0, i))
    return pl.pallas_call(
        body,
        grid=(2,),
        in_specs=[part] * 4 + [ANY] * len(deps),
        out_specs=[pl.BlockSpec((each, rows, columns), lambda i: (0, 0, i))] * count,
        out_shape=[jax.ShapeDtypeStruct((each, rows, wide), dtype)] * count,
        compiler_params=params(60),
        cost_estimate=cost(4 * blocks * rows * wide, 10 * blocks * rows * wide),
        name="total",
    )(*parts, *deps)


def input_back(core, hidden_grad, projected, weights, deps=()):
    half = SEQ // 2 // BLOCK

    def body(c, hid, a, b, d, w, *rest):
        mine, leave = rest[-2:]
        total = hid[...]
        for g, ref in enumerate((a, b, d)):
            for i in range(3):
                at = i * D + g * GROUP
                total = total + dot_nt(ref[i], w[:, at : at + GROUP])
        own = pl.program_id(0) // half == c[0]

        @pl.when(own)
        def _():
            mine[...] = total

        @pl.when(jnp.logical_not(own))
        def _():
            leave[...] = total

    row = pl.BlockSpec((BLOCK, D), lambda r, c: (r, 0))
    shape = jax.ShapeDtypeStruct((SEQ // 2, D), F32)
    return pl.pallas_call(
        body,
        grid_spec=pltpu.PrefetchScalarGridSpec(
            num_scalar_prefetch=1,
            grid=(SEQ // BLOCK,),
            in_specs=[row]
            + [pl.BlockSpec((3, BLOCK, GROUP), lambda r, c: (0, r, 0))] * 3
            + [pl.BlockSpec((D, 3 * D), lambda r, c: (0, 0))]
            + [ANY] * len(deps),
            out_specs=[
                pl.BlockSpec((BLOCK, D), lambda r, c: (jnp.clip(r - half * c[0], 0, half - 1), 0)),
                pl.BlockSpec(
                    (BLOCK, D), lambda r, c: (jnp.clip(r - half * (1 - c[0]), 0, half - 1), 0)
                ),
            ],
        ),
        out_shape=[shape, shape],
        compiler_params=params(60),
        cost_estimate=cost(6 * SEQ * D * D, 16 << 20),
        name="input_back",
    )(core[None], hidden_grad, *projected, weights, *deps)


def middle(index, source, ctx, cot, pieces):
    def norm(v):
        center = v - jnp.mean(v, axis=1, keepdims=True)
        scale = lax.rsqrt(jnp.mean(center * center, axis=1, keepdims=True) + EPSILON)
        return center * scale, scale

    def norm_back(u, hat, scale, gain):
        g = u * gain
        return scale * (
            g - jnp.mean(g, axis=1, keepdims=True) - hat * jnp.mean(g * hat, axis=1, keepdims=True)
        )

    def body(idx, x, ctx0, ctx1, ctx2, cot, *refs):
        pieces, refs = refs[:8], refs[8:]
        out, out_leave, gu_own, gu_other, down_own, down_other, hid_out, att_out, ctxg_out, sums = refs[:10]
        (
            w, wo, tail, nrm, factors, acts, low_t, mlp_t, mlp_s, back_s, hat_s, scale_s, pair_s, sem,
        ) = refs[10:]
        step = pl.program_id(0)
        core = idx[32]
        few = D // 32

        def loads(kind, which):
            copies = []
            for rest in (2 * which, 2 * which + 1):
                for s in range(8):
                    block = idx[rest * 8 + s]
                    at = pl.ds(pl.multiple_of(block * 48, 16), 48)
                    n = rest * 8 + s
                    gate, down = pieces[rest], pieces[4 + rest]
                    if kind == "gate":
                        copies.append(
                            pltpu.make_async_copy(
                                gate.at[s], w.at[which, at, pl.ds(0, 2 * HIDDEN)], sem.at[n]
                            )
                        )
                    elif kind == "down":
                        copies.append(
                            pltpu.make_async_copy(
                                down.at[s, :, pl.ds(0, HIDDEN)],
                                w.at[which, at, pl.ds(2 * HIDDEN, HIDDEN)],
                                sem.at[32 + n],
                            )
                        )
                    else:
                        owner = core if which == 0 else 1 - core
                        for part in range(2):
                            copies.append(
                                pltpu.make_async_copy(
                                    down.at[s, pl.ds(part * few, few), pl.ds(HIDDEN, REST)],
                                    tail.at[part, block * 2 + owner],
                                    sem.at[64 + n + 32 * part],
                                )
                            )
            return copies

        def arrive(kind, which):
            @pl.when(step == 0)
            def _():
                for cp in loads(kind, which):
                    cp.wait()

        @pl.when(step == 0)
        def _():
            for which in range(2):
                for cp in loads("tail", which):
                    cp.start()
            for which in range(2):
                for kind in ("gate", "down"):
                    for cp in loads(kind, which):
                        cp.start()

        arrive("tail", 0)
        arrive("tail", 1)

        @pl.when(step == 0)
        def _():
            joined = jnp.concatenate(
                [tail[0].reshape(D, REST), tail[1].reshape(D, REST)], axis=1
            )
            wo[...] = joined[:, :D]
            nrm[...] = joined[:, D : D + LANES].astype(F32).T[:8]
            sums[...] = jnp.zeros_like(sums)

        gain1, gain2, shift1, shift2 = (nrm[i : i + 1, :] for i in range(4))

        @pl.when(step < STEPS)
        def _():
            rows = pl.ds(pl.multiple_of(step * ROWS, ROWS), ROWS)
            context = jnp.concatenate([ctx0[...], ctx1[...], ctx2[...]], axis=1)
            hidden_in = x[...].astype(F32) + dot_nn(context, wo[...])
            hat1, scale1 = norm(hidden_in)
            hat_s[rows, :] = hat1
            scale_s[rows, :] = scale1
            normed = hat1 * gain1 + shift1
            low = normed.astype(BF16)
            low_t[:, rows] = low.T
            total = normed
            for half in range(2):
                arrive("gate", half)
                arrive("down", half)
                for n in range(HIDDEN // CHUNK):
                    g_at, u_at, d_at = (pl.ds(p * HIDDEN + n * CHUNK, CHUNK) for p in range(3))
                    gate = dot_nn(low, w[half, :, g_at])
                    up = dot_nn(low, w[half, :, u_at])
                    s = jax.nn.sigmoid(gate)
                    silu = gate * s
                    act = (silu * up).astype(BF16)
                    factors[half, rows, g_at] = (up * (s * (1.0 + gate * (1.0 - s)))).astype(BF16)
                    factors[half, rows, u_at] = silu.astype(BF16)
                    acts[half, rows, g_at] = act
                    total = total + dot_nt(act, w[half, :, d_at])
            hat2, scale2 = norm(total)
            result = (hat2 * gain2 + shift2).astype(BF16)
            own = step // (STEPS // 2) == core

            @pl.when(own)
            def _():
                out[...] = result

            @pl.when(jnp.logical_not(own))
            def _():
                out_leave[...] = result

            u2 = cot[...].astype(F32)
            resid = norm_back(u2, hat2, scale2, gain2)
            mlp = resid.astype(BF16)
            mlp_s[rows, :] = mlp
            mlp_t[:, rows] = mlp.T
            back_s[rows, :] = resid
            sums[1:2, :] += jnp.sum(u2 * hat2, axis=0, keepdims=True)
            sums[3:4, :] += jnp.sum(u2, axis=0, keepdims=True)

        @pl.when(jnp.logical_and(step >= STEPS, step < STEPS + PIECES))
        def _():
            at = step - STEPS
            half = 1 - at // (PIECES // 2)
            n = at % (PIECES // 2)
            g_at, u_at, d_at = (
                pl.ds(pl.multiple_of(p * HIDDEN + n * PIECE, PIECE), PIECE) for p in range(3)
            )

            @pl.loop(0, STEPS)
            def _(r):
                rows = pl.ds(pl.multiple_of(r * ROWS, ROWS), ROWS)
                grad = dot_nn(mlp_s[rows, :], w[half, :, d_at])
                gate_grad = (grad * factors[half, rows, g_at].astype(F32)).astype(BF16)
                up_grad = (grad * factors[half, rows, u_at].astype(F32)).astype(BF16)
                pair_s[0, rows, :] = gate_grad
                pair_s[1, rows, :] = up_grad
                back_s[rows, :] += dot_nt(gate_grad, w[half, :, g_at]) + dot_nt(
                    up_grad, w[half, :, u_at]
                )

            def store(gu, down):
                for i in range(2):
                    gu[i] = dot_nn(low_t[...], pair_s[i]).astype(BF16)
                down[0] = dot_nn(mlp_t[...], acts[half, :, g_at]).astype(BF16)

            @pl.when(half == 1)
            def _():
                store(gu_other, down_other)

            @pl.when(half == 0)
            def _():
                store(gu_own, down_own)

        @pl.when(step >= STEPS + PIECES)
        def _():
            r = step - STEPS - PIECES
            rows = pl.ds(pl.multiple_of(r * ROWS, ROWS), ROWS)
            back, hat1 = back_s[rows, :], hat_s[rows, :]
            hidden_grad = norm_back(back, hat1, scale_s[rows, :], gain1)
            hid_out[...] = hidden_grad
            att = hidden_grad.astype(BF16)
            att_out[...] = att
            ctxg_out[...] = dot_nt(att, wo[...]).astype(BF16)
            sums[0:1, :] += jnp.sum(back * hat1, axis=0, keepdims=True)
            sums[2:3, :] += jnp.sum(back, axis=0, keepdims=True)

    last = STEPS - 1
    row = lambda n: pl.BlockSpec((ROWS, n), lambda t, i: (jnp.minimum(t, last), 0))
    ending = pl.BlockSpec((ROWS, D), lambda t, i: (jnp.clip(t - STEPS - PIECES, 0, last), 0))
    half = STEPS // 2
    side = lambda t, mine: (jnp.clip(jnp.minimum(t, last) - half * mine, 0, half - 1), 0)
    mine = pl.BlockSpec((ROWS, D), lambda t, i: side(t, i[32]))
    leave = pl.BlockSpec((ROWS, D), lambda t, i: side(t, 1 - i[32]))
    each = PIECES // 2
    own = lambda lead: pl.BlockSpec(
        (lead, D, PIECE), lambda t, i: (0, 0, jnp.clip(t - STEPS - each, 0, each - 1))
    )
    theirs = lambda lead: pl.BlockSpec(
        (lead, D, PIECE), lambda t, i: (0, 0, jnp.clip(t - STEPS, 0, each - 1))
    )
    act = lambda n, t=BF16: jax.ShapeDtypeStruct((n, D), t)
    grads = lambda lead: jax.ShapeDtypeStruct((lead, D, HIDDEN), BF16)
    return pl.pallas_call(
        body,
        grid_spec=pltpu.PrefetchScalarGridSpec(
            num_scalar_prefetch=1,
            grid=(2 * STEPS + PIECES,),
            in_specs=[row(D)] + [row(GROUP)] * GROUPS + [row(D)] + [ANY] * 8,
            out_specs=[mine, leave, own(2), theirs(2), own(1), theirs(1)]
            + [ending] * 3
            + [pl.BlockSpec((8, D), lambda t, i: (0, 0))],
            scratch_shapes=[
                pltpu.VMEM((2, D, WIDE), BF16),
                pltpu.VMEM((D, D), BF16),
                pltpu.VMEM((2, 32, D // 32, REST), BF16),
                pltpu.VMEM((8, D), F32),
                pltpu.VMEM((2, SEQ, 2 * HIDDEN), BF16),
                pltpu.VMEM((2, SEQ, HIDDEN), BF16),
                pltpu.VMEM((D, SEQ), BF16),
                pltpu.VMEM((D, SEQ), BF16),
                pltpu.VMEM((SEQ, D), BF16),
                pltpu.VMEM((SEQ, D), F32),
                pltpu.VMEM((SEQ, D), F32),
                pltpu.VMEM((SEQ, 1), F32),
                pltpu.VMEM((2, SEQ, PIECE), BF16),
                pltpu.SemaphoreType.DMA((128,)),
            ],
        ),
        out_shape=[
            act(SEQ // 2),
            act(SEQ // 2),
            grads(2),
            grads(2),
            grads(1),
            grads(1),
            act(SEQ, F32),
            act(SEQ),
            act(SEQ),
            jax.ShapeDtypeStruct((8, D), F32),
        ],
        compiler_params=params(62),
        cost_estimate=cost(18 * SEQ * D * 2 * HIDDEN + 4 * SEQ * D * D, 40 << 20, 4 * SEQ * HIDDEN),
        name="middle",
    )(index, source, *ctx, cot, *pieces)


def rotary_lanes(segment_row):
    labels = jnp.arange(NDOC + 1, dtype=jnp.int32)
    before = jnp.sum((segment_row[None, :] < labels[:, None]).astype(jnp.int32), axis=1)
    member = segment_row[:, None] == labels[None, :]
    first = jnp.sum(jnp.where(member, before[None, :], 0), axis=1)
    position = (jnp.arange(SEQ, dtype=jnp.int32) - first).astype(F32)
    lane = jnp.arange(LANES) % (HEAD // 2)
    frequency = jnp.power(F32(1000.0), -2.0 * lane.astype(F32) / HEAD)
    angle = position[:, None] * frequency[None, :]
    sign = jnp.where(jnp.arange(LANES) % HEAD < HEAD // 2, -1.0, 1.0)
    ends = jnp.concatenate([before[1:], jnp.full((1,), SEQ, jnp.int32)])
    heads = segment_row[::BLOCK]
    tails = segment_row[BLOCK - 1 :: BLOCK]
    low = jnp.sum(jnp.where(heads[:, None] == labels[None, :], before[None, :], 0), axis=1)
    high = jnp.sum(jnp.where(tails[:, None] == labels[None, :], ends[None, :], 0), axis=1)
    bounds = jnp.concatenate([low // KEYS, (high + KEYS - 1) // KEYS]).astype(jnp.int32)
    return jnp.cos(angle), jnp.sin(angle) * sign[None, :], bounds


def sequence_device(
    tokens, segments, qkv_weight, out_weight, norm_gain, norm_shift, gate_up, down_weight, cotangent
):
    core = lax.axis_index("tensor")
    def ordered(mine, theirs):
        return jnp.where(
            core == 0, jnp.stack([mine, theirs], axis=0), jnp.stack([theirs, mine], axis=0)
        )

    pick = lambda a, i: lax.dynamic_index_in_dim(a, i, 0, keepdims=False)
    source = pick(tokens, core)
    segment_row = pick(segments, core)

    attn_block = qkv_weight.reshape(-1, 3 * D)
    gate_block = gate_up.reshape(-1, 2 * HIDDEN)
    tail_block = jnp.concatenate(
        [out_weight, norm_gain, norm_shift, jnp.zeros((D // 32, TAIL - D - 4), BF16)], axis=1
    )
    down_block = jnp.concatenate(
        [down_weight, jnp.concatenate([tail_block[:, :REST], tail_block[:, REST:]], axis=0)], axis=1
    )
    from_here, from_there = slot_blocks(-1, core), slot_blocks(-1, 1 - core)
    there_blocks = slot_blocks(1, core).reshape(2, 2, 4)
    to_here = there_blocks.transpose(1, 0, 2).reshape(16)
    deep_first = there_blocks.transpose(2, 1, 0).reshape(16)

    cot = ordered(pick(cotangent, core), core_swap(pick(cotangent, 1 - core))).reshape(SEQ, D)
    cosine, sine, bounds = rotary_lanes(segment_row)
    bounds = jnp.concatenate([bounds, core[None]]).astype(jnp.int32)
    tables = (cosine, sine, segment_row[:, None], segment_row[None, :])

    ahead = lambda parts: [part[None] for part in parts]
    attn_four = pile(ahead(depth_parts(attn_block)))
    gate_block = pile([gate_block[None]], deps=(attn_four,))[0]
    gate_parts = depth_ring(gate_block)
    attn_eight = pile([attn_four, first_swap(attn_four)], deps=(gate_parts[1], source, cot, *tables))
    attn_last = second_swap(attn_eight)
    index = jnp.concatenate([from_here * 2 + core, from_there * 2 + 1 - core]).astype(jnp.int32)
    weights = assemble(
        (attn_eight, attn_last),
        (core_swap(attn_eight), core_swap(attn_last)),
        index,
        deps=(gate_parts[3],),
    ).reshape(D, 3 * D)
    gate_four = pile(ahead(gate_parts))
    down_block = pile([down_block[None]], deps=(gate_four,))[0]
    saved0 = attn_forward(0, 1, bounds, source, weights, *tables, deps=(gate_four, down_block))
    down_four = pile(ahead(depth_parts(down_block)), deps=(saved0[4],))
    gate_eight = pile([gate_four, first_swap(gate_four)], deps=(down_four,))
    gate_last = second_swap(gate_eight)
    saved1 = attn_forward(1, 1, bounds, source, weights, *tables, deps=(gate_eight, down_four))
    down_eight = pile([down_four, first_swap(down_four)], deps=(saved1[4],))
    saved2 = attn_forward(2, 1, bounds, source, weights, *tables, deps=(down_eight,))
    down_last, late_logs = lax.optimization_barrier((second_swap(down_eight), saved2[4]))
    saved2 = (*saved2[:4], late_logs)
    pieces = (gate_eight, gate_last, core_swap(gate_eight), core_swap(gate_last))
    pieces += (down_eight, down_last, core_swap(down_eight), core_swap(down_last))

    index = jnp.concatenate([from_here, from_there, core[None]]).astype(jnp.int32)
    ctx = (saved0[3], saved1[3], saved2[3])
    (out, out_leave, gu_here, gu_there, down_here, down_there, hidden_grad, att_grad, ctx_grad, sums) = (
        middle(index, source, ctx, cot, pieces)
    )

    down_there, gu_there = core_swap(down_there), core_swap(gu_there)
    tail_mine, tail_theirs = out_grad(core, ctx, att_grad, sums)
    down_parts = join_rows(deep_first, down_here, down_there, 4)
    gu_keep, gu_send = join_rows(to_here, gu_here, gu_there, 2)
    gu_first = first_swap(gu_send)
    passing = depth_shift(down_parts[3], 1)

    common = (source,) + tables
    back0 = attn_backward(0, 0, bounds, saved0, ctx_grad, *common, deps=(gu_send, down_parts[0]))
    (passing,) = fold(passing, down_parts[2], 1, deps=(back0[1],))
    back1 = attn_backward(0, 1, bounds, saved1, ctx_grad, *common, deps=(passing,))
    passing = depth_shift(passing, 1)
    (passing,) = fold(passing, down_parts[1], 1, deps=(back1[1],))
    gu_keep, gu_send = fold(gu_keep, gu_first, 2, deps=(back1[1],))
    gu_second = second_swap(gu_send)
    early_keep, early_send = join_dealt(
        to_here,
        (back0[1], back1[1], tail_mine),
        (core_swap(back0[2]), core_swap(back1[2]), core_swap(tail_theirs)),
    )
    early_first = first_swap(early_send)
    back2 = attn_backward(0, 2, bounds, saved2, ctx_grad, *common, deps=(gu_send, early_send, passing))

    deep = lambda parts: [parts[0]] + [depth_shift(parts[k], k) for k in (1, 2, 3)]
    passing = depth_shift(passing, 1)
    gu_parts = fold(gu_keep, gu_second, 4, deps=(back2[1],))
    gu_total = gu_parts[3]
    for k in (2, 1):
        (gu_total,) = fold(depth_shift(gu_total, 1), gu_parts[k], 1)
    down_keep, down_send = fold(passing, down_parts[0], 2, deps=(gu_parts[0],))
    down_keep, down_send = fold(down_keep, first_swap(down_send), 2)
    down_second = second_swap(down_send)
    early_keep, early_send = fold(early_keep, early_first, 2, deps=(gu_parts[0],))
    early_second = second_swap(early_send)
    late_keep, late_send = join_dealt(
        to_here, (back2[1],), (core_swap(back2[2]),), deps=(early_send, down_keep)
    )
    grad, grad_leave = input_back(
        core, hidden_grad, (back0[0], back1[0], back2[0]), weights, deps=(late_send,)
    )
    late_keep, late_send = fold(late_keep, first_swap(late_send), 2, deps=(grad,))
    late_second = second_swap(late_send)
    (gu_total,) = fold(depth_shift(gu_total, 1), gu_parts[0], 1, F32, deps=(late_send,))
    early_parts = deep(fold(early_keep, early_second, 4, deps=(gu_total,)))
    late_parts = deep(fold(late_keep, late_second, 4, deps=(early_parts[0],)))
    down_total = (down_keep.astype(F32) + down_second.astype(F32))[0]
    (early_total,) = total4(early_parts, 1, F32)
    (late_total,) = total4(late_parts, 1, F32)
    gu_total, early_total, late_total = gu_total[0], early_total[0], late_total[0]

    rows = D // 32
    qkv_total = jnp.concatenate([early_total[:, : 6 * GROUP], late_total], axis=1)
    qkv_total = qkv_total.reshape(rows, GROUPS, 3, GROUP).transpose(0, 2, 1, 3).reshape(rows, 3, D)
    rest = early_total[:, 6 * GROUP :]

    return (
        place(core, out, core_swap(out_leave)),
        place(core, grad, core_swap(grad_leave)),
        qkv_total,
        rest[:, :D],
        rest[:, D : D + 2],
        rest[:, D + 2 : D + 4],
        gu_total.reshape(-1, 2, HIDDEN),
        down_total,
    )


def solution(mesh):
    in_specs = (
        P("dp", None, None),
        P("dp", None),
        P(("dp", "tensor"), None, None),
        P(("dp", "tensor"), None),
        P(("dp", "tensor"), None),
        P(("dp", "tensor"), None),
        P("dp", None, "tensor"),
        P("dp", "tensor"),
        P("dp", "tensor", None),
    )
    out_specs = (
        P("dp", "tensor", None),
        P("dp", "tensor", None),
        P(("dp", "tensor"), None, None),
        P(("dp", "tensor"), None),
        P(("dp", "tensor"), None),
        P(("dp", "tensor"), None),
        P("dp", None, "tensor"),
        P("dp", "tensor"),
    )
    sizes = dict(mesh.shape)

    def per_device(tokens, *others):
        if sizes["dp"] == 16 and sizes["tensor"] == 2 and tokens.shape[0] == 2:
            return sequence_device(tokens, *others)
        return general_device(tokens, *others)

    return jax.shard_map(
        per_device, mesh=mesh, in_specs=in_specs, out_specs=out_specs, check_vma=False
    )
```

```python
import jax
import jax.numpy as jnp
from jax import lax
from jax.experimental import pallas as pl
from jax.experimental.pallas import tpu as pltpu
from jax.sharding import PartitionSpec as P

D = 768
HEADS = 12
HEAD = 64
SEQ = 1024
NDOC = 8


EPSILON = 1e-05
MASKED = -1e30


def for_sending(value):
    return jax.tree.map(lambda a: a.astype(jnp.bfloat16) if a.dtype == jnp.float32 else a, value)


def rotary_tables(segment_row):
    labels = jnp.arange(NDOC + 1, dtype=jnp.int32)
    member = (segment_row[:, None] == labels[None, :]).astype(jnp.int32)
    counts = jnp.sum(member, axis=0)
    starts = jnp.concatenate([jnp.zeros((1,), jnp.int32), jnp.cumsum(counts)[:-1]])
    offset = jnp.sum(member * starts[None, :], axis=1)
    position = (jnp.arange(SEQ, dtype=jnp.int32) - offset).astype(jnp.float32)
    exponent = -2.0 * jnp.arange(HEAD // 2).astype(jnp.float32) / HEAD
    frequency = jnp.power(jnp.float32(1000.0), exponent)
    angle = position[:, None] * frequency[None, :]
    return (jnp.cos(angle)[:, None, :], jnp.sin(angle)[:, None, :])


def rotate(vector, cosine, sine):
    half = vector.shape[-1] // 2
    first_half = vector[..., :half]
    second_half = vector[..., half:]
    return jnp.concatenate(
        [first_half * cosine - second_half * sine, second_half * cosine + first_half * sine],
        axis=-1,
    )


def unrotate(gradient, cosine, sine):

    def turned(vector):
        return rotate(vector, cosine, sine)

    _, pullback = jax.vjp(turned, gradient)
    return pullback(gradient)[0]


def layer_norm(vector, gain, shift):
    center = vector - jnp.mean(vector, axis=-1, keepdims=True)
    variance = jnp.mean(center * center, axis=-1, keepdims=True)
    return center * lax.rsqrt(variance + EPSILON) * gain + shift


def swiglu_piece(gate, upper):
    return jax.nn.silu(gate) * upper


def accumulate(total, term):
    if total is None:
        return term
    return tuple((left + right for left, right in zip(total, term)))


def general_device(
    tokens, segments, qkv_weight, out_weight, norm_gain, norm_shift, gate_up, down_weight, cotangent
):
    tensor_size = lax.axis_size("tensor")
    own_rows = SEQ // tensor_size
    row_start = lax.axis_index("tensor") * own_rows
    score_scale = HEAD ** (-0.5)
    qkv_full, out_full, gain_full, shift_full = (
        lax.all_gather(qkv_weight, ("dp", "tensor"), axis=0, tiled=True),
        lax.all_gather(out_weight, ("dp", "tensor"), axis=0, tiled=True),
        lax.all_gather(norm_gain, ("dp", "tensor"), axis=0, tiled=True),
        lax.all_gather(norm_shift, ("dp", "tensor"), axis=0, tiled=True),
    )
    gains = gain_full.astype(jnp.float32)
    shifts = shift_full.astype(jnp.float32)
    gate_up_full, down_full = (
        lax.all_gather(gate_up, "dp", axis=0, tiled=True),
        lax.all_gather(down_weight, "dp", axis=0, tiled=True),
    )
    batches = tokens.shape[0]
    outputs = []
    input_grads = []
    attn_total = None
    mlp_total = None
    for batch_index in range(batches):
        source = tokens[batch_index]
        own_source = lax.dynamic_slice_in_dim(source, row_start, own_rows, 0)
        segment_row = segments[batch_index]
        cosine, sine = rotary_tables(segment_row)
        own_cos = lax.dynamic_slice_in_dim(cosine, row_start, own_rows, 0)
        own_sin = lax.dynamic_slice_in_dim(sine, row_start, own_rows, 0)
        query_proj = jnp.einsum(
            "sd,de->se", own_source, qkv_full[:, 0], preferred_element_type=jnp.float32
        )
        pair_proj = jnp.einsum(
            "sd,dke->ske", source, qkv_full[:, 1:], preferred_element_type=jnp.float32
        )
        keys = rotate(pair_proj[:, 0].reshape(SEQ, HEADS, HEAD), cosine, sine).astype(jnp.bfloat16)
        values = pair_proj[:, 1].reshape(SEQ, HEADS, HEAD).astype(jnp.bfloat16)
        queries = rotate(query_proj.reshape(own_rows, HEADS, HEAD), own_cos, own_sin).astype(
            jnp.bfloat16
        )
        own_segments = lax.dynamic_slice_in_dim(segment_row, row_start, own_rows, 0)
        allowed = (own_segments[:, None] == segment_row[None, :])[None]
        raw_scores = (
            jnp.einsum("qhe,khe->hqk", queries, keys, preferred_element_type=jnp.float32)
            * score_scale
        )
        masked = jnp.where(allowed, raw_scores, MASKED)
        top_score = jnp.max(masked, axis=-1, keepdims=True)
        logsum = top_score + jnp.log(jnp.sum(jnp.exp(masked - top_score), axis=-1, keepdims=True))
        probs_low = jnp.exp(masked - logsum).astype(jnp.bfloat16)
        context = (
            jnp.einsum("hqk,khe->qhe", probs_low, values, preferred_element_type=jnp.float32)
            .reshape(own_rows, D)
            .astype(jnp.bfloat16)
        )
        attended = jnp.dot(context, out_full, preferred_element_type=jnp.float32)
        hidden_in = own_source.astype(jnp.float32) + attended
        normed = layer_norm(hidden_in, gains[:, 0], shifts[:, 0])
        normed_all = lax.all_gather(normed.astype(jnp.bfloat16), "tensor", axis=0, tiled=True)
        gate_pair = jnp.einsum(
            "sd,dkf->skf", normed_all, gate_up_full, preferred_element_type=jnp.float32
        )
        swiglu = swiglu_piece(gate_pair[:, 0], gate_pair[:, 1]).astype(jnp.bfloat16)
        mlp_out = lax.psum_scatter(
            jnp.einsum("sf,df->sd", swiglu, down_full, preferred_element_type=jnp.float32).astype(
                jnp.bfloat16
            ),
            "tensor",
            scatter_dimension=0,
            tiled=True,
        ).astype(jnp.float32)
        resid = normed + mlp_out
        outputs.append(layer_norm(resid, gains[:, 1], shifts[:, 1]).astype(jnp.bfloat16))
        upstream = cotangent[batch_index].astype(jnp.float32)
        _, second_pull = jax.vjp(layer_norm, resid, gains[:, 1], shifts[:, 1])
        resid_grad, gain_two, shift_two = second_pull(upstream)
        mlp_grad = lax.all_gather(resid_grad.astype(jnp.bfloat16), "tensor", axis=0, tiled=True)
        swiglu_grad = jnp.einsum(
            "sd,df->sf", mlp_grad, down_full, preferred_element_type=jnp.float32
        )
        _, glu_pull = jax.vjp(swiglu_piece, gate_pair[:, 0], gate_pair[:, 1])
        gate_grad, upper_grad = glu_pull(swiglu_grad)
        pair_grad = jnp.stack([gate_grad, upper_grad], axis=1).astype(jnp.bfloat16)
        down_term = jnp.einsum("sd,sf->df", mlp_grad, swiglu, preferred_element_type=jnp.float32)
        gate_up_term = jnp.einsum(
            "sd,skf->dkf", normed_all, pair_grad, preferred_element_type=jnp.float32
        )
        normed_grad = resid_grad + lax.psum_scatter(
            jnp.einsum("skf,dkf->sd", pair_grad, gate_up_full, preferred_element_type=jnp.float32),
            "tensor",
            scatter_dimension=0,
            tiled=True,
        )
        _, first_pull = jax.vjp(layer_norm, hidden_in, gains[:, 0], shifts[:, 0])
        hidden_grad, gain_one, shift_one = first_pull(normed_grad)
        attended_grad = hidden_grad.astype(jnp.bfloat16)
        out_term = jnp.einsum(
            "sd,se->de", context, attended_grad, preferred_element_type=jnp.float32
        )
        context_grad = (
            jnp.einsum("se,de->sd", attended_grad, out_full, preferred_element_type=jnp.float32)
            .astype(jnp.bfloat16)
            .reshape(own_rows, HEADS, HEAD)
        )
        probs = jnp.exp(masked - logsum)
        weights_grad = jnp.einsum(
            "qhe,khe->hqk", context_grad, values, preferred_element_type=jnp.float32
        )
        row_delta = jnp.sum(probs * weights_grad, axis=-1, keepdims=True)
        score_grad = (probs * (weights_grad - row_delta)).astype(jnp.bfloat16)
        query_grad = (
            jnp.einsum("hqk,khe->qhe", score_grad, keys, preferred_element_type=jnp.float32)
            * score_scale
        )
        key_part = (
            jnp.einsum("hqk,qhe->khe", score_grad, queries, preferred_element_type=jnp.float32)
            * score_scale
        )
        value_part = jnp.einsum(
            "hqk,qhe->khe", probs_low, context_grad, preferred_element_type=jnp.float32
        )
        key_value = lax.psum_scatter(
            jnp.stack(
                [
                    key_part.reshape(lax.axis_size("tensor") * own_rows, D),
                    value_part.reshape(lax.axis_size("tensor") * own_rows, D),
                ],
                axis=1,
            ).astype(jnp.bfloat16),
            "tensor",
            scatter_dimension=0,
            tiled=True,
        ).astype(jnp.float32)
        query_back = unrotate(query_grad, own_cos, own_sin).reshape(own_rows, D)
        key_back = unrotate(
            key_value[:, 0].reshape(own_rows, HEADS, HEAD), own_cos, own_sin
        ).reshape(own_rows, D)
        proj_grad = jnp.stack([query_back, key_back, key_value[:, 1]], axis=1).astype(jnp.bfloat16)
        input_grads.append(
            hidden_grad
            + jnp.einsum("ske,dke->sd", proj_grad, qkv_full, preferred_element_type=jnp.float32)
        )
        qkv_term = jnp.einsum(
            "sd,ske->dke", own_source, proj_grad, preferred_element_type=jnp.float32
        )
        gain_term = jnp.stack([gain_one, gain_two], axis=1)
        shift_term = jnp.stack([shift_one, shift_two], axis=1)
        attn_terms = (qkv_term, out_term, gain_term, shift_term)
        mlp_terms = (gate_up_term, down_term)
        attn_total = accumulate(attn_total, attn_terms)
        mlp_total = accumulate(mlp_total, mlp_terms)
    attn_final = lax.psum_scatter(attn_total, ("dp", "tensor"), scatter_dimension=0, tiled=True)
    mlp_final = jax.tree.map(
        lambda part: part.astype(jnp.float32),
        lax.psum_scatter(for_sending(mlp_total), "dp", scatter_dimension=0, tiled=True),
    )
    return (
        jnp.stack(outputs, axis=0),
        jnp.stack(input_grads, axis=0),
        attn_final[0],
        attn_final[1],
        attn_final[2],
        attn_final[3],
        mlp_final[0],
        mlp_final[1],
    )


HIDDEN = 1536
WIDE = 3 * HIDDEN
REST = 512
TAIL = 2 * REST
GROUP = 4 * HEAD
GROUPS = D // GROUP
KEYS = 128
LANES = 2 * HEAD
BLOCK = 256
NBLOCK = SEQ // BLOCK
ROWS = 256
STEPS = SEQ // ROWS
CHUNK = 512
PIECE = 256
PIECES = 2 * HIDDEN // PIECE
LOG2E = 1.4426950408889634
F32 = jnp.float32
BF16 = jnp.bfloat16


def across(value, move):
    pairs = []
    for z in range(4):
        for y in range(2):
            for x in range(2):
                for c in range(2):
                    tz, ty, tx, tc = move(z, y, x, c)
                    pairs.append((((z * 2 + y) * 2 + x) * 2 + c, ((tz * 2 + ty) * 2 + tx) * 2 + tc))
    return lax.ppermute(value, ("dp", "tensor"), pairs)


def core_swap(value):
    return across(value, lambda z, y, x, c: (z, y, x, 1 - c))


def first_swap(value):
    return across(value, lambda z, y, x, c: (z, y, 1 - x, c) if c == 0 else (z, 1 - y, x, c))


def second_swap(value):
    return across(value, lambda z, y, x, c: (z, 1 - y, x, c) if c == 0 else (z, y, 1 - x, c))


def depth_shift(value, steps):
    return across(value, lambda z, y, x, c: ((z + steps) % 4, y, x, c))


def slot_blocks(sign, core):
    me = lax.axis_index("dp")
    z, y, x = me // 4, (me // 2) % 2, me % 2
    slot = jnp.arange(16, dtype=jnp.int32)
    second, first, depth = slot // 8, (slot // 4) % 2, slot % 4
    x_bit = jnp.where(core == 0, first, second)
    y_bit = jnp.where(core == 0, second, first)
    return (((z + sign * depth) % 4) * 4 + (y ^ y_bit) * 2 + (x ^ x_bit)).astype(jnp.int32)


def depth_parts(block):
    return [block] + [depth_shift(block, k) for k in (1, 2, 3)]


def depth_ring(block):
    parts = [block]
    for _ in range(3):
        parts.append(depth_shift(parts[-1], 1))
    return parts


def cost(flops, nbytes, trans=0):
    return pl.CostEstimate(flops=int(flops), bytes_accessed=int(nbytes), transcendentals=int(trans))


def params(vmem_mb, sem=("arbitrary",)):
    return pltpu.CompilerParams(dimension_semantics=sem, vmem_limit_bytes=vmem_mb << 20)


ANY = pl.BlockSpec(memory_space=pl.ANY)
AFTER = pl.BlockSpec(memory_space=pltpu.HBM)


def pile(parts, deps=()):
    spans, start = [], 0
    for part in parts:
        spans.append((start, part.shape[0]))
        start += part.shape[0]

    def body(*refs):
        ins, out, sem = refs[: len(parts)], refs[-2], refs[-1]
        copies = [
            pltpu.make_async_copy(ref, out.at[pl.ds(at, n)], sem.at[i])
            for i, (ref, (at, n)) in enumerate(zip(ins, spans))
        ]
        for cp in copies:
            cp.start()
        for cp in copies:
            cp.wait()

    shape = (start,) + parts[0].shape[1:]
    return pl.pallas_call(
        body,
        in_specs=[ANY] * len(parts) + [AFTER] * len(deps),
        out_specs=pl.BlockSpec(memory_space=pltpu.VMEM),
        out_shape=jax.ShapeDtypeStruct(shape, parts[0].dtype),
        scratch_shapes=[pltpu.SemaphoreType.DMA((len(parts),))],
        compiler_params=params(16, None),
        cost_estimate=cost(0, 4 * start * shape[1] * shape[2]),
        name="pile",
    )(*parts, *deps)


def place(core, mine, there):
    def body(c, a, b, out, sem):
        first = pltpu.make_async_copy(a, out.at[c[0]], sem.at[0])
        second = pltpu.make_async_copy(b, out.at[1 - c[0]], sem.at[1])
        first.start()
        second.start()
        first.wait()
        second.wait()

    return pl.pallas_call(
        body,
        grid_spec=pltpu.PrefetchScalarGridSpec(
            num_scalar_prefetch=1,
            grid=(1,),
            in_specs=[ANY, ANY],
            out_specs=pl.BlockSpec((2,) + mine.shape, lambda i, c: (0, 0, 0)),
            scratch_shapes=[pltpu.SemaphoreType.DMA((2,))],
        ),
        out_shape=jax.ShapeDtypeStruct((2,) + mine.shape, mine.dtype),
        compiler_params=params(16),
        cost_estimate=cost(0, 4 * mine.size),
        name="place",
    )(core[None], mine, there)


def assemble(own, other, index, deps=()):
    def body(idx, a, b, c, d, *rest):
        out, sem = rest[-2:]
        copies = []
        for i, ref in enumerate((a, b, c, d)):
            for s in range(8):
                copies.append(
                    pltpu.make_async_copy(ref.at[s], out.at[idx[i * 8 + s]], sem.at[i * 8 + s])
                )
        for cp in copies:
            cp.start()
        for cp in copies:
            cp.wait()

    rows, wide = own[0].shape[1:]
    return pl.pallas_call(
        body,
        grid_spec=pltpu.PrefetchScalarGridSpec(
            num_scalar_prefetch=1,
            grid=(1,),
            in_specs=[ANY] * 4 + [AFTER] * len(deps),
            out_specs=pl.BlockSpec((32, rows, wide), lambda i, c: (0, 0, 0)),
            scratch_shapes=[pltpu.SemaphoreType.DMA((32,))],
        ),
        out_shape=jax.ShapeDtypeStruct((32, rows, wide), BF16),
        compiler_params=params(60),
        cost_estimate=cost(0, 4 * 32 * rows * wide),
        name="assemble",
    )(index, *own, *other, *deps)


def turn(vector, cosine, sine):
    lane = lax.broadcasted_iota(jnp.int32, vector.shape, 1)
    swapped = jnp.where(
        lane % HEAD < HEAD // 2,
        pltpu.roll(vector, LANES - HEAD // 2, 1),
        pltpu.roll(vector, HEAD // 2, 1),
    )
    return vector * cosine + swapped * sine


def dot_nn(a, b):
    return lax.dot_general(a, b, (((1,), (0,)), ((), ())), preferred_element_type=F32)


def dot_nt(a, b):
    return lax.dot_general(a, b, (((1,), (1,)), ((), ())), preferred_element_type=F32)


def dot_tn(a, b):
    return lax.dot_general(a, b, (((0,), (0,)), ((), ())), preferred_element_type=F32)


def stacked(low_lane, pair):
    zero = jnp.zeros_like(pair)
    return jnp.concatenate(
        [jnp.where(low_lane, pair, zero), jnp.where(low_lane, zero, pair)], axis=0
    )


def windows(bnd, i, work):
    blocks = (bnd[NBLOCK + i] - bnd[i] + BLOCK // KEYS - 1) // (BLOCK // KEYS)
    for width in range(1, NBLOCK + 1):

        @pl.when(blocks == width)
        def _():
            low = jnp.minimum(bnd[i], (SEQ - width * BLOCK) // KEYS)
            work(pl.ds(pl.multiple_of(low * KEYS, KEYS), width * BLOCK))


def attn_forward(first, count, bounds, source, weights, cosine, sine, seg_col, seg_row, deps=()):
    def body(bnd, x, wq, wk, wv, cos, sin, sc, sr, *rest):
        q_out, k_out, v_out, ctx_out, lse_out, qm = rest[len(deps) :]
        low_lane = lax.broadcasted_iota(jnp.int32, (BLOCK, LANES), 1) < HEAD

        @pl.loop(0, NBLOCK)
        def _(r):
            rows = pl.ds(pl.multiple_of(r * BLOCK, BLOCK), BLOCK)
            xr, cr, sn = x[rows, :], cos[rows, :], sin[rows, :]
            q_proj, k_proj = dot_nn(xr, wq[...]), dot_nn(xr, wk[...])
            v_out[rows, :] = dot_nn(xr, wv[...]).astype(BF16)
            for p in range(GROUP // LANES):
                ln = slice(p * LANES, (p + 1) * LANES)
                q = turn(q_proj[:, ln], cr, sn).astype(BF16) * jnp.asarray(HEAD**-0.5, BF16)
                q_out[rows, ln] = q
                qm[p, r] = stacked(low_lane, q)
                k_out[rows, ln] = turn(k_proj[:, ln], cr, sn).astype(BF16)

        def block(i, _):
            rows = pl.ds(pl.multiple_of(i * BLOCK, BLOCK), BLOCK)
            own = jnp.concatenate([sc[rows, :], sc[rows, :]], axis=0)

            def work(cols):
                seen = own == sr[:, cols]
                for p in range(GROUP // LANES):
                    ln = slice(p * LANES, (p + 1) * LANES)
                    s = jnp.where(seen, dot_nt(qm[p, i], k_out[cols, ln]) * LOG2E, MASKED)
                    top = jnp.max(s, axis=1, keepdims=True)
                    e = jnp.exp2(s - top)
                    total = jnp.sum(e, axis=1, keepdims=True)
                    mixed = dot_nn(e.astype(BF16), v_out[cols, ln]) / total
                    ctx_out[rows, ln] = jnp.where(low_lane, mixed[:BLOCK], mixed[BLOCK:]).astype(BF16)
                    logs = top + jnp.log2(total)
                    flipped = jnp.where(low_lane, logs[:BLOCK], logs[BLOCK:]).T
                    lse_out[0, 2 * p : 2 * p + 1, rows] = flipped[0:1]
                    lse_out[0, 2 * p + 1 : 2 * p + 2, rows] = flipped[HEAD : HEAD + 1]

            windows(bnd, i, work)
            return 0

        lax.fori_loop(0, NBLOCK, block, 0)

    full = lambda shape: pl.BlockSpec(shape, lambda p, b: (0,) * len(shape))
    column = lambda shift: pl.BlockSpec((D, GROUP), lambda p, b: (0, shift * GROUPS + first + p))
    part = pl.BlockSpec((SEQ, GROUP), lambda p, b: (0, p))
    act = jax.ShapeDtypeStruct((SEQ, count * GROUP), BF16)
    return pl.pallas_call(
        body,
        grid_spec=pltpu.PrefetchScalarGridSpec(
            num_scalar_prefetch=1,
            grid=(count,),
            in_specs=[
                full((SEQ, D)),
                column(0),
                column(1),
                column(2),
                full((SEQ, LANES)),
                full((SEQ, LANES)),
                full((SEQ, 1)),
                full((1, SEQ)),
            ]
            + [AFTER] * len(deps),
            out_specs=[part] * 4 + [pl.BlockSpec((1, 8, SEQ), lambda p, b: (p, 0, 0))],
            scratch_shapes=[pltpu.VMEM((GROUP // LANES, NBLOCK, 2 * BLOCK, LANES), BF16)],
        ),
        out_shape=[act] * 4 + [jax.ShapeDtypeStruct((count, 8, SEQ), F32)],
        compiler_params=params(60),
        cost_estimate=cost(
            count * GROUP * (6 * SEQ * D + 16 * SEQ * SEQ), 8 << 20, count * 4 * SEQ * SEQ
        ),
        name="attn_forward",
    )(bounds, source, weights, weights, weights, cosine, sine, seg_col, seg_row, *deps)


def deal(core, whole, mine, theirs, columns):
    parts = whole.reshape(16, 2, D // 32, whole.shape[1])
    first, second = parts[:, 0], parts[:, 1]
    mine[:, :, columns] = jnp.where(core == 0, first, second).astype(BF16)
    theirs[:, :, columns] = jnp.where(core == 0, second, first).astype(BF16)


def attn_backward(at, grad_at, bounds, saved, ctx_grad, source, cosine, sine, seg_col, seg_row, deps=()):
    def body(bnd, q, k, v, o, do, lse, x, cos, sin, sc, sr, *rest):
        core = bnd[2 * NBLOCK]
        out, mine, theirs, qm, dm, dq, dk, dv, dl = rest[len(deps) :]
        low_lane = lax.broadcasted_iota(jnp.int32, (BLOCK, LANES), 1) < HEAD
        row = lax.broadcasted_iota(jnp.int32, (8, LANES), 0)
        lane = lax.broadcasted_iota(jnp.int32, (8, LANES), 1)
        pick = jnp.where(row == lane // HEAD, 1.0, 0.0).astype(F32)
        for p in range(GROUP // LANES):
            ln = slice(p * LANES, (p + 1) * LANES)

            @pl.loop(0, NBLOCK)
            def _(i):
                rows = pl.ds(pl.multiple_of(i * BLOCK, BLOCK), BLOCK)
                qm[p, i] = stacked(low_lane, q[rows, ln])
                dm[p, i] = stacked(low_lane, do[rows, ln])

            dl[p] = lax.dot_general(
                pick,
                do[:, ln].astype(F32) * o[:, ln].astype(F32),
                (((1,), (1,)), ((), ())),
                preferred_element_type=F32,
                precision=lax.Precision.HIGHEST,
            )
        dk[...] = jnp.zeros_like(dk)
        dv[...] = jnp.zeros_like(dv)

        def block(i, _):
            rows = pl.ds(pl.multiple_of(i * BLOCK, BLOCK), BLOCK)
            own = jnp.concatenate([sr[:, rows], sr[:, rows]], axis=1)

            def work(cols):
                seen = sc[cols, :] == own
                for p in range(GROUP // LANES):
                    ln = slice(p * LANES, (p + 1) * LANES)
                    keys, values, qq, dd = k[cols, ln], v[cols, ln], qm[p, i], dm[p, i]
                    logs = jnp.concatenate(
                        [lse[0, 2 * p : 2 * p + 1, rows], lse[0, 2 * p + 1 : 2 * p + 2, rows]], axis=1
                    )
                    deltas = jnp.concatenate([dl[p, 0:1, rows], dl[p, 1:2, rows]], axis=1)
                    s = dot_nt(keys, qq) * LOG2E - logs
                    probs = jnp.exp2(jnp.where(seen, s, MASKED))
                    g = (probs * (dot_nt(values, dd) - deltas)).astype(BF16)
                    dv[cols, ln] += dot_nn(probs.astype(BF16), dd)
                    dk[cols, ln] += dot_nn(g, qq)
                    both = dot_tn(g, keys)
                    dq[rows, ln] = jnp.where(low_lane, both[:BLOCK], both[BLOCK:])

            windows(bnd, i, work)
            return 0

        lax.fori_loop(0, NBLOCK, block, 0)

        @pl.loop(0, NBLOCK)
        def _(r):
            rows = pl.ds(pl.multiple_of(r * BLOCK, BLOCK), BLOCK)
            cr, sn = cos[rows, :], -sin[rows, :]
            for p in range(GROUP // LANES):
                ln = slice(p * LANES, (p + 1) * LANES)
                out[0, rows, ln] = turn(dq[rows, ln] * (HEAD**-0.5), cr, sn).astype(BF16)
                out[1, rows, ln] = turn(dk[rows, ln], cr, sn).astype(BF16)
                out[2, rows, ln] = dv[rows, ln].astype(BF16)

        for i in range(3):
            deal(core, dot_tn(x[...], out[i]), mine, theirs, slice(i * GROUP, (i + 1) * GROUP))

    full = lambda shape: pl.BlockSpec(shape, lambda p, b: (0,) * len(shape))
    part = pl.BlockSpec((SEQ, GROUP), lambda p, b: (0, at))
    low2 = pltpu.VMEM((GROUP // LANES, NBLOCK, 2 * BLOCK, LANES), BF16)
    wide = pltpu.VMEM((SEQ, GROUP), F32)
    dealt = (16, D // 32, 3 * GROUP)
    return pl.pallas_call(
        body,
        grid_spec=pltpu.PrefetchScalarGridSpec(
            num_scalar_prefetch=1,
            grid=(1,),
            in_specs=[part] * 4
            + [
                pl.BlockSpec((SEQ, GROUP), lambda p, b: (0, grad_at)),
                pl.BlockSpec((1, 8, SEQ), lambda p, b: (at, 0, 0)),
                full((SEQ, D)),
                full((SEQ, LANES)),
                full((SEQ, LANES)),
                full((SEQ, 1)),
                full((1, SEQ)),
            ]
            + [AFTER] * len(deps),
            out_specs=[full((3, SEQ, GROUP)), full(dealt), full(dealt)],
            scratch_shapes=[
                low2,
                low2,
                wide,
                wide,
                wide,
                pltpu.VMEM((GROUP // LANES, 8, SEQ), F32),
            ],
        ),
        out_shape=[
            jax.ShapeDtypeStruct((3, SEQ, GROUP), BF16),
            jax.ShapeDtypeStruct(dealt, BF16),
            jax.ShapeDtypeStruct(dealt, BF16),
        ],
        compiler_params=params(60),
        cost_estimate=cost(GROUP * (40 * SEQ * SEQ + 6 * SEQ * D), 10 << 20, 4 * SEQ * SEQ),
        name="attn_backward",
    )(bounds, *saved[:4], ctx_grad, saved[4], source, cosine, sine, seg_col, seg_row, *deps)


def join_rows(index, here, there, count, columns=512):
    lead, _, wide = here.shape
    rows = D // 16
    each = 16 // count
    steps = wide // columns

    def body(idx, a, b, *outs):
        for s in range(16):
            at = pl.ds(pl.multiple_of(idx[s] * rows, 16), rows)
            total = a[0, at, :].astype(F32) + b[0, at, :].astype(F32)
            outs[s // each][s % each] = total.astype(BF16)

    whole = pl.BlockSpec((1, D, columns), lambda l, n, i: (l, 0, n))
    part = pl.BlockSpec((each, rows, columns), lambda l, n, i: (0, 0, l * steps + n))
    return pl.pallas_call(
        body,
        grid_spec=pltpu.PrefetchScalarGridSpec(
            num_scalar_prefetch=1,
            grid=(lead, steps),
            in_specs=[whole, whole],
            out_specs=[part] * count,
        ),
        out_shape=[jax.ShapeDtypeStruct((each, rows, lead * wide), BF16)] * count,
        compiler_params=params(60, ("arbitrary", "arbitrary")),
        cost_estimate=cost(D * wide * lead, 6 * D * wide * lead),
        name="join_rows",
    )(index, here, there)


def out_grad(core, ctx, right, norms):
    def body(c, *refs):
        parts, (b, nrm, mine, theirs) = refs[:GROUPS], refs[GROUPS:]
        whole = jnp.concatenate([dot_tn(p[...], b[...]) for p in parts], axis=0)
        deal(c[0], whole, mine, theirs, slice(0, D))
        flipped = jnp.concatenate([nrm[...], jnp.zeros((LANES - 8, D), F32)], axis=0).T
        filled = jnp.concatenate([flipped, jnp.zeros((D, LANES), F32)], axis=1)
        deal(c[0], filled, mine, theirs, slice(D, TAIL))

    full = lambda shape: pl.BlockSpec(shape, lambda p, b: (0,) * len(shape))
    dealt = (16, D // 32, TAIL)
    return pl.pallas_call(
        body,
        grid_spec=pltpu.PrefetchScalarGridSpec(
            num_scalar_prefetch=1,
            grid=(1,),
            in_specs=[full((SEQ, GROUP))] * GROUPS + [full((SEQ, D)), full((8, D))],
            out_specs=[full(dealt), full(dealt)],
        ),
        out_shape=[jax.ShapeDtypeStruct(dealt, BF16)] * 2,
        compiler_params=params(60),
        cost_estimate=cost(2 * SEQ * D * D, 8 << 20),
        name="out_grad",
    )(core[None], *ctx, right, norms)


def join_dealt(index, mine, there, deps=()):
    widths = [m.shape[2] for m in mine]
    wide, rows, count = sum(widths), D // 32, len(mine)

    def body(idx, *refs):
        ours, others, keep, send = refs[:count], refs[count : 2 * count], refs[-2], refs[-1]
        for s in range(16):
            start = 0
            for a, b, n in zip(ours, others, widths):
                total = a[idx[s]].astype(F32) + b[idx[s]].astype(F32)
                (keep, send)[s // 8][s % 8, :, start : start + n] = total.astype(BF16)
                start += n

    full = lambda shape: pl.BlockSpec(shape, lambda p, b: (0,) * len(shape))
    half = (8, rows, wide)
    return pl.pallas_call(
        body,
        grid_spec=pltpu.PrefetchScalarGridSpec(
            num_scalar_prefetch=1,
            grid=(1,),
            in_specs=[full((16, rows, n)) for n in widths] * 2 + [AFTER] * len(deps),
            out_specs=[full(half), full(half)],
        ),
        out_shape=[jax.ShapeDtypeStruct(half, BF16)] * 2,
        compiler_params=params(24),
        cost_estimate=cost(D * wide // 2, 3 * D * wide),
        name="join_dealt",
    )(index, *mine, *there, *deps)


def fold(keep, there, count, dtype=BF16, deps=()):
    blocks, rows, wide = keep.shape
    each = blocks // count

    def body(a, b, *rest):
        for n, out in enumerate(rest[len(deps) :]):
            at = slice(n * each, (n + 1) * each)
            out[...] = (a[at].astype(F32) + b[at].astype(F32)).astype(dtype)

    steps = 2 if blocks * rows * wide > 1 << 19 else 1
    columns = wide // steps
    part = pl.BlockSpec((blocks, rows, columns), lambda i: (0, 0, i))
    return pl.pallas_call(
        body,
        grid=(steps,),
        in_specs=[part, part] + [AFTER] * len(deps),
        out_specs=[pl.BlockSpec((each, rows, columns), lambda i: (0, 0, i))] * count,
        out_shape=[jax.ShapeDtypeStruct((each, rows, wide), dtype)] * count,
        compiler_params=params(16),
        cost_estimate=cost(blocks * rows * wide, 6 * blocks * rows * wide),
        name="fold",
    )(keep, there, *deps)


def fold_pair(keep, there, deps=()):
    rows = keep[0].shape[1]
    widths = [k.shape[2] for k in keep]
    wide = sum(widths)

    def body(a, b, c, d, *rest):
        start = 0
        for p, q, n in ((a, c, widths[0]), (b, d, widths[1])):
            for at, out in enumerate(rest[len(deps) :]):
                four = slice(4 * at, 4 * at + 4)
                total = p[four].astype(F32) + q[four].astype(F32)
                out[:, :, start : start + n] = total.astype(BF16)
            start += n

    vmem = pl.BlockSpec(memory_space=pltpu.VMEM)
    return pl.pallas_call(
        body,
        in_specs=[vmem] * 4 + [AFTER] * len(deps),
        out_specs=[vmem] * 2,
        out_shape=[jax.ShapeDtypeStruct((4, rows, wide), BF16)] * 2,
        compiler_params=params(16, None),
        cost_estimate=cost(8 * rows * wide, 48 * rows * wide),
        name="fold_pair",
    )(*keep, *there, *deps)


def finish(parts):
    rows = D // 32

    def body(a, b, c, d, qkv, out, gain, shift):
        total = a[0].astype(F32) + b[0].astype(F32) + c[0].astype(F32) + d[0].astype(F32)
        places = [0, 3 * GROUP, 6 * GROUP + TAIL]
        for i in range(3):
            at = [slice(p + i * GROUP, p + (i + 1) * GROUP) for p in places]
            qkv[:, i, :] = jnp.concatenate([total[:, p] for p in at], axis=1)
        start = 6 * GROUP
        out[...] = total[:, start : start + D]
        gain[...] = total[:, start + D : start + D + 2]
        shift[...] = total[:, start + D + 2 : start + D + 4]

    vmem = pl.BlockSpec(memory_space=pltpu.VMEM)
    shapes = [(rows, 3, D), (rows, D), (rows, 2), (rows, 2)]
    return pl.pallas_call(
        body,
        in_specs=[vmem] * 4,
        out_specs=[vmem] * 4,
        out_shape=[jax.ShapeDtypeStruct(shape, F32) for shape in shapes],
        compiler_params=params(16, None),
        cost_estimate=cost(1 << 18, 1 << 20),
        name="finish",
    )(*parts)


def input_back(core, hidden_grad, projected, weights, deps=()):
    half = SEQ // 2 // BLOCK

    def body(c, hid, a, b, d, w, *rest):
        mine, leave = rest[-2:]
        total = hid[...]
        for g, ref in enumerate((a, b, d)):
            for i in range(3):
                at = i * D + g * GROUP
                total = total + dot_nt(ref[i], w[:, at : at + GROUP])
        own = pl.program_id(0) // half == c[0]

        @pl.when(own)
        def _():
            mine[...] = total

        @pl.when(jnp.logical_not(own))
        def _():
            leave[...] = total

    row = pl.BlockSpec((BLOCK, D), lambda r, c: (r, 0))
    shape = jax.ShapeDtypeStruct((SEQ // 2, D), F32)
    return pl.pallas_call(
        body,
        grid_spec=pltpu.PrefetchScalarGridSpec(
            num_scalar_prefetch=1,
            grid=(SEQ // BLOCK,),
            in_specs=[row]
            + [pl.BlockSpec((3, BLOCK, GROUP), lambda r, c: (0, r, 0))] * 3
            + [pl.BlockSpec((D, 3 * D), lambda r, c: (0, 0))]
            + [AFTER] * len(deps),
            out_specs=[
                pl.BlockSpec((BLOCK, D), lambda r, c: (jnp.clip(r - half * c[0], 0, half - 1), 0)),
                pl.BlockSpec(
                    (BLOCK, D), lambda r, c: (jnp.clip(r - half * (1 - c[0]), 0, half - 1), 0)
                ),
            ],
        ),
        out_shape=[shape, shape],
        compiler_params=params(60),
        cost_estimate=cost(6 * SEQ * D * D, 16 << 20),
        name="input_back",
    )(core[None], hidden_grad, *projected, weights, *deps)


def middle(index, source, ctx, cot, pieces):
    def norm(v):
        center = v - jnp.mean(v, axis=1, keepdims=True)
        scale = lax.rsqrt(jnp.mean(center * center, axis=1, keepdims=True) + EPSILON)
        return center * scale, scale

    def norm_back(u, hat, scale, gain):
        g = u * gain
        return scale * (
            g - jnp.mean(g, axis=1, keepdims=True) - hat * jnp.mean(g * hat, axis=1, keepdims=True)
        )

    def body(idx, x, ctx0, ctx1, ctx2, cot, *refs):
        pieces, refs = refs[:8], refs[8:]
        out, out_leave, gu_own, gu_other, down_own, down_other, hid_out, att_out, ctxg_out, sums = refs[:10]
        (
            w, wo, tail, nrm, factors, acts, low_t, mlp_t, mlp_s, back_s, hat_s, scale_s, pair_s, sem,
        ) = refs[10:]
        step = pl.program_id(0)
        core = idx[32]
        few = D // 32

        def loads(kind, which):
            copies = []
            for rest in (2 * which, 2 * which + 1):
                for s in range(8):
                    block = idx[(0 if kind == "gate" else 33) + rest * 8 + s]
                    at = pl.ds(pl.multiple_of(block * 48, 16), 48)
                    n = rest * 8 + s
                    gate, down = pieces[rest], pieces[4 + rest]
                    if kind == "gate":
                        copies.append(
                            pltpu.make_async_copy(
                                gate.at[s], w.at[which, at, pl.ds(0, 2 * HIDDEN)], sem.at[n]
                            )
                        )
                    elif kind == "down":
                        copies.append(
                            pltpu.make_async_copy(
                                down.at[s, :, pl.ds(0, HIDDEN)],
                                w.at[which, at, pl.ds(2 * HIDDEN, HIDDEN)],
                                sem.at[32 + n],
                            )
                        )
                    else:
                        owner = core if which == 0 else 1 - core
                        for part in range(2):
                            copies.append(
                                pltpu.make_async_copy(
                                    down.at[s, pl.ds(part * few, few), pl.ds(HIDDEN, REST)],
                                    tail.at[part, block * 2 + owner],
                                    sem.at[64 + n + 32 * part],
                                )
                            )
            return copies

        def arrive(kind, which):
            @pl.when(step == 0)
            def _():
                for cp in loads(kind, which):
                    cp.wait()

        @pl.when(step == 0)
        def _():
            for which in range(2):
                for cp in loads("tail", which):
                    cp.start()
            for which in range(2):
                for kind in ("gate", "down"):
                    for cp in loads(kind, which):
                        cp.start()

        arrive("tail", 0)
        arrive("tail", 1)

        @pl.when(step == 0)
        def _():
            joined = jnp.concatenate(
                [tail[0].reshape(D, REST), tail[1].reshape(D, REST)], axis=1
            )
            wo[...] = joined[:, :D]
            nrm[...] = joined[:, D : D + LANES].astype(F32).T[:8]
            sums[...] = jnp.zeros_like(sums)

        gain1, gain2, shift1, shift2 = (nrm[i : i + 1, :] for i in range(4))

        @pl.when(step < STEPS)
        def _():
            rows = pl.ds(pl.multiple_of(step * ROWS, ROWS), ROWS)
            context = jnp.concatenate([ctx0[...], ctx1[...], ctx2[...]], axis=1)
            hidden_in = x[...].astype(F32) + dot_nn(context, wo[...])
            hat1, scale1 = norm(hidden_in)
            hat_s[rows, :] = hat1
            scale_s[rows, :] = scale1
            normed = hat1 * gain1 + shift1
            low = normed.astype(BF16)
            low_t[:, rows] = low.T
            total = normed
            for half in range(2):
                arrive("gate", half)
                arrive("down", half)
                for n in range(HIDDEN // CHUNK):
                    g_at, u_at, d_at = (pl.ds(p * HIDDEN + n * CHUNK, CHUNK) for p in range(3))
                    gate = dot_nn(low, w[half, :, g_at])
                    up = dot_nn(low, w[half, :, u_at])
                    s = jax.nn.sigmoid(gate)
                    silu = gate * s
                    act = (silu * up).astype(BF16)
                    factors[half, rows, g_at] = (up * (s * (1.0 + gate * (1.0 - s)))).astype(BF16)
                    factors[half, rows, u_at] = silu.astype(BF16)
                    acts[half, rows, g_at] = act
                    total = total + dot_nt(act, w[half, :, d_at])
            hat2, scale2 = norm(total)
            result = (hat2 * gain2 + shift2).astype(BF16)
            own = step // (STEPS // 2) == core

            @pl.when(own)
            def _():
                out[...] = result

            @pl.when(jnp.logical_not(own))
            def _():
                out_leave[...] = result

            u2 = cot[...].astype(F32)
            resid = norm_back(u2, hat2, scale2, gain2)
            mlp = resid.astype(BF16)
            mlp_s[rows, :] = mlp
            mlp_t[:, rows] = mlp.T
            back_s[rows, :] = resid
            sums[1:2, :] += jnp.sum(u2 * hat2, axis=0, keepdims=True)
            sums[3:4, :] += jnp.sum(u2, axis=0, keepdims=True)

        @pl.when(jnp.logical_and(step >= STEPS, step < STEPS + PIECES))
        def _():
            at = step - STEPS
            half = 1 - at // (PIECES // 2)
            n = at % (PIECES // 2)
            g_at, u_at, d_at = (
                pl.ds(pl.multiple_of(p * HIDDEN + n * PIECE, PIECE), PIECE) for p in range(3)
            )

            for r in range(STEPS):
                rows = pl.ds(r * ROWS, ROWS)
                grad = dot_nn(mlp_s[rows, :], w[half, :, d_at])
                gate_grad = (grad * factors[half, rows, g_at].astype(F32)).astype(BF16)
                up_grad = (grad * factors[half, rows, u_at].astype(F32)).astype(BF16)
                pair_s[0, rows, :] = gate_grad
                pair_s[1, rows, :] = up_grad
                back_s[rows, :] += dot_nt(gate_grad, w[half, :, g_at]) + dot_nt(
                    up_grad, w[half, :, u_at]
                )

            def store(gu, down):
                for i in range(2):
                    gu[i] = dot_nn(low_t[...], pair_s[i]).astype(BF16)
                down[0] = dot_nn(mlp_t[...], acts[half, :, g_at]).astype(BF16)

            @pl.when(half == 1)
            def _():
                store(gu_other, down_other)

            @pl.when(half == 0)
            def _():
                store(gu_own, down_own)

        @pl.when(step >= STEPS + PIECES)
        def _():
            r = step - STEPS - PIECES
            rows = pl.ds(pl.multiple_of(r * ROWS, ROWS), ROWS)
            back, hat1 = back_s[rows, :], hat_s[rows, :]
            hidden_grad = norm_back(back, hat1, scale_s[rows, :], gain1)
            hid_out[...] = hidden_grad
            att = hidden_grad.astype(BF16)
            att_out[...] = att
            ctxg_out[...] = dot_nt(att, wo[...]).astype(BF16)
            sums[0:1, :] += jnp.sum(back * hat1, axis=0, keepdims=True)
            sums[2:3, :] += jnp.sum(back, axis=0, keepdims=True)

    last = STEPS - 1
    row = lambda n: pl.BlockSpec((ROWS, n), lambda t, i: (jnp.minimum(t, last), 0))
    ending = pl.BlockSpec((ROWS, D), lambda t, i: (jnp.clip(t - STEPS - PIECES, 0, last), 0))
    half = STEPS // 2
    side = lambda t, mine: (jnp.clip(jnp.minimum(t, last) - half * mine, 0, half - 1), 0)
    mine = pl.BlockSpec((ROWS, D), lambda t, i: side(t, i[32]))
    leave = pl.BlockSpec((ROWS, D), lambda t, i: side(t, 1 - i[32]))
    each = PIECES // 2
    own = lambda lead: pl.BlockSpec(
        (lead, D, PIECE), lambda t, i: (0, 0, jnp.clip(t - STEPS - each, 0, each - 1))
    )
    theirs = lambda lead: pl.BlockSpec(
        (lead, D, PIECE), lambda t, i: (0, 0, jnp.clip(t - STEPS, 0, each - 1))
    )
    act = lambda n, t=BF16: jax.ShapeDtypeStruct((n, D), t)
    grads = lambda lead: jax.ShapeDtypeStruct((lead, D, HIDDEN), BF16)
    return pl.pallas_call(
        body,
        grid_spec=pltpu.PrefetchScalarGridSpec(
            num_scalar_prefetch=1,
            grid=(2 * STEPS + PIECES,),
            in_specs=[row(D)] + [row(GROUP)] * GROUPS + [row(D)] + [ANY] * 8,
            out_specs=[mine, leave, own(2), theirs(2), own(1), theirs(1)]
            + [ending] * 3
            + [pl.BlockSpec((8, D), lambda t, i: (0, 0))],
            scratch_shapes=[
                pltpu.VMEM((2, D, WIDE), BF16),
                pltpu.VMEM((D, D), BF16),
                pltpu.VMEM((2, 32, D // 32, REST), BF16),
                pltpu.VMEM((8, D), F32),
                pltpu.VMEM((2, SEQ, 2 * HIDDEN), BF16),
                pltpu.VMEM((2, SEQ, HIDDEN), BF16),
                pltpu.VMEM((D, SEQ), BF16),
                pltpu.VMEM((D, SEQ), BF16),
                pltpu.VMEM((SEQ, D), BF16),
                pltpu.VMEM((SEQ, D), F32),
                pltpu.VMEM((SEQ, D), F32),
                pltpu.VMEM((SEQ, 1), F32),
                pltpu.VMEM((2, SEQ, PIECE), BF16),
                pltpu.SemaphoreType.DMA((128,)),
            ],
        ),
        out_shape=[
            act(SEQ // 2),
            act(SEQ // 2),
            grads(2),
            grads(2),
            grads(1),
            grads(1),
            act(SEQ, F32),
            act(SEQ),
            act(SEQ),
            jax.ShapeDtypeStruct((8, D), F32),
        ],
        compiler_params=params(62),
        cost_estimate=cost(18 * SEQ * D * 2 * HIDDEN + 4 * SEQ * D * D, 40 << 20, 4 * SEQ * HIDDEN),
        name="middle",
    )(index, source, *ctx, cot, *pieces)


def rotary_lanes(segment_row):
    labels = jnp.arange(NDOC + 1, dtype=jnp.int32)
    before = jnp.sum((segment_row[None, :] < labels[:, None]).astype(jnp.int32), axis=1)
    member = segment_row[:, None] == labels[None, :]
    first = jnp.sum(jnp.where(member, before[None, :], 0), axis=1)
    position = (jnp.arange(SEQ, dtype=jnp.int32) - first).astype(F32)
    lane = jnp.arange(LANES) % (HEAD // 2)
    frequency = jnp.power(F32(1000.0), -2.0 * lane.astype(F32) / HEAD)
    angle = position[:, None] * frequency[None, :]
    sign = jnp.where(jnp.arange(LANES) % HEAD < HEAD // 2, -1.0, 1.0)
    ends = jnp.concatenate([before[1:], jnp.full((1,), SEQ, jnp.int32)])
    heads = segment_row[::BLOCK]
    tails = segment_row[BLOCK - 1 :: BLOCK]
    low = jnp.sum(jnp.where(heads[:, None] == labels[None, :], before[None, :], 0), axis=1)
    high = jnp.sum(jnp.where(tails[:, None] == labels[None, :], ends[None, :], 0), axis=1)
    bounds = jnp.concatenate([low // KEYS, (high + KEYS - 1) // KEYS]).astype(jnp.int32)
    return jnp.cos(angle), jnp.sin(angle) * sign[None, :], bounds


def sequence_device(
    tokens, segments, qkv_weight, out_weight, norm_gain, norm_shift, gate_up, down_weight, cotangent
):
    core = lax.axis_index("tensor")
    def ordered(mine, theirs):
        return jnp.where(
            core == 0, jnp.stack([mine, theirs], axis=0), jnp.stack([theirs, mine], axis=0)
        )

    pick = lambda a, i: lax.dynamic_index_in_dim(a, i, 0, keepdims=False)
    source = pick(tokens, core)
    segment_row = pick(segments, core)

    attn_block = qkv_weight.reshape(-1, 3 * D)
    gate_block = gate_up.reshape(-1, 2 * HIDDEN)
    tail_block = jnp.concatenate(
        [out_weight, norm_gain, norm_shift, jnp.zeros((D // 32, TAIL - D - 4), BF16)], axis=1
    )
    down_block = jnp.concatenate(
        [down_weight, jnp.concatenate([tail_block[:, :REST], tail_block[:, REST:]], axis=0)], axis=1
    )
    from_here, from_there = slot_blocks(-1, core), slot_blocks(-1, 1 - core)
    there_blocks = slot_blocks(1, core).reshape(2, 2, 4)
    to_here = there_blocks.transpose(1, 0, 2).reshape(16)
    deep_first = there_blocks.transpose(2, 1, 0).reshape(16)

    cot = ordered(pick(cotangent, core), core_swap(pick(cotangent, 1 - core))).reshape(SEQ, D)
    cosine, sine, bounds = rotary_lanes(segment_row)
    bounds = jnp.concatenate([bounds, core[None]]).astype(jnp.int32)
    tables = (cosine, sine, segment_row[:, None], segment_row[None, :])

    ahead = lambda parts: [part[None] for part in parts]
    gate_parts = depth_ring(gate_block)
    attn_four = pile(ahead(depth_parts(attn_block)), deps=(gate_parts[1],))
    attn_eight = pile(
        [attn_four, first_swap(attn_four)], deps=(gate_parts[2], source, cot, *tables)
    )
    attn_last = second_swap(attn_eight)
    index = jnp.concatenate([from_here * 2 + core, from_there * 2 + 1 - core]).astype(jnp.int32)
    weights = assemble(
        (attn_eight, attn_last),
        (core_swap(attn_eight), core_swap(attn_last)),
        index,
        deps=(gate_parts[3],),
    ).reshape(D, 3 * D)
    gate_four = pile(ahead(gate_parts))
    down_pair = pile([down_block[None], first_swap(down_block)[None]], deps=(gate_four,))
    saved0 = attn_forward(0, 1, bounds, source, weights, *tables, deps=(gate_four, down_pair))
    gate_eight = pile([gate_four, first_swap(gate_four)], deps=(saved0[4],))
    gate_last = second_swap(gate_eight)
    saved1 = attn_forward(1, 1, bounds, source, weights, *tables, deps=(gate_eight,))
    down_eight = pile(depth_parts(down_pair), deps=(saved1[4],))
    saved2 = attn_forward(2, 1, bounds, source, weights, *tables, deps=(down_eight,))
    down_last, late_logs = lax.optimization_barrier((second_swap(down_eight), saved2[4]))
    saved2 = (*saved2[:4], late_logs)
    pieces = (gate_eight, gate_last, core_swap(gate_eight), core_swap(gate_last))
    pieces += (down_eight, down_last, core_swap(down_eight), core_swap(down_last))

    turned = lambda slots: slots.reshape(2, 2, 4).transpose(0, 2, 1).reshape(16)
    index = jnp.concatenate(
        [from_here, from_there, core[None], turned(from_here), turned(from_there)]
    ).astype(jnp.int32)
    ctx = (saved0[3], saved1[3], saved2[3])
    (out, out_leave, gu_here, gu_there, down_here, down_there, hidden_grad, att_grad, ctx_grad, sums) = (
        middle(index, source, ctx, cot, pieces)
    )

    down_there, gu_there = core_swap(down_there), core_swap(gu_there)
    tail_mine, tail_theirs = out_grad(core, ctx, att_grad, sums)
    down_parts = join_rows(deep_first, down_here, down_there, 4)
    gu_keep, gu_send = join_rows(to_here, gu_here, gu_there, 2)
    gu_first = first_swap(gu_send)
    passing = depth_shift(down_parts[3], 1)

    common = (source,) + tables
    back0 = attn_backward(0, 0, bounds, saved0, ctx_grad, *common, deps=(gu_send, down_parts[0]))
    (passing,) = fold(passing, down_parts[2], 1, deps=(back0[1],))
    back1 = attn_backward(0, 1, bounds, saved1, ctx_grad, *common, deps=(passing,))
    passing = depth_shift(passing, 1)
    (passing,) = fold(passing, down_parts[1], 1, deps=(back1[1],))
    gu_keep, gu_send = fold(gu_keep, gu_first, 2, deps=(back1[1],))
    gu_second = second_swap(gu_send)
    early_keep, early_send = join_dealt(
        to_here,
        (back0[1], back1[1], tail_mine),
        (core_swap(back0[2]), core_swap(back1[2]), core_swap(tail_theirs)),
    )
    early_first = first_swap(early_send)
    back2 = attn_backward(0, 2, bounds, saved2, ctx_grad, *common, deps=(gu_send, early_send, passing))

    deep = lambda parts: [parts[0]] + [depth_shift(parts[k], k) for k in (1, 2, 3)]
    passing = depth_shift(passing, 1)
    gu_parts = fold(gu_keep, gu_second, 4, deps=(back2[1],))
    (gu_total,) = fold(depth_shift(gu_parts[3], 1), gu_parts[2], 1)
    down_keep, down_send = fold(passing, down_parts[0], 2, deps=(gu_parts[0],))
    down_keep, down_send = fold(down_keep, first_swap(down_send), 2)
    down_second = second_swap(down_send)
    late_keep, late_send = join_dealt(
        to_here, (back2[1],), (core_swap(back2[2]),), deps=(down_keep, early_first)
    )
    grad, grad_leave = input_back(
        core, hidden_grad, (back0[0], back1[0], back2[0]), weights, deps=(late_send, gu_total)
    )
    (gu_total,) = fold(depth_shift(gu_total, 1), gu_parts[1], 1, deps=(grad,))
    attn_keep, attn_send = fold_pair(
        (early_keep, late_keep), (early_first, first_swap(late_send)), deps=(gu_total,)
    )
    attn_second = second_swap(attn_send)
    outputs = place(core, out, core_swap(out_leave)), place(core, grad, core_swap(grad_leave))
    (gu_total,) = fold(depth_shift(gu_total, 1), gu_parts[0], 1, F32, deps=(attn_send,))
    attn_parts = deep(fold(attn_keep, attn_second, 4, deps=(gu_total, *outputs)))
    down_total = (down_keep.astype(F32) + down_second.astype(F32))[0]
    gu_total = gu_total[0]
    qkv_total, out_total, gain_total, shift_total = finish(attn_parts)

    return (
        *outputs,
        qkv_total,
        out_total,
        gain_total,
        shift_total,
        gu_total.reshape(-1, 2, HIDDEN),
        down_total,
    )


def solution(mesh):
    in_specs = (
        P("dp", None, None),
        P("dp", None),
        P(("dp", "tensor"), None, None),
        P(("dp", "tensor"), None),
        P(("dp", "tensor"), None),
        P(("dp", "tensor"), None),
        P("dp", None, "tensor"),
        P("dp", "tensor"),
        P("dp", "tensor", None),
    )
    out_specs = (
        P("dp", "tensor", None),
        P("dp", "tensor", None),
        P(("dp", "tensor"), None, None),
        P(("dp", "tensor"), None),
        P(("dp", "tensor"), None),
        P(("dp", "tensor"), None),
        P("dp", None, "tensor"),
        P("dp", "tensor"),
    )
    sizes = dict(mesh.shape)

    def per_device(tokens, *others):
        if sizes["dp"] == 16 and sizes["tensor"] == 2 and tokens.shape[0] == 2:
            return sequence_device(tokens, *others)
        return general_device(tokens, *others)

    return jax.shard_map(
        per_device, mesh=mesh, in_specs=in_specs, out_specs=out_specs, check_vma=False
    )
```

```python
import jax
import jax.numpy as jnp
from jax import lax
from jax.experimental import pallas as pl
from jax.experimental.pallas import tpu as pltpu
from jax.sharding import PartitionSpec as P

D = 768
HEADS = 12
HEAD = 64
SEQ = 1024
NDOC = 8


EPSILON = 1e-05
MASKED = -1e30


def for_sending(value):
    return jax.tree.map(lambda a: a.astype(jnp.bfloat16) if a.dtype == jnp.float32 else a, value)


def rotary_tables(segment_row):
    labels = jnp.arange(NDOC + 1, dtype=jnp.int32)
    member = (segment_row[:, None] == labels[None, :]).astype(jnp.int32)
    counts = jnp.sum(member, axis=0)
    starts = jnp.concatenate([jnp.zeros((1,), jnp.int32), jnp.cumsum(counts)[:-1]])
    offset = jnp.sum(member * starts[None, :], axis=1)
    position = (jnp.arange(SEQ, dtype=jnp.int32) - offset).astype(jnp.float32)
    exponent = -2.0 * jnp.arange(HEAD // 2).astype(jnp.float32) / HEAD
    frequency = jnp.power(jnp.float32(1000.0), exponent)
    angle = position[:, None] * frequency[None, :]
    return (jnp.cos(angle)[:, None, :], jnp.sin(angle)[:, None, :])


def rotate(vector, cosine, sine):
    half = vector.shape[-1] // 2
    first_half = vector[..., :half]
    second_half = vector[..., half:]
    return jnp.concatenate(
        [first_half * cosine - second_half * sine, second_half * cosine + first_half * sine],
        axis=-1,
    )


def unrotate(gradient, cosine, sine):

    def turned(vector):
        return rotate(vector, cosine, sine)

    _, pullback = jax.vjp(turned, gradient)
    return pullback(gradient)[0]


def layer_norm(vector, gain, shift):
    center = vector - jnp.mean(vector, axis=-1, keepdims=True)
    variance = jnp.mean(center * center, axis=-1, keepdims=True)
    return center * lax.rsqrt(variance + EPSILON) * gain + shift


def swiglu_piece(gate, upper):
    return jax.nn.silu(gate) * upper


def accumulate(total, term):
    if total is None:
        return term
    return tuple((left + right for left, right in zip(total, term)))


def general_device(
    tokens, segments, qkv_weight, out_weight, norm_gain, norm_shift, gate_up, down_weight, cotangent
):
    tensor_size = lax.axis_size("tensor")
    own_rows = SEQ // tensor_size
    row_start = lax.axis_index("tensor") * own_rows
    score_scale = HEAD ** (-0.5)
    qkv_full, out_full, gain_full, shift_full = (
        lax.all_gather(qkv_weight, ("dp", "tensor"), axis=0, tiled=True),
        lax.all_gather(out_weight, ("dp", "tensor"), axis=0, tiled=True),
        lax.all_gather(norm_gain, ("dp", "tensor"), axis=0, tiled=True),
        lax.all_gather(norm_shift, ("dp", "tensor"), axis=0, tiled=True),
    )
    gains = gain_full.astype(jnp.float32)
    shifts = shift_full.astype(jnp.float32)
    gate_up_full, down_full = (
        lax.all_gather(gate_up, "dp", axis=0, tiled=True),
        lax.all_gather(down_weight, "dp", axis=0, tiled=True),
    )
    batches = tokens.shape[0]
    outputs = []
    input_grads = []
    attn_total = None
    mlp_total = None
    for batch_index in range(batches):
        source = tokens[batch_index]
        own_source = lax.dynamic_slice_in_dim(source, row_start, own_rows, 0)
        segment_row = segments[batch_index]
        cosine, sine = rotary_tables(segment_row)
        own_cos = lax.dynamic_slice_in_dim(cosine, row_start, own_rows, 0)
        own_sin = lax.dynamic_slice_in_dim(sine, row_start, own_rows, 0)
        query_proj = jnp.einsum(
            "sd,de->se", own_source, qkv_full[:, 0], preferred_element_type=jnp.float32
        )
        pair_proj = jnp.einsum(
            "sd,dke->ske", source, qkv_full[:, 1:], preferred_element_type=jnp.float32
        )
        keys = rotate(pair_proj[:, 0].reshape(SEQ, HEADS, HEAD), cosine, sine).astype(jnp.bfloat16)
        values = pair_proj[:, 1].reshape(SEQ, HEADS, HEAD).astype(jnp.bfloat16)
        queries = rotate(query_proj.reshape(own_rows, HEADS, HEAD), own_cos, own_sin).astype(
            jnp.bfloat16
        )
        own_segments = lax.dynamic_slice_in_dim(segment_row, row_start, own_rows, 0)
        allowed = (own_segments[:, None] == segment_row[None, :])[None]
        raw_scores = (
            jnp.einsum("qhe,khe->hqk", queries, keys, preferred_element_type=jnp.float32)
            * score_scale
        )
        masked = jnp.where(allowed, raw_scores, MASKED)
        top_score = jnp.max(masked, axis=-1, keepdims=True)
        logsum = top_score + jnp.log(jnp.sum(jnp.exp(masked - top_score), axis=-1, keepdims=True))
        probs_low = jnp.exp(masked - logsum).astype(jnp.bfloat16)
        context = (
            jnp.einsum("hqk,khe->qhe", probs_low, values, preferred_element_type=jnp.float32)
            .reshape(own_rows, D)
            .astype(jnp.bfloat16)
        )
        attended = jnp.dot(context, out_full, preferred_element_type=jnp.float32)
        hidden_in = own_source.astype(jnp.float32) + attended
        normed = layer_norm(hidden_in, gains[:, 0], shifts[:, 0])
        normed_all = lax.all_gather(normed.astype(jnp.bfloat16), "tensor", axis=0, tiled=True)
        gate_pair = jnp.einsum(
            "sd,dkf->skf", normed_all, gate_up_full, preferred_element_type=jnp.float32
        )
        swiglu = swiglu_piece(gate_pair[:, 0], gate_pair[:, 1]).astype(jnp.bfloat16)
        mlp_out = lax.psum_scatter(
            jnp.einsum("sf,df->sd", swiglu, down_full, preferred_element_type=jnp.float32).astype(
                jnp.bfloat16
            ),
            "tensor",
            scatter_dimension=0,
            tiled=True,
        ).astype(jnp.float32)
        resid = normed + mlp_out
        outputs.append(layer_norm(resid, gains[:, 1], shifts[:, 1]).astype(jnp.bfloat16))
        upstream = cotangent[batch_index].astype(jnp.float32)
        _, second_pull = jax.vjp(layer_norm, resid, gains[:, 1], shifts[:, 1])
        resid_grad, gain_two, shift_two = second_pull(upstream)
        mlp_grad = lax.all_gather(resid_grad.astype(jnp.bfloat16), "tensor", axis=0, tiled=True)
        swiglu_grad = jnp.einsum(
            "sd,df->sf", mlp_grad, down_full, preferred_element_type=jnp.float32
        )
        _, glu_pull = jax.vjp(swiglu_piece, gate_pair[:, 0], gate_pair[:, 1])
        gate_grad, upper_grad = glu_pull(swiglu_grad)
        pair_grad = jnp.stack([gate_grad, upper_grad], axis=1).astype(jnp.bfloat16)
        down_term = jnp.einsum("sd,sf->df", mlp_grad, swiglu, preferred_element_type=jnp.float32)
        gate_up_term = jnp.einsum(
            "sd,skf->dkf", normed_all, pair_grad, preferred_element_type=jnp.float32
        )
        normed_grad = resid_grad + lax.psum_scatter(
            jnp.einsum("skf,dkf->sd", pair_grad, gate_up_full, preferred_element_type=jnp.float32),
            "tensor",
            scatter_dimension=0,
            tiled=True,
        )
        _, first_pull = jax.vjp(layer_norm, hidden_in, gains[:, 0], shifts[:, 0])
        hidden_grad, gain_one, shift_one = first_pull(normed_grad)
        attended_grad = hidden_grad.astype(jnp.bfloat16)
        out_term = jnp.einsum(
            "sd,se->de", context, attended_grad, preferred_element_type=jnp.float32
        )
        context_grad = (
            jnp.einsum("se,de->sd", attended_grad, out_full, preferred_element_type=jnp.float32)
            .astype(jnp.bfloat16)
            .reshape(own_rows, HEADS, HEAD)
        )
        probs = jnp.exp(masked - logsum)
        weights_grad = jnp.einsum(
            "qhe,khe->hqk", context_grad, values, preferred_element_type=jnp.float32
        )
        row_delta = jnp.sum(probs * weights_grad, axis=-1, keepdims=True)
        score_grad = (probs * (weights_grad - row_delta)).astype(jnp.bfloat16)
        query_grad = (
            jnp.einsum("hqk,khe->qhe", score_grad, keys, preferred_element_type=jnp.float32)
            * score_scale
        )
        key_part = (
            jnp.einsum("hqk,qhe->khe", score_grad, queries, preferred_element_type=jnp.float32)
            * score_scale
        )
        value_part = jnp.einsum(
            "hqk,qhe->khe", probs_low, context_grad, preferred_element_type=jnp.float32
        )
        key_value = lax.psum_scatter(
            jnp.stack(
                [
                    key_part.reshape(lax.axis_size("tensor") * own_rows, D),
                    value_part.reshape(lax.axis_size("tensor") * own_rows, D),
                ],
                axis=1,
            ).astype(jnp.bfloat16),
            "tensor",
            scatter_dimension=0,
            tiled=True,
        ).astype(jnp.float32)
        query_back = unrotate(query_grad, own_cos, own_sin).reshape(own_rows, D)
        key_back = unrotate(
            key_value[:, 0].reshape(own_rows, HEADS, HEAD), own_cos, own_sin
        ).reshape(own_rows, D)
        proj_grad = jnp.stack([query_back, key_back, key_value[:, 1]], axis=1).astype(jnp.bfloat16)
        input_grads.append(
            hidden_grad
            + jnp.einsum("ske,dke->sd", proj_grad, qkv_full, preferred_element_type=jnp.float32)
        )
        qkv_term = jnp.einsum(
            "sd,ske->dke", own_source, proj_grad, preferred_element_type=jnp.float32
        )
        gain_term = jnp.stack([gain_one, gain_two], axis=1)
        shift_term = jnp.stack([shift_one, shift_two], axis=1)
        attn_terms = (qkv_term, out_term, gain_term, shift_term)
        mlp_terms = (gate_up_term, down_term)
        attn_total = accumulate(attn_total, attn_terms)
        mlp_total = accumulate(mlp_total, mlp_terms)
    attn_final = lax.psum_scatter(attn_total, ("dp", "tensor"), scatter_dimension=0, tiled=True)
    mlp_final = jax.tree.map(
        lambda part: part.astype(jnp.float32),
        lax.psum_scatter(for_sending(mlp_total), "dp", scatter_dimension=0, tiled=True),
    )
    return (
        jnp.stack(outputs, axis=0),
        jnp.stack(input_grads, axis=0),
        attn_final[0],
        attn_final[1],
        attn_final[2],
        attn_final[3],
        mlp_final[0],
        mlp_final[1],
    )


HIDDEN = 1536
WIDE = 3 * HIDDEN
REST = 512
TAIL = 2 * REST
GROUP = 4 * HEAD
GROUPS = D // GROUP
KEYS = 128
LANES = 2 * HEAD
BLOCK = 256
NBLOCK = SEQ // BLOCK
ROWS = 256
STEPS = SEQ // ROWS
CHUNK = 512
PIECE = 256
PIECES = 2 * HIDDEN // PIECE
LOG2E = 1.4426950408889634
F32 = jnp.float32
BF16 = jnp.bfloat16


def across(value, move):
    pairs = []
    for z in range(4):
        for y in range(2):
            for x in range(2):
                for c in range(2):
                    tz, ty, tx, tc = move(z, y, x, c)
                    pairs.append((((z * 2 + y) * 2 + x) * 2 + c, ((tz * 2 + ty) * 2 + tx) * 2 + tc))
    return lax.ppermute(value, ("dp", "tensor"), pairs)


def core_swap(value):
    return across(value, lambda z, y, x, c: (z, y, x, 1 - c))


def first_swap(value):
    return across(value, lambda z, y, x, c: (z, y, 1 - x, c) if c == 0 else (z, 1 - y, x, c))


def second_swap(value):
    return across(value, lambda z, y, x, c: (z, 1 - y, x, c) if c == 0 else (z, y, 1 - x, c))


def depth_shift(value, steps):
    return across(value, lambda z, y, x, c: ((z + steps) % 4, y, x, c))


def slot_blocks(sign, core):
    me = lax.axis_index("dp")
    z, y, x = me // 4, (me // 2) % 2, me % 2
    slot = jnp.arange(16, dtype=jnp.int32)
    second, first, depth = slot // 8, (slot // 4) % 2, slot % 4
    x_bit = jnp.where(core == 0, first, second)
    y_bit = jnp.where(core == 0, second, first)
    return (((z + sign * depth) % 4) * 4 + (y ^ y_bit) * 2 + (x ^ x_bit)).astype(jnp.int32)


def depth_parts(block):
    return [block] + [depth_shift(block, k) for k in (1, 2, 3)]


def depth_ring(block):
    parts = [block]
    for _ in range(3):
        parts.append(depth_shift(parts[-1], 1))
    return parts


def cost(flops, nbytes, trans=0):
    return pl.CostEstimate(flops=int(flops), bytes_accessed=int(nbytes), transcendentals=int(trans))


def params(vmem_mb, sem=("arbitrary",)):
    return pltpu.CompilerParams(dimension_semantics=sem, vmem_limit_bytes=vmem_mb << 20)


ANY = pl.BlockSpec(memory_space=pl.ANY)
AFTER = pl.BlockSpec(memory_space=pltpu.HBM)


def pile(parts, deps=()):
    spans, start = [], 0
    for part in parts:
        spans.append((start, part.shape[0]))
        start += part.shape[0]

    def body(*refs):
        ins, out, sem = refs[: len(parts)], refs[-2], refs[-1]
        copies = [
            pltpu.make_async_copy(ref, out.at[pl.ds(at, n)], sem.at[i])
            for i, (ref, (at, n)) in enumerate(zip(ins, spans))
        ]
        for cp in copies:
            cp.start()
        for cp in copies:
            cp.wait()

    shape = (start,) + parts[0].shape[1:]
    return pl.pallas_call(
        body,
        in_specs=[ANY] * len(parts) + [AFTER] * len(deps),
        out_specs=pl.BlockSpec(memory_space=pltpu.VMEM),
        out_shape=jax.ShapeDtypeStruct(shape, parts[0].dtype),
        scratch_shapes=[pltpu.SemaphoreType.DMA((len(parts),))],
        compiler_params=params(16, None),
        cost_estimate=cost(0, 4 * start * shape[1] * shape[2]),
        name="pile",
    )(*parts, *deps)


def place(core, mine, there):
    def body(c, a, b, out, sem):
        first = pltpu.make_async_copy(a, out.at[c[0]], sem.at[0])
        second = pltpu.make_async_copy(b, out.at[1 - c[0]], sem.at[1])
        first.start()
        second.start()
        first.wait()
        second.wait()

    return pl.pallas_call(
        body,
        grid_spec=pltpu.PrefetchScalarGridSpec(
            num_scalar_prefetch=1,
            grid=(1,),
            in_specs=[ANY, ANY],
            out_specs=pl.BlockSpec((2,) + mine.shape, lambda i, c: (0, 0, 0)),
            scratch_shapes=[pltpu.SemaphoreType.DMA((2,))],
        ),
        out_shape=jax.ShapeDtypeStruct((2,) + mine.shape, mine.dtype),
        compiler_params=params(60),
        cost_estimate=cost(0, 4 * mine.size),
        name="place",
    )(core[None], mine, there)


def assemble(own, other, index, deps=()):
    def body(idx, a, b, c, d, *rest):
        out, sem = rest[-2:]
        copies = []
        for i, ref in enumerate((a, b, c, d)):
            for s in range(8):
                copies.append(
                    pltpu.make_async_copy(ref.at[s], out.at[idx[i * 8 + s]], sem.at[i * 8 + s])
                )
        for cp in copies:
            cp.start()
        for cp in copies:
            cp.wait()

    rows, wide = own[0].shape[1:]
    return pl.pallas_call(
        body,
        grid_spec=pltpu.PrefetchScalarGridSpec(
            num_scalar_prefetch=1,
            grid=(1,),
            in_specs=[ANY] * 4 + [AFTER] * len(deps),
            out_specs=pl.BlockSpec((32, rows, wide), lambda i, c: (0, 0, 0)),
            scratch_shapes=[pltpu.SemaphoreType.DMA((32,))],
        ),
        out_shape=jax.ShapeDtypeStruct((32, rows, wide), BF16),
        compiler_params=params(60),
        cost_estimate=cost(0, 4 * 32 * rows * wide),
        name="assemble",
    )(index, *own, *other, *deps)


def turn(vector, cosine, sine):
    lane = lax.broadcasted_iota(jnp.int32, vector.shape, 1)
    swapped = jnp.where(
        lane % HEAD < HEAD // 2,
        pltpu.roll(vector, LANES - HEAD // 2, 1),
        pltpu.roll(vector, HEAD // 2, 1),
    )
    return vector * cosine + swapped * sine


def dot_nn(a, b):
    return lax.dot_general(a, b, (((1,), (0,)), ((), ())), preferred_element_type=F32)


def dot_nt(a, b):
    return lax.dot_general(a, b, (((1,), (1,)), ((), ())), preferred_element_type=F32)


def dot_tn(a, b):
    return lax.dot_general(a, b, (((0,), (0,)), ((), ())), preferred_element_type=F32)


def stacked(low_lane, pair):
    zero = jnp.zeros_like(pair)
    return jnp.concatenate(
        [jnp.where(low_lane, pair, zero), jnp.where(low_lane, zero, pair)], axis=0
    )


def windows(bnd, i, work):
    blocks = (bnd[NBLOCK + i] - bnd[i] + BLOCK // KEYS - 1) // (BLOCK // KEYS)
    for width in range(NBLOCK - 1, NBLOCK + 1):

        @pl.when(jnp.maximum(blocks, NBLOCK - 1) == width)
        def _():
            low = jnp.minimum(bnd[i], (SEQ - width * BLOCK) // KEYS)
            work(pl.ds(pl.multiple_of(low * KEYS, KEYS), width * BLOCK))


def attn_forward(first, count, bounds, source, weights, cosine, sine, seg_col, seg_row, deps=()):
    def body(bnd, x, wq, wk, wv, cos, sin, sc, sr, *rest):
        q_out, k_out, v_out, ctx_out, lse_out, qm = rest[len(deps) :]
        low_lane = lax.broadcasted_iota(jnp.int32, (BLOCK, LANES), 1) < HEAD

        @pl.loop(0, NBLOCK)
        def _(r):
            rows = pl.ds(pl.multiple_of(r * BLOCK, BLOCK), BLOCK)
            xr, cr, sn = x[rows, :], cos[rows, :], sin[rows, :]
            q_proj, k_proj = dot_nn(xr, wq[...]), dot_nn(xr, wk[...])
            v_out[rows, :] = dot_nn(xr, wv[...]).astype(BF16)
            for p in range(GROUP // LANES):
                ln = slice(p * LANES, (p + 1) * LANES)
                q = turn(q_proj[:, ln], cr, sn).astype(BF16) * jnp.asarray(HEAD**-0.5, BF16)
                q_out[rows, ln] = q
                qm[p, r] = stacked(low_lane, q)
                k_out[rows, ln] = turn(k_proj[:, ln], cr, sn).astype(BF16)

        def block(i, _):
            rows = pl.ds(pl.multiple_of(i * BLOCK, BLOCK), BLOCK)
            own = jnp.concatenate([sc[rows, :], sc[rows, :]], axis=0)

            def work(cols):
                seen = own == sr[:, cols]
                for p in range(GROUP // LANES):
                    ln = slice(p * LANES, (p + 1) * LANES)
                    s = jnp.where(seen, dot_nt(qm[p, i], k_out[cols, ln]) * LOG2E, MASKED)
                    top = jnp.max(s, axis=1, keepdims=True)
                    e = jnp.exp2(s - top)
                    total = jnp.sum(e, axis=1, keepdims=True)
                    mixed = dot_nn(e.astype(BF16), v_out[cols, ln]) / total
                    ctx_out[rows, ln] = jnp.where(low_lane, mixed[:BLOCK], mixed[BLOCK:]).astype(BF16)
                    logs = top + jnp.log2(total)
                    flipped = jnp.where(low_lane, logs[:BLOCK], logs[BLOCK:]).T
                    lse_out[0, 2 * p : 2 * p + 1, rows] = flipped[0:1]
                    lse_out[0, 2 * p + 1 : 2 * p + 2, rows] = flipped[HEAD : HEAD + 1]

            windows(bnd, i, work)
            return 0

        lax.fori_loop(0, NBLOCK, block, 0)

    full = lambda shape: pl.BlockSpec(shape, lambda p, b: (0,) * len(shape))
    column = lambda shift: pl.BlockSpec((D, GROUP), lambda p, b: (0, shift * GROUPS + first + p))
    part = pl.BlockSpec((SEQ, GROUP), lambda p, b: (0, p))
    act = jax.ShapeDtypeStruct((SEQ, count * GROUP), BF16)
    return pl.pallas_call(
        body,
        grid_spec=pltpu.PrefetchScalarGridSpec(
            num_scalar_prefetch=1,
            grid=(count,),
            in_specs=[
                full((SEQ, D)),
                column(0),
                column(1),
                column(2),
                full((SEQ, LANES)),
                full((SEQ, LANES)),
                full((SEQ, 1)),
                full((1, SEQ)),
            ]
            + [AFTER] * len(deps),
            out_specs=[part] * 4 + [pl.BlockSpec((1, 8, SEQ), lambda p, b: (p, 0, 0))],
            scratch_shapes=[pltpu.VMEM((GROUP // LANES, NBLOCK, 2 * BLOCK, LANES), BF16)],
        ),
        out_shape=[act] * 4 + [jax.ShapeDtypeStruct((count, 8, SEQ), F32)],
        compiler_params=params(60),
        cost_estimate=cost(
            count * GROUP * (6 * SEQ * D + 16 * SEQ * SEQ), 8 << 20, count * 4 * SEQ * SEQ
        ),
        name="attn_forward",
    )(bounds, source, weights, weights, weights, cosine, sine, seg_col, seg_row, *deps)


def deal(core, whole, mine, theirs, columns):
    parts = whole.reshape(16, 2, D // 32, whole.shape[1])
    first, second = parts[:, 0], parts[:, 1]
    mine[:, :, columns] = jnp.where(core == 0, first, second).astype(BF16)
    theirs[:, :, columns] = jnp.where(core == 0, second, first).astype(BF16)


def attn_backward(at, grad_at, bounds, saved, ctx_grad, source, cosine, sine, seg_col, seg_row, deps=()):
    def body(bnd, q, k, v, o, do, lse, x, cos, sin, sc, sr, *rest):
        core = bnd[2 * NBLOCK]
        out, mine, theirs, qm, dm, dq, dk, dv, dl = rest[len(deps) :]
        low_lane = lax.broadcasted_iota(jnp.int32, (BLOCK, LANES), 1) < HEAD
        row = lax.broadcasted_iota(jnp.int32, (8, LANES), 0)
        lane = lax.broadcasted_iota(jnp.int32, (8, LANES), 1)
        pick = jnp.where(row == lane // HEAD, 1.0, 0.0).astype(F32)
        for p in range(GROUP // LANES):
            ln = slice(p * LANES, (p + 1) * LANES)

            @pl.loop(0, NBLOCK)
            def _(i):
                rows = pl.ds(pl.multiple_of(i * BLOCK, BLOCK), BLOCK)
                qm[p, i] = stacked(low_lane, q[rows, ln])
                dm[p, i] = stacked(low_lane, do[rows, ln])

            dl[p] = lax.dot_general(
                pick,
                do[:, ln].astype(F32) * o[:, ln].astype(F32),
                (((1,), (1,)), ((), ())),
                preferred_element_type=F32,
                precision=lax.Precision.HIGHEST,
            )
        dk[...] = jnp.zeros_like(dk)
        dv[...] = jnp.zeros_like(dv)

        def block(i, _):
            rows = pl.ds(pl.multiple_of(i * BLOCK, BLOCK), BLOCK)
            own = jnp.concatenate([sr[:, rows], sr[:, rows]], axis=1)

            def work(cols):
                seen = sc[cols, :] == own
                for p in range(GROUP // LANES):
                    ln = slice(p * LANES, (p + 1) * LANES)
                    keys, values, qq, dd = k[cols, ln], v[cols, ln], qm[p, i], dm[p, i]
                    logs = jnp.concatenate(
                        [lse[0, 2 * p : 2 * p + 1, rows], lse[0, 2 * p + 1 : 2 * p + 2, rows]], axis=1
                    )
                    deltas = jnp.concatenate([dl[p, 0:1, rows], dl[p, 1:2, rows]], axis=1)
                    s = dot_nt(keys, qq) * LOG2E - logs
                    probs = jnp.exp2(jnp.where(seen, s, MASKED))
                    g = (probs * (dot_nt(values, dd) - deltas)).astype(BF16)
                    dv[cols, ln] += dot_nn(probs.astype(BF16), dd)
                    dk[cols, ln] += dot_nn(g, qq)
                    both = dot_tn(g, keys)
                    dq[rows, ln] = jnp.where(low_lane, both[:BLOCK], both[BLOCK:])

            windows(bnd, i, work)
            return 0

        lax.fori_loop(0, NBLOCK, block, 0)

        @pl.loop(0, NBLOCK)
        def _(r):
            rows = pl.ds(pl.multiple_of(r * BLOCK, BLOCK), BLOCK)
            cr, sn = cos[rows, :], -sin[rows, :]
            for p in range(GROUP // LANES):
                ln = slice(p * LANES, (p + 1) * LANES)
                out[0, rows, ln] = turn(dq[rows, ln] * (HEAD**-0.5), cr, sn).astype(BF16)
                out[1, rows, ln] = turn(dk[rows, ln], cr, sn).astype(BF16)
                out[2, rows, ln] = dv[rows, ln].astype(BF16)

        for i in range(3):
            deal(core, dot_tn(x[...], out[i]), mine, theirs, slice(i * GROUP, (i + 1) * GROUP))

    full = lambda shape: pl.BlockSpec(shape, lambda p, b: (0,) * len(shape))
    part = pl.BlockSpec((SEQ, GROUP), lambda p, b: (0, at))
    low2 = pltpu.VMEM((GROUP // LANES, NBLOCK, 2 * BLOCK, LANES), BF16)
    wide = pltpu.VMEM((SEQ, GROUP), F32)
    dealt = (16, D // 32, 3 * GROUP)
    return pl.pallas_call(
        body,
        grid_spec=pltpu.PrefetchScalarGridSpec(
            num_scalar_prefetch=1,
            grid=(1,),
            in_specs=[part] * 4
            + [
                pl.BlockSpec((SEQ, GROUP), lambda p, b: (0, grad_at)),
                pl.BlockSpec((1, 8, SEQ), lambda p, b: (at, 0, 0)),
                full((SEQ, D)),
                full((SEQ, LANES)),
                full((SEQ, LANES)),
                full((SEQ, 1)),
                full((1, SEQ)),
            ]
            + [AFTER] * len(deps),
            out_specs=[full((3, SEQ, GROUP)), full(dealt), full(dealt)],
            scratch_shapes=[
                low2,
                low2,
                wide,
                wide,
                wide,
                pltpu.VMEM((GROUP // LANES, 8, SEQ), F32),
            ],
        ),
        out_shape=[
            jax.ShapeDtypeStruct((3, SEQ, GROUP), BF16),
            jax.ShapeDtypeStruct(dealt, BF16),
            jax.ShapeDtypeStruct(dealt, BF16),
        ],
        compiler_params=params(60),
        cost_estimate=cost(GROUP * (40 * SEQ * SEQ + 6 * SEQ * D), 10 << 20, 4 * SEQ * SEQ),
        name="attn_backward",
    )(bounds, *saved[:4], ctx_grad, saved[4], source, cosine, sine, seg_col, seg_row, *deps)


def join_rows(index, here, there, count, deps=(), columns=512):
    lead, _, wide = here.shape
    rows = D // 16
    each = 16 // count
    steps = wide // columns

    def body(idx, a, b, *rest):
        outs = rest[len(deps) :]
        for s in range(16):
            at = pl.ds(pl.multiple_of(idx[s] * rows, 16), rows)
            total = a[0, at, :].astype(F32) + b[0, at, :].astype(F32)
            outs[s // each][s % each] = total.astype(BF16)

    whole = pl.BlockSpec((1, D, columns), lambda l, n, i: (l, 0, n))
    part = pl.BlockSpec((each, rows, columns), lambda l, n, i: (0, 0, l * steps + n))
    return pl.pallas_call(
        body,
        grid_spec=pltpu.PrefetchScalarGridSpec(
            num_scalar_prefetch=1,
            grid=(lead, steps),
            in_specs=[whole, whole] + [AFTER] * len(deps),
            out_specs=[part] * count,
        ),
        out_shape=[jax.ShapeDtypeStruct((each, rows, lead * wide), BF16)] * count,
        compiler_params=params(60, ("arbitrary", "arbitrary")),
        cost_estimate=cost(D * wide * lead, 6 * D * wide * lead),
        name="join_rows",
    )(index, here, there, *deps)


def out_grad(core, ctx, right, norms):
    def body(c, *refs):
        parts, (b, nrm, mine, theirs) = refs[:GROUPS], refs[GROUPS:]
        whole = jnp.concatenate([dot_tn(p[...], b[...]) for p in parts], axis=0)
        deal(c[0], whole, mine, theirs, slice(0, D))
        flipped = jnp.concatenate([nrm[...], jnp.zeros((LANES - 8, D), F32)], axis=0).T
        filled = jnp.concatenate([flipped, jnp.zeros((D, LANES), F32)], axis=1)
        deal(c[0], filled, mine, theirs, slice(D, TAIL))

    full = lambda shape: pl.BlockSpec(shape, lambda p, b: (0,) * len(shape))
    dealt = (16, D // 32, TAIL)
    return pl.pallas_call(
        body,
        grid_spec=pltpu.PrefetchScalarGridSpec(
            num_scalar_prefetch=1,
            grid=(1,),
            in_specs=[full((SEQ, GROUP))] * GROUPS + [full((SEQ, D)), full((8, D))],
            out_specs=[full(dealt), full(dealt)],
        ),
        out_shape=[jax.ShapeDtypeStruct(dealt, BF16)] * 2,
        compiler_params=params(60),
        cost_estimate=cost(2 * SEQ * D * D, 8 << 20),
        name="out_grad",
    )(core[None], *ctx, right, norms)


def join_dealt(index, mine, there, deps=()):
    widths = [m.shape[2] for m in mine]
    wide, rows, count = sum(widths), D // 32, len(mine)

    def body(idx, *refs):
        ours, others, keep, send = refs[:count], refs[count : 2 * count], refs[-2], refs[-1]
        for s in range(16):
            start = 0
            for a, b, n in zip(ours, others, widths):
                total = a[idx[s]].astype(F32) + b[idx[s]].astype(F32)
                (keep, send)[s // 8][s % 8, :, start : start + n] = total.astype(BF16)
                start += n

    full = lambda shape: pl.BlockSpec(shape, lambda p, b: (0,) * len(shape))
    half = (8, rows, wide)
    return pl.pallas_call(
        body,
        grid_spec=pltpu.PrefetchScalarGridSpec(
            num_scalar_prefetch=1,
            grid=(1,),
            in_specs=[full((16, rows, n)) for n in widths] * 2 + [AFTER] * len(deps),
            out_specs=[full(half), full(half)],
        ),
        out_shape=[jax.ShapeDtypeStruct(half, BF16)] * 2,
        compiler_params=params(24),
        cost_estimate=cost(D * wide // 2, 3 * D * wide),
        name="join_dealt",
    )(index, *mine, *there, *deps)


def fold(keep, there, count, dtype=BF16, deps=()):
    blocks, rows, wide = keep.shape
    each = blocks // count

    def body(a, b, *rest):
        for n, out in enumerate(rest[len(deps) :]):
            at = slice(n * each, (n + 1) * each)
            out[...] = (a[at].astype(F32) + b[at].astype(F32)).astype(dtype)

    steps = 2 if blocks * rows * wide > 1 << 19 else 1
    columns = wide // steps
    part = pl.BlockSpec((blocks, rows, columns), lambda i: (0, 0, i))
    return pl.pallas_call(
        body,
        grid=(steps,),
        in_specs=[part, part] + [AFTER] * len(deps),
        out_specs=[pl.BlockSpec((each, rows, columns), lambda i: (0, 0, i))] * count,
        out_shape=[jax.ShapeDtypeStruct((each, rows, wide), dtype)] * count,
        compiler_params=params(16),
        cost_estimate=cost(blocks * rows * wide, 6 * blocks * rows * wide),
        name="fold",
    )(keep, there, *deps)


def fold_pair(keep, there, deps=()):
    rows = keep[0].shape[1]
    widths = [k.shape[2] for k in keep]
    wide = sum(widths)

    def body(a, b, c, d, *rest):
        start = 0
        for p, q, n in ((a, c, widths[0]), (b, d, widths[1])):
            for at, out in enumerate(rest[len(deps) :]):
                four = slice(4 * at, 4 * at + 4)
                total = p[four].astype(F32) + q[four].astype(F32)
                out[:, :, start : start + n] = total.astype(BF16)
            start += n

    vmem = pl.BlockSpec(memory_space=pltpu.VMEM)
    return pl.pallas_call(
        body,
        in_specs=[vmem] * 4 + [AFTER] * len(deps),
        out_specs=[vmem] * 2,
        out_shape=[jax.ShapeDtypeStruct((4, rows, wide), BF16)] * 2,
        compiler_params=params(16, None),
        cost_estimate=cost(8 * rows * wide, 48 * rows * wide),
        name="fold_pair",
    )(*keep, *there, *deps)


def finish(parts, deps=()):
    rows = D // 32

    def body(a, b, c, d, *rest):
        qkv, out, gain, shift = rest[len(deps) :]
        total = a[0].astype(F32) + b[0].astype(F32) + c[0].astype(F32) + d[0].astype(F32)
        places = [0, 3 * GROUP, 6 * GROUP + TAIL]
        for i in range(3):
            at = [slice(p + i * GROUP, p + (i + 1) * GROUP) for p in places]
            qkv[:, i, :] = jnp.concatenate([total[:, p] for p in at], axis=1)
        start = 6 * GROUP
        out[...] = total[:, start : start + D]
        gain[...] = total[:, start + D : start + D + 2]
        shift[...] = total[:, start + D + 2 : start + D + 4]

    vmem = pl.BlockSpec(memory_space=pltpu.VMEM)
    shapes = [(rows, 3, D), (rows, D), (rows, 2), (rows, 2)]
    return pl.pallas_call(
        body,
        in_specs=[vmem] * 4 + [AFTER] * len(deps),
        out_specs=[vmem] * 4,
        out_shape=[jax.ShapeDtypeStruct(shape, F32) for shape in shapes],
        compiler_params=params(16, None),
        cost_estimate=cost(1 << 18, 1 << 20),
        name="finish",
    )(*parts, *deps)


def input_back(core, hidden_grad, projected, weights, deps=()):
    half = SEQ // 2 // BLOCK

    def body(c, hid, a, b, d, w, *rest):
        mine, leave = rest[-2:]
        total = hid[...]
        for g, ref in enumerate((a, b, d)):
            for i in range(3):
                at = i * D + g * GROUP
                total = total + dot_nt(ref[i], w[:, at : at + GROUP])
        own = pl.program_id(0) // half == c[0]

        @pl.when(own)
        def _():
            mine[...] = total

        @pl.when(jnp.logical_not(own))
        def _():
            leave[...] = total

    row = pl.BlockSpec((BLOCK, D), lambda r, c: (r, 0))
    shape = jax.ShapeDtypeStruct((SEQ // 2, D), F32)
    return pl.pallas_call(
        body,
        grid_spec=pltpu.PrefetchScalarGridSpec(
            num_scalar_prefetch=1,
            grid=(SEQ // BLOCK,),
            in_specs=[row]
            + [pl.BlockSpec((3, BLOCK, GROUP), lambda r, c: (0, r, 0))] * 3
            + [pl.BlockSpec((D, 3 * D), lambda r, c: (0, 0))]
            + [AFTER] * len(deps),
            out_specs=[
                pl.BlockSpec((BLOCK, D), lambda r, c: (jnp.clip(r - half * c[0], 0, half - 1), 0)),
                pl.BlockSpec(
                    (BLOCK, D), lambda r, c: (jnp.clip(r - half * (1 - c[0]), 0, half - 1), 0)
                ),
            ],
        ),
        out_shape=[shape, shape],
        compiler_params=params(60),
        cost_estimate=cost(6 * SEQ * D * D, 16 << 20),
        name="input_back",
    )(core[None], hidden_grad, *projected, weights, *deps)


def middle(index, source, ctx, cot, pieces):
    def norm(v):
        center = v - jnp.mean(v, axis=1, keepdims=True)
        scale = lax.rsqrt(jnp.mean(center * center, axis=1, keepdims=True) + EPSILON)
        return center * scale, scale

    def norm_back(u, hat, scale, gain):
        g = u * gain
        return scale * (
            g - jnp.mean(g, axis=1, keepdims=True) - hat * jnp.mean(g * hat, axis=1, keepdims=True)
        )

    def body(idx, x, ctx0, ctx1, ctx2, cot, *refs):
        pieces, refs = refs[:8], refs[8:]
        out, out_leave, gu_own, gu_other, down_own, down_other, hid_out, att_out, ctxg_out, sums = refs[:10]
        (
            w, wo, tail, nrm, factors, acts, low_t, mlp_t, mlp_s, back_s, hat_s, scale_s, pair_s, sem,
        ) = refs[10:]
        step = pl.program_id(0)
        core = idx[32]
        few = D // 32

        def loads(kind, which):
            copies = []
            for rest in (2 * which, 2 * which + 1):
                for s in range(8):
                    block = idx[(0 if kind == "gate" else 33) + rest * 8 + s]
                    at = pl.ds(pl.multiple_of(block * 48, 16), 48)
                    n = rest * 8 + s
                    gate, down = pieces[rest], pieces[4 + rest]
                    if kind == "gate":
                        copies.append(
                            pltpu.make_async_copy(
                                gate.at[s], w.at[which, at, pl.ds(0, 2 * HIDDEN)], sem.at[n]
                            )
                        )
                    elif kind == "down":
                        copies.append(
                            pltpu.make_async_copy(
                                down.at[s, :, pl.ds(0, HIDDEN)],
                                w.at[which, at, pl.ds(2 * HIDDEN, HIDDEN)],
                                sem.at[32 + n],
                            )
                        )
                    else:
                        owner = core if which == 0 else 1 - core
                        for part in range(2):
                            copies.append(
                                pltpu.make_async_copy(
                                    down.at[s, pl.ds(part * few, few), pl.ds(HIDDEN, REST)],
                                    tail.at[part, block * 2 + owner],
                                    sem.at[64 + n + 32 * part],
                                )
                            )
            return copies

        def arrive(kind, which):
            @pl.when(step == 0)
            def _():
                for cp in loads(kind, which):
                    cp.wait()

        @pl.when(step == 0)
        def _():
            for which in range(2):
                for cp in loads("tail", which):
                    cp.start()
            for which in range(2):
                for kind in ("gate", "down"):
                    for cp in loads(kind, which):
                        cp.start()

        arrive("tail", 0)
        arrive("tail", 1)

        @pl.when(step == 0)
        def _():
            joined = jnp.concatenate(
                [tail[0].reshape(D, REST), tail[1].reshape(D, REST)], axis=1
            )
            wo[...] = joined[:, :D]
            nrm[...] = joined[:, D : D + LANES].astype(F32).T[:8]
            sums[...] = jnp.zeros_like(sums)

        gain1, gain2, shift1, shift2 = (nrm[i : i + 1, :] for i in range(4))

        @pl.when(step < STEPS)
        def _():
            rows = pl.ds(pl.multiple_of(step * ROWS, ROWS), ROWS)
            context = jnp.concatenate([ctx0[...], ctx1[...], ctx2[...]], axis=1)
            hidden_in = x[...].astype(F32) + dot_nn(context, wo[...])
            hat1, scale1 = norm(hidden_in)
            hat_s[rows, :] = hat1
            scale_s[rows, :] = scale1
            normed = hat1 * gain1 + shift1
            low = normed.astype(BF16)
            low_t[:, rows] = low.T
            total = normed
            for half in range(2):
                arrive("gate", half)
                arrive("down", half)
                for n in range(HIDDEN // CHUNK):
                    g_at, u_at, d_at = (pl.ds(p * HIDDEN + n * CHUNK, CHUNK) for p in range(3))
                    gate = dot_nn(low, w[half, :, g_at])
                    up = dot_nn(low, w[half, :, u_at])
                    s = jax.nn.sigmoid(gate)
                    silu = gate * s
                    act = (silu * up).astype(BF16)
                    factors[half, rows, g_at] = (up * (s * (1.0 + gate * (1.0 - s)))).astype(BF16)
                    factors[half, rows, u_at] = silu.astype(BF16)
                    acts[half, rows, g_at] = act
                    total = total + dot_nt(act, w[half, :, d_at])
            hat2, scale2 = norm(total)
            result = (hat2 * gain2 + shift2).astype(BF16)
            own = step // (STEPS // 2) == core

            @pl.when(own)
            def _():
                out[...] = result

            @pl.when(jnp.logical_not(own))
            def _():
                out_leave[...] = result

            u2 = cot[...].astype(F32)
            resid = norm_back(u2, hat2, scale2, gain2)
            mlp = resid.astype(BF16)
            mlp_s[rows, :] = mlp
            mlp_t[:, rows] = mlp.T
            back_s[rows, :] = resid
            sums[1:2, :] += jnp.sum(u2 * hat2, axis=0, keepdims=True)
            sums[3:4, :] += jnp.sum(u2, axis=0, keepdims=True)

        @pl.when(jnp.logical_and(step >= STEPS, step < STEPS + PIECES))
        def _():
            at = step - STEPS
            half = 1 - at // (PIECES // 2)
            n = at % (PIECES // 2)
            g_at, u_at, d_at = (
                pl.ds(pl.multiple_of(p * HIDDEN + n * PIECE, PIECE), PIECE) for p in range(3)
            )

            for r in range(STEPS):
                rows = pl.ds(r * ROWS, ROWS)
                grad = dot_nn(mlp_s[rows, :], w[half, :, d_at])
                gate_grad = (grad * factors[half, rows, g_at].astype(F32)).astype(BF16)
                up_grad = (grad * factors[half, rows, u_at].astype(F32)).astype(BF16)
                pair_s[0, rows, :] = gate_grad
                pair_s[1, rows, :] = up_grad
                back_s[rows, :] += dot_nt(gate_grad, w[half, :, g_at]) + dot_nt(
                    up_grad, w[half, :, u_at]
                )

            def store(gu, down):
                for i in range(2):
                    gu[i] = dot_nn(low_t[...], pair_s[i]).astype(BF16)
                down[0] = dot_nn(mlp_t[...], acts[half, :, g_at]).astype(BF16)

            @pl.when(half == 1)
            def _():
                store(gu_other, down_other)

            @pl.when(half == 0)
            def _():
                store(gu_own, down_own)

        @pl.when(step >= STEPS + PIECES)
        def _():
            r = step - STEPS - PIECES
            rows = pl.ds(pl.multiple_of(r * ROWS, ROWS), ROWS)
            back, hat1 = back_s[rows, :], hat_s[rows, :]
            hidden_grad = norm_back(back, hat1, scale_s[rows, :], gain1)
            hid_out[...] = hidden_grad
            att = hidden_grad.astype(BF16)
            att_out[...] = att
            ctxg_out[...] = dot_nt(att, wo[...]).astype(BF16)
            sums[0:1, :] += jnp.sum(back * hat1, axis=0, keepdims=True)
            sums[2:3, :] += jnp.sum(back, axis=0, keepdims=True)

    last = STEPS - 1
    row = lambda n: pl.BlockSpec((ROWS, n), lambda t, i: (jnp.minimum(t, last), 0))
    ending = pl.BlockSpec((ROWS, D), lambda t, i: (jnp.clip(t - STEPS - PIECES, 0, last), 0))
    half = STEPS // 2
    side = lambda t, mine: (jnp.clip(jnp.minimum(t, last) - half * mine, 0, half - 1), 0)
    mine = pl.BlockSpec((ROWS, D), lambda t, i: side(t, i[32]))
    leave = pl.BlockSpec((ROWS, D), lambda t, i: side(t, 1 - i[32]))
    each = PIECES // 2
    own = lambda lead: pl.BlockSpec(
        (lead, D, PIECE), lambda t, i: (0, 0, jnp.clip(t - STEPS - each, 0, each - 1))
    )
    theirs = lambda lead: pl.BlockSpec(
        (lead, D, PIECE), lambda t, i: (0, 0, jnp.clip(t - STEPS, 0, each - 1))
    )
    act = lambda n, t=BF16: jax.ShapeDtypeStruct((n, D), t)
    grads = lambda lead: jax.ShapeDtypeStruct((lead, D, HIDDEN), BF16)
    return pl.pallas_call(
        body,
        grid_spec=pltpu.PrefetchScalarGridSpec(
            num_scalar_prefetch=1,
            grid=(2 * STEPS + PIECES,),
            in_specs=[row(D)] + [row(GROUP)] * GROUPS + [row(D)] + [ANY] * 8,
            out_specs=[mine, leave, own(2), theirs(2), own(1), theirs(1)]
            + [ending] * 3
            + [pl.BlockSpec((8, D), lambda t, i: (0, 0))],
            scratch_shapes=[
                pltpu.VMEM((2, D, WIDE), BF16),
                pltpu.VMEM((D, D), BF16),
                pltpu.VMEM((2, 32, D // 32, REST), BF16),
                pltpu.VMEM((8, D), F32),
                pltpu.VMEM((2, SEQ, 2 * HIDDEN), BF16),
                pltpu.VMEM((2, SEQ, HIDDEN), BF16),
                pltpu.VMEM((D, SEQ), BF16),
                pltpu.VMEM((D, SEQ), BF16),
                pltpu.VMEM((SEQ, D), BF16),
                pltpu.VMEM((SEQ, D), F32),
                pltpu.VMEM((SEQ, D), F32),
                pltpu.VMEM((SEQ, 1), F32),
                pltpu.VMEM((2, SEQ, PIECE), BF16),
                pltpu.SemaphoreType.DMA((128,)),
            ],
        ),
        out_shape=[
            act(SEQ // 2),
            act(SEQ // 2),
            grads(2),
            grads(2),
            grads(1),
            grads(1),
            act(SEQ, F32),
            act(SEQ),
            act(SEQ),
            jax.ShapeDtypeStruct((8, D), F32),
        ],
        compiler_params=params(62),
        cost_estimate=cost(18 * SEQ * D * 2 * HIDDEN + 4 * SEQ * D * D, 40 << 20, 4 * SEQ * HIDDEN),
        name="middle",
    )(index, source, *ctx, cot, *pieces)


def rotary_lanes(segment_row):
    labels = jnp.arange(NDOC + 1, dtype=jnp.int32)
    before = jnp.sum((segment_row[None, :] < labels[:, None]).astype(jnp.int32), axis=1)
    member = segment_row[:, None] == labels[None, :]
    first = jnp.sum(jnp.where(member, before[None, :], 0), axis=1)
    position = (jnp.arange(SEQ, dtype=jnp.int32) - first).astype(F32)
    lane = jnp.arange(LANES) % (HEAD // 2)
    frequency = jnp.power(F32(1000.0), -2.0 * lane.astype(F32) / HEAD)
    angle = position[:, None] * frequency[None, :]
    sign = jnp.where(jnp.arange(LANES) % HEAD < HEAD // 2, -1.0, 1.0)
    ends = jnp.concatenate([before[1:], jnp.full((1,), SEQ, jnp.int32)])
    heads = segment_row[::BLOCK]
    tails = segment_row[BLOCK - 1 :: BLOCK]
    low = jnp.sum(jnp.where(heads[:, None] == labels[None, :], before[None, :], 0), axis=1)
    high = jnp.sum(jnp.where(tails[:, None] == labels[None, :], ends[None, :], 0), axis=1)
    bounds = jnp.concatenate([low // KEYS, (high + KEYS - 1) // KEYS]).astype(jnp.int32)
    return jnp.cos(angle), jnp.sin(angle) * sign[None, :], bounds


def sequence_device(
    tokens, segments, qkv_weight, out_weight, norm_gain, norm_shift, gate_up, down_weight, cotangent
):
    core = lax.axis_index("tensor")
    def ordered(mine, theirs):
        return jnp.where(
            core == 0, jnp.stack([mine, theirs], axis=0), jnp.stack([theirs, mine], axis=0)
        )

    pick = lambda a, i: lax.dynamic_index_in_dim(a, i, 0, keepdims=False)
    source = pick(tokens, core)
    segment_row = pick(segments, core)

    attn_block = qkv_weight.reshape(-1, 3 * D)
    gate_block = gate_up.reshape(-1, 2 * HIDDEN)
    tail_block = jnp.concatenate(
        [out_weight, norm_gain, norm_shift, jnp.zeros((D // 32, TAIL - D - 4), BF16)], axis=1
    )
    down_block = jnp.concatenate(
        [down_weight, jnp.concatenate([tail_block[:, :REST], tail_block[:, REST:]], axis=0)], axis=1
    )
    from_here, from_there = slot_blocks(-1, core), slot_blocks(-1, 1 - core)
    there_blocks = slot_blocks(1, core).reshape(2, 2, 4)
    to_here = there_blocks.transpose(1, 0, 2).reshape(16)
    deep_first = there_blocks.transpose(2, 1, 0).reshape(16)

    cot = ordered(pick(cotangent, core), core_swap(pick(cotangent, 1 - core))).reshape(SEQ, D)
    cosine, sine, bounds = rotary_lanes(segment_row)
    bounds = jnp.concatenate([bounds, core[None]]).astype(jnp.int32)
    tables = (cosine, sine, segment_row[:, None], segment_row[None, :])

    ahead = lambda parts: [part[None] for part in parts]
    gate_parts = depth_ring(gate_block)
    attn_four = pile(ahead(depth_parts(attn_block)), deps=(gate_parts[1],))
    attn_eight = pile(
        [attn_four, first_swap(attn_four)], deps=(gate_parts[2], source, cot, *tables)
    )
    attn_last = second_swap(attn_eight)
    index = jnp.concatenate([from_here * 2 + core, from_there * 2 + 1 - core]).astype(jnp.int32)
    weights = assemble(
        (attn_eight, attn_last),
        (core_swap(attn_eight), core_swap(attn_last)),
        index,
        deps=(gate_parts[3],),
    ).reshape(D, 3 * D)
    gate_four = pile(ahead(gate_parts))
    down_pair = pile([down_block[None], first_swap(down_block)[None]], deps=(gate_four,))
    saved0 = attn_forward(0, 1, bounds, source, weights, *tables, deps=(gate_four, down_pair))
    near, far = depth_shift(down_pair, 1), depth_shift(down_pair, 3)
    gate_eight = pile([gate_four, first_swap(gate_four)], deps=(saved0[4], near, far))
    gate_last = second_swap(gate_eight)
    saved1 = attn_forward(1, 1, bounds, source, weights, *tables, deps=(gate_eight,))
    down_eight = pile([down_pair, near, depth_shift(down_pair, 2), far], deps=(saved1[4],))
    saved2 = attn_forward(2, 1, bounds, source, weights, *tables, deps=(down_eight,))
    down_last, late_logs = lax.optimization_barrier((second_swap(down_eight), saved2[4]))
    saved2 = (*saved2[:4], late_logs)
    pieces = (gate_eight, gate_last, core_swap(gate_eight), core_swap(gate_last))
    pieces += (down_eight, down_last, core_swap(down_eight), core_swap(down_last))

    turned = lambda slots: slots.reshape(2, 2, 4).transpose(0, 2, 1).reshape(16)
    index = jnp.concatenate(
        [from_here, from_there, core[None], turned(from_here), turned(from_there)]
    ).astype(jnp.int32)
    ctx = (saved0[3], saved1[3], saved2[3])
    (out, out_leave, gu_here, gu_there, down_here, down_there, hidden_grad, att_grad, ctx_grad, sums) = (
        middle(index, source, ctx, cot, pieces)
    )

    gu_there, down_there = core_swap(gu_there), core_swap(down_there)
    tail_mine, tail_theirs = out_grad(core, ctx, att_grad, sums)
    gu_keep, gu_send = join_rows(to_here, gu_here, gu_there, 2, deps=(tail_mine,))
    down_parts = join_rows(deep_first, down_here, down_there, 4, deps=(gu_send,))
    gu_first = first_swap(gu_send)
    passing = depth_shift(down_parts[3], 1)

    common = (source,) + tables
    back0 = attn_backward(0, 0, bounds, saved0, ctx_grad, *common, deps=(gu_send, down_parts[0]))
    (passing,) = fold(passing, down_parts[2], 1, deps=(back0[1],))
    back1 = attn_backward(0, 1, bounds, saved1, ctx_grad, *common, deps=(passing,))
    passing = depth_shift(passing, 1)
    (passing,) = fold(passing, down_parts[1], 1, deps=(back1[1],))
    gu_keep, gu_send = fold(gu_keep, gu_first, 2, deps=(back1[1],))
    gu_second = second_swap(gu_send)
    early_keep, early_send = join_dealt(
        to_here,
        (back0[1], back1[1], tail_mine),
        (core_swap(back0[2]), core_swap(back1[2]), core_swap(tail_theirs)),
        deps=(passing, gu_send),
    )
    early_first = first_swap(early_send)
    back2 = attn_backward(0, 2, bounds, saved2, ctx_grad, *common, deps=(gu_send, early_send, passing))

    deep = lambda parts: [parts[0]] + [depth_shift(parts[k], k) for k in (1, 2, 3)]
    passing = depth_shift(passing, 1)
    gu_parts = fold(gu_keep, gu_second, 4, deps=(back2[1],))
    down_keep, down_send = fold(passing, down_parts[0], 2, deps=(gu_parts[0],))
    late_keep, late_send = join_dealt(
        to_here, (back2[1],), (core_swap(back2[2]),), deps=(down_send, early_first)
    )
    late_first = first_swap(late_send)
    down_keep, down_send = fold(down_keep, first_swap(down_send), 2, deps=(late_send,))
    down_second = second_swap(down_send)
    (gu_total,) = fold(depth_shift(gu_parts[3], 1), gu_parts[2], 1, deps=(down_send,))
    attn_keep, attn_send = fold_pair(
        (early_keep, late_keep), (early_first, late_first), deps=(gu_total,)
    )
    attn_second = second_swap(attn_send)
    grad, grad_leave = input_back(
        core, hidden_grad, (back0[0], back1[0], back2[0]), weights, deps=(attn_send,)
    )
    (gu_total,) = fold(depth_shift(gu_total, 1), gu_parts[1], 1, deps=(grad,))
    attn_parts = deep(fold(attn_keep, attn_second, 4, deps=(gu_total,)))
    (gu_total,) = fold(depth_shift(gu_total, 1), gu_parts[0], 1, F32, deps=(attn_parts[0],))
    outputs = place(core, out, core_swap(out_leave)), place(core, grad, core_swap(grad_leave))
    down_total = (down_keep.astype(F32) + down_second.astype(F32))[0]
    gu_total = gu_total[0]
    qkv_total, out_total, gain_total, shift_total = finish(attn_parts, deps=outputs)

    return (
        *outputs,
        qkv_total,
        out_total,
        gain_total,
        shift_total,
        gu_total.reshape(-1, 2, HIDDEN),
        down_total,
    )


def solution(mesh):
    in_specs = (
        P("dp", None, None),
        P("dp", None),
        P(("dp", "tensor"), None, None),
        P(("dp", "tensor"), None),
        P(("dp", "tensor"), None),
        P(("dp", "tensor"), None),
        P("dp", None, "tensor"),
        P("dp", "tensor"),
        P("dp", "tensor", None),
    )
    out_specs = (
        P("dp", "tensor", None),
        P("dp", "tensor", None),
        P(("dp", "tensor"), None, None),
        P(("dp", "tensor"), None),
        P(("dp", "tensor"), None),
        P(("dp", "tensor"), None),
        P("dp", None, "tensor"),
        P("dp", "tensor"),
    )
    sizes = dict(mesh.shape)

    def per_device(tokens, *others):
        if sizes["dp"] == 16 and sizes["tensor"] == 2 and tokens.shape[0] == 2:
            return sequence_device(tokens, *others)
        return general_device(tokens, *others)

    return jax.shard_map(
        per_device, mesh=mesh, in_specs=in_specs, out_specs=out_specs, check_vma=False
    )
```

```python
import jax
import jax.numpy as jnp
from jax import lax
from jax.experimental import pallas as pl
from jax.experimental.pallas import tpu as pltpu
from jax.sharding import PartitionSpec as P

D = 768
HEADS = 12
HEAD = 64
SEQ = 1024
NDOC = 8


EPSILON = 1e-05
MASKED = -1e30


def for_sending(value):
    return jax.tree.map(lambda a: a.astype(jnp.bfloat16) if a.dtype == jnp.float32 else a, value)


def rotary_tables(segment_row):
    labels = jnp.arange(NDOC + 1, dtype=jnp.int32)
    member = (segment_row[:, None] == labels[None, :]).astype(jnp.int32)
    counts = jnp.sum(member, axis=0)
    starts = jnp.concatenate([jnp.zeros((1,), jnp.int32), jnp.cumsum(counts)[:-1]])
    offset = jnp.sum(member * starts[None, :], axis=1)
    position = (jnp.arange(SEQ, dtype=jnp.int32) - offset).astype(jnp.float32)
    exponent = -2.0 * jnp.arange(HEAD // 2).astype(jnp.float32) / HEAD
    frequency = jnp.power(jnp.float32(1000.0), exponent)
    angle = position[:, None] * frequency[None, :]
    return (jnp.cos(angle)[:, None, :], jnp.sin(angle)[:, None, :])


def rotate(vector, cosine, sine):
    half = vector.shape[-1] // 2
    first_half = vector[..., :half]
    second_half = vector[..., half:]
    return jnp.concatenate(
        [first_half * cosine - second_half * sine, second_half * cosine + first_half * sine],
        axis=-1,
    )


def unrotate(gradient, cosine, sine):

    def turned(vector):
        return rotate(vector, cosine, sine)

    _, pullback = jax.vjp(turned, gradient)
    return pullback(gradient)[0]


def layer_norm(vector, gain, shift):
    center = vector - jnp.mean(vector, axis=-1, keepdims=True)
    variance = jnp.mean(center * center, axis=-1, keepdims=True)
    return center * lax.rsqrt(variance + EPSILON) * gain + shift


def swiglu_piece(gate, upper):
    return jax.nn.silu(gate) * upper


def accumulate(total, term):
    if total is None:
        return term
    return tuple((left + right for left, right in zip(total, term)))


def general_device(
    tokens, segments, qkv_weight, out_weight, norm_gain, norm_shift, gate_up, down_weight, cotangent
):
    tensor_size = lax.axis_size("tensor")
    own_rows = SEQ // tensor_size
    row_start = lax.axis_index("tensor") * own_rows
    score_scale = HEAD ** (-0.5)
    qkv_full, out_full, gain_full, shift_full = (
        lax.all_gather(qkv_weight, ("dp", "tensor"), axis=0, tiled=True),
        lax.all_gather(out_weight, ("dp", "tensor"), axis=0, tiled=True),
        lax.all_gather(norm_gain, ("dp", "tensor"), axis=0, tiled=True),
        lax.all_gather(norm_shift, ("dp", "tensor"), axis=0, tiled=True),
    )
    gains = gain_full.astype(jnp.float32)
    shifts = shift_full.astype(jnp.float32)
    gate_up_full, down_full = (
        lax.all_gather(gate_up, "dp", axis=0, tiled=True),
        lax.all_gather(down_weight, "dp", axis=0, tiled=True),
    )
    batches = tokens.shape[0]
    outputs = []
    input_grads = []
    attn_total = None
    mlp_total = None
    for batch_index in range(batches):
        source = tokens[batch_index]
        own_source = lax.dynamic_slice_in_dim(source, row_start, own_rows, 0)
        segment_row = segments[batch_index]
        cosine, sine = rotary_tables(segment_row)
        own_cos = lax.dynamic_slice_in_dim(cosine, row_start, own_rows, 0)
        own_sin = lax.dynamic_slice_in_dim(sine, row_start, own_rows, 0)
        query_proj = jnp.einsum(
            "sd,de->se", own_source, qkv_full[:, 0], preferred_element_type=jnp.float32
        )
        pair_proj = jnp.einsum(
            "sd,dke->ske", source, qkv_full[:, 1:], preferred_element_type=jnp.float32
        )
        keys = rotate(pair_proj[:, 0].reshape(SEQ, HEADS, HEAD), cosine, sine).astype(jnp.bfloat16)
        values = pair_proj[:, 1].reshape(SEQ, HEADS, HEAD).astype(jnp.bfloat16)
        queries = rotate(query_proj.reshape(own_rows, HEADS, HEAD), own_cos, own_sin).astype(
            jnp.bfloat16
        )
        own_segments = lax.dynamic_slice_in_dim(segment_row, row_start, own_rows, 0)
        allowed = (own_segments[:, None] == segment_row[None, :])[None]
        raw_scores = (
            jnp.einsum("qhe,khe->hqk", queries, keys, preferred_element_type=jnp.float32)
            * score_scale
        )
        masked = jnp.where(allowed, raw_scores, MASKED)
        top_score = jnp.max(masked, axis=-1, keepdims=True)
        logsum = top_score + jnp.log(jnp.sum(jnp.exp(masked - top_score), axis=-1, keepdims=True))
        probs_low = jnp.exp(masked - logsum).astype(jnp.bfloat16)
        context = (
            jnp.einsum("hqk,khe->qhe", probs_low, values, preferred_element_type=jnp.float32)
            .reshape(own_rows, D)
            .astype(jnp.bfloat16)
        )
        attended = jnp.dot(context, out_full, preferred_element_type=jnp.float32)
        hidden_in = own_source.astype(jnp.float32) + attended
        normed = layer_norm(hidden_in, gains[:, 0], shifts[:, 0])
        normed_all = lax.all_gather(normed.astype(jnp.bfloat16), "tensor", axis=0, tiled=True)
        gate_pair = jnp.einsum(
            "sd,dkf->skf", normed_all, gate_up_full, preferred_element_type=jnp.float32
        )
        swiglu = swiglu_piece(gate_pair[:, 0], gate_pair[:, 1]).astype(jnp.bfloat16)
        mlp_out = lax.psum_scatter(
            jnp.einsum("sf,df->sd", swiglu, down_full, preferred_element_type=jnp.float32).astype(
                jnp.bfloat16
            ),
            "tensor",
            scatter_dimension=0,
            tiled=True,
        ).astype(jnp.float32)
        resid = normed + mlp_out
        outputs.append(layer_norm(resid, gains[:, 1], shifts[:, 1]).astype(jnp.bfloat16))
        upstream = cotangent[batch_index].astype(jnp.float32)
        _, second_pull = jax.vjp(layer_norm, resid, gains[:, 1], shifts[:, 1])
        resid_grad, gain_two, shift_two = second_pull(upstream)
        mlp_grad = lax.all_gather(resid_grad.astype(jnp.bfloat16), "tensor", axis=0, tiled=True)
        swiglu_grad = jnp.einsum(
            "sd,df->sf", mlp_grad, down_full, preferred_element_type=jnp.float32
        )
        _, glu_pull = jax.vjp(swiglu_piece, gate_pair[:, 0], gate_pair[:, 1])
        gate_grad, upper_grad = glu_pull(swiglu_grad)
        pair_grad = jnp.stack([gate_grad, upper_grad], axis=1).astype(jnp.bfloat16)
        down_term = jnp.einsum("sd,sf->df", mlp_grad, swiglu, preferred_element_type=jnp.float32)
        gate_up_term = jnp.einsum(
            "sd,skf->dkf", normed_all, pair_grad, preferred_element_type=jnp.float32
        )
        normed_grad = resid_grad + lax.psum_scatter(
            jnp.einsum("skf,dkf->sd", pair_grad, gate_up_full, preferred_element_type=jnp.float32),
            "tensor",
            scatter_dimension=0,
            tiled=True,
        )
        _, first_pull = jax.vjp(layer_norm, hidden_in, gains[:, 0], shifts[:, 0])
        hidden_grad, gain_one, shift_one = first_pull(normed_grad)
        attended_grad = hidden_grad.astype(jnp.bfloat16)
        out_term = jnp.einsum(
            "sd,se->de", context, attended_grad, preferred_element_type=jnp.float32
        )
        context_grad = (
            jnp.einsum("se,de->sd", attended_grad, out_full, preferred_element_type=jnp.float32)
            .astype(jnp.bfloat16)
            .reshape(own_rows, HEADS, HEAD)
        )
        probs = jnp.exp(masked - logsum)
        weights_grad = jnp.einsum(
            "qhe,khe->hqk", context_grad, values, preferred_element_type=jnp.float32
        )
        row_delta = jnp.sum(probs * weights_grad, axis=-1, keepdims=True)
        score_grad = (probs * (weights_grad - row_delta)).astype(jnp.bfloat16)
        query_grad = (
            jnp.einsum("hqk,khe->qhe", score_grad, keys, preferred_element_type=jnp.float32)
            * score_scale
        )
        key_part = (
            jnp.einsum("hqk,qhe->khe", score_grad, queries, preferred_element_type=jnp.float32)
            * score_scale
        )
        value_part = jnp.einsum(
            "hqk,qhe->khe", probs_low, context_grad, preferred_element_type=jnp.float32
        )
        key_value = lax.psum_scatter(
            jnp.stack(
                [
                    key_part.reshape(lax.axis_size("tensor") * own_rows, D),
                    value_part.reshape(lax.axis_size("tensor") * own_rows, D),
                ],
                axis=1,
            ).astype(jnp.bfloat16),
            "tensor",
            scatter_dimension=0,
            tiled=True,
        ).astype(jnp.float32)
        query_back = unrotate(query_grad, own_cos, own_sin).reshape(own_rows, D)
        key_back = unrotate(
            key_value[:, 0].reshape(own_rows, HEADS, HEAD), own_cos, own_sin
        ).reshape(own_rows, D)
        proj_grad = jnp.stack([query_back, key_back, key_value[:, 1]], axis=1).astype(jnp.bfloat16)
        input_grads.append(
            hidden_grad
            + jnp.einsum("ske,dke->sd", proj_grad, qkv_full, preferred_element_type=jnp.float32)
        )
        qkv_term = jnp.einsum(
            "sd,ske->dke", own_source, proj_grad, preferred_element_type=jnp.float32
        )
        gain_term = jnp.stack([gain_one, gain_two], axis=1)
        shift_term = jnp.stack([shift_one, shift_two], axis=1)
        attn_terms = (qkv_term, out_term, gain_term, shift_term)
        mlp_terms = (gate_up_term, down_term)
        attn_total = accumulate(attn_total, attn_terms)
        mlp_total = accumulate(mlp_total, mlp_terms)
    attn_final = lax.psum_scatter(attn_total, ("dp", "tensor"), scatter_dimension=0, tiled=True)
    mlp_final = jax.tree.map(
        lambda part: part.astype(jnp.float32),
        lax.psum_scatter(for_sending(mlp_total), "dp", scatter_dimension=0, tiled=True),
    )
    return (
        jnp.stack(outputs, axis=0),
        jnp.stack(input_grads, axis=0),
        attn_final[0],
        attn_final[1],
        attn_final[2],
        attn_final[3],
        mlp_final[0],
        mlp_final[1],
    )


HIDDEN = 1536
WIDE = 3 * HIDDEN
REST = 512
TAIL = 2 * REST
GROUP = 4 * HEAD
GROUPS = D // GROUP
KEYS = 128
LANES = 2 * HEAD
BLOCK = 256
NBLOCK = SEQ // BLOCK
ROWS = 256
STEPS = SEQ // ROWS
CHUNK = 512
PIECE = 256
PIECES = 2 * HIDDEN // PIECE
LOG2E = 1.4426950408889634
F32 = jnp.float32
BF16 = jnp.bfloat16


def across(value, move):
    pairs = []
    for z in range(4):
        for y in range(2):
            for x in range(2):
                for c in range(2):
                    tz, ty, tx, tc = move(z, y, x, c)
                    pairs.append((((z * 2 + y) * 2 + x) * 2 + c, ((tz * 2 + ty) * 2 + tx) * 2 + tc))
    return lax.ppermute(value, ("dp", "tensor"), pairs)


def core_swap(value):
    return across(value, lambda z, y, x, c: (z, y, x, 1 - c))


def first_swap(value):
    return across(value, lambda z, y, x, c: (z, y, 1 - x, c) if c == 0 else (z, 1 - y, x, c))


def second_swap(value):
    return across(value, lambda z, y, x, c: (z, 1 - y, x, c) if c == 0 else (z, y, 1 - x, c))


def depth_shift(value, steps):
    return across(value, lambda z, y, x, c: ((z + steps) % 4, y, x, c))


def slot_blocks(sign, core):
    me = lax.axis_index("dp")
    z, y, x = me // 4, (me // 2) % 2, me % 2
    slot = jnp.arange(16, dtype=jnp.int32)
    second, first, depth = slot // 8, (slot // 4) % 2, slot % 4
    x_bit = jnp.where(core == 0, first, second)
    y_bit = jnp.where(core == 0, second, first)
    return (((z + sign * depth) % 4) * 4 + (y ^ y_bit) * 2 + (x ^ x_bit)).astype(jnp.int32)


def depth_parts(block):
    return [block] + [depth_shift(block, k) for k in (1, 2, 3)]


def depth_ring(block):
    parts = [block]
    for _ in range(3):
        parts.append(depth_shift(parts[-1], 1))
    return parts


def cost(flops, nbytes, trans=0):
    return pl.CostEstimate(flops=int(flops), bytes_accessed=int(nbytes), transcendentals=int(trans))


def params(vmem_mb, sem=("arbitrary",)):
    return pltpu.CompilerParams(dimension_semantics=sem, vmem_limit_bytes=vmem_mb << 20)


ANY = pl.BlockSpec(memory_space=pl.ANY)
AFTER = pl.BlockSpec(memory_space=pltpu.HBM)


def pile(parts, deps=()):
    spans, start = [], 0
    for part in parts:
        spans.append((start, part.shape[0]))
        start += part.shape[0]

    def body(*refs):
        ins, out, sem = refs[: len(parts)], refs[-2], refs[-1]
        copies = [
            pltpu.make_async_copy(ref, out.at[pl.ds(at, n)], sem.at[i])
            for i, (ref, (at, n)) in enumerate(zip(ins, spans))
        ]
        for cp in copies:
            cp.start()
        for cp in copies:
            cp.wait()

    shape = (start,) + parts[0].shape[1:]
    return pl.pallas_call(
        body,
        in_specs=[ANY] * len(parts) + [AFTER] * len(deps),
        out_specs=pl.BlockSpec(memory_space=pltpu.VMEM),
        out_shape=jax.ShapeDtypeStruct(shape, parts[0].dtype),
        scratch_shapes=[pltpu.SemaphoreType.DMA((len(parts),))],
        compiler_params=params(16, None),
        cost_estimate=cost(0, 4 * start * shape[1] * shape[2]),
        name="pile",
    )(*parts, *deps)


def place(core, mine, there):
    def body(c, a, b, out, token, held, sem):
        first = pltpu.make_async_copy(a, held.at[c[0]], sem.at[0])
        second = pltpu.make_async_copy(b, held.at[1 - c[0]], sem.at[1])
        first.start()
        second.start()
        first.wait()
        second.wait()
        last = pltpu.make_async_copy(held, out, sem.at[2])
        last.start()
        last.wait()
        token[...] = jnp.zeros_like(token)

    return pl.pallas_call(
        body,
        grid_spec=pltpu.PrefetchScalarGridSpec(
            num_scalar_prefetch=1,
            grid=(1,),
            in_specs=[ANY, ANY],
            out_specs=[AFTER, pl.BlockSpec((8, LANES), lambda i, c: (0, 0))],
            scratch_shapes=[
                pltpu.VMEM((2,) + mine.shape, mine.dtype),
                pltpu.SemaphoreType.DMA((3,)),
            ],
        ),
        out_shape=[jax.ShapeDtypeStruct((2,) + mine.shape, mine.dtype), TOKEN],
        compiler_params=params(60),
        cost_estimate=cost(0, 4 * mine.size),
        name="place",
    )(core[None], mine, there)


def assemble(own, other, index, deps=()):
    def body(idx, a, b, c, d, *rest):
        out, sem = rest[-2:]
        copies = []
        for i, ref in enumerate((a, b, c, d)):
            for s in range(8):
                copies.append(
                    pltpu.make_async_copy(ref.at[s], out.at[idx[i * 8 + s]], sem.at[i * 8 + s])
                )
        for cp in copies:
            cp.start()
        for cp in copies:
            cp.wait()

    rows, wide = own[0].shape[1:]
    return pl.pallas_call(
        body,
        grid_spec=pltpu.PrefetchScalarGridSpec(
            num_scalar_prefetch=1,
            grid=(1,),
            in_specs=[ANY] * 4 + [AFTER] * len(deps),
            out_specs=pl.BlockSpec((32, rows, wide), lambda i, c: (0, 0, 0)),
            scratch_shapes=[pltpu.SemaphoreType.DMA((32,))],
        ),
        out_shape=jax.ShapeDtypeStruct((32, rows, wide), BF16),
        compiler_params=params(60),
        cost_estimate=cost(0, 4 * 32 * rows * wide),
        name="assemble",
    )(index, *own, *other, *deps)


def turn(vector, cosine, sine):
    lane = lax.broadcasted_iota(jnp.int32, vector.shape, 1)
    swapped = jnp.where(
        lane % HEAD < HEAD // 2,
        pltpu.roll(vector, LANES - HEAD // 2, 1),
        pltpu.roll(vector, HEAD // 2, 1),
    )
    return vector * cosine + swapped * sine


def dot_nn(a, b):
    return lax.dot_general(a, b, (((1,), (0,)), ((), ())), preferred_element_type=F32)


def dot_nt(a, b):
    return lax.dot_general(a, b, (((1,), (1,)), ((), ())), preferred_element_type=F32)


def dot_tn(a, b):
    return lax.dot_general(a, b, (((0,), (0,)), ((), ())), preferred_element_type=F32)


TOKEN = jax.ShapeDtypeStruct((8, LANES), F32)


def stacked(low_lane, pair):
    zero = jnp.zeros_like(pair)
    return jnp.concatenate(
        [jnp.where(low_lane, pair, zero), jnp.where(low_lane, zero, pair)], axis=0
    )


def windows(bnd, i, work):
    blocks = (bnd[NBLOCK + i] - bnd[i] + BLOCK // KEYS - 1) // (BLOCK // KEYS)
    for width in range(NBLOCK - 1, NBLOCK + 1):

        @pl.when(jnp.maximum(blocks, NBLOCK - 1) == width)
        def _():
            low = jnp.minimum(bnd[i], (SEQ - width * BLOCK) // KEYS)
            work(pl.ds(pl.multiple_of(low * KEYS, KEYS), width * BLOCK))


def attn_forward(first, count, bounds, source, weights, cosine, sine, seg_col, seg_row, deps=()):
    def body(bnd, x, wq, wk, wv, cos, sin, sc, sr, *rest):
        q_out, k_out, v_out, ctx_out, lse_out, qm = rest[len(deps) :]
        low_lane = lax.broadcasted_iota(jnp.int32, (BLOCK, LANES), 1) < HEAD

        @pl.loop(0, NBLOCK)
        def _(r):
            rows = pl.ds(pl.multiple_of(r * BLOCK, BLOCK), BLOCK)
            xr, cr, sn = x[rows, :], cos[rows, :], sin[rows, :]
            q_proj, k_proj = dot_nn(xr, wq[...]), dot_nn(xr, wk[...])
            v_out[rows, :] = dot_nn(xr, wv[...]).astype(BF16)
            for p in range(GROUP // LANES):
                ln = slice(p * LANES, (p + 1) * LANES)
                q = turn(q_proj[:, ln], cr, sn).astype(BF16) * jnp.asarray(HEAD**-0.5, BF16)
                q_out[rows, ln] = q
                qm[p, r] = stacked(low_lane, q)
                k_out[rows, ln] = turn(k_proj[:, ln], cr, sn).astype(BF16)

        def block(i, _):
            rows = pl.ds(pl.multiple_of(i * BLOCK, BLOCK), BLOCK)
            own = jnp.concatenate([sc[rows, :], sc[rows, :]], axis=0)

            def work(cols):
                seen = own == sr[:, cols]
                for p in range(GROUP // LANES):
                    ln = slice(p * LANES, (p + 1) * LANES)
                    s = jnp.where(seen, dot_nt(qm[p, i], k_out[cols, ln]) * LOG2E, MASKED)
                    top = jnp.max(s, axis=1, keepdims=True)
                    e = jnp.exp2(s - top)
                    total = jnp.sum(e, axis=1, keepdims=True)
                    mixed = dot_nn(e.astype(BF16), v_out[cols, ln]) / total
                    ctx_out[rows, ln] = jnp.where(low_lane, mixed[:BLOCK], mixed[BLOCK:]).astype(BF16)
                    logs = top + jnp.log2(total)
                    flipped = jnp.where(low_lane, logs[:BLOCK], logs[BLOCK:]).T
                    lse_out[0, 2 * p : 2 * p + 1, rows] = flipped[0:1]
                    lse_out[0, 2 * p + 1 : 2 * p + 2, rows] = flipped[HEAD : HEAD + 1]

            windows(bnd, i, work)
            return 0

        lax.fori_loop(0, NBLOCK, block, 0)

    full = lambda shape: pl.BlockSpec(shape, lambda p, b: (0,) * len(shape))
    column = lambda shift: pl.BlockSpec((D, GROUP), lambda p, b: (0, shift * GROUPS + first + p))
    part = pl.BlockSpec((SEQ, GROUP), lambda p, b: (0, p))
    act = jax.ShapeDtypeStruct((SEQ, count * GROUP), BF16)
    return pl.pallas_call(
        body,
        grid_spec=pltpu.PrefetchScalarGridSpec(
            num_scalar_prefetch=1,
            grid=(count,),
            in_specs=[
                full((SEQ, D)),
                column(0),
                column(1),
                column(2),
                full((SEQ, LANES)),
                full((SEQ, LANES)),
                full((SEQ, 1)),
                full((1, SEQ)),
            ]
            + [AFTER] * len(deps),
            out_specs=[part] * 4 + [pl.BlockSpec((1, 8, SEQ), lambda p, b: (p, 0, 0))],
            scratch_shapes=[pltpu.VMEM((GROUP // LANES, NBLOCK, 2 * BLOCK, LANES), BF16)],
        ),
        out_shape=[act] * 4 + [jax.ShapeDtypeStruct((count, 8, SEQ), F32)],
        compiler_params=params(60),
        cost_estimate=cost(
            count * GROUP * (6 * SEQ * D + 16 * SEQ * SEQ), 8 << 20, count * 4 * SEQ * SEQ
        ),
        name="attn_forward",
    )(bounds, source, weights, weights, weights, cosine, sine, seg_col, seg_row, *deps)


def deal(core, whole, mine, theirs, columns):
    parts = whole.reshape(16, 2, D // 32, whole.shape[1])
    first, second = parts[:, 0], parts[:, 1]
    mine[:, :, columns] = jnp.where(core == 0, first, second).astype(BF16)
    theirs[:, :, columns] = jnp.where(core == 0, second, first).astype(BF16)


def attn_backward(at, grad_at, bounds, saved, ctx_grad, source, cosine, sine, seg_col, seg_row, deps=()):
    def body(bnd, q, k, v, o, do, lse, x, cos, sin, sc, sr, *rest):
        core = bnd[2 * NBLOCK]
        out, mine, theirs, token, qm, dm, dq, dk, dv, dl = rest[len(deps) :]
        token[...] = jnp.zeros_like(token)
        low_lane = lax.broadcasted_iota(jnp.int32, (BLOCK, LANES), 1) < HEAD
        row = lax.broadcasted_iota(jnp.int32, (8, LANES), 0)
        lane = lax.broadcasted_iota(jnp.int32, (8, LANES), 1)
        pick = jnp.where(row == lane // HEAD, 1.0, 0.0).astype(F32)
        for p in range(GROUP // LANES):
            ln = slice(p * LANES, (p + 1) * LANES)

            @pl.loop(0, NBLOCK)
            def _(i):
                rows = pl.ds(pl.multiple_of(i * BLOCK, BLOCK), BLOCK)
                qm[p, i] = stacked(low_lane, q[rows, ln])
                dm[p, i] = stacked(low_lane, do[rows, ln])

            dl[p] = lax.dot_general(
                pick,
                do[:, ln].astype(F32) * o[:, ln].astype(F32),
                (((1,), (1,)), ((), ())),
                preferred_element_type=F32,
                precision=lax.Precision.HIGHEST,
            )
        dk[...] = jnp.zeros_like(dk)
        dv[...] = jnp.zeros_like(dv)

        def block(i, _):
            rows = pl.ds(pl.multiple_of(i * BLOCK, BLOCK), BLOCK)
            own = jnp.concatenate([sr[:, rows], sr[:, rows]], axis=1)

            def work(cols):
                seen = sc[cols, :] == own
                for p in range(GROUP // LANES):
                    ln = slice(p * LANES, (p + 1) * LANES)
                    keys, values, qq, dd = k[cols, ln], v[cols, ln], qm[p, i], dm[p, i]
                    logs = jnp.concatenate(
                        [lse[0, 2 * p : 2 * p + 1, rows], lse[0, 2 * p + 1 : 2 * p + 2, rows]], axis=1
                    )
                    deltas = jnp.concatenate([dl[p, 0:1, rows], dl[p, 1:2, rows]], axis=1)
                    s = dot_nt(keys, qq) * LOG2E - logs
                    probs = jnp.exp2(jnp.where(seen, s, MASKED))
                    g = (probs * (dot_nt(values, dd) - deltas)).astype(BF16)
                    dv[cols, ln] += dot_nn(probs.astype(BF16), dd)
                    dk[cols, ln] += dot_nn(g, qq)
                    both = dot_tn(g, keys)
                    dq[rows, ln] = jnp.where(low_lane, both[:BLOCK], both[BLOCK:])

            windows(bnd, i, work)
            return 0

        lax.fori_loop(0, NBLOCK, block, 0)

        @pl.loop(0, NBLOCK)
        def _(r):
            rows = pl.ds(pl.multiple_of(r * BLOCK, BLOCK), BLOCK)
            cr, sn = cos[rows, :], -sin[rows, :]
            for p in range(GROUP // LANES):
                ln = slice(p * LANES, (p + 1) * LANES)
                out[0, rows, ln] = turn(dq[rows, ln] * (HEAD**-0.5), cr, sn).astype(BF16)
                out[1, rows, ln] = turn(dk[rows, ln], cr, sn).astype(BF16)
                out[2, rows, ln] = dv[rows, ln].astype(BF16)

        for i in range(3):
            deal(core, dot_tn(x[...], out[i]), mine, theirs, slice(i * GROUP, (i + 1) * GROUP))

    full = lambda shape: pl.BlockSpec(shape, lambda p, b: (0,) * len(shape))
    part = pl.BlockSpec((SEQ, GROUP), lambda p, b: (0, at))
    low2 = pltpu.VMEM((GROUP // LANES, NBLOCK, 2 * BLOCK, LANES), BF16)
    wide = pltpu.VMEM((SEQ, GROUP), F32)
    dealt = (16, D // 32, 3 * GROUP)
    return pl.pallas_call(
        body,
        grid_spec=pltpu.PrefetchScalarGridSpec(
            num_scalar_prefetch=1,
            grid=(1,),
            in_specs=[part] * 4
            + [
                pl.BlockSpec((SEQ, GROUP), lambda p, b: (0, grad_at)),
                pl.BlockSpec((1, 8, SEQ), lambda p, b: (at, 0, 0)),
                full((SEQ, D)),
                full((SEQ, LANES)),
                full((SEQ, LANES)),
                full((SEQ, 1)),
                full((1, SEQ)),
            ]
            + [AFTER] * len(deps),
            out_specs=[full((3, SEQ, GROUP)), full(dealt), full(dealt), full((8, LANES))],
            scratch_shapes=[
                low2,
                low2,
                wide,
                wide,
                wide,
                pltpu.VMEM((GROUP // LANES, 8, SEQ), F32),
            ],
        ),
        out_shape=[
            jax.ShapeDtypeStruct((3, SEQ, GROUP), BF16),
            jax.ShapeDtypeStruct(dealt, BF16),
            jax.ShapeDtypeStruct(dealt, BF16),
            TOKEN,
        ],
        compiler_params=params(60),
        cost_estimate=cost(GROUP * (40 * SEQ * SEQ + 6 * SEQ * D), 10 << 20, 4 * SEQ * SEQ),
        name="attn_backward",
    )(bounds, *saved[:4], ctx_grad, saved[4], source, cosine, sine, seg_col, seg_row, *deps)


def join_rows(index, here, there, count, deps=(), columns=512):
    lead, _, wide = here.shape
    rows = D // 16
    each = 16 // count
    steps = wide // columns

    def body(idx, a, b, *rest):
        outs = rest[len(deps) :]
        for s in range(16):
            at = pl.ds(pl.multiple_of(idx[s] * rows, 16), rows)
            total = a[0, at, :].astype(F32) + b[0, at, :].astype(F32)
            outs[s // each][s % each] = total.astype(BF16)

    whole = pl.BlockSpec((1, D, columns), lambda l, n, i: (l, 0, n))
    part = pl.BlockSpec((each, rows, columns), lambda l, n, i: (0, 0, l * steps + n))
    return pl.pallas_call(
        body,
        grid_spec=pltpu.PrefetchScalarGridSpec(
            num_scalar_prefetch=1,
            grid=(lead, steps),
            in_specs=[whole, whole] + [AFTER] * len(deps),
            out_specs=[part] * count,
        ),
        out_shape=[jax.ShapeDtypeStruct((each, rows, lead * wide), BF16)] * count,
        compiler_params=params(60, ("arbitrary", "arbitrary")),
        cost_estimate=cost(D * wide * lead, 6 * D * wide * lead),
        name="join_rows",
    )(index, here, there, *deps)


def out_grad(core, ctx, right, norms):
    def body(c, *refs):
        parts, (b, nrm, mine, theirs) = refs[:GROUPS], refs[GROUPS:]
        whole = jnp.concatenate([dot_tn(p[...], b[...]) for p in parts], axis=0)
        deal(c[0], whole, mine, theirs, slice(0, D))
        flipped = jnp.concatenate([nrm[...], jnp.zeros((LANES - 8, D), F32)], axis=0).T
        filled = jnp.concatenate([flipped, jnp.zeros((D, LANES), F32)], axis=1)
        deal(c[0], filled, mine, theirs, slice(D, TAIL))

    full = lambda shape: pl.BlockSpec(shape, lambda p, b: (0,) * len(shape))
    dealt = (16, D // 32, TAIL)
    return pl.pallas_call(
        body,
        grid_spec=pltpu.PrefetchScalarGridSpec(
            num_scalar_prefetch=1,
            grid=(1,),
            in_specs=[full((SEQ, GROUP))] * GROUPS + [full((SEQ, D)), full((8, D))],
            out_specs=[full(dealt), full(dealt)],
        ),
        out_shape=[jax.ShapeDtypeStruct(dealt, BF16)] * 2,
        compiler_params=params(60),
        cost_estimate=cost(2 * SEQ * D * D, 8 << 20),
        name="out_grad",
    )(core[None], *ctx, right, norms)


def join_dealt(index, mine, there, deps=()):
    widths = [m.shape[2] for m in mine]
    wide, rows, count = sum(widths), D // 32, len(mine)

    def body(idx, *refs):
        ours, others, keep, send = refs[:count], refs[count : 2 * count], refs[-2], refs[-1]
        for s in range(16):
            start = 0
            for a, b, n in zip(ours, others, widths):
                total = a[idx[s]].astype(F32) + b[idx[s]].astype(F32)
                (keep, send)[s // 8][s % 8, :, start : start + n] = total.astype(BF16)
                start += n

    full = lambda shape: pl.BlockSpec(shape, lambda p, b: (0,) * len(shape))
    half = (8, rows, wide)
    return pl.pallas_call(
        body,
        grid_spec=pltpu.PrefetchScalarGridSpec(
            num_scalar_prefetch=1,
            grid=(1,),
            in_specs=[full((16, rows, n)) for n in widths] * 2 + [AFTER] * len(deps),
            out_specs=[full(half), full(half)],
        ),
        out_shape=[jax.ShapeDtypeStruct(half, BF16)] * 2,
        compiler_params=params(24),
        cost_estimate=cost(D * wide // 2, 3 * D * wide),
        name="join_dealt",
    )(index, *mine, *there, *deps)


def fold(keep, there, count, dtype=BF16, deps=()):
    blocks, rows, wide = keep.shape
    each = blocks // count

    def body(a, b, *rest):
        for n, out in enumerate(rest[len(deps) :]):
            at = slice(n * each, (n + 1) * each)
            out[...] = (a[at].astype(F32) + b[at].astype(F32)).astype(dtype)

    steps = 2 if blocks * rows * wide > 1 << 19 else 1
    columns = wide // steps
    part = pl.BlockSpec((blocks, rows, columns), lambda i: (0, 0, i))
    return pl.pallas_call(
        body,
        grid=(steps,),
        in_specs=[part, part] + [AFTER] * len(deps),
        out_specs=[pl.BlockSpec((each, rows, columns), lambda i: (0, 0, i))] * count,
        out_shape=[jax.ShapeDtypeStruct((each, rows, wide), dtype)] * count,
        compiler_params=params(16),
        cost_estimate=cost(blocks * rows * wide, 6 * blocks * rows * wide),
        name="fold",
    )(keep, there, *deps)


def fold_pair(keep, there, deps=()):
    rows = keep[0].shape[1]
    widths = [k.shape[2] for k in keep]
    wide = sum(widths)

    def body(a, b, c, d, *rest):
        start = 0
        for p, q, n in ((a, c, widths[0]), (b, d, widths[1])):
            for at, out in enumerate(rest[len(deps) :]):
                four = slice(4 * at, 4 * at + 4)
                total = p[four].astype(F32) + q[four].astype(F32)
                out[:, :, start : start + n] = total.astype(BF16)
            start += n

    vmem = pl.BlockSpec(memory_space=pltpu.VMEM)
    return pl.pallas_call(
        body,
        in_specs=[vmem] * 4 + [AFTER] * len(deps),
        out_specs=[vmem] * 2,
        out_shape=[jax.ShapeDtypeStruct((4, rows, wide), BF16)] * 2,
        compiler_params=params(16, None),
        cost_estimate=cost(8 * rows * wide, 48 * rows * wide),
        name="fold_pair",
    )(*keep, *there, *deps)


def finish(parts, deps=()):
    rows = D // 32

    def body(a, b, c, d, *rest):
        qkv, out, gain, shift = rest[len(deps) :]
        total = a[0].astype(F32) + b[0].astype(F32) + c[0].astype(F32) + d[0].astype(F32)
        places = [0, 3 * GROUP, 6 * GROUP + TAIL]
        for i in range(3):
            at = [slice(p + i * GROUP, p + (i + 1) * GROUP) for p in places]
            qkv[:, i, :] = jnp.concatenate([total[:, p] for p in at], axis=1)
        start = 6 * GROUP
        out[...] = total[:, start : start + D]
        gain[...] = total[:, start + D : start + D + 2]
        shift[...] = total[:, start + D + 2 : start + D + 4]

    vmem = pl.BlockSpec(memory_space=pltpu.VMEM)
    shapes = [(rows, 3, D), (rows, D), (rows, 2), (rows, 2)]
    return pl.pallas_call(
        body,
        in_specs=[vmem] * 4 + [AFTER] * len(deps),
        out_specs=[vmem] * 4,
        out_shape=[jax.ShapeDtypeStruct(shape, F32) for shape in shapes],
        compiler_params=params(16, None),
        cost_estimate=cost(1 << 18, 1 << 20),
        name="finish",
    )(*parts, *deps)


def input_back(core, hidden_grad, projected, weights, deps=()):
    half = SEQ // 2 // BLOCK

    def body(c, hid, a, b, d, w, *rest):
        mine, leave, token = rest[-3:]
        token[...] = jnp.zeros_like(token)
        total = hid[...]
        for g, ref in enumerate((a, b, d)):
            for i in range(3):
                at = i * D + g * GROUP
                total = total + dot_nt(ref[i], w[:, at : at + GROUP])
        own = pl.program_id(0) // half == c[0]

        @pl.when(own)
        def _():
            mine[...] = total

        @pl.when(jnp.logical_not(own))
        def _():
            leave[...] = total

    row = pl.BlockSpec((BLOCK, D), lambda r, c: (r, 0))
    shape = jax.ShapeDtypeStruct((SEQ // 2, D), F32)
    return pl.pallas_call(
        body,
        grid_spec=pltpu.PrefetchScalarGridSpec(
            num_scalar_prefetch=1,
            grid=(SEQ // BLOCK,),
            in_specs=[row]
            + [pl.BlockSpec((3, BLOCK, GROUP), lambda r, c: (0, r, 0))] * 3
            + [pl.BlockSpec((D, 3 * D), lambda r, c: (0, 0))]
            + [AFTER] * len(deps),
            out_specs=[
                pl.BlockSpec((BLOCK, D), lambda r, c: (jnp.clip(r - half * c[0], 0, half - 1), 0)),
                pl.BlockSpec(
                    (BLOCK, D), lambda r, c: (jnp.clip(r - half * (1 - c[0]), 0, half - 1), 0)
                ),
                pl.BlockSpec((8, LANES), lambda r, c: (0, 0)),
            ],
        ),
        out_shape=[shape, shape, TOKEN],
        compiler_params=params(60),
        cost_estimate=cost(6 * SEQ * D * D, 16 << 20),
        name="input_back",
    )(core[None], hidden_grad, *projected, weights, *deps)


def middle(index, source, ctx, cot, pieces):
    def norm(v):
        center = v - jnp.mean(v, axis=1, keepdims=True)
        scale = lax.rsqrt(jnp.mean(center * center, axis=1, keepdims=True) + EPSILON)
        return center * scale, scale

    def norm_back(u, hat, scale, gain):
        g = u * gain
        return scale * (
            g - jnp.mean(g, axis=1, keepdims=True) - hat * jnp.mean(g * hat, axis=1, keepdims=True)
        )

    def body(idx, x, ctx0, ctx1, ctx2, cot, *refs):
        pieces, refs = refs[:8], refs[8:]
        out, out_leave, gu_own, gu_other, down_own, down_other, hid_out, att_out, ctxg_out, sums = refs[:10]
        (
            w, wo, tail, nrm, factors, acts, low_t, mlp_t, mlp_s, back_s, hat_s, scale_s, pair_s, sem,
        ) = refs[10:]
        step = pl.program_id(0)
        core = idx[32]
        few = D // 32

        def loads(kind, which):
            copies = []
            for rest in (2 * which, 2 * which + 1):
                for s in range(8):
                    block = idx[(0 if kind == "gate" else 33) + rest * 8 + s]
                    at = pl.ds(pl.multiple_of(block * 48, 16), 48)
                    n = rest * 8 + s
                    gate, down = pieces[rest], pieces[4 + rest]
                    if kind == "gate":
                        copies.append(
                            pltpu.make_async_copy(
                                gate.at[s], w.at[which, at, pl.ds(0, 2 * HIDDEN)], sem.at[n]
                            )
                        )
                    elif kind == "down":
                        copies.append(
                            pltpu.make_async_copy(
                                down.at[s, :, pl.ds(0, HIDDEN)],
                                w.at[which, at, pl.ds(2 * HIDDEN, HIDDEN)],
                                sem.at[32 + n],
                            )
                        )
                    else:
                        owner = core if which == 0 else 1 - core
                        for part in range(2):
                            copies.append(
                                pltpu.make_async_copy(
                                    down.at[s, pl.ds(part * few, few), pl.ds(HIDDEN, REST)],
                                    tail.at[part, block * 2 + owner],
                                    sem.at[64 + n + 32 * part],
                                )
                            )
            return copies

        def arrive(kind, which):
            @pl.when(step == 0)
            def _():
                for cp in loads(kind, which):
                    cp.wait()

        @pl.when(step == 0)
        def _():
            for which in range(2):
                for cp in loads("tail", which):
                    cp.start()
            for which in range(2):
                for kind in ("gate", "down"):
                    for cp in loads(kind, which):
                        cp.start()

        arrive("tail", 0)
        arrive("tail", 1)

        @pl.when(step == 0)
        def _():
            joined = jnp.concatenate(
                [tail[0].reshape(D, REST), tail[1].reshape(D, REST)], axis=1
            )
            wo[...] = joined[:, :D]
            nrm[...] = joined[:, D : D + LANES].astype(F32).T[:8]
            sums[...] = jnp.zeros_like(sums)

        gain1, gain2, shift1, shift2 = (nrm[i : i + 1, :] for i in range(4))

        @pl.when(step < STEPS)
        def _():
            rows = pl.ds(pl.multiple_of(step * ROWS, ROWS), ROWS)
            context = jnp.concatenate([ctx0[...], ctx1[...], ctx2[...]], axis=1)
            hidden_in = x[...].astype(F32) + dot_nn(context, wo[...])
            hat1, scale1 = norm(hidden_in)
            hat_s[rows, :] = hat1
            scale_s[rows, :] = scale1
            normed = hat1 * gain1 + shift1
            low = normed.astype(BF16)
            low_t[:, rows] = low.T
            total = normed
            for half in range(2):
                arrive("gate", half)
                arrive("down", half)
                for n in range(HIDDEN // CHUNK):
                    g_at, u_at, d_at = (pl.ds(p * HIDDEN + n * CHUNK, CHUNK) for p in range(3))
                    gate = dot_nn(low, w[half, :, g_at])
                    up = dot_nn(low, w[half, :, u_at])
                    s = jax.nn.sigmoid(gate)
                    silu = gate * s
                    act = (silu * up).astype(BF16)
                    factors[half, rows, g_at] = (up * (s * (1.0 + gate * (1.0 - s)))).astype(BF16)
                    factors[half, rows, u_at] = silu.astype(BF16)
                    acts[half, rows, g_at] = act
                    total = total + dot_nt(act, w[half, :, d_at])
            hat2, scale2 = norm(total)
            result = (hat2 * gain2 + shift2).astype(BF16)
            own = step // (STEPS // 2) == core

            @pl.when(own)
            def _():
                out[...] = result

            @pl.when(jnp.logical_not(own))
            def _():
                out_leave[...] = result

            u2 = cot[...].astype(F32)
            resid = norm_back(u2, hat2, scale2, gain2)
            mlp = resid.astype(BF16)
            mlp_s[rows, :] = mlp
            mlp_t[:, rows] = mlp.T
            back_s[rows, :] = resid
            sums[1:2, :] += jnp.sum(u2 * hat2, axis=0, keepdims=True)
            sums[3:4, :] += jnp.sum(u2, axis=0, keepdims=True)

        @pl.when(jnp.logical_and(step >= STEPS, step < STEPS + PIECES))
        def _():
            at = step - STEPS
            half = 1 - at // (PIECES // 2)
            n = at % (PIECES // 2)
            g_at, u_at, d_at = (
                pl.ds(pl.multiple_of(p * HIDDEN + n * PIECE, PIECE), PIECE) for p in range(3)
            )

            for r in range(STEPS):
                rows = pl.ds(r * ROWS, ROWS)
                grad = dot_nn(mlp_s[rows, :], w[half, :, d_at])
                gate_grad = (grad * factors[half, rows, g_at].astype(F32)).astype(BF16)
                up_grad = (grad * factors[half, rows, u_at].astype(F32)).astype(BF16)
                pair_s[0, rows, :] = gate_grad
                pair_s[1, rows, :] = up_grad
                back_s[rows, :] += dot_nt(gate_grad, w[half, :, g_at]) + dot_nt(
                    up_grad, w[half, :, u_at]
                )

            def store(gu, down):
                for i in range(2):
                    gu[i] = dot_nn(low_t[...], pair_s[i]).astype(BF16)
                down[0] = dot_nn(mlp_t[...], acts[half, :, g_at]).astype(BF16)

            @pl.when(half == 1)
            def _():
                store(gu_other, down_other)

            @pl.when(half == 0)
            def _():
                store(gu_own, down_own)

        @pl.when(step >= STEPS + PIECES)
        def _():
            r = step - STEPS - PIECES
            rows = pl.ds(pl.multiple_of(r * ROWS, ROWS), ROWS)
            back, hat1 = back_s[rows, :], hat_s[rows, :]
            hidden_grad = norm_back(back, hat1, scale_s[rows, :], gain1)
            hid_out[...] = hidden_grad
            att = hidden_grad.astype(BF16)
            att_out[...] = att
            ctxg_out[...] = dot_nt(att, wo[...]).astype(BF16)
            sums[0:1, :] += jnp.sum(back * hat1, axis=0, keepdims=True)
            sums[2:3, :] += jnp.sum(back, axis=0, keepdims=True)

    last = STEPS - 1
    row = lambda n: pl.BlockSpec((ROWS, n), lambda t, i: (jnp.minimum(t, last), 0))
    ending = pl.BlockSpec((ROWS, D), lambda t, i: (jnp.clip(t - STEPS - PIECES, 0, last), 0))
    half = STEPS // 2
    side = lambda t, mine: (jnp.clip(jnp.minimum(t, last) - half * mine, 0, half - 1), 0)
    mine = pl.BlockSpec((ROWS, D), lambda t, i: side(t, i[32]))
    leave = pl.BlockSpec((ROWS, D), lambda t, i: side(t, 1 - i[32]))
    each = PIECES // 2
    own = lambda lead: pl.BlockSpec(
        (lead, D, PIECE), lambda t, i: (0, 0, jnp.clip(t - STEPS - each, 0, each - 1))
    )
    theirs = lambda lead: pl.BlockSpec(
        (lead, D, PIECE), lambda t, i: (0, 0, jnp.clip(t - STEPS, 0, each - 1))
    )
    act = lambda n, t=BF16: jax.ShapeDtypeStruct((n, D), t)
    grads = lambda lead: jax.ShapeDtypeStruct((lead, D, HIDDEN), BF16)
    return pl.pallas_call(
        body,
        grid_spec=pltpu.PrefetchScalarGridSpec(
            num_scalar_prefetch=1,
            grid=(2 * STEPS + PIECES,),
            in_specs=[row(D)] + [row(GROUP)] * GROUPS + [row(D)] + [ANY] * 8,
            out_specs=[mine, leave, own(2), theirs(2), own(1), theirs(1)]
            + [ending] * 3
            + [pl.BlockSpec((8, D), lambda t, i: (0, 0))],
            scratch_shapes=[
                pltpu.VMEM((2, D, WIDE), BF16),
                pltpu.VMEM((D, D), BF16),
                pltpu.VMEM((2, 32, D // 32, REST), BF16),
                pltpu.VMEM((8, D), F32),
                pltpu.VMEM((2, SEQ, 2 * HIDDEN), BF16),
                pltpu.VMEM((2, SEQ, HIDDEN), BF16),
                pltpu.VMEM((D, SEQ), BF16),
                pltpu.VMEM((D, SEQ), BF16),
                pltpu.VMEM((SEQ, D), BF16),
                pltpu.VMEM((SEQ, D), F32),
                pltpu.VMEM((SEQ, D), F32),
                pltpu.VMEM((SEQ, 1), F32),
                pltpu.VMEM((2, SEQ, PIECE), BF16),
                pltpu.SemaphoreType.DMA((128,)),
            ],
        ),
        out_shape=[
            act(SEQ // 2),
            act(SEQ // 2),
            grads(2),
            grads(2),
            grads(1),
            grads(1),
            act(SEQ, F32),
            act(SEQ),
            act(SEQ),
            jax.ShapeDtypeStruct((8, D), F32),
        ],
        compiler_params=params(62),
        cost_estimate=cost(18 * SEQ * D * 2 * HIDDEN + 4 * SEQ * D * D, 40 << 20, 4 * SEQ * HIDDEN),
        name="middle",
    )(index, source, *ctx, cot, *pieces)


def rotary_lanes(segment_row):
    labels = jnp.arange(NDOC + 1, dtype=jnp.int32)
    before = jnp.sum((segment_row[None, :] < labels[:, None]).astype(jnp.int32), axis=1)
    member = segment_row[:, None] == labels[None, :]
    first = jnp.sum(jnp.where(member, before[None, :], 0), axis=1)
    position = (jnp.arange(SEQ, dtype=jnp.int32) - first).astype(F32)
    lane = jnp.arange(LANES) % (HEAD // 2)
    frequency = jnp.power(F32(1000.0), -2.0 * lane.astype(F32) / HEAD)
    angle = position[:, None] * frequency[None, :]
    sign = jnp.where(jnp.arange(LANES) % HEAD < HEAD // 2, -1.0, 1.0)
    ends = jnp.concatenate([before[1:], jnp.full((1,), SEQ, jnp.int32)])
    heads = segment_row[::BLOCK]
    tails = segment_row[BLOCK - 1 :: BLOCK]
    low = jnp.sum(jnp.where(heads[:, None] == labels[None, :], before[None, :], 0), axis=1)
    high = jnp.sum(jnp.where(tails[:, None] == labels[None, :], ends[None, :], 0), axis=1)
    bounds = jnp.concatenate([low // KEYS, (high + KEYS - 1) // KEYS]).astype(jnp.int32)
    return jnp.cos(angle), jnp.sin(angle) * sign[None, :], bounds


def sequence_device(
    tokens, segments, qkv_weight, out_weight, norm_gain, norm_shift, gate_up, down_weight, cotangent
):
    core = lax.axis_index("tensor")
    def ordered(mine, theirs):
        return jnp.where(
            core == 0, jnp.stack([mine, theirs], axis=0), jnp.stack([theirs, mine], axis=0)
        )

    pick = lambda a, i: lax.dynamic_index_in_dim(a, i, 0, keepdims=False)
    source = pick(tokens, core)
    segment_row = pick(segments, core)

    attn_block = qkv_weight.reshape(-1, 3 * D)
    gate_block = gate_up.reshape(-1, 2 * HIDDEN)
    tail_block = jnp.concatenate(
        [out_weight, norm_gain, norm_shift, jnp.zeros((D // 32, TAIL - D - 4), BF16)], axis=1
    )
    down_block = jnp.concatenate(
        [down_weight, jnp.concatenate([tail_block[:, :REST], tail_block[:, REST:]], axis=0)], axis=1
    )
    from_here, from_there = slot_blocks(-1, core), slot_blocks(-1, 1 - core)
    there_blocks = slot_blocks(1, core).reshape(2, 2, 4)
    to_here = there_blocks.transpose(1, 0, 2).reshape(16)
    deep_first = there_blocks.transpose(2, 1, 0).reshape(16)

    cot = ordered(pick(cotangent, core), core_swap(pick(cotangent, 1 - core))).reshape(SEQ, D)
    cosine, sine, bounds = rotary_lanes(segment_row)
    bounds = jnp.concatenate([bounds, core[None]]).astype(jnp.int32)
    tables = (cosine, sine, segment_row[:, None], segment_row[None, :])

    ahead = lambda parts: [part[None] for part in parts]
    gate_parts = depth_ring(gate_block)
    attn_four = pile(ahead(depth_parts(attn_block)), deps=(gate_parts[1],))
    attn_eight = pile(
        [attn_four, first_swap(attn_four)], deps=(gate_parts[2], source, cot, *tables)
    )
    attn_last = second_swap(attn_eight)
    index = jnp.concatenate([from_here * 2 + core, from_there * 2 + 1 - core]).astype(jnp.int32)
    weights = assemble(
        (attn_eight, attn_last),
        (core_swap(attn_eight), core_swap(attn_last)),
        index,
        deps=(gate_parts[3],),
    ).reshape(D, 3 * D)
    gate_four = pile(ahead(gate_parts))
    down_pair = pile([down_block[None], first_swap(down_block)[None]], deps=(gate_four,))
    saved0 = attn_forward(0, 1, bounds, source, weights, *tables, deps=(gate_four, down_pair))
    near, far = depth_shift(down_pair, 1), depth_shift(down_pair, 3)
    gate_eight = pile([gate_four, first_swap(gate_four)], deps=(saved0[4], near, far))
    gate_last = second_swap(gate_eight)
    saved1 = attn_forward(1, 1, bounds, source, weights, *tables, deps=(gate_eight,))
    down_eight = pile([down_pair, near, depth_shift(down_pair, 2), far], deps=(saved1[4],))
    saved2 = attn_forward(2, 1, bounds, source, weights, *tables, deps=(down_eight,))
    down_last, late_logs = lax.optimization_barrier((second_swap(down_eight), saved2[4]))
    saved2 = (*saved2[:4], late_logs)
    pieces = (gate_eight, gate_last, core_swap(gate_eight), core_swap(gate_last))
    pieces += (down_eight, down_last, core_swap(down_eight), core_swap(down_last))

    turned = lambda slots: slots.reshape(2, 2, 4).transpose(0, 2, 1).reshape(16)
    index = jnp.concatenate(
        [from_here, from_there, core[None], turned(from_here), turned(from_there)]
    ).astype(jnp.int32)
    ctx = (saved0[3], saved1[3], saved2[3])
    (out, out_leave, gu_here, gu_there, down_here, down_there, hidden_grad, att_grad, ctx_grad, sums) = (
        middle(index, source, ctx, cot, pieces)
    )

    gu_there, down_there = core_swap(gu_there), core_swap(down_there)
    output, placed = place(core, out, core_swap(out_leave))
    tail_mine, tail_theirs = out_grad(core, ctx, att_grad, sums)
    gu_keep, gu_send = join_rows(to_here, gu_here, gu_there, 2, deps=(tail_mine, placed))
    down_parts = join_rows(deep_first, down_here, down_there, 4, deps=(gu_send,))
    gu_first = first_swap(gu_send)
    passing = depth_shift(down_parts[3], 1)

    common = (source,) + tables
    back0 = attn_backward(0, 0, bounds, saved0, ctx_grad, *common, deps=(gu_send, down_parts[0]))
    (passing,) = fold(passing, down_parts[2], 1, deps=(back0[3],))
    back1 = attn_backward(0, 1, bounds, saved1, ctx_grad, *common, deps=(passing,))
    passing = depth_shift(passing, 1)
    (passing,) = fold(passing, down_parts[1], 1, deps=(back1[3],))
    gu_keep, gu_send = fold(gu_keep, gu_first, 2, deps=(back1[3],))
    gu_second = second_swap(gu_send)
    early_keep, early_send = join_dealt(
        to_here,
        (back0[1], back1[1], tail_mine),
        (core_swap(back0[2]), core_swap(back1[2]), core_swap(tail_theirs)),
        deps=(passing, gu_send),
    )
    early_first = first_swap(early_send)
    back2 = attn_backward(0, 2, bounds, saved2, ctx_grad, *common, deps=(gu_send, early_send, passing))

    deep = lambda parts: [parts[0]] + [depth_shift(parts[k], k) for k in (1, 2, 3)]
    passing = depth_shift(passing, 1)
    gu_parts = fold(gu_keep, gu_second, 4, deps=(back2[3],))
    down_keep, down_send = fold(passing, down_parts[0], 2, deps=(gu_parts[0],))
    late_keep, late_send = join_dealt(
        to_here, (back2[1],), (core_swap(back2[2]),), deps=(down_send, early_first)
    )
    late_first = first_swap(late_send)
    down_keep, down_send = fold(down_keep, first_swap(down_send), 2, deps=(late_send,))
    down_second = second_swap(down_send)
    (gu_total,) = fold(depth_shift(gu_parts[3], 1), gu_parts[2], 1, deps=(down_send,))
    attn_keep, attn_send = fold_pair(
        (early_keep, late_keep), (early_first, late_first), deps=(gu_total,)
    )
    attn_second = second_swap(attn_send)
    grad, grad_leave, added = input_back(
        core, hidden_grad, (back0[0], back1[0], back2[0]), weights, deps=(attn_send,)
    )
    (gu_total,) = fold(depth_shift(gu_total, 1), gu_parts[1], 1, deps=(added,))
    attn_parts = list(fold(attn_keep, attn_second, 4, deps=(gu_total,)))
    grad_leave, attn_parts[0] = lax.optimization_barrier((grad_leave, attn_parts[0]))
    attn_parts = deep(attn_parts)
    grad, placed = place(core, grad, core_swap(grad_leave))
    (gu_total,) = fold(depth_shift(gu_total, 1), gu_parts[0], 1, F32)
    down_total = (down_keep.astype(F32) + down_second.astype(F32))[0]
    gu_total = gu_total[0]
    qkv_total, out_total, gain_total, shift_total = finish(attn_parts, deps=(placed,))

    return (
        output,
        grad,
        qkv_total,
        out_total,
        gain_total,
        shift_total,
        gu_total.reshape(-1, 2, HIDDEN),
        down_total,
    )


def solution(mesh):
    in_specs = (
        P("dp", None, None),
        P("dp", None),
        P(("dp", "tensor"), None, None),
        P(("dp", "tensor"), None),
        P(("dp", "tensor"), None),
        P(("dp", "tensor"), None),
        P("dp", None, "tensor"),
        P("dp", "tensor"),
        P("dp", "tensor", None),
    )
    out_specs = (
        P("dp", "tensor", None),
        P("dp", "tensor", None),
        P(("dp", "tensor"), None, None),
        P(("dp", "tensor"), None),
        P(("dp", "tensor"), None),
        P(("dp", "tensor"), None),
        P("dp", None, "tensor"),
        P("dp", "tensor"),
    )
    sizes = dict(mesh.shape)

    def per_device(tokens, *others):
        if sizes["dp"] == 16 and sizes["tensor"] == 2 and tokens.shape[0] == 2:
            return sequence_device(tokens, *others)
        return general_device(tokens, *others)

    return jax.shard_map(
        per_device, mesh=mesh, in_specs=in_specs, out_specs=out_specs, check_vma=False
    )
```

```python
import jax
import jax.numpy as jnp
from jax import lax
from jax.experimental import pallas as pl
from jax.experimental.pallas import tpu as pltpu
from jax.sharding import PartitionSpec as P

D = 768
HEADS = 12
HEAD = 64
SEQ = 1024
NDOC = 8


EPSILON = 1e-05
MASKED = -1e30


def for_sending(value):
    return jax.tree.map(lambda a: a.astype(jnp.bfloat16) if a.dtype == jnp.float32 else a, value)


def rotary_tables(segment_row):
    labels = jnp.arange(NDOC + 1, dtype=jnp.int32)
    member = (segment_row[:, None] == labels[None, :]).astype(jnp.int32)
    counts = jnp.sum(member, axis=0)
    starts = jnp.concatenate([jnp.zeros((1,), jnp.int32), jnp.cumsum(counts)[:-1]])
    offset = jnp.sum(member * starts[None, :], axis=1)
    position = (jnp.arange(SEQ, dtype=jnp.int32) - offset).astype(jnp.float32)
    exponent = -2.0 * jnp.arange(HEAD // 2).astype(jnp.float32) / HEAD
    frequency = jnp.power(jnp.float32(1000.0), exponent)
    angle = position[:, None] * frequency[None, :]
    return (jnp.cos(angle)[:, None, :], jnp.sin(angle)[:, None, :])


def rotate(vector, cosine, sine):
    half = vector.shape[-1] // 2
    first_half = vector[..., :half]
    second_half = vector[..., half:]
    return jnp.concatenate(
        [first_half * cosine - second_half * sine, second_half * cosine + first_half * sine],
        axis=-1,
    )


def unrotate(gradient, cosine, sine):

    def turned(vector):
        return rotate(vector, cosine, sine)

    _, pullback = jax.vjp(turned, gradient)
    return pullback(gradient)[0]


def layer_norm(vector, gain, shift):
    center = vector - jnp.mean(vector, axis=-1, keepdims=True)
    variance = jnp.mean(center * center, axis=-1, keepdims=True)
    return center * lax.rsqrt(variance + EPSILON) * gain + shift


def swiglu_piece(gate, upper):
    return jax.nn.silu(gate) * upper


def accumulate(total, term):
    if total is None:
        return term
    return tuple((left + right for left, right in zip(total, term)))


def general_device(
    tokens, segments, qkv_weight, out_weight, norm_gain, norm_shift, gate_up, down_weight, cotangent
):
    tensor_size = lax.axis_size("tensor")
    own_rows = SEQ // tensor_size
    row_start = lax.axis_index("tensor") * own_rows
    score_scale = HEAD ** (-0.5)
    qkv_full, out_full, gain_full, shift_full = (
        lax.all_gather(qkv_weight, ("dp", "tensor"), axis=0, tiled=True),
        lax.all_gather(out_weight, ("dp", "tensor"), axis=0, tiled=True),
        lax.all_gather(norm_gain, ("dp", "tensor"), axis=0, tiled=True),
        lax.all_gather(norm_shift, ("dp", "tensor"), axis=0, tiled=True),
    )
    gains = gain_full.astype(jnp.float32)
    shifts = shift_full.astype(jnp.float32)
    gate_up_full, down_full = (
        lax.all_gather(gate_up, "dp", axis=0, tiled=True),
        lax.all_gather(down_weight, "dp", axis=0, tiled=True),
    )
    batches = tokens.shape[0]
    outputs = []
    input_grads = []
    attn_total = None
    mlp_total = None
    for batch_index in range(batches):
        source = tokens[batch_index]
        own_source = lax.dynamic_slice_in_dim(source, row_start, own_rows, 0)
        segment_row = segments[batch_index]
        cosine, sine = rotary_tables(segment_row)
        own_cos = lax.dynamic_slice_in_dim(cosine, row_start, own_rows, 0)
        own_sin = lax.dynamic_slice_in_dim(sine, row_start, own_rows, 0)
        query_proj = jnp.einsum(
            "sd,de->se", own_source, qkv_full[:, 0], preferred_element_type=jnp.float32
        )
        pair_proj = jnp.einsum(
            "sd,dke->ske", source, qkv_full[:, 1:], preferred_element_type=jnp.float32
        )
        keys = rotate(pair_proj[:, 0].reshape(SEQ, HEADS, HEAD), cosine, sine).astype(jnp.bfloat16)
        values = pair_proj[:, 1].reshape(SEQ, HEADS, HEAD).astype(jnp.bfloat16)
        queries = rotate(query_proj.reshape(own_rows, HEADS, HEAD), own_cos, own_sin).astype(
            jnp.bfloat16
        )
        own_segments = lax.dynamic_slice_in_dim(segment_row, row_start, own_rows, 0)
        allowed = (own_segments[:, None] == segment_row[None, :])[None]
        raw_scores = (
            jnp.einsum("qhe,khe->hqk", queries, keys, preferred_element_type=jnp.float32)
            * score_scale
        )
        masked = jnp.where(allowed, raw_scores, MASKED)
        top_score = jnp.max(masked, axis=-1, keepdims=True)
        logsum = top_score + jnp.log(jnp.sum(jnp.exp(masked - top_score), axis=-1, keepdims=True))
        probs_low = jnp.exp(masked - logsum).astype(jnp.bfloat16)
        context = (
            jnp.einsum("hqk,khe->qhe", probs_low, values, preferred_element_type=jnp.float32)
            .reshape(own_rows, D)
            .astype(jnp.bfloat16)
        )
        attended = jnp.dot(context, out_full, preferred_element_type=jnp.float32)
        hidden_in = own_source.astype(jnp.float32) + attended
        normed = layer_norm(hidden_in, gains[:, 0], shifts[:, 0])
        normed_all = lax.all_gather(normed.astype(jnp.bfloat16), "tensor", axis=0, tiled=True)
        gate_pair = jnp.einsum(
            "sd,dkf->skf", normed_all, gate_up_full, preferred_element_type=jnp.float32
        )
        swiglu = swiglu_piece(gate_pair[:, 0], gate_pair[:, 1]).astype(jnp.bfloat16)
        mlp_out = lax.psum_scatter(
            jnp.einsum("sf,df->sd", swiglu, down_full, preferred_element_type=jnp.float32).astype(
                jnp.bfloat16
            ),
            "tensor",
            scatter_dimension=0,
            tiled=True,
        ).astype(jnp.float32)
        resid = normed + mlp_out
        outputs.append(layer_norm(resid, gains[:, 1], shifts[:, 1]).astype(jnp.bfloat16))
        upstream = cotangent[batch_index].astype(jnp.float32)
        _, second_pull = jax.vjp(layer_norm, resid, gains[:, 1], shifts[:, 1])
        resid_grad, gain_two, shift_two = second_pull(upstream)
        mlp_grad = lax.all_gather(resid_grad.astype(jnp.bfloat16), "tensor", axis=0, tiled=True)
        swiglu_grad = jnp.einsum(
            "sd,df->sf", mlp_grad, down_full, preferred_element_type=jnp.float32
        )
        _, glu_pull = jax.vjp(swiglu_piece, gate_pair[:, 0], gate_pair[:, 1])
        gate_grad, upper_grad = glu_pull(swiglu_grad)
        pair_grad = jnp.stack([gate_grad, upper_grad], axis=1).astype(jnp.bfloat16)
        down_term = jnp.einsum("sd,sf->df", mlp_grad, swiglu, preferred_element_type=jnp.float32)
        gate_up_term = jnp.einsum(
            "sd,skf->dkf", normed_all, pair_grad, preferred_element_type=jnp.float32
        )
        normed_grad = resid_grad + lax.psum_scatter(
            jnp.einsum("skf,dkf->sd", pair_grad, gate_up_full, preferred_element_type=jnp.float32),
            "tensor",
            scatter_dimension=0,
            tiled=True,
        )
        _, first_pull = jax.vjp(layer_norm, hidden_in, gains[:, 0], shifts[:, 0])
        hidden_grad, gain_one, shift_one = first_pull(normed_grad)
        attended_grad = hidden_grad.astype(jnp.bfloat16)
        out_term = jnp.einsum(
            "sd,se->de", context, attended_grad, preferred_element_type=jnp.float32
        )
        context_grad = (
            jnp.einsum("se,de->sd", attended_grad, out_full, preferred_element_type=jnp.float32)
            .astype(jnp.bfloat16)
            .reshape(own_rows, HEADS, HEAD)
        )
        probs = jnp.exp(masked - logsum)
        weights_grad = jnp.einsum(
            "qhe,khe->hqk", context_grad, values, preferred_element_type=jnp.float32
        )
        row_delta = jnp.sum(probs * weights_grad, axis=-1, keepdims=True)
        score_grad = (probs * (weights_grad - row_delta)).astype(jnp.bfloat16)
        query_grad = (
            jnp.einsum("hqk,khe->qhe", score_grad, keys, preferred_element_type=jnp.float32)
            * score_scale
        )
        key_part = (
            jnp.einsum("hqk,qhe->khe", score_grad, queries, preferred_element_type=jnp.float32)
            * score_scale
        )
        value_part = jnp.einsum(
            "hqk,qhe->khe", probs_low, context_grad, preferred_element_type=jnp.float32
        )
        key_value = lax.psum_scatter(
            jnp.stack(
                [
                    key_part.reshape(lax.axis_size("tensor") * own_rows, D),
                    value_part.reshape(lax.axis_size("tensor") * own_rows, D),
                ],
                axis=1,
            ).astype(jnp.bfloat16),
            "tensor",
            scatter_dimension=0,
            tiled=True,
        ).astype(jnp.float32)
        query_back = unrotate(query_grad, own_cos, own_sin).reshape(own_rows, D)
        key_back = unrotate(
            key_value[:, 0].reshape(own_rows, HEADS, HEAD), own_cos, own_sin
        ).reshape(own_rows, D)
        proj_grad = jnp.stack([query_back, key_back, key_value[:, 1]], axis=1).astype(jnp.bfloat16)
        input_grads.append(
            hidden_grad
            + jnp.einsum("ske,dke->sd", proj_grad, qkv_full, preferred_element_type=jnp.float32)
        )
        qkv_term = jnp.einsum(
            "sd,ske->dke", own_source, proj_grad, preferred_element_type=jnp.float32
        )
        gain_term = jnp.stack([gain_one, gain_two], axis=1)
        shift_term = jnp.stack([shift_one, shift_two], axis=1)
        attn_terms = (qkv_term, out_term, gain_term, shift_term)
        mlp_terms = (gate_up_term, down_term)
        attn_total = accumulate(attn_total, attn_terms)
        mlp_total = accumulate(mlp_total, mlp_terms)
    attn_final = lax.psum_scatter(attn_total, ("dp", "tensor"), scatter_dimension=0, tiled=True)
    mlp_final = jax.tree.map(
        lambda part: part.astype(jnp.float32),
        lax.psum_scatter(for_sending(mlp_total), "dp", scatter_dimension=0, tiled=True),
    )
    return (
        jnp.stack(outputs, axis=0),
        jnp.stack(input_grads, axis=0),
        attn_final[0],
        attn_final[1],
        attn_final[2],
        attn_final[3],
        mlp_final[0],
        mlp_final[1],
    )


HIDDEN = 1536
WIDE = 3 * HIDDEN
REST = 512
TAIL = 2 * REST
GROUP = 4 * HEAD
GROUPS = D // GROUP
KEYS = 128
LANES = 2 * HEAD
BLOCK = 256
NBLOCK = SEQ // BLOCK
ROWS = 256
STEPS = SEQ // ROWS
CHUNK = 768
PIECE = 256
PIECES = 2 * HIDDEN // PIECE
LOG2E = 1.4426950408889634
F32 = jnp.float32
BF16 = jnp.bfloat16


def across(value, move):
    pairs = []
    for z in range(4):
        for y in range(2):
            for x in range(2):
                for c in range(2):
                    tz, ty, tx, tc = move(z, y, x, c)
                    pairs.append((((z * 2 + y) * 2 + x) * 2 + c, ((tz * 2 + ty) * 2 + tx) * 2 + tc))
    return lax.ppermute(value, ("dp", "tensor"), pairs)


def core_swap(value):
    return across(value, lambda z, y, x, c: (z, y, x, 1 - c))


def first_swap(value):
    return across(value, lambda z, y, x, c: (z, y, 1 - x, c) if c == 0 else (z, 1 - y, x, c))


def second_swap(value):
    return across(value, lambda z, y, x, c: (z, 1 - y, x, c) if c == 0 else (z, y, 1 - x, c))


def depth_shift(value, steps):
    return across(value, lambda z, y, x, c: ((z + steps) % 4, y, x, c))


def slot_blocks(sign, core):
    me = lax.axis_index("dp")
    z, y, x = me // 4, (me // 2) % 2, me % 2
    slot = jnp.arange(16, dtype=jnp.int32)
    second, first, depth = slot // 8, (slot // 4) % 2, slot % 4
    x_bit = jnp.where(core == 0, first, second)
    y_bit = jnp.where(core == 0, second, first)
    return (((z + sign * depth) % 4) * 4 + (y ^ y_bit) * 2 + (x ^ x_bit)).astype(jnp.int32)


def depth_parts(block):
    return [block] + [depth_shift(block, k) for k in (1, 2, 3)]


def depth_ring(block):
    parts = [block]
    for _ in range(3):
        parts.append(depth_shift(parts[-1], 1))
    return parts


def cost(flops, nbytes, trans=0):
    return pl.CostEstimate(flops=int(flops), bytes_accessed=int(nbytes), transcendentals=int(trans))


def params(vmem_mb, sem=("arbitrary",)):
    return pltpu.CompilerParams(dimension_semantics=sem, vmem_limit_bytes=vmem_mb << 20)


ANY = pl.BlockSpec(memory_space=pl.ANY)
AFTER = pl.BlockSpec(memory_space=pltpu.HBM)


def pile(parts, deps=()):
    spans, start = [], 0
    for part in parts:
        spans.append((start, part.shape[0]))
        start += part.shape[0]

    def body(*refs):
        ins, out, sem = refs[: len(parts)], refs[-2], refs[-1]
        copies = [
            pltpu.make_async_copy(ref, out.at[pl.ds(at, n)], sem.at[i])
            for i, (ref, (at, n)) in enumerate(zip(ins, spans))
        ]
        for cp in copies:
            cp.start()
        for cp in copies:
            cp.wait()

    shape = (start,) + parts[0].shape[1:]
    return pl.pallas_call(
        body,
        in_specs=[ANY] * len(parts) + [AFTER] * len(deps),
        out_specs=pl.BlockSpec(memory_space=pltpu.VMEM),
        out_shape=jax.ShapeDtypeStruct(shape, parts[0].dtype),
        scratch_shapes=[pltpu.SemaphoreType.DMA((len(parts),))],
        compiler_params=params(16, None),
        cost_estimate=cost(0, 4 * start * shape[1] * shape[2]),
        name="pile",
    )(*parts, *deps)


def place(core, mine, there):
    def body(c, a, b, out, token, held, sem):
        first = pltpu.make_async_copy(a, held.at[c[0]], sem.at[0])
        second = pltpu.make_async_copy(b, held.at[1 - c[0]], sem.at[1])
        first.start()
        second.start()
        first.wait()
        second.wait()
        last = pltpu.make_async_copy(held, out, sem.at[2])
        last.start()
        last.wait()
        token[...] = jnp.zeros_like(token)

    return pl.pallas_call(
        body,
        grid_spec=pltpu.PrefetchScalarGridSpec(
            num_scalar_prefetch=1,
            grid=(1,),
            in_specs=[ANY, ANY],
            out_specs=[AFTER, pl.BlockSpec((8, LANES), lambda i, c: (0, 0))],
            scratch_shapes=[
                pltpu.VMEM((2,) + mine.shape, mine.dtype),
                pltpu.SemaphoreType.DMA((3,)),
            ],
        ),
        out_shape=[jax.ShapeDtypeStruct((2,) + mine.shape, mine.dtype), TOKEN],
        compiler_params=params(60),
        cost_estimate=cost(0, 4 * mine.size),
        name="place",
    )(core[None], mine, there)


def assemble(own, other, index, deps=()):
    def body(idx, a, b, c, d, *rest):
        out, sem = rest[-2:]
        copies = []
        for i, ref in enumerate((a, b, c, d)):
            for s in range(8):
                copies.append(
                    pltpu.make_async_copy(ref.at[s], out.at[idx[i * 8 + s]], sem.at[i * 8 + s])
                )
        for cp in copies:
            cp.start()
        for cp in copies:
            cp.wait()

    rows, wide = own[0].shape[1:]
    return pl.pallas_call(
        body,
        grid_spec=pltpu.PrefetchScalarGridSpec(
            num_scalar_prefetch=1,
            grid=(1,),
            in_specs=[ANY] * 4 + [AFTER] * len(deps),
            out_specs=pl.BlockSpec((32, rows, wide), lambda i, c: (0, 0, 0)),
            scratch_shapes=[pltpu.SemaphoreType.DMA((32,))],
        ),
        out_shape=jax.ShapeDtypeStruct((32, rows, wide), BF16),
        compiler_params=params(60),
        cost_estimate=cost(0, 4 * 32 * rows * wide),
        name="assemble",
    )(index, *own, *other, *deps)


def turn(vector, cosine, sine):
    lane = lax.broadcasted_iota(jnp.int32, vector.shape, 1)
    swapped = jnp.where(
        lane % HEAD < HEAD // 2,
        pltpu.roll(vector, LANES - HEAD // 2, 1),
        pltpu.roll(vector, HEAD // 2, 1),
    )
    return vector * cosine + swapped * sine


def dot_nn(a, b):
    return lax.dot_general(a, b, (((1,), (0,)), ((), ())), preferred_element_type=F32)


def dot_nt(a, b):
    return lax.dot_general(a, b, (((1,), (1,)), ((), ())), preferred_element_type=F32)


def dot_tn(a, b):
    return lax.dot_general(a, b, (((0,), (0,)), ((), ())), preferred_element_type=F32)


TOKEN = jax.ShapeDtypeStruct((8, LANES), F32)


def stacked(low_lane, pair):
    zero = jnp.zeros_like(pair)
    return jnp.concatenate(
        [jnp.where(low_lane, pair, zero), jnp.where(low_lane, zero, pair)], axis=0
    )


def windows(bnd, i, work):
    blocks = (bnd[NBLOCK + i] - bnd[i] + BLOCK // KEYS - 1) // (BLOCK // KEYS)
    for width in range(NBLOCK - 1, NBLOCK + 1):

        @pl.when(jnp.maximum(blocks, NBLOCK - 1) == width)
        def _():
            low = jnp.minimum(bnd[i], (SEQ - width * BLOCK) // KEYS)
            work(pl.ds(pl.multiple_of(low * KEYS, KEYS), width * BLOCK))


def attn_forward(first, count, bounds, source, weights, cosine, sine, seg_col, seg_row, deps=()):
    def body(bnd, x, wq, wk, wv, cos, sin, sc, sr, *rest):
        q_out, k_out, v_out, ctx_out, lse_out, qm = rest[len(deps) :]
        low_lane = lax.broadcasted_iota(jnp.int32, (BLOCK, LANES), 1) < HEAD

        @pl.loop(0, NBLOCK)
        def _(r):
            rows = pl.ds(pl.multiple_of(r * BLOCK, BLOCK), BLOCK)
            xr, cr, sn = x[rows, :], cos[rows, :], sin[rows, :]
            q_proj, k_proj = dot_nn(xr, wq[...]), dot_nn(xr, wk[...])
            v_out[rows, :] = dot_nn(xr, wv[...]).astype(BF16)
            for p in range(GROUP // LANES):
                ln = slice(p * LANES, (p + 1) * LANES)
                q = turn(q_proj[:, ln], cr, sn).astype(BF16) * jnp.asarray(HEAD**-0.5, BF16)
                q_out[rows, ln] = q
                qm[p, r] = stacked(low_lane, q)
                k_out[rows, ln] = turn(k_proj[:, ln], cr, sn).astype(BF16)

        def block(i, _):
            rows = pl.ds(pl.multiple_of(i * BLOCK, BLOCK), BLOCK)
            own = jnp.concatenate([sc[rows, :], sc[rows, :]], axis=0)

            def work(cols):
                seen = own == sr[:, cols]
                for p in range(GROUP // LANES):
                    ln = slice(p * LANES, (p + 1) * LANES)
                    s = jnp.where(seen, dot_nt(qm[p, i], k_out[cols, ln]) * LOG2E, MASKED)
                    top = jnp.max(s, axis=1, keepdims=True)
                    e = jnp.exp2(s - top)
                    total = jnp.sum(e, axis=1, keepdims=True)
                    mixed = dot_nn(e.astype(BF16), v_out[cols, ln]) / total
                    ctx_out[rows, ln] = jnp.where(low_lane, mixed[:BLOCK], mixed[BLOCK:]).astype(BF16)
                    logs = top + jnp.log2(total)
                    flipped = jnp.where(low_lane, logs[:BLOCK], logs[BLOCK:]).T
                    lse_out[0, 2 * p : 2 * p + 1, rows] = flipped[0:1]
                    lse_out[0, 2 * p + 1 : 2 * p + 2, rows] = flipped[HEAD : HEAD + 1]

            windows(bnd, i, work)
            return 0

        lax.fori_loop(0, NBLOCK, block, 0)

    full = lambda shape: pl.BlockSpec(shape, lambda p, b: (0,) * len(shape))
    column = lambda shift: pl.BlockSpec((D, GROUP), lambda p, b: (0, shift * GROUPS + first + p))
    part = pl.BlockSpec((SEQ, GROUP), lambda p, b: (0, p))
    act = jax.ShapeDtypeStruct((SEQ, count * GROUP), BF16)
    return pl.pallas_call(
        body,
        grid_spec=pltpu.PrefetchScalarGridSpec(
            num_scalar_prefetch=1,
            grid=(count,),
            in_specs=[
                full((SEQ, D)),
                column(0),
                column(1),
                column(2),
                full((SEQ, LANES)),
                full((SEQ, LANES)),
                full((SEQ, 1)),
                full((1, SEQ)),
            ]
            + [AFTER] * len(deps),
            out_specs=[part] * 4 + [pl.BlockSpec((1, 8, SEQ), lambda p, b: (p, 0, 0))],
            scratch_shapes=[pltpu.VMEM((GROUP // LANES, NBLOCK, 2 * BLOCK, LANES), BF16)],
        ),
        out_shape=[act] * 4 + [jax.ShapeDtypeStruct((count, 8, SEQ), F32)],
        compiler_params=params(60),
        cost_estimate=cost(
            count * GROUP * (6 * SEQ * D + 16 * SEQ * SEQ), 8 << 20, count * 4 * SEQ * SEQ
        ),
        name="attn_forward",
    )(bounds, source, weights, weights, weights, cosine, sine, seg_col, seg_row, *deps)


def deal(core, whole, mine, theirs, columns):
    parts = whole.reshape(16, 2, D // 32, whole.shape[1])
    first, second = parts[:, 0], parts[:, 1]
    mine[:, :, columns] = jnp.where(core == 0, first, second).astype(BF16)
    theirs[:, :, columns] = jnp.where(core == 0, second, first).astype(BF16)


def attn_backward(at, grad_at, bounds, saved, ctx_grad, source, cosine, sine, seg_col, seg_row, deps=()):
    def body(bnd, q, k, v, o, do, lse, x, cos, sin, sc, sr, *rest):
        core = bnd[2 * NBLOCK]
        out, mine, theirs, token, qm, dm, dq, dk, dv, dl = rest[len(deps) :]
        token[...] = jnp.zeros_like(token)
        low_lane = lax.broadcasted_iota(jnp.int32, (BLOCK, LANES), 1) < HEAD
        row = lax.broadcasted_iota(jnp.int32, (8, LANES), 0)
        lane = lax.broadcasted_iota(jnp.int32, (8, LANES), 1)
        pick = jnp.where(row == lane // HEAD, 1.0, 0.0).astype(F32)
        for p in range(GROUP // LANES):
            ln = slice(p * LANES, (p + 1) * LANES)

            @pl.loop(0, NBLOCK)
            def _(i):
                rows = pl.ds(pl.multiple_of(i * BLOCK, BLOCK), BLOCK)
                qm[p, i] = stacked(low_lane, q[rows, ln])
                dm[p, i] = stacked(low_lane, do[rows, ln])

            dl[p] = lax.dot_general(
                pick,
                do[:, ln].astype(F32) * o[:, ln].astype(F32),
                (((1,), (1,)), ((), ())),
                preferred_element_type=F32,
                precision=lax.Precision.HIGHEST,
            )
        dk[...] = jnp.zeros_like(dk)
        dv[...] = jnp.zeros_like(dv)

        def block(i, _):
            rows = pl.ds(pl.multiple_of(i * BLOCK, BLOCK), BLOCK)
            own = jnp.concatenate([sr[:, rows], sr[:, rows]], axis=1)

            def work(cols):
                seen = sc[cols, :] == own
                for p in range(GROUP // LANES):
                    ln = slice(p * LANES, (p + 1) * LANES)
                    keys, values, qq, dd = k[cols, ln], v[cols, ln], qm[p, i], dm[p, i]
                    logs = jnp.concatenate(
                        [lse[0, 2 * p : 2 * p + 1, rows], lse[0, 2 * p + 1 : 2 * p + 2, rows]], axis=1
                    )
                    deltas = jnp.concatenate([dl[p, 0:1, rows], dl[p, 1:2, rows]], axis=1)
                    s = dot_nt(keys, qq) * LOG2E - logs
                    probs = jnp.exp2(jnp.where(seen, s, MASKED))
                    g = (probs * (dot_nt(values, dd) - deltas)).astype(BF16)
                    dv[cols, ln] += dot_nn(probs.astype(BF16), dd)
                    dk[cols, ln] += dot_nn(g, qq)
                    both = dot_tn(g, keys)
                    dq[rows, ln] = jnp.where(low_lane, both[:BLOCK], both[BLOCK:])

            windows(bnd, i, work)
            return 0

        lax.fori_loop(0, NBLOCK, block, 0)

        @pl.loop(0, NBLOCK)
        def _(r):
            rows = pl.ds(pl.multiple_of(r * BLOCK, BLOCK), BLOCK)
            cr, sn = cos[rows, :], -sin[rows, :]
            for p in range(GROUP // LANES):
                ln = slice(p * LANES, (p + 1) * LANES)
                out[0, rows, ln] = turn(dq[rows, ln] * (HEAD**-0.5), cr, sn).astype(BF16)
                out[1, rows, ln] = turn(dk[rows, ln], cr, sn).astype(BF16)
                out[2, rows, ln] = dv[rows, ln].astype(BF16)

        grads = jnp.concatenate([out[i] for i in range(3)], axis=1)
        deal(core, dot_tn(x[...], grads), mine, theirs, slice(0, 3 * GROUP))

    full = lambda shape: pl.BlockSpec(shape, lambda p, b: (0,) * len(shape))
    part = pl.BlockSpec((SEQ, GROUP), lambda p, b: (0, at))
    low2 = pltpu.VMEM((GROUP // LANES, NBLOCK, 2 * BLOCK, LANES), BF16)
    wide = pltpu.VMEM((SEQ, GROUP), F32)
    dealt = (16, D // 32, 3 * GROUP)
    return pl.pallas_call(
        body,
        grid_spec=pltpu.PrefetchScalarGridSpec(
            num_scalar_prefetch=1,
            grid=(1,),
            in_specs=[part] * 4
            + [
                pl.BlockSpec((SEQ, GROUP), lambda p, b: (0, grad_at)),
                pl.BlockSpec((1, 8, SEQ), lambda p, b: (at, 0, 0)),
                full((SEQ, D)),
                full((SEQ, LANES)),
                full((SEQ, LANES)),
                full((SEQ, 1)),
                full((1, SEQ)),
            ]
            + [AFTER] * len(deps),
            out_specs=[full((3, SEQ, GROUP)), full(dealt), full(dealt), full((8, LANES))],
            scratch_shapes=[
                low2,
                low2,
                wide,
                wide,
                wide,
                pltpu.VMEM((GROUP // LANES, 8, SEQ), F32),
            ],
        ),
        out_shape=[
            jax.ShapeDtypeStruct((3, SEQ, GROUP), BF16),
            jax.ShapeDtypeStruct(dealt, BF16),
            jax.ShapeDtypeStruct(dealt, BF16),
            TOKEN,
        ],
        compiler_params=params(60),
        cost_estimate=cost(GROUP * (40 * SEQ * SEQ + 6 * SEQ * D), 10 << 20, 4 * SEQ * SEQ),
        name="attn_backward",
    )(bounds, *saved[:4], ctx_grad, saved[4], source, cosine, sine, seg_col, seg_row, *deps)


def join_rows(index, here, there, count, deps=(), columns=512):
    lead, _, wide = here.shape
    rows = D // 16
    each = 16 // count
    steps = wide // columns

    def body(idx, a, b, *rest):
        outs = rest[len(deps) :]
        for s in range(16):
            at = pl.ds(pl.multiple_of(idx[s] * rows, 16), rows)
            total = a[0, at, :].astype(F32) + b[0, at, :].astype(F32)
            outs[s // each][s % each] = total.astype(BF16)

    whole = pl.BlockSpec((1, D, columns), lambda l, n, i: (l, 0, n))
    part = pl.BlockSpec((each, rows, columns), lambda l, n, i: (0, 0, l * steps + n))
    return pl.pallas_call(
        body,
        grid_spec=pltpu.PrefetchScalarGridSpec(
            num_scalar_prefetch=1,
            grid=(lead, steps),
            in_specs=[whole, whole] + [AFTER] * len(deps),
            out_specs=[part] * count,
        ),
        out_shape=[jax.ShapeDtypeStruct((each, rows, lead * wide), BF16)] * count,
        compiler_params=params(60, ("arbitrary", "arbitrary")),
        cost_estimate=cost(D * wide * lead, 6 * D * wide * lead),
        name="join_rows",
    )(index, here, there, *deps)


def out_grad(core, ctx, right, norms):
    def body(c, *refs):
        parts, (b, nrm, mine, theirs) = refs[:GROUPS], refs[GROUPS:]
        whole = jnp.concatenate([dot_tn(p[...], b[...]) for p in parts], axis=0)
        deal(c[0], whole, mine, theirs, slice(0, D))
        flipped = jnp.concatenate([nrm[...], jnp.zeros((LANES - 8, D), F32)], axis=0).T
        filled = jnp.concatenate([flipped, jnp.zeros((D, LANES), F32)], axis=1)
        deal(c[0], filled, mine, theirs, slice(D, TAIL))

    full = lambda shape: pl.BlockSpec(shape, lambda p, b: (0,) * len(shape))
    dealt = (16, D // 32, TAIL)
    return pl.pallas_call(
        body,
        grid_spec=pltpu.PrefetchScalarGridSpec(
            num_scalar_prefetch=1,
            grid=(1,),
            in_specs=[full((SEQ, GROUP))] * GROUPS + [full((SEQ, D)), full((8, D))],
            out_specs=[full(dealt), full(dealt)],
        ),
        out_shape=[jax.ShapeDtypeStruct(dealt, BF16)] * 2,
        compiler_params=params(60),
        cost_estimate=cost(2 * SEQ * D * D, 8 << 20),
        name="out_grad",
    )(core[None], *ctx, right, norms)


def join_dealt(index, mine, there, deps=()):
    widths = [m.shape[2] for m in mine]
    wide, rows, count = sum(widths), D // 32, len(mine)

    def body(idx, *refs):
        ours, others, keep, send = refs[:count], refs[count : 2 * count], refs[-2], refs[-1]
        for s in range(16):
            start = 0
            for a, b, n in zip(ours, others, widths):
                total = a[idx[s]].astype(F32) + b[idx[s]].astype(F32)
                (keep, send)[s // 8][s % 8, :, start : start + n] = total.astype(BF16)
                start += n

    full = lambda shape: pl.BlockSpec(shape, lambda p, b: (0,) * len(shape))
    half = (8, rows, wide)
    return pl.pallas_call(
        body,
        grid_spec=pltpu.PrefetchScalarGridSpec(
            num_scalar_prefetch=1,
            grid=(1,),
            in_specs=[full((16, rows, n)) for n in widths] * 2 + [AFTER] * len(deps),
            out_specs=[full(half), full(half)],
        ),
        out_shape=[jax.ShapeDtypeStruct(half, BF16)] * 2,
        compiler_params=params(24),
        cost_estimate=cost(D * wide // 2, 3 * D * wide),
        name="join_dealt",
    )(index, *mine, *there, *deps)


def fold(keep, there, count, dtype=BF16, deps=()):
    blocks, rows, wide = keep.shape
    each = blocks // count

    def body(a, b, *rest):
        for n, out in enumerate(rest[len(deps) :]):
            at = slice(n * each, (n + 1) * each)
            out[...] = (a[at].astype(F32) + b[at].astype(F32)).astype(dtype)

    steps = 2 if blocks * rows * wide > 1 << 19 else 1
    columns = wide // steps
    part = pl.BlockSpec((blocks, rows, columns), lambda i: (0, 0, i))
    return pl.pallas_call(
        body,
        grid=(steps,),
        in_specs=[part, part] + [AFTER] * len(deps),
        out_specs=[pl.BlockSpec((each, rows, columns), lambda i: (0, 0, i))] * count,
        out_shape=[jax.ShapeDtypeStruct((each, rows, wide), dtype)] * count,
        compiler_params=params(16),
        cost_estimate=cost(blocks * rows * wide, 6 * blocks * rows * wide),
        name="fold",
    )(keep, there, *deps)


def fold_pair(keep, there, deps=()):
    rows = keep[0].shape[1]
    widths = [k.shape[2] for k in keep]
    wide = sum(widths)

    def body(a, b, c, d, *rest):
        start = 0
        for p, q, n in ((a, c, widths[0]), (b, d, widths[1])):
            for at, out in enumerate(rest[len(deps) :]):
                four = slice(4 * at, 4 * at + 4)
                total = p[four].astype(F32) + q[four].astype(F32)
                out[:, :, start : start + n] = total.astype(BF16)
            start += n

    vmem = pl.BlockSpec(memory_space=pltpu.VMEM)
    return pl.pallas_call(
        body,
        in_specs=[vmem] * 4 + [AFTER] * len(deps),
        out_specs=[vmem] * 2,
        out_shape=[jax.ShapeDtypeStruct((4, rows, wide), BF16)] * 2,
        compiler_params=params(16, None),
        cost_estimate=cost(8 * rows * wide, 48 * rows * wide),
        name="fold_pair",
    )(*keep, *there, *deps)


def finish(parts, deps=()):
    rows = D // 32

    def body(a, b, c, d, *rest):
        qkv, out, gain, shift = rest[len(deps) :]
        total = a[0].astype(F32) + b[0].astype(F32) + c[0].astype(F32) + d[0].astype(F32)
        places = [0, 3 * GROUP, 6 * GROUP + TAIL]
        for i in range(3):
            at = [slice(p + i * GROUP, p + (i + 1) * GROUP) for p in places]
            qkv[:, i, :] = jnp.concatenate([total[:, p] for p in at], axis=1)
        start = 6 * GROUP
        out[...] = total[:, start : start + D]
        gain[...] = total[:, start + D : start + D + 2]
        shift[...] = total[:, start + D + 2 : start + D + 4]

    vmem = pl.BlockSpec(memory_space=pltpu.VMEM)
    shapes = [(rows, 3, D), (rows, D), (rows, 2), (rows, 2)]
    return pl.pallas_call(
        body,
        in_specs=[vmem] * 4 + [AFTER] * len(deps),
        out_specs=[vmem] * 4,
        out_shape=[jax.ShapeDtypeStruct(shape, F32) for shape in shapes],
        compiler_params=params(16, None),
        cost_estimate=cost(1 << 18, 1 << 20),
        name="finish",
    )(*parts, *deps)


def input_back(core, hidden_grad, projected, weights, deps=()):
    half = SEQ // 2 // BLOCK

    def body(c, hid, a, b, d, w, *rest):
        mine, leave, token = rest[-3:]
        token[...] = jnp.zeros_like(token)
        grads = jnp.concatenate([ref[i] for i in range(3) for ref in (a, b, d)], axis=1)
        total = hid[...] + dot_nt(grads, w[...])
        own = pl.program_id(0) // half == c[0]

        @pl.when(own)
        def _():
            mine[...] = total

        @pl.when(jnp.logical_not(own))
        def _():
            leave[...] = total

    row = pl.BlockSpec((BLOCK, D), lambda r, c: (r, 0))
    shape = jax.ShapeDtypeStruct((SEQ // 2, D), F32)
    return pl.pallas_call(
        body,
        grid_spec=pltpu.PrefetchScalarGridSpec(
            num_scalar_prefetch=1,
            grid=(SEQ // BLOCK,),
            in_specs=[row]
            + [pl.BlockSpec((3, BLOCK, GROUP), lambda r, c: (0, r, 0))] * 3
            + [pl.BlockSpec((D, 3 * D), lambda r, c: (0, 0))]
            + [AFTER] * len(deps),
            out_specs=[
                pl.BlockSpec((BLOCK, D), lambda r, c: (jnp.clip(r - half * c[0], 0, half - 1), 0)),
                pl.BlockSpec(
                    (BLOCK, D), lambda r, c: (jnp.clip(r - half * (1 - c[0]), 0, half - 1), 0)
                ),
                pl.BlockSpec((8, LANES), lambda r, c: (0, 0)),
            ],
        ),
        out_shape=[shape, shape, TOKEN],
        compiler_params=params(60),
        cost_estimate=cost(6 * SEQ * D * D, 16 << 20),
        name="input_back",
    )(core[None], hidden_grad, *projected, weights, *deps)


def middle(index, source, ctx, cot, pieces):
    def norm(v):
        center = v - jnp.mean(v, axis=1, keepdims=True)
        scale = lax.rsqrt(jnp.mean(center * center, axis=1, keepdims=True) + EPSILON)
        return center * scale, scale

    def norm_back(u, hat, scale, gain):
        g = u * gain
        return scale * (
            g - jnp.mean(g, axis=1, keepdims=True) - hat * jnp.mean(g * hat, axis=1, keepdims=True)
        )

    def body(idx, x, ctx0, ctx1, ctx2, cot, *refs):
        pieces, refs = refs[:8], refs[8:]
        out, out_leave, gu_own, gu_other, down_own, down_other, hid_out, att_out, ctxg_out, sums = refs[:10]
        (
            w, wo, tail, nrm, factors, acts, low_t, mlp_t, mlp_s, back_s, hat_s, scale_s, pair_s, sem,
        ) = refs[10:]
        step = pl.program_id(0)
        core = idx[32]
        few = D // 32

        def loads(kind, which):
            copies = []
            for rest in (2 * which, 2 * which + 1):
                for s in range(8):
                    block = idx[(0 if kind == "gate" else 33) + rest * 8 + s]
                    at = pl.ds(pl.multiple_of(block * 48, 16), 48)
                    n = rest * 8 + s
                    gate, down = pieces[rest], pieces[4 + rest]
                    if kind == "gate":
                        copies.append(
                            pltpu.make_async_copy(
                                gate.at[s], w.at[which, at, pl.ds(0, 2 * HIDDEN)], sem.at[n]
                            )
                        )
                    elif kind == "down":
                        copies.append(
                            pltpu.make_async_copy(
                                down.at[s, :, pl.ds(0, HIDDEN)],
                                w.at[which, at, pl.ds(2 * HIDDEN, HIDDEN)],
                                sem.at[32 + n],
                            )
                        )
                    else:
                        owner = core if which == 0 else 1 - core
                        for part in range(2):
                            copies.append(
                                pltpu.make_async_copy(
                                    down.at[s, pl.ds(part * few, few), pl.ds(HIDDEN, REST)],
                                    tail.at[part, block * 2 + owner],
                                    sem.at[64 + n + 32 * part],
                                )
                            )
            return copies

        def arrive(kind, which):
            @pl.when(step == 0)
            def _():
                for cp in loads(kind, which):
                    cp.wait()

        @pl.when(step == 0)
        def _():
            for which in range(2):
                for cp in loads("tail", which):
                    cp.start()
            for which in range(2):
                for kind in ("gate", "down"):
                    for cp in loads(kind, which):
                        cp.start()

        arrive("tail", 0)
        arrive("tail", 1)

        @pl.when(step == 0)
        def _():
            joined = jnp.concatenate(
                [tail[0].reshape(D, REST), tail[1].reshape(D, REST)], axis=1
            )
            wo[...] = joined[:, :D]
            nrm[...] = joined[:, D : D + LANES].astype(F32).T[:8]
            sums[...] = jnp.zeros_like(sums)

        gain1, gain2, shift1, shift2 = (nrm[i : i + 1, :] for i in range(4))

        @pl.when(step < STEPS)
        def _():
            rows = pl.ds(pl.multiple_of(step * ROWS, ROWS), ROWS)
            context = jnp.concatenate([ctx0[...], ctx1[...], ctx2[...]], axis=1)
            hidden_in = x[...].astype(F32) + dot_nn(context, wo[...])
            hat1, scale1 = norm(hidden_in)
            hat_s[rows, :] = hat1
            scale_s[rows, :] = scale1
            normed = hat1 * gain1 + shift1
            low = normed.astype(BF16)
            low_t[:, rows] = low.T
            total = normed
            for half in range(2):
                arrive("gate", half)
                arrive("down", half)
                for n in range(HIDDEN // CHUNK):
                    g_at, u_at, d_at = (pl.ds(p * HIDDEN + n * CHUNK, CHUNK) for p in range(3))
                    gate = dot_nn(low, w[half, :, g_at])
                    up = dot_nn(low, w[half, :, u_at])
                    s = jax.nn.sigmoid(gate)
                    silu = gate * s
                    act = (silu * up).astype(BF16)
                    factors[half, rows, g_at] = (up * (s * (1.0 + gate * (1.0 - s)))).astype(BF16)
                    factors[half, rows, u_at] = silu.astype(BF16)
                    acts[half, rows, g_at] = act
                    total = total + dot_nt(act, w[half, :, d_at])
            hat2, scale2 = norm(total)
            result = (hat2 * gain2 + shift2).astype(BF16)
            own = step // (STEPS // 2) == core

            @pl.when(own)
            def _():
                out[...] = result

            @pl.when(jnp.logical_not(own))
            def _():
                out_leave[...] = result

            u2 = cot[...].astype(F32)
            resid = norm_back(u2, hat2, scale2, gain2)
            mlp = resid.astype(BF16)
            mlp_s[rows, :] = mlp
            mlp_t[:, rows] = mlp.T
            back_s[rows, :] = resid
            sums[1:2, :] += jnp.sum(u2 * hat2, axis=0, keepdims=True)
            sums[3:4, :] += jnp.sum(u2, axis=0, keepdims=True)

        @pl.when(jnp.logical_and(step >= STEPS, step < STEPS + PIECES))
        def _():
            at = step - STEPS
            half = 1 - at // (PIECES // 2)
            n = at % (PIECES // 2)
            g_at, u_at, d_at = (
                pl.ds(pl.multiple_of(p * HIDDEN + n * PIECE, PIECE), PIECE) for p in range(3)
            )

            for r in range(STEPS):
                rows = pl.ds(r * ROWS, ROWS)
                grad = dot_nn(mlp_s[rows, :], w[half, :, d_at])
                gate_grad = (grad * factors[half, rows, g_at].astype(F32)).astype(BF16)
                up_grad = (grad * factors[half, rows, u_at].astype(F32)).astype(BF16)
                pair_s[0, rows, :] = gate_grad
                pair_s[1, rows, :] = up_grad
                back_s[rows, :] += dot_nt(gate_grad, w[half, :, g_at]) + dot_nt(
                    up_grad, w[half, :, u_at]
                )

            def store(gu, down):
                for i in range(2):
                    gu[i] = dot_nn(low_t[...], pair_s[i]).astype(BF16)
                down[0] = dot_nn(mlp_t[...], acts[half, :, g_at]).astype(BF16)

            @pl.when(half == 1)
            def _():
                store(gu_other, down_other)

            @pl.when(half == 0)
            def _():
                store(gu_own, down_own)

        @pl.when(step >= STEPS + PIECES)
        def _():
            r = step - STEPS - PIECES
            rows = pl.ds(pl.multiple_of(r * ROWS, ROWS), ROWS)
            back, hat1 = back_s[rows, :], hat_s[rows, :]
            hidden_grad = norm_back(back, hat1, scale_s[rows, :], gain1)
            hid_out[...] = hidden_grad
            att = hidden_grad.astype(BF16)
            att_out[...] = att
            ctxg_out[...] = dot_nt(att, wo[...]).astype(BF16)
            sums[0:1, :] += jnp.sum(back * hat1, axis=0, keepdims=True)
            sums[2:3, :] += jnp.sum(back, axis=0, keepdims=True)

    last = STEPS - 1
    row = lambda n: pl.BlockSpec((ROWS, n), lambda t, i: (jnp.minimum(t, last), 0))
    ending = pl.BlockSpec((ROWS, D), lambda t, i: (jnp.clip(t - STEPS - PIECES, 0, last), 0))
    half = STEPS // 2
    side = lambda t, mine: (jnp.clip(jnp.minimum(t, last) - half * mine, 0, half - 1), 0)
    mine = pl.BlockSpec((ROWS, D), lambda t, i: side(t, i[32]))
    leave = pl.BlockSpec((ROWS, D), lambda t, i: side(t, 1 - i[32]))
    each = PIECES // 2
    own = lambda lead: pl.BlockSpec(
        (lead, D, PIECE), lambda t, i: (0, 0, jnp.clip(t - STEPS - each, 0, each - 1))
    )
    theirs = lambda lead: pl.BlockSpec(
        (lead, D, PIECE), lambda t, i: (0, 0, jnp.clip(t - STEPS, 0, each - 1))
    )
    act = lambda n, t=BF16: jax.ShapeDtypeStruct((n, D), t)
    grads = lambda lead: jax.ShapeDtypeStruct((lead, D, HIDDEN), BF16)
    return pl.pallas_call(
        body,
        grid_spec=pltpu.PrefetchScalarGridSpec(
            num_scalar_prefetch=1,
            grid=(2 * STEPS + PIECES,),
            in_specs=[row(D)] + [row(GROUP)] * GROUPS + [row(D)] + [ANY] * 8,
            out_specs=[mine, leave, own(2), theirs(2), own(1), theirs(1)]
            + [ending] * 3
            + [pl.BlockSpec((8, D), lambda t, i: (0, 0))],
            scratch_shapes=[
                pltpu.VMEM((2, D, WIDE), BF16),
                pltpu.VMEM((D, D), BF16),
                pltpu.VMEM((2, 32, D // 32, REST), BF16),
                pltpu.VMEM((8, D), F32),
                pltpu.VMEM((2, SEQ, 2 * HIDDEN), BF16),
                pltpu.VMEM((2, SEQ, HIDDEN), BF16),
                pltpu.VMEM((D, SEQ), BF16),
                pltpu.VMEM((D, SEQ), BF16),
                pltpu.VMEM((SEQ, D), BF16),
                pltpu.VMEM((SEQ, D), F32),
                pltpu.VMEM((SEQ, D), F32),
                pltpu.VMEM((SEQ, 1), F32),
                pltpu.VMEM((2, SEQ, PIECE), BF16),
                pltpu.SemaphoreType.DMA((128,)),
            ],
        ),
        out_shape=[
            act(SEQ // 2),
            act(SEQ // 2),
            grads(2),
            grads(2),
            grads(1),
            grads(1),
            act(SEQ, F32),
            act(SEQ),
            act(SEQ),
            jax.ShapeDtypeStruct((8, D), F32),
        ],
        compiler_params=params(62),
        cost_estimate=cost(18 * SEQ * D * 2 * HIDDEN + 4 * SEQ * D * D, 40 << 20, 4 * SEQ * HIDDEN),
        name="middle",
    )(index, source, *ctx, cot, *pieces)


def rotary_lanes(segment_row):
    labels = jnp.arange(NDOC + 1, dtype=jnp.int32)
    before = jnp.sum((segment_row[None, :] < labels[:, None]).astype(jnp.int32), axis=1)
    member = segment_row[:, None] == labels[None, :]
    first = jnp.sum(jnp.where(member, before[None, :], 0), axis=1)
    position = (jnp.arange(SEQ, dtype=jnp.int32) - first).astype(F32)
    lane = jnp.arange(LANES) % (HEAD // 2)
    frequency = jnp.power(F32(1000.0), -2.0 * lane.astype(F32) / HEAD)
    angle = position[:, None] * frequency[None, :]
    sign = jnp.where(jnp.arange(LANES) % HEAD < HEAD // 2, -1.0, 1.0)
    ends = jnp.concatenate([before[1:], jnp.full((1,), SEQ, jnp.int32)])
    heads = segment_row[::BLOCK]
    tails = segment_row[BLOCK - 1 :: BLOCK]
    low = jnp.sum(jnp.where(heads[:, None] == labels[None, :], before[None, :], 0), axis=1)
    high = jnp.sum(jnp.where(tails[:, None] == labels[None, :], ends[None, :], 0), axis=1)
    bounds = jnp.concatenate([low // KEYS, (high + KEYS - 1) // KEYS]).astype(jnp.int32)
    return jnp.cos(angle), jnp.sin(angle) * sign[None, :], bounds


def sequence_device(
    tokens, segments, qkv_weight, out_weight, norm_gain, norm_shift, gate_up, down_weight, cotangent
):
    core = lax.axis_index("tensor")
    def ordered(mine, theirs):
        return jnp.where(
            core == 0, jnp.stack([mine, theirs], axis=0), jnp.stack([theirs, mine], axis=0)
        )

    pick = lambda a, i: lax.dynamic_index_in_dim(a, i, 0, keepdims=False)
    source = pick(tokens, core)
    segment_row = pick(segments, core)

    attn_block = qkv_weight.reshape(-1, 3 * D)
    gate_block = gate_up.reshape(-1, 2 * HIDDEN)
    tail_block = jnp.concatenate(
        [out_weight, norm_gain, norm_shift, jnp.zeros((D // 32, TAIL - D - 4), BF16)], axis=1
    )
    down_block = jnp.concatenate(
        [down_weight, jnp.concatenate([tail_block[:, :REST], tail_block[:, REST:]], axis=0)], axis=1
    )
    from_here, from_there = slot_blocks(-1, core), slot_blocks(-1, 1 - core)
    there_blocks = slot_blocks(1, core).reshape(2, 2, 4)
    to_here = there_blocks.transpose(1, 0, 2).reshape(16)
    deep_first = there_blocks.transpose(2, 1, 0).reshape(16)

    cot = ordered(pick(cotangent, core), core_swap(pick(cotangent, 1 - core))).reshape(SEQ, D)
    cosine, sine, bounds = rotary_lanes(segment_row)
    bounds = jnp.concatenate([bounds, core[None]]).astype(jnp.int32)
    tables = (cosine, sine, segment_row[:, None], segment_row[None, :])

    ahead = lambda parts: [part[None] for part in parts]
    gate_parts = depth_ring(gate_block)
    attn_four = pile(ahead(depth_parts(attn_block)), deps=(gate_parts[1],))
    attn_eight = pile(
        [attn_four, first_swap(attn_four)], deps=(gate_parts[2], source, cot, *tables)
    )
    attn_last = second_swap(attn_eight)
    index = jnp.concatenate([from_here * 2 + core, from_there * 2 + 1 - core]).astype(jnp.int32)
    weights = assemble(
        (attn_eight, attn_last),
        (core_swap(attn_eight), core_swap(attn_last)),
        index,
        deps=(gate_parts[3],),
    ).reshape(D, 3 * D)
    gate_four = pile(ahead(gate_parts))
    down_pair = pile([down_block[None], first_swap(down_block)[None]], deps=(gate_four,))
    saved0 = attn_forward(0, 1, bounds, source, weights, *tables, deps=(gate_four, down_pair))
    near, far = depth_shift(down_pair, 1), depth_shift(down_pair, 3)
    gate_eight = pile([gate_four, first_swap(gate_four)], deps=(saved0[4], near, far))
    gate_last = second_swap(gate_eight)
    saved1 = attn_forward(1, 1, bounds, source, weights, *tables, deps=(gate_eight,))
    down_eight = pile([down_pair, near, depth_shift(down_pair, 2), far], deps=(saved1[4],))
    saved2 = attn_forward(2, 1, bounds, source, weights, *tables, deps=(down_eight,))
    down_last, late_logs = lax.optimization_barrier((second_swap(down_eight), saved2[4]))
    saved2 = (*saved2[:4], late_logs)
    pieces = (gate_eight, gate_last, core_swap(gate_eight), core_swap(gate_last))
    pieces += (down_eight, down_last, core_swap(down_eight), core_swap(down_last))

    turned = lambda slots: slots.reshape(2, 2, 4).transpose(0, 2, 1).reshape(16)
    index = jnp.concatenate(
        [from_here, from_there, core[None], turned(from_here), turned(from_there)]
    ).astype(jnp.int32)
    ctx = (saved0[3], saved1[3], saved2[3])
    (out, out_leave, gu_here, gu_there, down_here, down_there, hidden_grad, att_grad, ctx_grad, sums) = (
        middle(index, source, ctx, cot, pieces)
    )

    gu_there, down_there = core_swap(gu_there), core_swap(down_there)
    output, placed = place(core, out, core_swap(out_leave))
    tail_mine, tail_theirs = out_grad(core, ctx, att_grad, sums)
    gu_keep, gu_send = join_rows(to_here, gu_here, gu_there, 2, deps=(tail_mine,))
    down_parts = join_rows(deep_first, down_here, down_there, 4, deps=(gu_send,))
    gu_first = first_swap(gu_send)
    passing = depth_shift(down_parts[3], 1)

    common = (source,) + tables
    back0 = attn_backward(0, 0, bounds, saved0, ctx_grad, *common, deps=(gu_send, down_parts[0], placed))
    (passing,) = fold(passing, down_parts[2], 1, deps=(back0[3],))
    back1 = attn_backward(0, 1, bounds, saved1, ctx_grad, *common, deps=(passing,))
    passing = depth_shift(passing, 1)
    (passing,) = fold(passing, down_parts[1], 1, deps=(back1[3],))
    gu_keep, gu_send = fold(gu_keep, gu_first, 2, deps=(back1[3],))
    gu_second = second_swap(gu_send)
    early_keep, early_send = join_dealt(
        to_here,
        (back0[1], back1[1], tail_mine),
        (core_swap(back0[2]), core_swap(back1[2]), core_swap(tail_theirs)),
        deps=(passing, gu_send),
    )
    early_first = first_swap(early_send)
    back2 = attn_backward(0, 2, bounds, saved2, ctx_grad, *common, deps=(gu_send, early_send, passing))

    deep = lambda parts: [parts[0]] + [depth_shift(parts[k], k) for k in (1, 2, 3)]
    passing = depth_shift(passing, 1)
    gu_parts = fold(gu_keep, gu_second, 4, deps=(back2[3],))
    down_keep, down_send = fold(passing, down_parts[0], 2, deps=(gu_parts[0],))
    late_keep, late_send = join_dealt(
        to_here, (back2[1],), (core_swap(back2[2]),), deps=(down_send, early_first)
    )
    late_first = first_swap(late_send)
    down_keep, down_send = fold(down_keep, first_swap(down_send), 2, deps=(late_send,))
    down_second = second_swap(down_send)
    (gu_total,) = fold(depth_shift(gu_parts[3], 1), gu_parts[2], 1, deps=(down_send,))
    attn_keep, attn_send = fold_pair(
        (early_keep, late_keep), (early_first, late_first), deps=(gu_total,)
    )
    attn_second = second_swap(attn_send)
    grad, grad_leave, added = input_back(
        core, hidden_grad, (back0[0], back1[0], back2[0]), weights, deps=(attn_send,)
    )
    (gu_total,) = fold(depth_shift(gu_total, 1), gu_parts[1], 1, deps=(added,))
    attn_parts = list(fold(attn_keep, attn_second, 4, deps=(gu_total,)))
    grad_leave, attn_parts[0] = lax.optimization_barrier((grad_leave, attn_parts[0]))
    attn_parts = deep(attn_parts)
    grad, placed = place(core, grad, core_swap(grad_leave))
    (gu_total,) = fold(depth_shift(gu_total, 1), gu_parts[0], 1, F32)
    down_total = (down_keep.astype(F32) + down_second.astype(F32))[0]
    gu_total = gu_total[0]
    qkv_total, out_total, gain_total, shift_total = finish(attn_parts, deps=(placed,))

    return (
        output,
        grad,
        qkv_total,
        out_total,
        gain_total,
        shift_total,
        gu_total.reshape(-1, 2, HIDDEN),
        down_total,
    )


def solution(mesh):
    in_specs = (
        P("dp", None, None),
        P("dp", None),
        P(("dp", "tensor"), None, None),
        P(("dp", "tensor"), None),
        P(("dp", "tensor"), None),
        P(("dp", "tensor"), None),
        P("dp", None, "tensor"),
        P("dp", "tensor"),
        P("dp", "tensor", None),
    )
    out_specs = (
        P("dp", "tensor", None),
        P("dp", "tensor", None),
        P(("dp", "tensor"), None, None),
        P(("dp", "tensor"), None),
        P(("dp", "tensor"), None),
        P(("dp", "tensor"), None),
        P("dp", None, "tensor"),
        P("dp", "tensor"),
    )
    sizes = dict(mesh.shape)

    def per_device(tokens, *others):
        if sizes["dp"] == 16 and sizes["tensor"] == 2 and tokens.shape[0] == 2:
            return sequence_device(tokens, *others)
        return general_device(tokens, *others)

    return jax.shard_map(
        per_device, mesh=mesh, in_specs=in_specs, out_specs=out_specs, check_vma=False
    )
```
